32 devices in a mesh: dp: 16 (over z, y, core), fsdp: 2 (over x).
Axes of the slice: x: 2, y: 2, z: 4, core: 2. Of those that a mesh axis runs over, the one named last changes fastest.
Arguments:
- tokens: bfloat16 [64, 512, 1536], P(('dp', 'fsdp')), may hold values from -6 to 6
- cotangent: bfloat16 [64, 512, 1536], P(('dp', 'fsdp')), may hold values from -6 to 6
- lengths: int32 [64], replicated, may hold values from 1 to 512, as said below
- balance: int32 [64], replicated, may hold values from 0 to 63, as said below
- norm_gain: float32 [1536], P(('dp', 'fsdp')), may hold values from 0.5 to 1.5
- in_weight: float32 [1536, 6448], P(('dp', 'fsdp')), may hold values from -0.15625 to 0.15625
- conv_weight: float32 [3328, 4], P(('dp', 'fsdp')), may hold values from -3 to 3
- conv_bias: float32 [3328], P(('dp', 'fsdp')), may hold values from -3 to 3
- step_bias: float32 [48], replicated, may hold values from -6.9 to -2.3
- decay_log: float32 [48], replicated, may hold values from 0 to 2.77
- skip_weight: float32 [48], replicated, may hold values from 0.5 to 1.5
- inner_gain: float32 [3072], P(('dp', 'fsdp')), may hold values from 0.5 to 1.5
- out_weight: float32 [3072, 1536], P(('dp', 'fsdp')), may hold values from -0.109375 to 0.109375
Outputs:
- output: bfloat16 [64, 512, 1536], P(('dp', 'fsdp'))
- input_grad: bfloat16 [64, 512, 1536], P(('dp', 'fsdp'))
- grad_norm_gain: float32 [1536], P(('dp', 'fsdp'))
- grad_in_weight: float32 [1536, 6448], P(('dp', 'fsdp'))
- grad_conv_weight: float32 [3328, 4], P(('dp', 'fsdp'))
- grad_conv_bias: float32 [3328], P(('dp', 'fsdp'))
- grad_step_bias: float32 [48], replicated
- grad_decay_log: float32 [48], replicated
- grad_skip_weight: float32 [48], replicated
- grad_inner_gain: float32 [3072], P(('dp', 'fsdp'))
- grad_out_weight: float32 [3072, 1536], P(('dp', 'fsdp'))
The draws below stay inside these ranges and needn't reach their ends.
Inputs may be any that keep to these rules, and one draw needn't show every extreme that they name: `lengths`: the longest slot has exactly 512 live positions. `balance`: a permutation; balanced slots 2d and 2d+1 stand on device d of the flat dp+fsdp order; balanced slot 2d is one of device d's own two loader slots, and balanced slot 2d+1 is the loader slot that device d's partner on dp (dp index differing in its lowest bit, same fsdp index) does not keep.
All inputs are finite; a program needn't handle non-finite values.
Results may differ from the reference program's by a relative error of at most 0.012.
Values may be sent and summed in bfloat16 or wider, within the bound.
A program may use at most 384 MiB of HBM per device.

```python
import jax
import jax.numpy as jnp
from jax import lax

D = 1536
INNER = 3072
HEADS = 48
HEADDIM = 64
STATE = 128
CONV = 4
BLOCK = 256
LMAX = 512
XBC = 3328
PROJ = 6448
SEQS = 64
PAIR_STRIDE = 2
DEVICES = 32


def draw_lengths(key, part):
    heavy_key = jax.random.fold_in(key, 11)
    long_key = jax.random.fold_in(key, 12)
    short_key = jax.random.fold_in(key, 13)
    device = jnp.arange(DEVICES, dtype=jnp.int32)
    pair_index = device // (2 * PAIR_STRIDE) * PAIR_STRIDE + device % PAIR_STRIDE
    coins = jax.random.randint(heavy_key, (DEVICES // 2,), 0, 2).astype(jnp.int32)
    heavy = device // PAIR_STRIDE % 2 == coins[pair_index]
    longer = jax.random.randint(long_key, (DEVICES, 2), LMAX // 2, LMAX + 1).astype(jnp.int32)
    shorter = jax.random.randint(short_key, (DEVICES, 2), 1, LMAX // 4 + 1).astype(jnp.int32)
    chosen = jnp.where(heavy[:, None], longer, shorter).reshape(SEQS)
    slot_index = jnp.arange(SEQS, dtype=jnp.int32)
    chosen = jnp.where(slot_index == 0, LMAX, chosen)
    chosen = jnp.where(slot_index == SEQS - 1, 1, chosen)
    return chosen.astype(jnp.int32)


def draw_balance(key, part):
    coin_key = jax.random.fold_in(key, 21)
    coins = jax.random.randint(coin_key, (DEVICES,), 0, 2).astype(jnp.int32)
    device = jnp.arange(DEVICES, dtype=jnp.int32)
    partner = jnp.where(device // PAIR_STRIDE % 2 == 0, device + PAIR_STRIDE, device - PAIR_STRIDE)
    first_slot = 2 * device + coins
    second_slot = 2 * partner + 1 - coins[partner]
    return jnp.stack([first_slot, second_slot], axis=1).reshape(SEQS).astype(jnp.int32)


def raised(values, key, source, target, blocks, factor):
    owner, partner = [(jnp.arange(values.shape[dim]) // (values.shape[dim] // blocks)).reshape([-1 if axis == dim else 1 for axis in range(values.ndim)]) for dim in (source, target)]
    chosen = jax.random.permutation(key, blocks)[partner]
    strong = (owner == chosen) | (owner == (partner + blocks // 2) % blocks)
    return jnp.where(strong, factor * values, values)


def levels(own_key, shape, pieces, smallest, top_value):
    gain, own = 1.0, jax.random.fold_in(own_key, 6)
    for dim, blocks in pieces:
        heights = jnp.exp(jax.random.uniform(jax.random.fold_in(own, dim), (blocks,), jnp.float32, smallest / len(pieces), top_value / len(pieces)))
        gain = gain * jnp.repeat(heights, shape[dim] // blocks).reshape([-1 if axis == dim else 1 for axis in range(len(shape))])
    return gain


def bell_draw(stream_key, shape, scale, most, cuts=(), kind=jnp.bfloat16):
    entries = scale * jax.random.normal(stream_key, shape, jnp.float32)
    if cuts:
        entries = entries * levels(stream_key, shape, cuts, -0.22, 0.18)
    return jnp.clip(entries, -most, most).astype(kind)


def heavy_noise(rng, dims, width, most, split, heavy, held_as=jnp.bfloat16):
    values = width * jax.random.normal(rng, dims, jnp.float32)
    if split:
        values = values * levels(rng, dims, split, -0.22, 0.18)
    return jnp.clip(raised(values, jax.random.fold_in(rng, 3), *heavy), -most, most).astype(held_as)


def setup_inputs(seed: int = 0) -> dict:
    key_list = jax.random.split(jax.random.key(seed), 14)
    return {
        "tokens": bell_draw(key_list[0], (SEQS, LMAX, D), 1.0, 6.0, ((0, 32),)),
        "cotangent": heavy_noise(key_list[1], (SEQS, LMAX, D), 1.0, 6.0, ((0, 32),), (0, 2, 32, 2.75)),
        "lengths": draw_lengths(jax.random.fold_in(key_list[13], 71), 0),
        "balance": draw_balance(jax.random.fold_in(key_list[13], 71), 0),
        "norm_gain": jnp.clip(1.0 + 0.1 * jax.random.normal(key_list[4], (D,), jnp.float32), 0.5, 1.5),
        "in_weight": bell_draw(key_list[5], (D, PROJ), D ** -0.5, 0.15625, ((0, 32),), jnp.float32),
        "conv_weight": bell_draw(key_list[6], (XBC, CONV), CONV ** -0.5, 3.0, ((0, 32),), jnp.float32),
        "conv_bias": bell_draw(key_list[7], (XBC,), 0.5, 3.0, ((0, 32),), jnp.float32),
        "step_bias": jnp.clip(jax.random.uniform(key_list[8], (HEADS,), jnp.float32, -6.9, -2.3), -6.9, -2.3),
        "decay_log": jnp.clip(jax.random.uniform(key_list[9], (HEADS,), jnp.float32, 0.0, 2.77), 0.0, 2.77),
        "skip_weight": jnp.clip(jax.random.uniform(key_list[10], (HEADS,), jnp.float32, 0.5, 1.5), 0.5, 1.5),
        "inner_gain": jnp.clip(1.0 + 0.1 * jax.random.normal(key_list[11], (INNER,), jnp.float32), 0.5, 1.5),
        "out_weight": bell_draw(key_list[12], (INNER, D), INNER ** -0.5, 0.109375, ((0, 32),), jnp.float32),
    }


highest = lax.Precision.HIGHEST
epsilon = 1e-05
group_slots = 8

@jax.custom_vjp
def low(v):
    return lax.optimization_barrier(v.astype(jnp.bfloat16)).astype(jnp.float32)

@jax.custom_vjp
def low_back(v):
    return v

def low_keep(v):
    return (low(v), None)

def low_pass(kept, grad):
    return (grad,)

def back_keep(v):
    return (v, None)

def back_low(kept, grad):
    return (low(grad),)
low.defvjp(low_keep, low_pass)
low_back.defvjp(back_keep, back_low)

def state_space(values, key_part, query_part, step_size, decay_rate):
    seq_length = values.shape[0]
    block_count = seq_length // BLOCK
    head_values = values.reshape(block_count, BLOCK, HEADS, HEADDIM)
    key_blocks = key_part.reshape(block_count, BLOCK, STATE)
    queries = query_part.reshape(block_count, BLOCK, STATE)
    step_blocks = jnp.transpose(step_size.reshape(block_count, BLOCK, HEADS), (0, 2, 1))
    cumulative = jnp.cumsum(step_blocks * decay_rate[None, :, None], axis=2)
    lower_mask = jnp.tril(jnp.ones((BLOCK, BLOCK), dtype=bool))
    spread = cumulative[:, :, :, None] - cumulative[:, :, None, :]
    decay_mask = jnp.exp(jnp.where(lower_mask, spread, -jnp.inf))
    scores = jnp.einsum('ctn,csn->cts', queries, key_blocks, precision=highest)
    mixing = scores[:, None, :, :] * decay_mask * step_blocks[:, :, None, :]
    inside = jnp.einsum('chts,cshp->cthp', mixing, head_values, precision=highest)
    tail_weight = jnp.exp(cumulative[:, :, -1:] - cumulative) * step_blocks
    weighted = head_values * jnp.transpose(tail_weight, (0, 2, 1))[:, :, :, None]
    block_states = jnp.einsum('cshp,csn->chpn', weighted, key_blocks, precision=highest)
    block_decay = jnp.exp(cumulative[:, :, -1])

    def carry_state(carried, inputs):
        new_state, factor = inputs
        return (carried * factor[:, None, None] + new_state, carried)
    _, entering = lax.scan(carry_state, jnp.zeros((HEADS, HEADDIM, STATE), values.dtype), (block_states, block_decay))
    across = jnp.einsum('ctn,chpn->cthp', queries, entering, precision=highest)
    across = across * jnp.transpose(jnp.exp(cumulative), (0, 2, 1))[:, :, :, None]
    return (inside + across).reshape(seq_length, HEADS, HEADDIM)

def mixer(projected, conv_weight, conv_bias, step_bias, decay_log, skip_weight, inner_gain):
    seq_length = projected.shape[0]
    gate_part = projected[:, :INNER]
    conv_input = projected[:, INNER:INNER + XBC]
    step_raw = projected[:, INNER + XBC:]
    padded = jnp.concatenate([jnp.zeros((CONV - 1, XBC), projected.dtype), conv_input], axis=0)
    conv_out = conv_bias + conv_weight[:, 0] * padded[0:seq_length]
    for offset in range(1, CONV):
        conv_out = conv_out + conv_weight[:, offset] * padded[offset:offset + seq_length]
    activated = jax.nn.silu(conv_out)
    values = activated[:, :INNER].reshape(seq_length, HEADS, HEADDIM)
    key_part = activated[:, INNER:INNER + STATE]
    query_part = activated[:, INNER + STATE:]
    step_size = jax.nn.softplus(step_raw + step_bias)
    decay_rate = -jnp.exp(decay_log)
    scanned = state_space(values, key_part, query_part, step_size, decay_rate) + skip_weight[None, :, None] * values
    gated = scanned.reshape(seq_length, INNER) * jax.nn.silu(gate_part)
    rms_scale = lax.rsqrt(lax.optimization_barrier(jnp.mean(gated * gated, axis=-1, keepdims=True)) + epsilon)
    return gated * rms_scale * inner_gain

def layer(group_x, group_len, norm_gain, in_weight, conv_weight, conv_bias, step_bias, decay_log, skip_weight, inner_gain, out_weight):
    norm_scale = lax.rsqrt(lax.optimization_barrier(jnp.mean(group_x * group_x, axis=-1, keepdims=True)) + epsilon)
    normed = low(group_x * norm_scale * low(norm_gain))
    projected = low_back(jnp.einsum('gld,df->glf', normed, low(in_weight), precision=highest))
    mixed = jax.vmap(mixer, in_axes=(0, None, None, None, None, None, None))(projected, low(conv_weight), low(conv_bias), step_bias, decay_log, skip_weight, low(inner_gain))
    branch = jnp.einsum('gle,ed->gld', low(mixed), low(out_weight), precision=highest)
    position = jnp.arange(group_x.shape[1])
    live_mask = position[None, :, None] < group_len[:, None, None]
    return jnp.where(live_mask, group_x + branch, 0.0)

def reference(tokens, cotangent, lengths, balance, norm_gain, in_weight, conv_weight, conv_bias, step_bias, decay_log, skip_weight, inner_gain, out_weight):
    weights = (norm_gain, in_weight, conv_weight, conv_bias, step_bias, decay_log, skip_weight, inner_gain, out_weight)
    group_count = SEQS // group_slots
    bal_x = tokens[balance].astype(jnp.float32).reshape(group_count, group_slots, LMAX, D)
    bal_len = lengths[balance].reshape(group_count, group_slots)
    bal_cot = cotangent.astype(jnp.float32).reshape(group_count, group_slots, LMAX, D)

    def group_step(totals, inputs):
        group_x, group_len, group_cot = inputs

        def forward(x_value, *params):
            return layer(x_value, group_len, *params)
        result, pull_back = jax.vjp(forward, group_x, *weights)
        gradients = pull_back(group_cot)
        summed = tuple((before + added for before, added in zip(totals, gradients[1:])))
        return (summed, (result.astype(jnp.bfloat16), gradients[0].astype(jnp.bfloat16)))
    start_totals = tuple((jnp.zeros_like(weight_item) for weight_item in weights))
    totals, (results, back_grads) = lax.scan(group_step, start_totals, (bal_x, bal_len, bal_cot))
    output = results.reshape(SEQS, LMAX, D)
    input_grad = jnp.zeros((SEQS, LMAX, D), jnp.bfloat16).at[balance].set(back_grads.reshape(SEQS, LMAX, D))
    return (output, input_grad, totals[0], totals[1], totals[2], totals[3], totals[4], totals[5], totals[6], totals[7], totals[8])
```

```python
import functools
import jax
import jax.numpy as jnp
from jax import lax
from jax.experimental import pallas as pl
from jax.experimental.pallas import tpu as pltpu
from jax.sharding import PartitionSpec as P

D = 1536
INNER = 3072
HEADS = 48
HEADDIM = 64
STATE = 128
CONV = 4
XBC = 3328
PROJ = 6448
XE = XBC + 128
Q = 128
PAIRS = HEADS // 2

f32 = jnp.float32
bf16 = jnp.bfloat16
epsilon = 1e-05
AXES = ("dp", "fsdp")


def sigmoid(v):
    return 0.5 * jnp.tanh(0.5 * v) + 0.5


def dot_nn(a, b, precision=None):
    return jnp.dot(a, b, preferred_element_type=f32, precision=precision)


def dot_nt(a, b):
    return lax.dot_general(a, b, (((1,), (1,)), ((), ())), preferred_element_type=f32)


def dot_tn(a, b):
    return lax.dot_general(a, b, (((0,), (0,)), ((), ())), preferred_element_type=f32)


def lane_iota(shape):
    return lax.broadcasted_iota(jnp.int32, shape, len(shape) - 1)


def row_iota(shape):
    return lax.broadcasted_iota(jnp.int32, shape, len(shape) - 2)


def source_chunk(meta, k, slot_chunks):
    return jnp.where(k < meta[1], k, k - meta[1] + slot_chunks)


def live_rows(meta, k):
    inside = k < meta[1]
    return jnp.where(inside, meta[2] - k * Q, meta[3] - (k - meta[1]) * Q)


def last_live(meta, k):
    return jnp.minimum(k, meta[0] - 1)


def last_padded(meta, k):
    return jnp.minimum(k, meta[0] + lax.rem(meta[0], 2) - 1)


def for_blocks(total, blocks, body):
    for b in range(blocks):
        pl.when(total >= 2 * b + 2)(functools.partial(body, b, 2 * Q))
        pl.when(total == 2 * b + 1)(functools.partial(body, b, Q))


def cost(flops, moved, transcendentals=0):
    return pl.CostEstimate(flops=int(flops), bytes_accessed=int(moved), transcendentals=int(transcendentals))


def params(**kw):
    return pltpu.CompilerParams(vmem_limit_bytes=60 * 1024 * 1024, **kw)


def project_kernel(slot_chunks, steps, tile, meta, u_ref, g_ref, w_ref, proj_ref, e_ref, ht_ref, h_ref):
    j = pl.program_id(0)
    total = meta[0]
    chunks = 2 * slot_chunks

    @pl.when(j == 0)
    def _():
        for k in range(chunks):

            @pl.when(k < total)
            def _():
                start = pl.multiple_of(source_chunk(meta, k, slot_chunks) * Q, Q)
                x = u_ref[pl.ds(start, Q), :].astype(f32)
                scale = lax.rsqrt(jnp.mean(x * x, axis=-1, keepdims=True) + epsilon)
                normed = x * scale * g_ref[...]
                h_ref[k * Q : (k + 1) * Q, :] = normed.astype(bf16)
                ht_ref[:, k * Q : (k + 1) * Q] = normed.T.astype(bf16)

            @pl.when(k >= total)
            def _():
                ht_ref[:, k * Q : (k + 1) * Q] = jnp.zeros((D, Q), bf16)

    edge = XBC + INNER - (steps - 1) * tile

    def block(b, rows):
        r = slice(b * 2 * Q, b * 2 * Q + rows)
        acc = dot_nn(h_ref[r, :], w_ref[...])
        proj_ref[r, :] = acc.astype(bf16)

        @pl.when(j == steps - 1)
        def _():
            tail = dot_nn(h_ref[r, :], w_ref[:, edge : edge + 128])
            e_ref[r, :] = jnp.where(lane_iota(tail.shape) < HEADS, tail, 0.0)

    for_blocks(total, chunks // 2, block)


def project(meta, u, g1, w1):
    rows = u.shape[0]
    tile = 512
    steps = pl.cdiv(PROJ, tile)
    return pl.pallas_call(
        functools.partial(project_kernel, rows // Q // 2, steps, tile),
        out_shape=(
            jax.ShapeDtypeStruct((rows, PROJ), bf16),
            jax.ShapeDtypeStruct((rows, 128), f32),
            jax.ShapeDtypeStruct((D, rows), bf16),
        ),
        grid_spec=pltpu.PrefetchScalarGridSpec(
            num_scalar_prefetch=1,
            grid=(steps,),
            in_specs=[
                pl.BlockSpec((rows, D), lambda j, m: (0, 0)),
                pl.BlockSpec((1, D), lambda j, m: (0, 0)),
                pl.BlockSpec((D, tile), lambda j, m: (0, j)),
            ],
            out_specs=[
                pl.BlockSpec((rows, tile), lambda j, m: (0, j)),
                pl.BlockSpec((rows, 128), lambda j, m: (0, 0)),
                pl.BlockSpec((D, rows), lambda j, m: (0, 0)),
            ],
            scratch_shapes=[pltpu.VMEM((rows, D), bf16)],
        ),
        compiler_params=params(),
        cost_estimate=cost(2 * rows * D * PROJ, 2 * (D * PROJ + rows * PROJ)),
        name="project",
    )(meta, u, g1, w1)


def conv_tile(buf, wc_ref, lanes):
    c = wc_ref[CONV : CONV + 1, lanes]
    for tap in range(CONV):
        c = c + wc_ref[tap : tap + 1, lanes] * buf[5 + tap : 5 + tap + Q, lanes]
    return c


def step_sizes(e_ref, par_ref):
    raw = e_ref[...] + par_ref[0:1, :]
    dt = jnp.maximum(raw, 0.0) + jnp.log1p(jnp.exp(-jnp.abs(raw)))
    decay = par_ref[1:2, :]
    lower = (row_iota((Q, Q)) >= lane_iota((Q, Q))).astype(f32)
    cum = dot_nn(lower, dt * decay, precision=lax.Precision.HIGHEST)
    return raw, dt, cum


def spread_heads(cum, dt, col_ref, dtp_ref):
    low = lane_iota((Q, 128)) < HEADDIM
    for p in range(PAIRS):
        for h in (2 * p, 2 * p + 1):
            col_ref[h] = jnp.broadcast_to(cum[:, h : h + 1], (Q, 128))
        dtp_ref[p] = jnp.where(
            low,
            jnp.broadcast_to(dt[:, 2 * p : 2 * p + 1], (Q, 128)),
            jnp.broadcast_to(dt[:, 2 * p + 1 : 2 * p + 2], (Q, 128)),
        )


def split_pair(v, low):
    zero = jnp.zeros_like(v)
    return jnp.concatenate([jnp.where(low, v, zero), jnp.where(low, zero, v)], axis=0)


def mixer_kernel(
    unroll, meta, proj_ref, e_ref, wc_ref, par_ref, skip_ref, g_ref,
    o_ref, ot_ref, y_ref, sin_ref,
    buf, state, col_ref, dtp_ref, row_ref, q_ref,
):
    k = pl.program_id(0)
    total = meta[0]

    @pl.when((k == total) & (lax.rem(total, 2) == 1))
    def _():
        o_ref[...] = jnp.zeros_like(o_ref)
        ot_ref[...] = jnp.zeros_like(ot_ref)

    @pl.when(k < total)
    def _():
        first = (k == 0) | (k == meta[1])

        @pl.when(first)
        def _():
            buf[0:8, :] = jnp.zeros((8, XBC), f32)
            state[...] = jnp.zeros_like(state)

        @pl.when(jnp.logical_not(first))
        def _():
            buf[0:8, :] = buf[Q : Q + 8, :]

        buf[8 : 8 + Q, :] = proj_ref[:, INNER : INNER + XBC].astype(f32)
        tail_lanes = slice(INNER, XBC)
        c = conv_tile(buf, wc_ref, tail_lanes)
        act = c * sigmoid(c)
        keys = act[:, :STATE]
        queries = act[:, STATE:].astype(bf16)
        keys_t = keys.T.astype(bf16)
        scores = dot_nn(queries, keys_t)
        _, dt, cum = step_sizes(e_ref, par_ref)
        row_ref[...] = cum.T
        spread_heads(cum, dt, col_ref, dtp_ref)
        lower = row_iota((Q, Q)) >= lane_iota((Q, Q))
        low = lane_iota((Q, 128)) < HEADDIM
        scores = jnp.where(lower, scores, 0.0)

        def pair(p):
            lanes = pl.ds(pl.multiple_of(p * 128, 128), 128)
            c = conv_tile(buf, wc_ref, lanes)
            values = c * sigmoid(c)
            col0, col1 = col_ref[2 * p], col_ref[2 * p + 1]
            both = jnp.where(low, col0, col1)
            end = both[Q - 1 : Q, :]
            stepped = values * dtp_ref[p]
            parts = split_pair(stepped.astype(bf16), low)
            mix = []
            for n, col in enumerate((col0, col1)):
                decay = jnp.exp(jnp.minimum(col - row_ref[pl.ds(2 * p + n, 1), :], 0.0))
                mix.append((scores * decay).astype(bf16))
            y = dot_nn(jnp.concatenate(mix, axis=1), parts)
            before = state[:, lanes]
            before_low = before.astype(bf16)
            sin_ref[0, :, lanes] = before_low
            y = y + dot_nn(queries, before_low) * jnp.exp(both)
            y = y + skip_ref[:, lanes] * values
            state[:, lanes] = before * jnp.exp(end) + dot_nn(
                keys_t, (stepped * jnp.exp(end - both)).astype(bf16)
            )
            z = proj_ref[:, lanes].astype(f32)
            gated = y * (z * sigmoid(z))
            y_ref[:, lanes] = y.astype(bf16)
            q_ref[:, lanes] = gated
            return gated * gated

        def body(i, squares):
            for n in range(unroll):
                squares = squares + pair(i * unroll + n)
            return squares

        squares = lax.fori_loop(0, PAIRS // unroll, body, jnp.zeros((Q, 128), f32))
        scale = lax.rsqrt(jnp.sum(squares, axis=-1, keepdims=True) / INNER + epsilon)

        def finish(p, _):
            lanes = pl.ds(pl.multiple_of(p * 128, 128), 128)
            out = q_ref[:, lanes] * scale * g_ref[:, lanes]
            o_ref[:, lanes] = out.astype(bf16)
            ot_ref[lanes, :] = out.T.astype(bf16)
            return 0

        lax.fori_loop(0, PAIRS, finish, 0, unroll=2)


def mixer(meta, proj, e, wc, par, skip, g2):
    rows = proj.shape[0]
    chunks = rows // Q
    const = lambda k, m: (0, 0)
    live = lambda k, m: (last_live(m, k), 0)
    return pl.pallas_call(
        functools.partial(mixer_kernel, 2),
        out_shape=(
            jax.ShapeDtypeStruct((rows, INNER), bf16),
            jax.ShapeDtypeStruct((INNER, rows), bf16),
            jax.ShapeDtypeStruct((rows, INNER), bf16),
            jax.ShapeDtypeStruct((chunks, STATE, INNER), bf16),
        ),
        grid_spec=pltpu.PrefetchScalarGridSpec(
            num_scalar_prefetch=1,
            grid=(chunks,),
            in_specs=[
                pl.BlockSpec((Q, PROJ), live),
                pl.BlockSpec((Q, 128), live),
                pl.BlockSpec((8, XBC), const),
                pl.BlockSpec((8, 128), const),
                pl.BlockSpec((1, INNER), const),
                pl.BlockSpec((1, INNER), const),
            ],
            out_specs=[
                pl.BlockSpec((Q, INNER), lambda k, m: (last_padded(m, k), 0)),
                pl.BlockSpec((INNER, Q), lambda k, m: (0, last_padded(m, k))),
                pl.BlockSpec((Q, INNER), live),
                pl.BlockSpec((1, STATE, INNER), lambda k, m: (last_live(m, k), 0, 0)),
            ],
            scratch_shapes=[
                pltpu.VMEM((Q + 8, XBC), f32),
                pltpu.VMEM((STATE, INNER), f32),
                pltpu.VMEM((HEADS, Q, 128), f32),
                pltpu.VMEM((PAIRS, Q, 128), f32),
                pltpu.VMEM((128, Q), f32),
                pltpu.VMEM((Q, INNER), f32),
            ],
        ),
        compiler_params=params(),
        cost_estimate=cost(chunks * PAIRS * 8 * 2 * Q * 128 * 128, 2 * rows * (PROJ + 3 * INNER)),
        name="mixer",
    )(meta, proj, e, wc, par, skip, g2)


def gate_kernel(
    slot_chunks, meta, u_ref, cot_ref, w_ref, o_ref, y_ref, z_ref, g_ref,
    out_ref, err_ref, dy_ref, dz_ref, gi_ref,
    do_ref,
):
    b = pl.program_id(0)
    total = meta[0]

    @pl.when(b == 0)
    def _():
        out_ref[...] = jnp.zeros_like(out_ref)
        gi_ref[...] = jnp.zeros_like(gi_ref)

    def body(rows):
        halves = rows // Q
        if halves == 1:
            err_ref[Q:, :] = jnp.zeros((Q, D), bf16)
            dz_ref[Q:, :] = jnp.zeros((Q, INNER), bf16)
        starts = []
        for n in range(halves):
            k = 2 * b + n
            start = pl.multiple_of(source_chunk(meta, k, slot_chunks) * Q, Q)
            starts.append(start)
            cot = cot_ref[pl.ds(start, Q), :]
            live = row_iota((Q, D)) < live_rows(meta, k)
            err_ref[n * Q : (n + 1) * Q, :] = jnp.where(live, cot.astype(f32), 0.0).astype(bf16)
        branch = dot_nn(o_ref[0:rows, :], w_ref[...])
        for n in range(halves):
            live = row_iota((Q, D)) < live_rows(meta, 2 * b + n)
            here = pl.ds(starts[n], Q)
            value = u_ref[here, :].astype(f32) + branch[n * Q : (n + 1) * Q, :]
            out_ref[here, :] = jnp.where(live, value, 0.0).astype(bf16)
        do_ref[0:rows, :] = dot_nt(err_ref[0:rows, :], w_ref[...])

        def sums(p, carry):
            squares, crossed = carry
            lanes = pl.ds(pl.multiple_of(p * 128, 128), 128)
            z = z_ref[0:rows, lanes].astype(f32)
            q = y_ref[0:rows, lanes].astype(f32) * (z * sigmoid(z))
            return squares + q * q, crossed + q * g_ref[:, lanes] * do_ref[0:rows, lanes]

        zero = jnp.zeros((rows, 128), f32)
        squares, crossed = lax.fori_loop(0, PAIRS, sums, (zero, zero), unroll=2)
        scale = lax.rsqrt(jnp.sum(squares, axis=-1, keepdims=True) / INNER + epsilon)
        factor = scale * scale * scale * (jnp.sum(crossed, axis=-1, keepdims=True) / INNER)

        def back(p, _):
            lanes = pl.ds(pl.multiple_of(p * 128, 128), 128)
            z = z_ref[0:rows, lanes].astype(f32)
            y = y_ref[0:rows, lanes].astype(f32)
            s = sigmoid(z)
            gate = z * s
            q = y * gate
            do = do_ref[0:rows, lanes]
            gi_ref[:, lanes] += jnp.sum(do * q * scale, axis=0, keepdims=True)
            dq = scale * (g_ref[:, lanes] * do) - q * factor
            dy_ref[0:rows, lanes] = (dq * gate).astype(bf16)
            dz_ref[0:rows, lanes] = (dq * y * (s * (1.0 + z * (1.0 - s)))).astype(bf16)
            return 0

        lax.fori_loop(0, PAIRS, back, 0, unroll=2)

    pl.when(total >= 2 * b + 2)(functools.partial(body, 2 * Q))
    pl.when(total == 2 * b + 1)(functools.partial(body, Q))


def last_block(m, b):
    return jnp.minimum(b, (m[0] + 1) // 2 - 1)


def gate(meta, u, cot, w2, o, y, proj, g2):
    rows = u.shape[0]
    blocks = rows // (2 * Q)
    const = lambda b, m: (0, 0)
    live = lambda b, m: (last_block(m, b), 0)
    once = pl.Buffered(1)
    return pl.pallas_call(
        functools.partial(gate_kernel, rows // Q // 2),
        out_shape=(
            jax.ShapeDtypeStruct((rows, D), bf16),
            jax.ShapeDtypeStruct((rows, D), bf16),
            jax.ShapeDtypeStruct((rows, INNER), bf16),
            jax.ShapeDtypeStruct((rows, INNER), bf16),
            jax.ShapeDtypeStruct((1, INNER), f32),
        ),
        grid_spec=pltpu.PrefetchScalarGridSpec(
            num_scalar_prefetch=1,
            grid=(blocks,),
            in_specs=[
                pl.BlockSpec((rows, D), const, pipeline_mode=once),
                pl.BlockSpec((rows, D), const, pipeline_mode=once),
                pl.BlockSpec((INNER, D), const, pipeline_mode=once),
                pl.BlockSpec((2 * Q, INNER), live),
                pl.BlockSpec((2 * Q, INNER), live),
                pl.BlockSpec((2 * Q, INNER), live),
                pl.BlockSpec((1, INNER), const),
            ],
            out_specs=[
                pl.BlockSpec((rows, D), const),
                pl.BlockSpec((2 * Q, D), live),
                pl.BlockSpec((2 * Q, INNER), live),
                pl.BlockSpec((2 * Q, INNER), live),
                pl.BlockSpec((1, INNER), const),
            ],
            scratch_shapes=[pltpu.VMEM((2 * Q, INNER), f32)],
        ),
        compiler_params=params(),
        cost_estimate=cost(4 * rows * D * INNER, 2 * (D * INNER + 5 * rows * INNER)),
        name="gate",
    )(meta, u, cot, w2, o, y, proj, g2)


def back_kernel(
    unroll, chunks, meta, x_ref, prev_ref, e_ref, dy_ref, sin_ref, wc_ref, par_ref, skip_ref,
    dx_ref, gconv_ref, gpar_ref, gskip_ref,
    buf, dbuf, dstate, col_ref, dtp_ref, row_ref, da_ref,
):
    i = pl.program_id(0)
    total = meta[0]
    k = total - i

    @pl.when(i == 0)
    def _():
        gconv_ref[...] = jnp.zeros_like(gconv_ref)
        gpar_ref[...] = jnp.zeros_like(gpar_ref)
        gskip_ref[...] = jnp.zeros_like(gskip_ref)
        da_ref[...] = jnp.zeros_like(da_ref)

        @pl.when(lax.rem(total, 2) == 1)
        def _():
            dx_ref[...] = jnp.zeros_like(dx_ref)

    @pl.when((i >= 1) & (i <= total))
    def _():
        first = (k == 0) | (k == meta[1])
        last = (k == total - 1) | (k == meta[1] - 1)

        @pl.when(first)
        def _():
            buf[0:8, :] = jnp.zeros((8, XBC), f32)

        @pl.when(jnp.logical_not(first))
        def _():
            buf[0:8, :] = prev_ref[8:16, INNER : INNER + XBC].astype(f32)

        @pl.when(last)
        def _():
            dbuf[Q : Q + 8, :] = jnp.zeros((8, XBC), f32)
            dstate[...] = jnp.zeros_like(dstate)

        @pl.when(jnp.logical_not(last))
        def _():
            dbuf[Q : Q + 8, :] = dbuf[0:8, :]

        buf[8 : 8 + Q, :] = x_ref[:, INNER : INNER + XBC].astype(f32)
        tail_lanes = slice(INNER, XBC)
        c_tail = conv_tile(buf, wc_ref, tail_lanes)
        s_tail = sigmoid(c_tail)
        act = c_tail * s_tail
        keys = act[:, :STATE].astype(bf16)
        queries = act[:, STATE:].astype(bf16)
        queries_t = act[:, STATE:].T.astype(bf16)
        scores = dot_nn(keys, queries_t)
        raw, dt, cum = step_sizes(e_ref, par_ref)
        row_ref[...] = cum.T
        spread_heads(cum, dt, col_ref, dtp_ref)
        upper = row_iota((Q, Q)) <= lane_iota((Q, Q))
        strict = row_iota((Q, Q)) < lane_iota((Q, Q))
        after = (row_iota((Q, Q)) >= lane_iota((Q, Q))).astype(bf16)
        low = lane_iota((Q, 128)) < HEADDIM
        scores = jnp.where(upper, scores, 0.0)
        half = (lax.broadcasted_iota(jnp.int32, (128, 128), 0) >= HEADDIM).astype(jnp.int32)
        head_lane = lane_iota((128, 128))

        def conv_back(lanes, dc):
            dbuf[0:Q, lanes] = dc
            dxbc = wc_ref[CONV - 1 : CONV, lanes] * dc
            for tap in range(CONV - 1):
                dxbc = dxbc + wc_ref[tap : tap + 1, lanes] * dbuf[3 - tap : 3 - tap + Q, lanes]
            dx_ref[:, lanes] = dxbc.astype(bf16)
            for tap in range(CONV):
                gconv_ref[tap : tap + 1, lanes] += jnp.sum(dc * buf[5 + tap : 5 + tap + Q, lanes], axis=0, keepdims=True)
            gconv_ref[CONV : CONV + 1, lanes] += jnp.sum(dc, axis=0, keepdims=True)

        def pair(p, carry):
            dscores, dquery, dkey, from_start, to_end, direct, thru = carry
            lanes = pl.ds(pl.multiple_of(p * 128, 128), 128)
            c = conv_tile(buf, wc_ref, lanes)
            s = sigmoid(c)
            values = c * s
            col0, col1 = col_ref[2 * p], col_ref[2 * p + 1]
            both = jnp.where(low, col0, col1)
            end = both[Q - 1 : Q, :]
            grown = jnp.exp(both)
            rest = jnp.exp(end - both)
            dtp = dtp_ref[p]
            stepped = values * dtp
            dy_low = dy_ref[:, lanes]
            dy = dy_low.astype(f32)
            parts = split_pair(dy_low, low)
            stepped_low = stepped.astype(bf16)
            dmix = dot_nt(stepped_low, parts)
            mix = []
            for n, col in enumerate((col0, col1)):
                decay = jnp.exp(jnp.minimum(row_ref[pl.ds(2 * p + n, 1), :] - col, 0.0))
                weighted = dmix[:, n * Q : (n + 1) * Q] * decay
                dscores = dscores + weighted
                mix.append((scores * decay).astype(bf16))
                passed = dot_nn((weighted * scores).astype(bf16), after)
                da_ref[pl.ds(2 * p + n, 1), :] = jnp.sum(jnp.where(strict, passed, 0.0), axis=0, keepdims=True)
            dstepped = dot_nn(jnp.concatenate(mix, axis=1), parts)
            dafter = dstate[:, lanes]
            dafter_low = dafter.astype(bf16)
            before_low = sin_ref[0, :, lanes]
            dend = dot_nn(keys, dafter_low) * rest
            grown_dy = (dy * grown).astype(bf16)
            select = (head_lane == 2 * p + half).astype(bf16)
            across = dot_nn(queries, before_low)
            from_start = from_start + dot_nn((across * grown * dy).astype(bf16), select)
            to_end = to_end + dot_nn((stepped * dend).astype(bf16), select)
            dstepped = dstepped + dend
            direct = direct + dot_nn((values * dstepped).astype(bf16), select)
            dquery = dquery + dot_nt(grown_dy, before_low)
            dkey = dkey + dot_nt((stepped * rest).astype(bf16), dafter_low)
            kept = jnp.exp(end) * dafter
            held = jnp.sum((kept * before_low.astype(f32)).reshape(8, 16, 128), axis=0)
            thru = thru + dot_nn(held.astype(bf16), select)
            dstate[:, lanes] = kept + dot_nn(queries_t, grown_dy)
            dvalues = dstepped * dtp + skip_ref[:, lanes] * dy
            gskip_ref[:, lanes] += jnp.sum(dy * values, axis=0, keepdims=True)
            conv_back(lanes, dvalues * (s * (1.0 + c * (1.0 - s))))
            return dscores, dquery, dkey, from_start, to_end, direct, thru

        def body(n, carry):
            for m in range(unroll):
                carry = pair(n * unroll + m, carry)
            return carry

        zero = jnp.zeros((Q, 128), f32)
        start = (zero,) * 6 + (jnp.zeros((16, 128), f32),)
        carry = lax.fori_loop(0, PAIRS // unroll, body, start)
        dscores, dquery, dkey, from_start, to_end, direct, thru = carry
        dscores = jnp.where(upper, dscores, 0.0)
        dkey = dkey + dot_nn(dscores.astype(bf16), queries)
        dquery = dquery + dot_nn(dscores.T.astype(bf16), keys)
        slope = s_tail * (1.0 + c_tail * (1.0 - s_tail))
        conv_back(slice(INNER, INNER + STATE), dkey * slope[:, :STATE])
        conv_back(slice(INNER + STATE, XBC), dquery * slope[:, STATE:])

        tail_sum = (row_iota((Q, Q)) <= lane_iota((Q, Q))).astype(f32)
        head_sum = (row_iota((Q, Q)) > lane_iota((Q, Q))).astype(f32)
        da = (
            da_ref[...].T
            + dot_nn(tail_sum, from_start, precision=lax.Precision.HIGHEST)
            + dot_nn(head_sum, to_end, precision=lax.Precision.HIGHEST)
            + jnp.sum(thru, axis=0, keepdims=True)
        )
        ddt = par_ref[1:2, :] * da + direct
        de = ddt * sigmoid(raw)
        de = jnp.where(lane_iota((Q, 128)) < HEADS, de, 0.0)
        dx_ref[:, XBC:] = de.astype(bf16)
        gpar_ref[0:1, :] += jnp.sum(de, axis=0, keepdims=True)
        gpar_ref[1:2, :] += jnp.sum(dt * da, axis=0, keepdims=True)


def back(meta, proj, e, dy, sin, wc, par, skip):
    rows = proj.shape[0]
    chunks = rows // Q
    const = lambda i, m: (0, 0)

    def chunk(i, m):
        return jnp.clip(m[0] - i, 0, m[0] - 1)

    def padded(i, m):
        return jnp.where(i == 0, last_padded(m, m[0]), chunk(i, m))

    here = lambda i, m: (chunk(i, m), 0)
    return pl.pallas_call(
        functools.partial(back_kernel, 2, chunks),
        out_shape=(
            jax.ShapeDtypeStruct((rows, XE), bf16),
            jax.ShapeDtypeStruct((8, XBC), f32),
            jax.ShapeDtypeStruct((8, 128), f32),
            jax.ShapeDtypeStruct((1, INNER), f32),
        ),
        grid_spec=pltpu.PrefetchScalarGridSpec(
            num_scalar_prefetch=1,
            grid=(chunks + 1,),
            in_specs=[
                pl.BlockSpec((Q, PROJ), here),
                pl.BlockSpec((16, PROJ), lambda i, m: (jnp.maximum(chunk(i, m) * (Q // 16) - 1, 0), 0)),
                pl.BlockSpec((Q, 128), here),
                pl.BlockSpec((Q, INNER), here),
                pl.BlockSpec((1, STATE, INNER), lambda i, m: (chunk(i, m), 0, 0)),
                pl.BlockSpec((8, XBC), const),
                pl.BlockSpec((8, 128), const),
                pl.BlockSpec((1, INNER), const),
            ],
            out_specs=[
                pl.BlockSpec((Q, XE), lambda i, m: (padded(i, m), 0)),
                pl.BlockSpec((8, XBC), const),
                pl.BlockSpec((8, 128), const),
                pl.BlockSpec((1, INNER), const),
            ],
            scratch_shapes=[
                pltpu.VMEM((Q + 8, XBC), f32),
                pltpu.VMEM((Q + 8, XBC), f32),
                pltpu.VMEM((STATE, INNER), f32),
                pltpu.VMEM((HEADS, Q, 128), f32),
                pltpu.VMEM((PAIRS, Q, 128), f32),
                pltpu.VMEM((128, Q), f32),
                pltpu.VMEM((128, Q), f32),
            ],
        ),
        compiler_params=params(),
        cost_estimate=cost(chunks * PAIRS * 20 * 2 * Q * 128 * 128, 2 * rows * (PROJ + 3 * INNER)),
        name="back",
    )(meta, proj, proj, e, dy, sin, wc, par, skip)


def weight_kernel(rows, block, meta, at_ref, b_ref, out_ref):
    used = (meta[0] + 1) // 2
    height = at_ref.shape[0]

    def part(width):
        def step(m, _):
            here = pl.ds(pl.multiple_of(m * block, block), block)
            out_ref[here, :] = dot_nn(at_ref[here, 0:width], b_ref[0:width, :]).astype(bf16)
            return 0

        lax.fori_loop(0, height // block, step, 0)

    for n in range(1, rows // (2 * Q) + 1):
        pl.when(used == n)(functools.partial(part, n * 2 * Q))


def weight_grad(meta, at, b, width, tile, block=512):
    height, rows = at.shape
    return pl.pallas_call(
        functools.partial(weight_kernel, rows, block),
        out_shape=jax.ShapeDtypeStruct((height, width), bf16),
        grid_spec=pltpu.PrefetchScalarGridSpec(
            num_scalar_prefetch=1,
            grid=(pl.cdiv(width, tile),),
            in_specs=[
                pl.BlockSpec((height, rows), lambda j, m: (0, 0)),
                pl.BlockSpec((rows, tile), lambda j, m: (0, j)),
            ],
            out_specs=pl.BlockSpec((height, tile), lambda j, m: (0, j)),
        ),
        compiler_params=params(),
        cost_estimate=cost(2 * rows * height * width, 2 * (rows * (height + width) + height * width)),
        name="weight_grad",
    )(meta, at, b)


def input_kernel(slot_chunks, steps, tile, meta, u_ref, cot_ref, g_ref, dz_ref, dx_ref, w_ref, out_ref, gn_ref, dh_ref):
    j = pl.program_id(0)
    total = meta[0]
    chunks = 2 * slot_chunks
    last = w_ref[:, INNER + XBC :]
    cols = pl.ds(pl.multiple_of(j * tile, tile), tile)

    def block(b, rows):
        r = slice(b * 2 * Q, b * 2 * Q + rows)
        dh_ref[r, cols] = (
            dot_nt(dz_ref[r, :], w_ref[:, 0:INNER])
            + dot_nt(dx_ref[r, 0:XBC], w_ref[:, INNER : INNER + XBC])
            + dot_nt(dx_ref[r, XBC : XBC + HEADS], last)
        )

    for_blocks(total, chunks // 2, block)

    @pl.when(j == steps - 1)
    def _():
        out_ref[...] = jnp.zeros_like(out_ref)
        gn_ref[...] = jnp.zeros_like(gn_ref)
        for k in range(chunks):

            @pl.when(k < total)
            def _():
                start = pl.multiple_of(source_chunk(meta, k, slot_chunks) * Q, Q)
                u = u_ref[pl.ds(start, Q), :].astype(f32)
                live = row_iota((Q, D)) < live_rows(meta, k)
                err = jnp.where(live, cot_ref[pl.ds(start, Q), :].astype(f32), 0.0)
                scale = lax.rsqrt(jnp.mean(u * u, axis=-1, keepdims=True) + epsilon)
                dh = dh_ref[k * Q : (k + 1) * Q, :]
                gn_ref[...] += jnp.sum(dh * (u * scale), axis=0, keepdims=True)
                n = dh * g_ref[...]
                inner = jnp.mean(u * n, axis=-1, keepdims=True)
                du = err + scale * n - u * (scale * scale * scale * inner)
                out_ref[pl.ds(start, Q), :] = du.astype(bf16)


def input_grad_of(meta, u, cot, g1, dz, dx, w1):
    rows = u.shape[0]
    tile = 256
    steps = D // tile
    const = lambda j, m: (0, 0)
    once = pl.Buffered(1)
    return pl.pallas_call(
        functools.partial(input_kernel, rows // Q // 2, steps, tile),
        out_shape=(jax.ShapeDtypeStruct((rows, D), bf16), jax.ShapeDtypeStruct((1, D), f32)),
        grid_spec=pltpu.PrefetchScalarGridSpec(
            num_scalar_prefetch=1,
            grid=(steps,),
            in_specs=[
                pl.BlockSpec((rows, D), const, pipeline_mode=once),
                pl.BlockSpec((rows, D), const, pipeline_mode=once),
                pl.BlockSpec((1, D), const),
                pl.BlockSpec((rows, INNER), const, pipeline_mode=once),
                pl.BlockSpec((rows, XE), const, pipeline_mode=once),
                pl.BlockSpec((tile, PROJ), lambda j, m: (j, 0)),
            ],
            out_specs=[pl.BlockSpec((rows, D), const), pl.BlockSpec((1, D), const)],
            scratch_shapes=[pltpu.VMEM((rows, D), f32)],
        ),
        compiler_params=params(),
        cost_estimate=cost(2 * rows * D * PROJ, 2 * (D * PROJ + rows * PROJ)),
        name="input_grad",
    )(meta, u, cot, g1, dz, dx, w1)


def partner(value, axis, bit):
    mask = 2**bit
    pairs = [(source, source ^ mask) for source in range(lax.axis_size(axis))]
    return lax.ppermute(value, axis, pairs)


def scatter(partial):
    return lax.psum_scatter(partial, AXES, scatter_dimension=0, tiled=True).astype(f32)


def on_device(
    tokens, cotangent, lengths, balance, norm_gain, in_weight, conv_weight, conv_bias,
    step_bias, decay_log, skip_weight, inner_gain, out_weight,
):
    device = lax.axis_index(AXES)
    count = lax.axis_size(AXES)
    slot = tokens.shape[1]
    rows = 2 * slot
    first_source = balance[2 * device]
    second_source = balance[2 * device + 1]
    keep_second = first_source - 2 * device == 1
    outgoing = jnp.where(keep_second, tokens[0], tokens[1])
    incoming = partner(outgoing, "dp", 0)
    u = jnp.concatenate([jnp.where(keep_second, tokens[1], tokens[0]), incoming], axis=0)
    cot = cotangent.reshape(rows, D)
    lens = [lengths[first_source], lengths[second_source]]
    chunks = [(n + Q - 1) // Q for n in lens]
    meta = jnp.stack([chunks[0] + chunks[1], chunks[0], lens[0], lens[1]]).astype(jnp.int32)

    small = [norm_gain, conv_weight.reshape(-1), conv_bias, inner_gain]
    sizes = [v.shape[0] for v in small]
    packed = lax.all_gather(jnp.concatenate(small).astype(bf16)[None, :], AXES, axis=0, tiled=True).astype(f32)
    cuts = [sum(sizes[:n]) for n in range(len(sizes) + 1)]
    norm_full, conv_full, bias_full, inner_full = (
        packed[:, cuts[n] : cuts[n + 1]].reshape(-1) for n in range(4)
    )
    w1 = lax.all_gather(in_weight.astype(bf16), AXES, axis=0, tiled=True)
    w2 = lax.all_gather(out_weight.astype(bf16), AXES, axis=0, tiled=True)

    wc = jnp.concatenate([conv_full.reshape(XBC, CONV).T, bias_full[None], jnp.zeros((3, XBC), f32)])
    rate = -jnp.exp(decay_log)
    par = jnp.zeros((8, 128), f32).at[0, :HEADS].set(step_bias).at[1, :HEADS].set(rate)
    skip = jnp.repeat(skip_weight, HEADDIM)[None]
    g1 = norm_full[None]
    g2 = inner_full[None]

    proj, e, ht = project(meta, u, g1, w1)
    o, ot, y, sin = mixer(meta, proj, e, wc, par, skip, g2)
    out, err, dy, dz, gi = gate(meta, u, cot, w2, o, y, proj, g2)
    grad_out = scatter(weight_grad(meta, ot, err, D, 512))
    grad_z = scatter(weight_grad(meta, ht, dz, INNER, 512))
    dx, gconv, gpar, gskip = back(meta, proj, e, dy, sin, wc, par, skip)
    grad_x = scatter(weight_grad(meta, ht, dx, PROJ - INNER, 384))
    returned, gn = input_grad_of(meta, u, cot, g1, dz, dx, w1)
    grad_in = jnp.concatenate([grad_z, grad_x], axis=1)

    back_half = partner(returned[slot:], "dp", 0)
    kept_half = returned[:slot]
    input_grad = jnp.stack(
        [jnp.where(keep_second, back_half, kept_half), jnp.where(keep_second, kept_half, back_half)]
    )
    heads = jnp.concatenate(
        [gpar[0, :HEADS], gpar[1, :HEADS] * rate, gskip.reshape(HEADS, HEADDIM).sum(axis=1)]
    )
    grads = [gconv[:CONV].T.reshape(-1), gconv[CONV], gi[0]]
    flat = lax.psum(jnp.concatenate(grads + [heads]), AXES)
    norm_sum = lax.psum(gn[0], AXES)

    def owned(total, size):
        return lax.dynamic_slice(total, (device * size,), (size,))

    ends = [0, XBC * CONV, XBC * CONV + XBC, XBC * CONV + XBC + INNER]
    grad_conv = owned(flat[ends[0] : ends[1]], sizes[1]).reshape(-1, CONV)
    grad_bias = owned(flat[ends[1] : ends[2]], sizes[2])
    grad_inner = owned(flat[ends[2] : ends[3]], sizes[3])
    heads = flat[ends[3] :]
    return (
        out.reshape(2, slot, D),
        input_grad,
        owned(norm_sum, sizes[0]),
        grad_in,
        grad_conv,
        grad_bias,
        heads[:HEADS],
        heads[HEADS : 2 * HEADS],
        heads[2 * HEADS :],
        grad_inner,
        grad_out,
    )


def solution(mesh):
    flat = P(AXES)
    rowed = P(AXES, None)
    slots = P(AXES, None, None)
    return jax.shard_map(
        on_device,
        mesh=mesh,
        in_specs=(slots, slots, P(), P(), flat, rowed, rowed, flat, P(), P(), P(), flat, rowed),
        out_specs=(slots, slots, flat, rowed, rowed, flat, P(), P(), P(), flat, rowed),
        check_vma=False,
    )
```

```python
import functools
import jax
import jax.numpy as jnp
from jax import lax
from jax.experimental import pallas as pl
from jax.experimental.pallas import tpu as pltpu
from jax.sharding import PartitionSpec as P

D = 1536
INNER = 3072
HEADS = 48
HEADDIM = 64
STATE = 128
CONV = 4
XBC = 3328
PROJ = 6448
XE = XBC + 128
Q = 128
PAIRS = HEADS // 2

f32 = jnp.float32
bf16 = jnp.bfloat16
epsilon = 1e-05
AXES = ("dp", "fsdp")


def sigmoid(v):
    return 0.5 * jnp.tanh(0.5 * v) + 0.5


def dot_nn(a, b, precision=None):
    return jnp.dot(a, b, preferred_element_type=f32, precision=precision)


def dot_nt(a, b):
    return lax.dot_general(a, b, (((1,), (1,)), ((), ())), preferred_element_type=f32)


def dot_tn(a, b):
    return lax.dot_general(a, b, (((0,), (0,)), ((), ())), preferred_element_type=f32)


def lane_iota(shape):
    return lax.broadcasted_iota(jnp.int32, shape, len(shape) - 1)


def row_iota(shape):
    return lax.broadcasted_iota(jnp.int32, shape, len(shape) - 2)


H_UNIT = 48
H_TABLE = 4
O_UNIT = 32
O_TABLE = H_TABLE + D // H_UNIT


def source_chunk(meta, k, slot_chunks):
    return jnp.where(k < meta[1], k, k - meta[1] + slot_chunks)


def live_rows(meta, k):
    inside = k < meta[1]
    return jnp.where(inside, meta[2] - k * Q, meta[3] - (k - meta[1]) * Q)


def last_live(meta, k):
    return jnp.minimum(k, meta[0] - 1)


def last_padded(meta, k):
    return jnp.minimum(k, meta[0] + lax.rem(meta[0], 2) - 1)


def for_blocks(total, blocks, body):
    for b in range(blocks):
        pl.when(total >= 2 * b + 2)(functools.partial(body, b, 2 * Q))
        pl.when(total == 2 * b + 1)(functools.partial(body, b, Q))


def cost(flops, moved, transcendentals=0):
    return pl.CostEstimate(flops=int(flops), bytes_accessed=int(moved), transcendentals=int(transcendentals))


def params(**kw):
    return pltpu.CompilerParams(vmem_limit_bytes=60 * 1024 * 1024, **kw)


def project_kernel(slot_chunks, steps, tile, meta, u_ref, g_ref, w_ref, proj_ref, e_ref, ht_ref, h_ref):
    j = pl.program_id(0)
    total = meta[0]
    chunks = 2 * slot_chunks

    @pl.when(j == 0)
    def _():
        for k in range(chunks):

            @pl.when(k < total)
            def _():
                start = pl.multiple_of(source_chunk(meta, k, slot_chunks) * Q, Q)
                x = u_ref[pl.ds(start, Q), :].astype(f32)
                scale = lax.rsqrt(jnp.mean(x * x, axis=-1, keepdims=True) + epsilon)
                normed = x * scale * g_ref[...]
                h_ref[k * Q : (k + 1) * Q, :] = normed.astype(bf16)
                turned = normed.T.astype(bf16)
                for n in range(D // H_UNIT):
                    there = pl.ds(pl.multiple_of(meta[H_TABLE + n], 16), H_UNIT)
                    ht_ref[there, k * Q : (k + 1) * Q] = turned[n * H_UNIT : (n + 1) * H_UNIT, :]

            @pl.when(k >= total)
            def _():
                ht_ref[:, k * Q : (k + 1) * Q] = jnp.zeros((D, Q), bf16)

    edge = XBC + INNER - (steps - 1) * tile

    def block(b, rows):
        r = slice(b * 2 * Q, b * 2 * Q + rows)
        acc = dot_nn(h_ref[r, :], w_ref[...])
        proj_ref[r, :] = acc.astype(bf16)

        @pl.when(j == steps - 1)
        def _():
            tail = dot_nn(h_ref[r, :], w_ref[:, edge : edge + 128])
            e_ref[r, :] = jnp.where(lane_iota(tail.shape) < HEADS, tail, 0.0)

    for_blocks(total, chunks // 2, block)


def project(meta, u, g1, w1):
    rows = u.shape[0]
    tile = 512
    steps = pl.cdiv(PROJ, tile)
    return pl.pallas_call(
        functools.partial(project_kernel, rows // Q // 2, steps, tile),
        out_shape=(
            jax.ShapeDtypeStruct((rows, PROJ), bf16),
            jax.ShapeDtypeStruct((rows, 128), f32),
            jax.ShapeDtypeStruct((D, rows), bf16),
        ),
        grid_spec=pltpu.PrefetchScalarGridSpec(
            num_scalar_prefetch=1,
            grid=(steps,),
            in_specs=[
                pl.BlockSpec((rows, D), lambda j, m: (0, 0)),
                pl.BlockSpec((1, D), lambda j, m: (0, 0)),
                pl.BlockSpec((D, tile), lambda j, m: (0, j)),
            ],
            out_specs=[
                pl.BlockSpec((rows, tile), lambda j, m: (0, j)),
                pl.BlockSpec((rows, 128), lambda j, m: (0, 0)),
                pl.BlockSpec((D, rows), lambda j, m: (0, 0)),
            ],
            scratch_shapes=[pltpu.VMEM((rows, D), bf16)],
        ),
        compiler_params=params(),
        cost_estimate=cost(2 * rows * D * PROJ, 2 * (D * PROJ + rows * PROJ)),
        name="project",
    )(meta, u, g1, w1)


def conv_tile(buf, wc_ref, lanes):
    c = wc_ref[CONV : CONV + 1, lanes]
    for tap in range(CONV):
        c = c + wc_ref[tap : tap + 1, lanes] * buf[5 + tap : 5 + tap + Q, lanes]
    return c


def step_sizes(e_ref, par_ref):
    raw = e_ref[...] + par_ref[0:1, :]
    dt = jnp.maximum(raw, 0.0) + jnp.log1p(jnp.exp(-jnp.abs(raw)))
    decay = par_ref[1:2, :]
    lower = (row_iota((Q, Q)) >= lane_iota((Q, Q))).astype(f32)
    cum = dot_nn(lower, dt * decay, precision=lax.Precision.HIGHEST)
    return raw, dt, cum


def spread_heads(cum, dt, col_ref, dtp_ref):
    low = lane_iota((Q, 128)) < HEADDIM
    for p in range(PAIRS):
        for h in (2 * p, 2 * p + 1):
            col_ref[h] = jnp.broadcast_to(cum[:, h : h + 1], (Q, 128))
        dtp_ref[p] = jnp.where(
            low,
            jnp.broadcast_to(dt[:, 2 * p : 2 * p + 1], (Q, 128)),
            jnp.broadcast_to(dt[:, 2 * p + 1 : 2 * p + 2], (Q, 128)),
        )


def split_pair(v, low):
    zero = jnp.zeros_like(v)
    return jnp.concatenate([jnp.where(low, v, zero), jnp.where(low, zero, v)], axis=0)


def mixer_kernel(
    unroll, meta, proj_ref, e_ref, wc_ref, par_ref, skip_ref, g_ref,
    o_ref, ot_ref, y_ref, sin_ref,
    buf, state, col_ref, dtp_ref, row_ref, q_ref,
):
    k = pl.program_id(0)
    total = meta[0]

    @pl.when((k == total) & (lax.rem(total, 2) == 1))
    def _():
        o_ref[...] = jnp.zeros_like(o_ref)
        ot_ref[...] = jnp.zeros_like(ot_ref)

    @pl.when(k < total)
    def _():
        first = (k == 0) | (k == meta[1])

        @pl.when(first)
        def _():
            buf[0:8, :] = jnp.zeros((8, XBC), f32)
            state[...] = jnp.zeros_like(state)

        @pl.when(jnp.logical_not(first))
        def _():
            buf[0:8, :] = buf[Q : Q + 8, :]

        buf[8 : 8 + Q, :] = proj_ref[:, INNER : INNER + XBC].astype(f32)
        tail_lanes = slice(INNER, XBC)
        c = conv_tile(buf, wc_ref, tail_lanes)
        act = c * sigmoid(c)
        keys = act[:, :STATE]
        queries = act[:, STATE:].astype(bf16)
        keys_t = keys.T.astype(bf16)
        scores = dot_nn(queries, keys_t)
        _, dt, cum = step_sizes(e_ref, par_ref)
        row_ref[...] = cum.T
        spread_heads(cum, dt, col_ref, dtp_ref)
        lower = row_iota((Q, Q)) >= lane_iota((Q, Q))
        low = lane_iota((Q, 128)) < HEADDIM
        scores = jnp.where(lower, scores, 0.0)

        def pair(p):
            lanes = pl.ds(pl.multiple_of(p * 128, 128), 128)
            c = conv_tile(buf, wc_ref, lanes)
            values = c * sigmoid(c)
            col0, col1 = col_ref[2 * p], col_ref[2 * p + 1]
            both = jnp.where(low, col0, col1)
            end = both[Q - 1 : Q, :]
            stepped = values * dtp_ref[p]
            parts = split_pair(stepped.astype(bf16), low)
            mix = []
            for n, col in enumerate((col0, col1)):
                decay = jnp.exp(jnp.minimum(col - row_ref[pl.ds(2 * p + n, 1), :], 0.0))
                mix.append((scores * decay).astype(bf16))
            y = dot_nn(jnp.concatenate(mix, axis=1), parts)
            before = state[:, lanes]
            before_low = before.astype(bf16)
            sin_ref[0, :, lanes] = before_low
            y = y + dot_nn(queries, before_low) * jnp.exp(both)
            y = y + skip_ref[:, lanes] * values
            state[:, lanes] = before * jnp.exp(end) + dot_nn(
                keys_t, (stepped * jnp.exp(end - both)).astype(bf16)
            )
            z = proj_ref[:, lanes].astype(f32)
            gated = y * (z * sigmoid(z))
            y_ref[:, lanes] = y.astype(bf16)
            q_ref[:, lanes] = gated
            return gated * gated

        def body(i, squares):
            for n in range(unroll):
                squares = squares + pair(i * unroll + n)
            return squares

        squares = lax.fori_loop(0, PAIRS // unroll, body, jnp.zeros((Q, 128), f32))
        scale = lax.rsqrt(jnp.sum(squares, axis=-1, keepdims=True) / INNER + epsilon)

        def finish(p, _):
            lanes = pl.ds(pl.multiple_of(p * 128, 128), 128)
            out = q_ref[:, lanes] * scale * g_ref[:, lanes]
            o_ref[:, lanes] = out.astype(bf16)
            turned = out.T.astype(bf16)
            for n in range(128 // O_UNIT):
                there = pl.ds(pl.multiple_of(meta[O_TABLE + p * (128 // O_UNIT) + n], O_UNIT), O_UNIT)
                ot_ref[there, :] = turned[n * O_UNIT : (n + 1) * O_UNIT, :]
            return 0

        lax.fori_loop(0, PAIRS, finish, 0, unroll=2)


def mixer(meta, proj, e, wc, par, skip, g2):
    rows = proj.shape[0]
    chunks = rows // Q
    const = lambda k, m: (0, 0)
    live = lambda k, m: (last_live(m, k), 0)
    return pl.pallas_call(
        functools.partial(mixer_kernel, 2),
        out_shape=(
            jax.ShapeDtypeStruct((rows, INNER), bf16),
            jax.ShapeDtypeStruct((INNER, rows), bf16),
            jax.ShapeDtypeStruct((rows, INNER), bf16),
            jax.ShapeDtypeStruct((chunks, STATE, INNER), bf16),
        ),
        grid_spec=pltpu.PrefetchScalarGridSpec(
            num_scalar_prefetch=1,
            grid=(chunks,),
            in_specs=[
                pl.BlockSpec((Q, PROJ), live),
                pl.BlockSpec((Q, 128), live),
                pl.BlockSpec((8, XBC), const),
                pl.BlockSpec((8, 128), const),
                pl.BlockSpec((1, INNER), const),
                pl.BlockSpec((1, INNER), const),
            ],
            out_specs=[
                pl.BlockSpec((Q, INNER), lambda k, m: (last_padded(m, k), 0)),
                pl.BlockSpec((INNER, Q), lambda k, m: (0, last_padded(m, k))),
                pl.BlockSpec((Q, INNER), live),
                pl.BlockSpec((1, STATE, INNER), lambda k, m: (last_live(m, k), 0, 0)),
            ],
            scratch_shapes=[
                pltpu.VMEM((Q + 8, XBC), f32),
                pltpu.VMEM((STATE, INNER), f32),
                pltpu.VMEM((HEADS, Q, 128), f32),
                pltpu.VMEM((PAIRS, Q, 128), f32),
                pltpu.VMEM((128, Q), f32),
                pltpu.VMEM((Q, INNER), f32),
            ],
        ),
        compiler_params=params(),
        cost_estimate=cost(chunks * PAIRS * 8 * 2 * Q * 128 * 128, 2 * rows * (PROJ + 3 * INNER)),
        name="mixer",
    )(meta, proj, e, wc, par, skip, g2)


def gate_kernel(
    slot_chunks, meta, u_ref, cot_ref, w_ref, o_ref, y_ref, z_ref, g_ref,
    out_ref, err_ref, dy_ref, dz_ref, gi_ref,
    do_ref,
):
    b = pl.program_id(0)
    total = meta[0]

    @pl.when(b == 0)
    def _():
        out_ref[...] = jnp.zeros_like(out_ref)
        gi_ref[...] = jnp.zeros_like(gi_ref)

    def body(rows):
        halves = rows // Q
        if halves == 1:
            err_ref[Q:, :] = jnp.zeros((Q, D), bf16)
            dz_ref[Q:, :] = jnp.zeros((Q, INNER), bf16)
        starts = []
        for n in range(halves):
            k = 2 * b + n
            start = pl.multiple_of(source_chunk(meta, k, slot_chunks) * Q, Q)
            starts.append(start)
            cot = cot_ref[pl.ds(start, Q), :]
            live = row_iota((Q, D)) < live_rows(meta, k)
            err_ref[n * Q : (n + 1) * Q, :] = jnp.where(live, cot.astype(f32), 0.0).astype(bf16)
        branch = dot_nn(o_ref[0:rows, :], w_ref[...])
        for n in range(halves):
            live = row_iota((Q, D)) < live_rows(meta, 2 * b + n)
            here = pl.ds(starts[n], Q)
            value = u_ref[here, :].astype(f32) + branch[n * Q : (n + 1) * Q, :]
            out_ref[here, :] = jnp.where(live, value, 0.0).astype(bf16)
        do_ref[0:rows, :] = dot_nt(err_ref[0:rows, :], w_ref[...])

        def sums(p, carry):
            squares, crossed = carry
            lanes = pl.ds(pl.multiple_of(p * 128, 128), 128)
            z = z_ref[0:rows, lanes].astype(f32)
            q = y_ref[0:rows, lanes].astype(f32) * (z * sigmoid(z))
            return squares + q * q, crossed + q * g_ref[:, lanes] * do_ref[0:rows, lanes]

        zero = jnp.zeros((rows, 128), f32)
        squares, crossed = lax.fori_loop(0, PAIRS, sums, (zero, zero), unroll=2)
        scale = lax.rsqrt(jnp.sum(squares, axis=-1, keepdims=True) / INNER + epsilon)
        factor = scale * scale * scale * (jnp.sum(crossed, axis=-1, keepdims=True) / INNER)

        def back(p, _):
            lanes = pl.ds(pl.multiple_of(p * 128, 128), 128)
            z = z_ref[0:rows, lanes].astype(f32)
            y = y_ref[0:rows, lanes].astype(f32)
            s = sigmoid(z)
            gate = z * s
            q = y * gate
            do = do_ref[0:rows, lanes]
            gi_ref[:, lanes] += jnp.sum(do * q * scale, axis=0, keepdims=True)
            dq = scale * (g_ref[:, lanes] * do) - q * factor
            dy_ref[0:rows, lanes] = (dq * gate).astype(bf16)
            dz_ref[0:rows, lanes] = (dq * y * (s * (1.0 + z * (1.0 - s)))).astype(bf16)
            return 0

        lax.fori_loop(0, PAIRS, back, 0, unroll=2)

    pl.when(total >= 2 * b + 2)(functools.partial(body, 2 * Q))
    pl.when(total == 2 * b + 1)(functools.partial(body, Q))


def last_block(m, b):
    return jnp.minimum(b, (m[0] + 1) // 2 - 1)


def gate(meta, u, cot, w2, o, y, proj, g2):
    rows = u.shape[0]
    blocks = rows // (2 * Q)
    const = lambda b, m: (0, 0)
    live = lambda b, m: (last_block(m, b), 0)
    once = pl.Buffered(1)
    return pl.pallas_call(
        functools.partial(gate_kernel, rows // Q // 2),
        out_shape=(
            jax.ShapeDtypeStruct((rows, D), bf16),
            jax.ShapeDtypeStruct((rows, D), bf16),
            jax.ShapeDtypeStruct((rows, INNER), bf16),
            jax.ShapeDtypeStruct((rows, INNER), bf16),
            jax.ShapeDtypeStruct((1, INNER), f32),
        ),
        grid_spec=pltpu.PrefetchScalarGridSpec(
            num_scalar_prefetch=1,
            grid=(blocks,),
            in_specs=[
                pl.BlockSpec((rows, D), const, pipeline_mode=once),
                pl.BlockSpec((rows, D), const, pipeline_mode=once),
                pl.BlockSpec((INNER, D), const, pipeline_mode=once),
                pl.BlockSpec((2 * Q, INNER), live),
                pl.BlockSpec((2 * Q, INNER), live),
                pl.BlockSpec((2 * Q, INNER), live),
                pl.BlockSpec((1, INNER), const),
            ],
            out_specs=[
                pl.BlockSpec((rows, D), const),
                pl.BlockSpec((2 * Q, D), live),
                pl.BlockSpec((2 * Q, INNER), live),
                pl.BlockSpec((2 * Q, INNER), live),
                pl.BlockSpec((1, INNER), const),
            ],
            scratch_shapes=[pltpu.VMEM((2 * Q, INNER), f32)],
        ),
        compiler_params=params(),
        cost_estimate=cost(4 * rows * D * INNER, 2 * (D * INNER + 5 * rows * INNER)),
        name="gate",
    )(meta, u, cot, w2, o, y, proj, g2)


def back_kernel(
    unroll, part, parts, meta, x_ref, prev_ref, e_ref, dy_ref, sin_ref, wc_ref, par_ref, skip_ref, *rest
):
    carried, rest = (rest[:6], rest[6:]) if part > 0 else ((), rest)
    dx_ref, gconv_ref, gpar_ref, gskip_ref = rest[:4]
    passed_on, rest = (rest[4:6], rest[6:]) if part < parts - 1 else ((), rest[4:])
    buf, dbuf, dstate, col_ref, dtp_ref, row_ref, da_ref = rest
    i = pl.program_id(0)
    total = meta[0]
    begin, end = part_span(meta, part, parts)
    k = total - begin - i

    @pl.when(i == 0)
    def _():
        da_ref[...] = jnp.zeros_like(da_ref)
        if part == 0:
            gconv_ref[...] = jnp.zeros_like(gconv_ref)
            gpar_ref[...] = jnp.zeros_like(gpar_ref)
            gskip_ref[...] = jnp.zeros_like(gskip_ref)

            @pl.when(lax.rem(total, 2) == 1)
            def _():
                dx_ref[...] = jnp.zeros_like(dx_ref)

        else:
            for to, came in zip((gconv_ref, gpar_ref, gskip_ref, dstate), carried[1:5]):
                to[...] = came[...]
            dbuf[0:8, :] = carried[5][...]

    @pl.when((i >= 1) & (i <= end - begin))
    def _():
        first = (k == 0) | (k == meta[1])
        last = (k == total - 1) | (k == meta[1] - 1)

        @pl.when(first)
        def _():
            buf[0:8, :] = jnp.zeros((8, XBC), f32)

        @pl.when(jnp.logical_not(first))
        def _():
            buf[0:8, :] = prev_ref[8:16, INNER : INNER + XBC].astype(f32)

        @pl.when(last)
        def _():
            dbuf[Q : Q + 8, :] = jnp.zeros((8, XBC), f32)
            dstate[...] = jnp.zeros_like(dstate)

        @pl.when(jnp.logical_not(last))
        def _():
            dbuf[Q : Q + 8, :] = dbuf[0:8, :]

        buf[8 : 8 + Q, :] = x_ref[:, INNER : INNER + XBC].astype(f32)
        tail_lanes = slice(INNER, XBC)
        c_tail = conv_tile(buf, wc_ref, tail_lanes)
        s_tail = sigmoid(c_tail)
        act = c_tail * s_tail
        keys = act[:, :STATE].astype(bf16)
        queries = act[:, STATE:].astype(bf16)
        queries_t = act[:, STATE:].T.astype(bf16)
        scores = dot_nn(keys, queries_t)
        raw, dt, cum = step_sizes(e_ref, par_ref)
        row_ref[...] = cum.T
        spread_heads(cum, dt, col_ref, dtp_ref)
        upper = row_iota((Q, Q)) <= lane_iota((Q, Q))
        strict = row_iota((Q, Q)) < lane_iota((Q, Q))
        after = (row_iota((Q, Q)) >= lane_iota((Q, Q))).astype(bf16)
        low = lane_iota((Q, 128)) < HEADDIM
        scores = jnp.where(upper, scores, 0.0)
        half = (lax.broadcasted_iota(jnp.int32, (128, 128), 0) >= HEADDIM).astype(jnp.int32)
        head_lane = lane_iota((128, 128))

        def conv_back(lanes, dc):
            dbuf[0:Q, lanes] = dc
            dxbc = wc_ref[CONV - 1 : CONV, lanes] * dc
            for tap in range(CONV - 1):
                dxbc = dxbc + wc_ref[tap : tap + 1, lanes] * dbuf[3 - tap : 3 - tap + Q, lanes]
            dx_ref[:, lanes] = dxbc.astype(bf16)
            for tap in range(CONV):
                gconv_ref[tap : tap + 1, lanes] += jnp.sum(dc * buf[5 + tap : 5 + tap + Q, lanes], axis=0, keepdims=True)
            gconv_ref[CONV : CONV + 1, lanes] += jnp.sum(dc, axis=0, keepdims=True)

        def pair(p, carry):
            dscores, dquery, dkey, from_start, to_end, direct, thru = carry
            lanes = pl.ds(pl.multiple_of(p * 128, 128), 128)
            c = conv_tile(buf, wc_ref, lanes)
            s = sigmoid(c)
            values = c * s
            col0, col1 = col_ref[2 * p], col_ref[2 * p + 1]
            both = jnp.where(low, col0, col1)
            end = both[Q - 1 : Q, :]
            grown = jnp.exp(both)
            rest = jnp.exp(end - both)
            dtp = dtp_ref[p]
            stepped = values * dtp
            dy_low = dy_ref[:, lanes]
            dy = dy_low.astype(f32)
            parts = split_pair(dy_low, low)
            stepped_low = stepped.astype(bf16)
            dmix = dot_nt(stepped_low, parts)
            mix = []
            for n, col in enumerate((col0, col1)):
                decay = jnp.exp(jnp.minimum(row_ref[pl.ds(2 * p + n, 1), :] - col, 0.0))
                weighted = dmix[:, n * Q : (n + 1) * Q] * decay
                dscores = dscores + weighted
                mix.append((scores * decay).astype(bf16))
                passed = dot_nn((weighted * scores).astype(bf16), after)
                da_ref[pl.ds(2 * p + n, 1), :] = jnp.sum(jnp.where(strict, passed, 0.0), axis=0, keepdims=True)
            dstepped = dot_nn(jnp.concatenate(mix, axis=1), parts)
            dafter = dstate[:, lanes]
            dafter_low = dafter.astype(bf16)
            before_low = sin_ref[0, :, lanes]
            dend = dot_nn(keys, dafter_low) * rest
            grown_dy = (dy * grown).astype(bf16)
            select = (head_lane == 2 * p + half).astype(bf16)
            across = dot_nn(queries, before_low)
            from_start = from_start + dot_nn((across * grown * dy).astype(bf16), select)
            to_end = to_end + dot_nn((stepped * dend).astype(bf16), select)
            dstepped = dstepped + dend
            direct = direct + dot_nn((values * dstepped).astype(bf16), select)
            dquery = dquery + dot_nt(grown_dy, before_low)
            dkey = dkey + dot_nt((stepped * rest).astype(bf16), dafter_low)
            kept = jnp.exp(end) * dafter
            held = jnp.sum((kept * before_low.astype(f32)).reshape(8, 16, 128), axis=0)
            thru = thru + dot_nn(held.astype(bf16), select)
            dstate[:, lanes] = kept + dot_nn(queries_t, grown_dy)
            dvalues = dstepped * dtp + skip_ref[:, lanes] * dy
            gskip_ref[:, lanes] += jnp.sum(dy * values, axis=0, keepdims=True)
            conv_back(lanes, dvalues * (s * (1.0 + c * (1.0 - s))))
            return dscores, dquery, dkey, from_start, to_end, direct, thru

        def body(n, carry):
            for m in range(unroll):
                carry = pair(n * unroll + m, carry)
            return carry

        zero = jnp.zeros((Q, 128), f32)
        start = (zero,) * 6 + (jnp.zeros((16, 128), f32),)
        carry = lax.fori_loop(0, PAIRS // unroll, body, start)
        dscores, dquery, dkey, from_start, to_end, direct, thru = carry
        dscores = jnp.where(upper, dscores, 0.0)
        dkey = dkey + dot_nn(dscores.astype(bf16), queries)
        dquery = dquery + dot_nn(dscores.T.astype(bf16), keys)
        slope = s_tail * (1.0 + c_tail * (1.0 - s_tail))
        conv_back(slice(INNER, INNER + STATE), dkey * slope[:, :STATE])
        conv_back(slice(INNER + STATE, XBC), dquery * slope[:, STATE:])

        tail_sum = (row_iota((Q, Q)) <= lane_iota((Q, Q))).astype(f32)
        head_sum = (row_iota((Q, Q)) > lane_iota((Q, Q))).astype(f32)
        da = (
            da_ref[...].T
            + dot_nn(tail_sum, from_start, precision=lax.Precision.HIGHEST)
            + dot_nn(head_sum, to_end, precision=lax.Precision.HIGHEST)
            + jnp.sum(thru, axis=0, keepdims=True)
        )
        ddt = par_ref[1:2, :] * da + direct
        de = ddt * sigmoid(raw)
        de = jnp.where(lane_iota((Q, 128)) < HEADS, de, 0.0)
        dx_ref[:, XBC:] = de.astype(bf16)
        gpar_ref[0:1, :] += jnp.sum(de, axis=0, keepdims=True)
        gpar_ref[1:2, :] += jnp.sum(dt * da, axis=0, keepdims=True)

    if passed_on:

        @pl.when(i == pl.num_programs(0) - 1)
        def _():
            passed_on[0][...] = dstate[...]
            passed_on[1][...] = dbuf[0:8, :]


def part_span(meta, part, parts):
    return (meta[0] * part + parts - 1) // parts, (meta[0] * (part + 1) + parts - 1) // parts


def back(meta, part, parts, carried, proj, e, dy, sin, wc, par, skip):
    rows = proj.shape[0]
    chunks = rows // Q
    const = lambda i, m: (0, 0)

    def chunk(i, m):
        begin, end = part_span(m, part, parts)
        return jnp.clip(m[0] - begin - jnp.clip(i, 1, jnp.maximum(end - begin, 1)), 0, m[0] - 1)

    def written(i, m):
        begin, end = part_span(m, part, parts)
        block = jnp.where(end > begin, chunk(i, m), chunks)
        return jnp.where(i == 0, last_padded(m, m[0]), block) if part == 0 else block

    here = lambda i, m: (chunk(i, m), 0)
    out_shape = [
        jax.ShapeDtypeStruct((rows + Q, XE), bf16),
        jax.ShapeDtypeStruct((8, XBC), f32),
        jax.ShapeDtypeStruct((8, 128), f32),
        jax.ShapeDtypeStruct((1, INNER), f32),
    ]
    sums = [pl.BlockSpec((8, XBC), const), pl.BlockSpec((8, 128), const), pl.BlockSpec((1, INNER), const)]
    state = [pl.BlockSpec((STATE, INNER), const), pl.BlockSpec((8, XBC), const)]
    in_specs = [
        pl.BlockSpec((Q, PROJ), here),
        pl.BlockSpec((16, PROJ), lambda i, m: (jnp.maximum(chunk(i, m) * (Q // 16) - 1, 0), 0)),
        pl.BlockSpec((Q, 128), here),
        pl.BlockSpec((Q, INNER), here),
        pl.BlockSpec((1, STATE, INNER), lambda i, m: (chunk(i, m), 0, 0)),
        pl.BlockSpec((8, XBC), const),
        pl.BlockSpec((8, 128), const),
        pl.BlockSpec((1, INNER), const),
    ]
    out_specs = [pl.BlockSpec((Q, XE), lambda i, m: (written(i, m), 0))] + sums
    if part > 0:
        in_specs += [pl.BlockSpec(memory_space=pl.ANY)] + sums + state
    if part < parts - 1:
        out_shape += [jax.ShapeDtypeStruct((STATE, INNER), f32), jax.ShapeDtypeStruct((8, XBC), f32)]
        out_specs += state
    steps = -(-chunks // parts)
    return pl.pallas_call(
        functools.partial(back_kernel, 2, part, parts),
        out_shape=out_shape,
        grid_spec=pltpu.PrefetchScalarGridSpec(
            num_scalar_prefetch=1,
            grid=(steps + 1,),
            in_specs=in_specs,
            out_specs=out_specs,
            scratch_shapes=[
                pltpu.VMEM((Q + 8, XBC), f32),
                pltpu.VMEM((Q + 8, XBC), f32),
                pltpu.VMEM((STATE, INNER), f32),
                pltpu.VMEM((HEADS, Q, 128), f32),
                pltpu.VMEM((PAIRS, Q, 128), f32),
                pltpu.VMEM((128, Q), f32),
                pltpu.VMEM((128, Q), f32),
            ],
        ),
        input_output_aliases={9: 0} if part > 0 else {},
        compiler_params=params(),
        cost_estimate=cost(steps * PAIRS * 20 * 2 * Q * 128 * 128, 2 * steps * Q * (PROJ + 3 * INNER)),
        name="back",
    )(meta, proj, proj, e, dy, sin, wc, par, skip, *carried)


def weight_kernel(rows, block, swap, meta, at_ref, b_ref, mine_ref, other_ref):
    used = (meta[0] + 1) // 2
    half = at_ref.shape[0] // 2
    part_rows = half // 4

    def part(width):
        for c, out_ref in enumerate((mine_ref, other_ref)):

            def step(m, _):
                here = pl.ds(pl.multiple_of(c * half + m * block, block), block)
                res = dot_nn(at_ref[here, 0:width], b_ref[0:width, :]).astype(bf16)
                if swap:
                    for n in range(2):
                        there = pl.ds(pl.multiple_of((2 * n + m) * part_rows, part_rows), part_rows)
                        out_ref[there, :] = res[n * part_rows : (n + 1) * part_rows, :]
                else:
                    out_ref[pl.ds(pl.multiple_of(m * block, block), block), :] = res
                return 0

            lax.fori_loop(0, half // block, step, 0)

    for n in range(1, rows // (2 * Q) + 1):
        pl.when(used == n)(functools.partial(part, n * 2 * Q))


def weight_grad(meta, at, b, first, width, tile, block, swap):
    height, rows = at.shape
    offset = first // tile
    half = jax.ShapeDtypeStruct((height // 2, width), bf16)
    half_spec = pl.BlockSpec((height // 2, tile), lambda j, m: (0, j))
    return pl.pallas_call(
        functools.partial(weight_kernel, rows, block, swap),
        out_shape=(half, half),
        grid_spec=pltpu.PrefetchScalarGridSpec(
            num_scalar_prefetch=1,
            grid=(pl.cdiv(width, tile),),
            in_specs=[
                pl.BlockSpec((height, rows), lambda j, m: (0, 0)),
                pl.BlockSpec((rows, tile), lambda j, m: (0, j + offset)),
            ],
            out_specs=(half_spec, half_spec),
        ),
        compiler_params=params(),
        cost_estimate=cost(2 * rows * height * width, 2 * (rows * (height + width) + height * width)),
        name="weight_grad",
    )(meta, at, b)


def input_kernel(slot_chunks, steps, tile, meta, u_ref, cot_ref, g_ref, dz_ref, dx_ref, w_ref, out_ref, gn_ref, dh_ref):
    j = pl.program_id(0)
    total = meta[0]
    chunks = 2 * slot_chunks
    last = w_ref[:, INNER + XBC :]
    cols = pl.ds(pl.multiple_of(j * tile, tile), tile)

    def block(b, rows):
        r = slice(b * 2 * Q, b * 2 * Q + rows)
        dh_ref[r, cols] = (
            dot_nt(dz_ref[r, :], w_ref[:, 0:INNER])
            + dot_nt(dx_ref[r, 0:XBC], w_ref[:, INNER : INNER + XBC])
            + dot_nt(dx_ref[r, XBC : XBC + HEADS], last)
        )

    for_blocks(total, chunks // 2, block)

    @pl.when(j == steps - 1)
    def _():
        out_ref[...] = jnp.zeros_like(out_ref)
        gn_ref[...] = jnp.zeros_like(gn_ref)
        for k in range(chunks):

            @pl.when(k < total)
            def _():
                start = pl.multiple_of(source_chunk(meta, k, slot_chunks) * Q, Q)
                u = u_ref[pl.ds(start, Q), :].astype(f32)
                live = row_iota((Q, D)) < live_rows(meta, k)
                err = jnp.where(live, cot_ref[pl.ds(start, Q), :].astype(f32), 0.0)
                scale = lax.rsqrt(jnp.mean(u * u, axis=-1, keepdims=True) + epsilon)
                dh = dh_ref[k * Q : (k + 1) * Q, :]
                gn_ref[...] += jnp.sum(dh * (u * scale), axis=0, keepdims=True)
                n = dh * g_ref[...]
                inner = jnp.mean(u * n, axis=-1, keepdims=True)
                du = err + scale * n - u * (scale * scale * scale * inner)
                out_ref[pl.ds(start, Q), :] = du.astype(bf16)


def input_grad_of(meta, u, cot, g1, dz, dx, w1):
    rows = u.shape[0]
    tile = 256
    steps = D // tile
    const = lambda j, m: (0, 0)
    once = pl.Buffered(1)
    return pl.pallas_call(
        functools.partial(input_kernel, rows // Q // 2, steps, tile),
        out_shape=(jax.ShapeDtypeStruct((rows, D), bf16), jax.ShapeDtypeStruct((1, D), f32)),
        grid_spec=pltpu.PrefetchScalarGridSpec(
            num_scalar_prefetch=1,
            grid=(steps,),
            in_specs=[
                pl.BlockSpec((rows, D), const, pipeline_mode=once),
                pl.BlockSpec((rows, D), const, pipeline_mode=once),
                pl.BlockSpec((1, D), const),
                pl.BlockSpec((rows, INNER), const, pipeline_mode=once),
                pl.BlockSpec((rows, XE), const, pipeline_mode=once),
                pl.BlockSpec((tile, PROJ), lambda j, m: (j, 0)),
            ],
            out_specs=[pl.BlockSpec((rows, D), const), pl.BlockSpec((1, D), const)],
            scratch_shapes=[pltpu.VMEM((rows, D), f32)],
        ),
        compiler_params=params(),
        cost_estimate=cost(2 * rows * D * PROJ, 2 * (D * PROJ + rows * PROJ)),
        name="input_grad",
    )(meta, u, cot, g1, dz, dx, w1)


def partner(value, axis, bit):
    mask = 2**bit
    pairs = [(source, source ^ mask) for source in range(lax.axis_size(axis))]
    return lax.ppermute(value, axis, pairs)


def log2(size):
    return size.bit_length() - 1


def halving_order(swap):
    fsdp = [("fsdp", bit) for bit in range(log2(lax.axis_size("fsdp")))]
    near = [("dp", 1)]
    far = [("dp", bit) for bit in range(2, log2(lax.axis_size("dp")))]
    return [("dp", 0)] + (near + fsdp if swap else fsdp + near) + far


def flat_bit(axis, bit):
    return bit + (log2(lax.axis_size("fsdp")) if axis == "dp" else 0)


def kept_at(order, owner):
    away = owner ^ lax.axis_index(AXES)
    place = jnp.zeros_like(away)
    for axis, bit in order:
        place = 2 * place + ((away >> flat_bit(axis, bit)) & 1)
    return place


def owner_at(order, place):
    away = jnp.zeros_like(place)
    for n, (axis, bit) in enumerate(order):
        away = away + (((place >> (len(order) - 1 - n)) & 1) << flat_bit(axis, bit))
    return away ^ lax.axis_index(AXES)


class Chain:
    def __init__(self, halves, swap, grouped):
        self.order = halving_order(swap)
        mine, other = halves
        if not grouped:
            count = lax.axis_size(AXES)
            whole = jnp.concatenate([mine, other])
            whole = whole.reshape(count, -1, whole.shape[1])[owner_at(self.order, jnp.arange(count))]
            mine, other = whole.reshape(2, -1, whole.shape[2])
        self.terms = [mine]
        self.sent = other
        self.phase = 0

    def exchange(self):
        if self.sent is not None:
            self.terms.append(partner(self.sent, *self.order[self.phase]))
            self.sent = None
            self.phase += 1

    def halve(self):
        if self.phase < len(self.order) and self.sent is None:
            half = self.terms[0].shape[0] // 2
            self.sent = sum(term[half:].astype(f32) for term in self.terms).astype(bf16)
            self.terms = [term[:half] for term in self.terms]

    def finish(self):
        while self.phase < len(self.order):
            self.halve()
            self.exchange()
        return sum(term.astype(f32) for term in self.terms)


def tick(meta, chains, after):
    arrived = [chain for chain in chains if chain.sent is None]
    if arrived:
        *came, _ = lax.optimization_barrier([chain.terms[-1] for chain in arrived] + [after])
        for chain, term in zip(arrived, came):
            chain.terms[-1] = term
            chain.halve()
    sending = [chain for chain in chains if chain.sent is not None]
    *sent, meta = lax.optimization_barrier([chain.sent for chain in sending] + [meta])
    for chain, value in zip(sending, sent):
        chain.sent = value
        chain.exchange()
    return meta


def sum_kernel(count, inner, sent_ref, out_ref, came, send_sem, recv_sem):
    me = lax.axis_index("dp") * inner + lax.axis_index("fsdp")

    def copy(n):
        other = jnp.bitwise_xor(me, n)
        return pltpu.make_async_remote_copy(
            src_ref=sent_ref.at[other],
            dst_ref=came.at[n],
            send_sem=send_sem.at[n],
            recv_sem=recv_sem.at[n],
            device_id=(other // inner, other % inner),
            device_id_type=pl.DeviceIdType.MESH,
        )

    def start(n, _):
        copy(n).start()
        return 0

    def add(n, total):
        copy(n).wait()
        return total + came[n]

    lax.fori_loop(1, count, start, 0)
    out_ref[...] = lax.fori_loop(1, count, add, sent_ref[me])


def sum_small(tiles):
    count = tiles.shape[0]
    whole = pl.BlockSpec(memory_space=pltpu.VMEM)
    return pl.pallas_call(
        functools.partial(sum_kernel, count, lax.axis_size("fsdp")),
        out_shape=jax.ShapeDtypeStruct(tiles.shape[1:], f32),
        in_specs=[whole],
        out_specs=whole,
        scratch_shapes=[
            pltpu.VMEM(tiles.shape, f32),
            pltpu.SemaphoreType.DMA((count,)),
            pltpu.SemaphoreType.DMA((count,)),
        ],
        compiler_params=pltpu.CompilerParams(has_side_effects=True),
        cost_estimate=cost(count * 1024, 8 * count * 1024),
        name="sum_small",
    )(tiles)


def on_device(
    tokens, cotangent, lengths, balance, norm_gain, in_weight, conv_weight, conv_bias,
    step_bias, decay_log, skip_weight, inner_gain, out_weight,
):
    device = lax.axis_index(AXES)
    count = lax.axis_size(AXES)
    slot = tokens.shape[1]
    rows = 2 * slot
    first_source = balance[2 * device]
    second_source = balance[2 * device + 1]
    keep_second = first_source - 2 * device == 1
    outgoing = jnp.where(keep_second, tokens[0], tokens[1])
    incoming = partner(outgoing, "dp", 0)
    u = jnp.concatenate([jnp.where(keep_second, tokens[1], tokens[0]), incoming], axis=0)
    cot = cotangent.reshape(rows, D)
    lens = [lengths[first_source], lengths[second_source]]
    chunks = [(n + Q - 1) // Q for n in lens]
    grouped = D // count == H_UNIT
    h_units = jnp.arange(D // H_UNIT)
    o_units = jnp.arange(INNER // O_UNIT)
    if grouped:
        order = halving_order(False)
        each = INNER // count // O_UNIT
        h_units = kept_at(order, h_units)
        o_units = kept_at(order, o_units // each) * each + o_units % each
    meta = jnp.concatenate(
        [jnp.stack([chunks[0] + chunks[1], chunks[0], lens[0], lens[1]]), h_units * H_UNIT, o_units * O_UNIT]
    ).astype(jnp.int32)

    small = [norm_gain, conv_weight.reshape(-1), conv_bias, inner_gain]
    sizes = [v.shape[0] for v in small]
    packed = lax.all_gather(jnp.concatenate(small).astype(bf16)[None, :], AXES, axis=0, tiled=True).astype(f32)
    cuts = [sum(sizes[:n]) for n in range(len(sizes) + 1)]
    norm_full, conv_full, bias_full, inner_full = (
        packed[:, cuts[n] : cuts[n + 1]].reshape(-1) for n in range(4)
    )
    w1 = lax.all_gather(in_weight.astype(bf16), AXES, axis=0, tiled=True)
    w2 = lax.all_gather(out_weight.astype(bf16), AXES, axis=0, tiled=True)

    wc = jnp.concatenate([conv_full.reshape(XBC, CONV).T, bias_full[None], jnp.zeros((3, XBC), f32)])
    rate = -jnp.exp(decay_log)
    par = jnp.zeros((8, 128), f32).at[0, :HEADS].set(step_bias).at[1, :HEADS].set(rate)
    skip = jnp.repeat(skip_weight, HEADDIM)[None]
    g1 = norm_full[None]
    g2 = inner_full[None]

    proj, e, ht = project(meta, u, g1, w1)
    o, ot, y, sin = mixer(meta, proj, e, wc, par, skip, g2)
    out, err, dy, dz, gi = gate(meta, u, cot, w2, o, y, proj, g2)
    parts = 3
    c_out = Chain(weight_grad(meta, ot, err, 0, D, 512, 512, False), False, grouped)
    meta = tick(meta, [c_out], err)
    c_z = Chain(weight_grad(meta, ht, dz, 0, INNER, 512, 384, grouped), True, grouped)
    carried = ()
    for part in range(parts):
        meta = tick(meta, [c_out, c_z], carried[2] if carried else c_z.sent)
        carried = back(meta, part, parts, carried, proj, e, dy, sin, wc, par, skip)
    dx, gconv, gpar, gskip = carried
    meta = tick(meta, [c_out, c_z], gpar)
    cut = 1792
    c_x0 = Chain(weight_grad(meta, ht, dx, 0, cut, 896, 384, False), False, grouped)
    meta = tick(meta, [c_out, c_z, c_x0], c_x0.sent)
    c_x1 = Chain(weight_grad(meta, ht, dx, cut, XE - cut, 896, 384, grouped), True, grouped)
    meta = tick(meta, [c_out, c_z, c_x0, c_x1], c_x1.sent)
    meta = tick(meta, [c_x1], c_x1.terms[-1])
    returned, gn = input_grad_of(meta, u, cot, g1, dz, dx, w1)
    meta = tick(meta, [c_x0, c_x1], gn)
    heads = jnp.concatenate(
        [gpar[0, :HEADS], gpar[1, :HEADS] * rate, gskip.reshape(HEADS, HEADDIM).sum(axis=1)]
    )
    owned = [gconv[:CONV].T.reshape(count, -1), gconv[CONV].reshape(count, -1), gi.reshape(count, -1)]
    tiles = jnp.concatenate(owned + [jnp.broadcast_to(heads, (count, 3 * HEADS)), gn.reshape(count, -1)], axis=1)
    tiles = jnp.pad(tiles, ((0, 0), (0, 1024 - tiles.shape[1]))).reshape(count, 8, 128)
    tiles, meta = lax.optimization_barrier([tiles, meta])
    sums = sum_small(tiles).reshape(-1)
    grad_out = c_out.finish()
    grad_in = jnp.concatenate([c_z.finish(), c_x0.finish(), c_x1.finish()[:, : PROJ - INNER - cut]], axis=1)

    back_half = partner(returned[slot:], "dp", 0)
    kept_half = returned[:slot]
    input_grad = jnp.stack(
        [jnp.where(keep_second, back_half, kept_half), jnp.where(keep_second, kept_half, back_half)]
    )
    ends = [sum(v.shape[1] for v in owned[:n]) for n in range(4)]
    grad_conv = sums[: ends[1]].reshape(-1, CONV)
    grad_bias = sums[ends[1] : ends[2]]
    grad_inner = sums[ends[2] : ends[3]]
    heads = sums[ends[3] : ends[3] + 3 * HEADS]
    grad_norm = sums[ends[3] + 3 * HEADS :][: sizes[0]]
    return (
        out.reshape(2, slot, D),
        input_grad,
        grad_norm,
        grad_in,
        grad_conv,
        grad_bias,
        heads[:HEADS],
        heads[HEADS : 2 * HEADS],
        heads[2 * HEADS :],
        grad_inner,
        grad_out,
    )


def solution(mesh):
    flat = P(AXES)
    rowed = P(AXES, None)
    slots = P(AXES, None, None)
    return jax.shard_map(
        on_device,
        mesh=mesh,
        in_specs=(slots, slots, P(), P(), flat, rowed, rowed, flat, P(), P(), P(), flat, rowed),
        out_specs=(slots, slots, flat, rowed, rowed, flat, P(), P(), P(), flat, rowed),
        check_vma=False,
    )
```

```python
import functools
import jax
import jax.numpy as jnp
from jax import lax
from jax.experimental import pallas as pl
from jax.experimental.pallas import tpu as pltpu
from jax.sharding import PartitionSpec as P

D = 1536
INNER = 3072
HEADS = 48
HEADDIM = 64
STATE = 128
CONV = 4
XBC = 3328
PROJ = 6448
XE = XBC + 128
Q = 128
PAIRS = HEADS // 2

f32 = jnp.float32
bf16 = jnp.bfloat16
epsilon = 1e-05
AXES = ("dp", "fsdp")


def sigmoid(v):
    return 0.5 * jnp.tanh(0.5 * v) + 0.5


def dot_nn(a, b, precision=None):
    return jnp.dot(a, b, preferred_element_type=f32, precision=precision)


def dot_nt(a, b):
    return lax.dot_general(a, b, (((1,), (1,)), ((), ())), preferred_element_type=f32)


def dot_tn(a, b):
    return lax.dot_general(a, b, (((0,), (0,)), ((), ())), preferred_element_type=f32)


def lane_iota(shape):
    return lax.broadcasted_iota(jnp.int32, shape, len(shape) - 1)


def row_iota(shape):
    return lax.broadcasted_iota(jnp.int32, shape, len(shape) - 2)


H_UNIT = 48
H_TABLE = 4
O_UNIT = 32
O_TABLE = H_TABLE + D // H_UNIT


def source_chunk(meta, k, slot_chunks):
    return jnp.where(k < meta[1], k, k - meta[1] + slot_chunks)


def live_rows(meta, k):
    inside = k < meta[1]
    return jnp.where(inside, meta[2] - k * Q, meta[3] - (k - meta[1]) * Q)


def last_live(meta, k):
    return jnp.minimum(k, meta[0] - 1)


def last_padded(meta, k):
    return jnp.minimum(k, meta[0] + lax.rem(meta[0], 2) - 1)


def for_blocks(total, blocks, body):
    for b in range(blocks):
        pl.when(total >= 2 * b + 2)(functools.partial(body, b, 2 * Q))
        pl.when(total == 2 * b + 1)(functools.partial(body, b, Q))


def cost(flops, moved, transcendentals=0):
    return pl.CostEstimate(flops=int(flops), bytes_accessed=int(moved), transcendentals=int(transcendentals))


def params(**kw):
    return pltpu.CompilerParams(vmem_limit_bytes=60 * 1024 * 1024, **kw)


def project_kernel(slot_chunks, steps, tile, meta, u_ref, g_ref, w_ref, proj_ref, e_ref, ht_ref, h_ref):
    j = pl.program_id(0)
    total = meta[0]
    chunks = 2 * slot_chunks

    @pl.when(j == 0)
    def _():
        for k in range(chunks):

            @pl.when(k < total)
            def _():
                start = pl.multiple_of(source_chunk(meta, k, slot_chunks) * Q, Q)
                x = u_ref[pl.ds(start, Q), :].astype(f32)
                scale = lax.rsqrt(jnp.mean(x * x, axis=-1, keepdims=True) + epsilon)
                normed = x * scale * g_ref[...]
                h_ref[k * Q : (k + 1) * Q, :] = normed.astype(bf16)
                turned = normed.T.astype(bf16)
                for n in range(D // H_UNIT):
                    there = pl.ds(pl.multiple_of(meta[H_TABLE + n], 16), H_UNIT)
                    ht_ref[there, k * Q : (k + 1) * Q] = turned[n * H_UNIT : (n + 1) * H_UNIT, :]

            @pl.when(k >= total)
            def _():
                ht_ref[:, k * Q : (k + 1) * Q] = jnp.zeros((D, Q), bf16)

    edge = XBC + INNER - (steps - 1) * tile

    def block(b, rows):
        r = slice(b * 2 * Q, b * 2 * Q + rows)
        acc = dot_nn(h_ref[r, :], w_ref[...])
        proj_ref[r, :] = acc.astype(bf16)

        @pl.when(j == steps - 1)
        def _():
            tail = dot_nn(h_ref[r, :], w_ref[:, edge : edge + 128])
            e_ref[r, :] = jnp.where(lane_iota(tail.shape) < HEADS, tail, 0.0)

    for_blocks(total, chunks // 2, block)


def project(meta, u, g1, w1):
    rows = u.shape[0]
    tile = 512
    steps = pl.cdiv(PROJ, tile)
    return pl.pallas_call(
        functools.partial(project_kernel, rows // Q // 2, steps, tile),
        out_shape=(
            jax.ShapeDtypeStruct((rows, PROJ), bf16),
            jax.ShapeDtypeStruct((rows, 128), f32),
            jax.ShapeDtypeStruct((D, rows), bf16),
        ),
        grid_spec=pltpu.PrefetchScalarGridSpec(
            num_scalar_prefetch=1,
            grid=(steps,),
            in_specs=[
                pl.BlockSpec((rows, D), lambda j, m: (0, 0)),
                pl.BlockSpec((1, D), lambda j, m: (0, 0)),
                pl.BlockSpec((D, tile), lambda j, m: (0, j)),
            ],
            out_specs=[
                pl.BlockSpec((rows, tile), lambda j, m: (0, j)),
                pl.BlockSpec((rows, 128), lambda j, m: (0, 0)),
                pl.BlockSpec((D, rows), lambda j, m: (0, 0)),
            ],
            scratch_shapes=[pltpu.VMEM((rows, D), bf16)],
        ),
        compiler_params=params(),
        cost_estimate=cost(2 * rows * D * PROJ, 2 * (D * PROJ + rows * PROJ)),
        name="project",
    )(meta, u, g1, w1)


def conv_tile(buf, wc_ref, lanes):
    c = wc_ref[CONV : CONV + 1, lanes]
    for tap in range(CONV):
        c = c + wc_ref[tap : tap + 1, lanes] * buf[5 + tap : 5 + tap + Q, lanes]
    return c


def step_sizes(e_ref, par_ref):
    raw = e_ref[...] + par_ref[0:1, :]
    dt = jnp.maximum(raw, 0.0) + jnp.log1p(jnp.exp(-jnp.abs(raw)))
    decay = par_ref[1:2, :]
    lower = (row_iota((Q, Q)) >= lane_iota((Q, Q))).astype(f32)
    cum = dot_nn(lower, dt * decay, precision=lax.Precision.HIGHEST)
    return raw, dt, cum


def spread_heads(cum, dt, col_ref, dtp_ref):
    low = lane_iota((Q, 128)) < HEADDIM
    for p in range(PAIRS):
        for h in (2 * p, 2 * p + 1):
            col_ref[h] = jnp.broadcast_to(cum[:, h : h + 1], (Q, 128))
        dtp_ref[p] = jnp.where(
            low,
            jnp.broadcast_to(dt[:, 2 * p : 2 * p + 1], (Q, 128)),
            jnp.broadcast_to(dt[:, 2 * p + 1 : 2 * p + 2], (Q, 128)),
        )


def split_pair(v, low):
    zero = jnp.zeros_like(v)
    return jnp.concatenate([jnp.where(low, v, zero), jnp.where(low, zero, v)], axis=0)


def mixer_kernel(
    unroll, meta, proj_ref, e_ref, cot_ref, wc_ref, par_ref, skip_ref, g_ref,
    o_ref, ot_ref, y_ref, sin_ref, err_ref,
    buf, state, col_ref, dtp_ref, row_ref, q_ref,
):
    k = pl.program_id(0)
    total = meta[0]

    @pl.when((k == total) & (lax.rem(total, 2) == 1))
    def _():
        o_ref[...] = jnp.zeros_like(o_ref)
        ot_ref[...] = jnp.zeros_like(ot_ref)
        err_ref[...] = jnp.zeros_like(err_ref)

    @pl.when(k < total)
    def _():
        live = row_iota((Q, D)) < live_rows(meta, k)
        err_ref[...] = jnp.where(live, cot_ref[...].astype(f32), 0.0).astype(bf16)
        first = (k == 0) | (k == meta[1])

        @pl.when(first)
        def _():
            buf[0:8, :] = jnp.zeros((8, XBC), f32)
            state[...] = jnp.zeros_like(state)

        @pl.when(jnp.logical_not(first))
        def _():
            buf[0:8, :] = buf[Q : Q + 8, :]

        buf[8 : 8 + Q, :] = proj_ref[:, INNER : INNER + XBC].astype(f32)
        tail_lanes = slice(INNER, XBC)
        c = conv_tile(buf, wc_ref, tail_lanes)
        act = c * sigmoid(c)
        keys = act[:, :STATE]
        queries = act[:, STATE:].astype(bf16)
        keys_t = keys.T.astype(bf16)
        scores = dot_nn(queries, keys_t)
        _, dt, cum = step_sizes(e_ref, par_ref)
        row_ref[...] = cum.T
        spread_heads(cum, dt, col_ref, dtp_ref)
        lower = row_iota((Q, Q)) >= lane_iota((Q, Q))
        low = lane_iota((Q, 128)) < HEADDIM
        scores = jnp.where(lower, scores, 0.0)

        def pair(p):
            lanes = pl.ds(pl.multiple_of(p * 128, 128), 128)
            c = conv_tile(buf, wc_ref, lanes)
            values = c * sigmoid(c)
            col0, col1 = col_ref[2 * p], col_ref[2 * p + 1]
            both = jnp.where(low, col0, col1)
            end = both[Q - 1 : Q, :]
            stepped = values * dtp_ref[p]
            parts = split_pair(stepped.astype(bf16), low)
            mix = []
            for n, col in enumerate((col0, col1)):
                decay = jnp.exp(jnp.minimum(col - row_ref[pl.ds(2 * p + n, 1), :], 0.0))
                mix.append((scores * decay).astype(bf16))
            y = dot_nn(jnp.concatenate(mix, axis=1), parts)
            before = state[:, lanes]
            before_low = before.astype(bf16)
            sin_ref[0, :, lanes] = before_low
            y = y + dot_nn(queries, before_low) * jnp.exp(both)
            y = y + skip_ref[:, lanes] * values
            state[:, lanes] = before * jnp.exp(end) + dot_nn(
                keys_t, (stepped * jnp.exp(end - both)).astype(bf16)
            )
            z = proj_ref[:, lanes].astype(f32)
            gated = y * (z * sigmoid(z))
            y_ref[:, lanes] = y.astype(bf16)
            q_ref[:, lanes] = gated
            return gated * gated

        def body(i, squares):
            for n in range(unroll):
                squares = squares + pair(i * unroll + n)
            return squares

        squares = lax.fori_loop(0, PAIRS // unroll, body, jnp.zeros((Q, 128), f32))
        scale = lax.rsqrt(jnp.sum(squares, axis=-1, keepdims=True) / INNER + epsilon)

        def finish(p, _):
            lanes = pl.ds(pl.multiple_of(p * 128, 128), 128)
            out = q_ref[:, lanes] * scale * g_ref[:, lanes]
            o_ref[:, lanes] = out.astype(bf16)
            turned = out.T.astype(bf16)
            for n in range(128 // O_UNIT):
                there = pl.ds(pl.multiple_of(meta[O_TABLE + p * (128 // O_UNIT) + n], O_UNIT), O_UNIT)
                ot_ref[there, :] = turned[n * O_UNIT : (n + 1) * O_UNIT, :]
            return 0

        lax.fori_loop(0, PAIRS, finish, 0, unroll=2)


def mixer(meta, proj, e, cot, wc, par, skip, g2):
    rows = proj.shape[0]
    chunks = rows // Q
    const = lambda k, m: (0, 0)
    live = lambda k, m: (last_live(m, k), 0)
    return pl.pallas_call(
        functools.partial(mixer_kernel, 2),
        out_shape=(
            jax.ShapeDtypeStruct((rows, INNER), bf16),
            jax.ShapeDtypeStruct((INNER, rows), bf16),
            jax.ShapeDtypeStruct((rows, INNER), bf16),
            jax.ShapeDtypeStruct((chunks, STATE, INNER), bf16),
            jax.ShapeDtypeStruct((rows, D), bf16),
        ),
        grid_spec=pltpu.PrefetchScalarGridSpec(
            num_scalar_prefetch=1,
            grid=(chunks,),
            in_specs=[
                pl.BlockSpec((Q, PROJ), live),
                pl.BlockSpec((Q, 128), live),
                pl.BlockSpec((Q, D), lambda k, m: (source_chunk(m, last_live(m, k), chunks // 2), 0)),
                pl.BlockSpec((8, XBC), const),
                pl.BlockSpec((8, 128), const),
                pl.BlockSpec((1, INNER), const),
                pl.BlockSpec((1, INNER), const),
            ],
            out_specs=[
                pl.BlockSpec((Q, INNER), lambda k, m: (last_padded(m, k), 0)),
                pl.BlockSpec((INNER, Q), lambda k, m: (0, last_padded(m, k))),
                pl.BlockSpec((Q, INNER), live),
                pl.BlockSpec((1, STATE, INNER), lambda k, m: (last_live(m, k), 0, 0)),
                pl.BlockSpec((Q, D), lambda k, m: (last_padded(m, k), 0)),
            ],
            scratch_shapes=[
                pltpu.VMEM((Q + 8, XBC), f32),
                pltpu.VMEM((STATE, INNER), f32),
                pltpu.VMEM((HEADS, Q, 128), f32),
                pltpu.VMEM((PAIRS, Q, 128), f32),
                pltpu.VMEM((128, Q), f32),
                pltpu.VMEM((Q, INNER), f32),
            ],
        ),
        compiler_params=params(),
        cost_estimate=cost(chunks * PAIRS * 8 * 2 * Q * 128 * 128, 2 * rows * (PROJ + 3 * INNER)),
        name="mixer",
    )(meta, proj, e, cot, wc, par, skip, g2)


def gate_kernel(
    slot_chunks, meta, u_ref, err_ref, w_ref, o_ref, y_ref, z_ref, g_ref,
    out_ref, dy_ref, dz_ref, gi_ref,
    do_ref,
):
    b = pl.program_id(0)
    total = meta[0]

    @pl.when(b == 0)
    def _():
        out_ref[...] = jnp.zeros_like(out_ref)
        gi_ref[...] = jnp.zeros_like(gi_ref)

    def body(rows):
        halves = rows // Q
        if halves == 1:
            dz_ref[Q:, :] = jnp.zeros((Q, INNER), bf16)
        starts = []
        for n in range(halves):
            k = 2 * b + n
            start = pl.multiple_of(source_chunk(meta, k, slot_chunks) * Q, Q)
            starts.append(start)
        branch = dot_nn(o_ref[0:rows, :], w_ref[...])
        for n in range(halves):
            live = row_iota((Q, D)) < live_rows(meta, 2 * b + n)
            here = pl.ds(starts[n], Q)
            value = u_ref[here, :].astype(f32) + branch[n * Q : (n + 1) * Q, :]
            out_ref[here, :] = jnp.where(live, value, 0.0).astype(bf16)
        do_ref[0:rows, :] = dot_nt(err_ref[0:rows, :], w_ref[...])

        def sums(p, carry):
            squares, crossed = carry
            lanes = pl.ds(pl.multiple_of(p * 128, 128), 128)
            z = z_ref[0:rows, lanes].astype(f32)
            q = y_ref[0:rows, lanes].astype(f32) * (z * sigmoid(z))
            return squares + q * q, crossed + q * g_ref[:, lanes] * do_ref[0:rows, lanes]

        zero = jnp.zeros((rows, 128), f32)
        squares, crossed = lax.fori_loop(0, PAIRS, sums, (zero, zero), unroll=2)
        scale = lax.rsqrt(jnp.sum(squares, axis=-1, keepdims=True) / INNER + epsilon)
        factor = scale * scale * scale * (jnp.sum(crossed, axis=-1, keepdims=True) / INNER)

        def back(p, _):
            lanes = pl.ds(pl.multiple_of(p * 128, 128), 128)
            z = z_ref[0:rows, lanes].astype(f32)
            y = y_ref[0:rows, lanes].astype(f32)
            s = sigmoid(z)
            gate = z * s
            q = y * gate
            do = do_ref[0:rows, lanes]
            gi_ref[:, lanes] += jnp.sum(do * q * scale, axis=0, keepdims=True)
            dq = scale * (g_ref[:, lanes] * do) - q * factor
            dy_ref[0:rows, lanes] = (dq * gate).astype(bf16)
            dz_ref[0:rows, lanes] = (dq * y * (s * (1.0 + z * (1.0 - s)))).astype(bf16)
            return 0

        lax.fori_loop(0, PAIRS, back, 0, unroll=2)

    pl.when(total >= 2 * b + 2)(functools.partial(body, 2 * Q))
    pl.when(total == 2 * b + 1)(functools.partial(body, Q))


def last_block(m, b):
    return jnp.minimum(b, (m[0] + 1) // 2 - 1)


def gate(meta, u, err, w2, o, y, proj, g2):
    rows = u.shape[0]
    blocks = rows // (2 * Q)
    const = lambda b, m: (0, 0)
    live = lambda b, m: (last_block(m, b), 0)
    once = pl.Buffered(1)
    return pl.pallas_call(
        functools.partial(gate_kernel, rows // Q // 2),
        out_shape=(
            jax.ShapeDtypeStruct((rows, D), bf16),
            jax.ShapeDtypeStruct((rows, INNER), bf16),
            jax.ShapeDtypeStruct((rows, INNER), bf16),
            jax.ShapeDtypeStruct((1, INNER), f32),
        ),
        grid_spec=pltpu.PrefetchScalarGridSpec(
            num_scalar_prefetch=1,
            grid=(blocks,),
            in_specs=[
                pl.BlockSpec((rows, D), const, pipeline_mode=once),
                pl.BlockSpec((2 * Q, D), live),
                pl.BlockSpec((INNER, D), const, pipeline_mode=once),
                pl.BlockSpec((2 * Q, INNER), live),
                pl.BlockSpec((2 * Q, INNER), live),
                pl.BlockSpec((2 * Q, INNER), live),
                pl.BlockSpec((1, INNER), const),
            ],
            out_specs=[
                pl.BlockSpec((rows, D), const),
                pl.BlockSpec((2 * Q, INNER), live),
                pl.BlockSpec((2 * Q, INNER), live),
                pl.BlockSpec((1, INNER), const),
            ],
            scratch_shapes=[pltpu.VMEM((2 * Q, INNER), f32)],
        ),
        compiler_params=params(),
        cost_estimate=cost(4 * rows * D * INNER, 2 * (D * INNER + 5 * rows * INNER)),
        name="gate",
    )(meta, u, err, w2, o, y, proj, g2)


def back_kernel(
    unroll, part, parts, meta, x_ref, prev_ref, e_ref, dy_ref, sin_ref, wc_ref, par_ref, skip_ref, *rest
):
    carried, rest = (rest[:6], rest[6:]) if part > 0 else ((), rest)
    dx_ref, gconv_ref, gpar_ref, gskip_ref = rest[:4]
    passed_on, rest = (rest[4:6], rest[6:]) if part < parts - 1 else ((), rest[4:])
    buf, dbuf, dstate, col_ref, dtp_ref, row_ref, da_ref = rest
    i = pl.program_id(0)
    total = meta[0]
    begin, end = part_span(meta, part, parts)
    k = total - begin - i

    @pl.when(i == 0)
    def _():
        da_ref[...] = jnp.zeros_like(da_ref)
        if part == 0:
            gconv_ref[...] = jnp.zeros_like(gconv_ref)
            gpar_ref[...] = jnp.zeros_like(gpar_ref)
            gskip_ref[...] = jnp.zeros_like(gskip_ref)

            @pl.when(lax.rem(total, 2) == 1)
            def _():
                dx_ref[...] = jnp.zeros_like(dx_ref)

        else:
            for to, came in zip((gconv_ref, gpar_ref, gskip_ref, dstate), carried[1:5]):
                to[...] = came[...]
            dbuf[0:8, :] = carried[5][...]

    @pl.when((i >= 1) & (i <= end - begin))
    def _():
        first = (k == 0) | (k == meta[1])
        last = (k == total - 1) | (k == meta[1] - 1)

        @pl.when(first)
        def _():
            buf[0:8, :] = jnp.zeros((8, XBC), f32)

        @pl.when(jnp.logical_not(first))
        def _():
            buf[0:8, :] = prev_ref[8:16, INNER : INNER + XBC].astype(f32)

        @pl.when(last)
        def _():
            dbuf[Q : Q + 8, :] = jnp.zeros((8, XBC), f32)
            dstate[...] = jnp.zeros_like(dstate)

        @pl.when(jnp.logical_not(last))
        def _():
            dbuf[Q : Q + 8, :] = dbuf[0:8, :]

        buf[8 : 8 + Q, :] = x_ref[:, INNER : INNER + XBC].astype(f32)
        tail_lanes = slice(INNER, XBC)
        c_tail = conv_tile(buf, wc_ref, tail_lanes)
        s_tail = sigmoid(c_tail)
        act = c_tail * s_tail
        keys = act[:, :STATE].astype(bf16)
        queries = act[:, STATE:].astype(bf16)
        queries_t = act[:, STATE:].T.astype(bf16)
        scores = dot_nn(keys, queries_t)
        raw, dt, cum = step_sizes(e_ref, par_ref)
        row_ref[...] = cum.T
        spread_heads(cum, dt, col_ref, dtp_ref)
        upper = row_iota((Q, Q)) <= lane_iota((Q, Q))
        strict = row_iota((Q, Q)) < lane_iota((Q, Q))
        after = (row_iota((Q, Q)) >= lane_iota((Q, Q))).astype(bf16)
        low = lane_iota((Q, 128)) < HEADDIM
        scores = jnp.where(upper, scores, 0.0)
        half = (lax.broadcasted_iota(jnp.int32, (128, 128), 0) >= HEADDIM).astype(jnp.int32)
        head_lane = lane_iota((128, 128))

        def conv_back(lanes, dc):
            dbuf[0:Q, lanes] = dc
            dxbc = wc_ref[CONV - 1 : CONV, lanes] * dc
            for tap in range(CONV - 1):
                dxbc = dxbc + wc_ref[tap : tap + 1, lanes] * dbuf[3 - tap : 3 - tap + Q, lanes]
            dx_ref[:, lanes] = dxbc.astype(bf16)
            for tap in range(CONV):
                gconv_ref[tap : tap + 1, lanes] += jnp.sum(dc * buf[5 + tap : 5 + tap + Q, lanes], axis=0, keepdims=True)
            gconv_ref[CONV : CONV + 1, lanes] += jnp.sum(dc, axis=0, keepdims=True)

        def pair(p, carry):
            dscores, dquery, dkey, from_start, to_end, direct, thru = carry
            lanes = pl.ds(pl.multiple_of(p * 128, 128), 128)
            c = conv_tile(buf, wc_ref, lanes)
            s = sigmoid(c)
            values = c * s
            col0, col1 = col_ref[2 * p], col_ref[2 * p + 1]
            both = jnp.where(low, col0, col1)
            end = both[Q - 1 : Q, :]
            grown = jnp.exp(both)
            rest = jnp.exp(end - both)
            dtp = dtp_ref[p]
            stepped = values * dtp
            dy_low = dy_ref[:, lanes]
            dy = dy_low.astype(f32)
            parts = split_pair(dy_low, low)
            stepped_low = stepped.astype(bf16)
            dmix = dot_nt(stepped_low, parts)
            mix = []
            for n, col in enumerate((col0, col1)):
                decay = jnp.exp(jnp.minimum(row_ref[pl.ds(2 * p + n, 1), :] - col, 0.0))
                weighted = dmix[:, n * Q : (n + 1) * Q] * decay
                dscores = dscores + weighted
                mix.append((scores * decay).astype(bf16))
                passed = dot_nn((weighted * scores).astype(bf16), after)
                da_ref[pl.ds(2 * p + n, 1), :] = jnp.sum(jnp.where(strict, passed, 0.0), axis=0, keepdims=True)
            dstepped = dot_nn(jnp.concatenate(mix, axis=1), parts)
            dafter = dstate[:, lanes]
            dafter_low = dafter.astype(bf16)
            before_low = sin_ref[0, :, lanes]
            dend = dot_nn(keys, dafter_low) * rest
            grown_dy = (dy * grown).astype(bf16)
            select = (head_lane == 2 * p + half).astype(bf16)
            across = dot_nn(queries, before_low)
            from_start = from_start + dot_nn((across * grown * dy).astype(bf16), select)
            to_end = to_end + dot_nn((stepped * dend).astype(bf16), select)
            dstepped = dstepped + dend
            direct = direct + dot_nn((values * dstepped).astype(bf16), select)
            dquery = dquery + dot_nt(grown_dy, before_low)
            dkey = dkey + dot_nt((stepped * rest).astype(bf16), dafter_low)
            kept = jnp.exp(end) * dafter
            held = jnp.sum((kept * before_low.astype(f32)).reshape(8, 16, 128), axis=0)
            thru = thru + dot_nn(held.astype(bf16), select)
            dstate[:, lanes] = kept + dot_nn(queries_t, grown_dy)
            dvalues = dstepped * dtp + skip_ref[:, lanes] * dy
            gskip_ref[:, lanes] += jnp.sum(dy * values, axis=0, keepdims=True)
            conv_back(lanes, dvalues * (s * (1.0 + c * (1.0 - s))))
            return dscores, dquery, dkey, from_start, to_end, direct, thru

        def body(n, carry):
            for m in range(unroll):
                carry = pair(n * unroll + m, carry)
            return carry

        zero = jnp.zeros((Q, 128), f32)
        start = (zero,) * 6 + (jnp.zeros((16, 128), f32),)
        carry = lax.fori_loop(0, PAIRS // unroll, body, start)
        dscores, dquery, dkey, from_start, to_end, direct, thru = carry
        dscores = jnp.where(upper, dscores, 0.0)
        dkey = dkey + dot_nn(dscores.astype(bf16), queries)
        dquery = dquery + dot_nn(dscores.T.astype(bf16), keys)
        slope = s_tail * (1.0 + c_tail * (1.0 - s_tail))
        conv_back(slice(INNER, INNER + STATE), dkey * slope[:, :STATE])
        conv_back(slice(INNER + STATE, XBC), dquery * slope[:, STATE:])

        tail_sum = (row_iota((Q, Q)) <= lane_iota((Q, Q))).astype(f32)
        head_sum = (row_iota((Q, Q)) > lane_iota((Q, Q))).astype(f32)
        da = (
            da_ref[...].T
            + dot_nn(tail_sum, from_start, precision=lax.Precision.HIGHEST)
            + dot_nn(head_sum, to_end, precision=lax.Precision.HIGHEST)
            + jnp.sum(thru, axis=0, keepdims=True)
        )
        ddt = par_ref[1:2, :] * da + direct
        de = ddt * sigmoid(raw)
        de = jnp.where(lane_iota((Q, 128)) < HEADS, de, 0.0)
        dx_ref[:, XBC:] = de.astype(bf16)
        gpar_ref[0:1, :] += jnp.sum(de, axis=0, keepdims=True)
        gpar_ref[1:2, :] += jnp.sum(dt * da, axis=0, keepdims=True)

    if passed_on:

        @pl.when(i == pl.num_programs(0) - 1)
        def _():
            passed_on[0][...] = dstate[...]
            passed_on[1][...] = dbuf[0:8, :]


def part_span(meta, part, parts):
    return (meta[0] * part + parts - 1) // parts, (meta[0] * (part + 1) + parts - 1) // parts


def back(meta, part, parts, carried, proj, e, dy, sin, wc, par, skip):
    rows = proj.shape[0]
    chunks = rows // Q
    const = lambda i, m: (0, 0)

    def chunk(i, m):
        begin, end = part_span(m, part, parts)
        return jnp.clip(m[0] - begin - jnp.clip(i, 1, jnp.maximum(end - begin, 1)), 0, m[0] - 1)

    def written(i, m):
        begin, end = part_span(m, part, parts)
        block = jnp.where(end > begin, chunk(i, m), chunks)
        return jnp.where(i == 0, last_padded(m, m[0]), block) if part == 0 else block

    here = lambda i, m: (chunk(i, m), 0)
    out_shape = [
        jax.ShapeDtypeStruct((rows + Q, XE), bf16),
        jax.ShapeDtypeStruct((8, XBC), f32),
        jax.ShapeDtypeStruct((8, 128), f32),
        jax.ShapeDtypeStruct((1, INNER), f32),
    ]
    sums = [pl.BlockSpec((8, XBC), const), pl.BlockSpec((8, 128), const), pl.BlockSpec((1, INNER), const)]
    state = [pl.BlockSpec((STATE, INNER), const), pl.BlockSpec((8, XBC), const)]
    in_specs = [
        pl.BlockSpec((Q, PROJ), here),
        pl.BlockSpec((16, PROJ), lambda i, m: (jnp.maximum(chunk(i, m) * (Q // 16) - 1, 0), 0)),
        pl.BlockSpec((Q, 128), here),
        pl.BlockSpec((Q, INNER), here),
        pl.BlockSpec((1, STATE, INNER), lambda i, m: (chunk(i, m), 0, 0)),
        pl.BlockSpec((8, XBC), const),
        pl.BlockSpec((8, 128), const),
        pl.BlockSpec((1, INNER), const),
    ]
    out_specs = [pl.BlockSpec((Q, XE), lambda i, m: (written(i, m), 0))] + sums
    if part > 0:
        in_specs += [pl.BlockSpec(memory_space=pl.ANY)] + sums + state
    if part < parts - 1:
        out_shape += [jax.ShapeDtypeStruct((STATE, INNER), f32), jax.ShapeDtypeStruct((8, XBC), f32)]
        out_specs += state
    steps = -(-chunks // parts)
    return pl.pallas_call(
        functools.partial(back_kernel, 2, part, parts),
        out_shape=out_shape,
        grid_spec=pltpu.PrefetchScalarGridSpec(
            num_scalar_prefetch=1,
            grid=(steps + 1,),
            in_specs=in_specs,
            out_specs=out_specs,
            scratch_shapes=[
                pltpu.VMEM((Q + 8, XBC), f32),
                pltpu.VMEM((Q + 8, XBC), f32),
                pltpu.VMEM((STATE, INNER), f32),
                pltpu.VMEM((HEADS, Q, 128), f32),
                pltpu.VMEM((PAIRS, Q, 128), f32),
                pltpu.VMEM((128, Q), f32),
                pltpu.VMEM((128, Q), f32),
            ],
        ),
        input_output_aliases={9: 0} if part > 0 else {},
        compiler_params=params(),
        cost_estimate=cost(steps * PAIRS * 20 * 2 * Q * 128 * 128, 2 * steps * Q * (PROJ + 3 * INNER)),
        name="back",
    )(meta, proj, proj, e, dy, sin, wc, par, skip, *carried)


def weight_kernel(rows, swap_from, meta, at_ref, b_ref, mine_ref, other_ref):
    used = (meta[0] + 1) // 2
    half = at_ref.shape[0] // 2
    part_rows = half // 4
    swap = pl.program_id(0) >= swap_from

    def part(width):
        for c, out_ref in enumerate((mine_ref, other_ref)):

            def step(m, _):
                here = pl.ds(pl.multiple_of(c * half + 2 * m * part_rows, part_rows), 2 * part_rows)
                res = dot_nn(at_ref[here, 0:width], b_ref[0:width, :]).astype(bf16)
                for n in range(2):
                    place = jnp.where(swap, 2 * n + m, 2 * m + n)
                    there = pl.ds(pl.multiple_of(place * part_rows, part_rows), part_rows)
                    out_ref[there, :] = res[n * part_rows : (n + 1) * part_rows, :]
                return 0

            lax.fori_loop(0, 2, step, 0)

    for n in range(1, rows // (2 * Q) + 1):
        pl.when(used == n)(functools.partial(part, n * 2 * Q))


def weight_grad(meta, at, b, first, width, tile, swap_from):
    height, rows = at.shape
    offset = first // tile
    half = jax.ShapeDtypeStruct((height // 2, width), bf16)
    half_spec = pl.BlockSpec((height // 2, tile), lambda j, m: (0, j))
    return pl.pallas_call(
        functools.partial(weight_kernel, rows, swap_from),
        out_shape=(half, half),
        grid_spec=pltpu.PrefetchScalarGridSpec(
            num_scalar_prefetch=1,
            grid=(pl.cdiv(width, tile),),
            in_specs=[
                pl.BlockSpec((height, rows), lambda j, m: (0, 0)),
                pl.BlockSpec((rows, tile), lambda j, m: (0, j + offset)),
            ],
            out_specs=(half_spec, half_spec),
        ),
        compiler_params=params(),
        cost_estimate=cost(2 * rows * height * width, 2 * (rows * (height + width) + height * width)),
        name="weight_grad",
    )(meta, at, b)


def input_kernel(
    slot_chunks, steps, tile, meta, u_ref, err_ref, g_ref, dz_ref, dx_ref, w_ref, out0_ref, out1_ref, gn_ref, dh_ref
):
    j = pl.program_id(0)
    total = meta[0]
    chunks = 2 * slot_chunks
    last = w_ref[:, INNER + XBC : PROJ]
    cols = pl.ds(pl.multiple_of(j * tile, tile), tile)

    def block(b, rows):
        r = slice(b * 2 * Q, b * 2 * Q + rows)
        dh_ref[r, cols] = (
            dot_nt(dz_ref[r, :], w_ref[:, 0:INNER])
            + dot_nt(dx_ref[r, 0:XBC], w_ref[:, INNER : INNER + XBC])
            + dot_nt(dx_ref[r, XBC : XBC + HEADS], last)
        )

    for_blocks(total, chunks // 2, block)

    @pl.when(j == steps - 1)
    def _():
        out0_ref[...] = jnp.zeros_like(out0_ref)
        out1_ref[...] = jnp.zeros_like(out1_ref)
        gn_ref[...] = jnp.zeros_like(gn_ref)
        for k in range(chunks):

            @pl.when(k < total)
            def _():
                start = pl.multiple_of(source_chunk(meta, k, slot_chunks) * Q, Q)
                u = u_ref[pl.ds(start, Q), :].astype(f32)
                err = err_ref[k * Q : (k + 1) * Q, :].astype(f32)
                scale = lax.rsqrt(jnp.mean(u * u, axis=-1, keepdims=True) + epsilon)
                dh = dh_ref[k * Q : (k + 1) * Q, :]
                gn_ref[...] += jnp.sum(dh * (u * scale), axis=0, keepdims=True)
                n = dh * g_ref[...]
                inner = jnp.mean(u * n, axis=-1, keepdims=True)
                du = (err + scale * n - u * (scale * scale * scale * inner)).astype(bf16)

                @pl.when(k < meta[1])
                def _():
                    out0_ref[pl.ds(start, Q), :] = du

                @pl.when(k >= meta[1])
                def _():
                    out1_ref[pl.ds(pl.multiple_of(start - slot_chunks * Q, Q), Q), :] = du


def input_grad_of(meta, u, err, g1, dz, dx, w1):
    rows = u.shape[0]
    tile = 256
    steps = D // tile
    const = lambda j, m: (0, 0)
    once = pl.Buffered(1)
    return pl.pallas_call(
        functools.partial(input_kernel, rows // Q // 2, steps, tile),
        out_shape=(
            jax.ShapeDtypeStruct((rows // 2, D), bf16),
            jax.ShapeDtypeStruct((rows // 2, D), bf16),
            jax.ShapeDtypeStruct((1, D), f32),
        ),
        grid_spec=pltpu.PrefetchScalarGridSpec(
            num_scalar_prefetch=1,
            grid=(steps,),
            in_specs=[
                pl.BlockSpec((rows, D), const, pipeline_mode=once),
                pl.BlockSpec((rows, D), const, pipeline_mode=once),
                pl.BlockSpec((1, D), const),
                pl.BlockSpec((rows, INNER), const, pipeline_mode=once),
                pl.BlockSpec((rows, XE), const, pipeline_mode=once),
                pl.BlockSpec((tile, w1.shape[1]), lambda j, m: (j, 0)),
            ],
            out_specs=[
                pl.BlockSpec((rows // 2, D), const),
                pl.BlockSpec((rows // 2, D), const),
                pl.BlockSpec((1, D), const),
            ],
            scratch_shapes=[pltpu.VMEM((rows, D), f32)],
        ),
        compiler_params=params(),
        cost_estimate=cost(2 * rows * D * PROJ, 2 * (D * PROJ + rows * PROJ)),
        name="input_grad",
    )(meta, u, err, g1, dz, dx, w1)


def partner(value, axis, bit):
    mask = 2**bit
    pairs = [(source, source ^ mask) for source in range(lax.axis_size(axis))]
    return lax.ppermute(value, axis, pairs)


def log2(size):
    return size.bit_length() - 1


def halving_order(swap):
    fsdp = [("fsdp", bit) for bit in range(log2(lax.axis_size("fsdp")))]
    near = [("dp", 1)]
    far = [("dp", bit) for bit in range(2, log2(lax.axis_size("dp")))]
    return [("dp", 0)] + (near + fsdp if swap else fsdp + near) + far


def flat_bit(axis, bit):
    return bit + (log2(lax.axis_size("fsdp")) if axis == "dp" else 0)


def kept_at(order, owner):
    away = owner ^ lax.axis_index(AXES)
    place = jnp.zeros_like(away)
    for axis, bit in order:
        place = 2 * place + ((away >> flat_bit(axis, bit)) & 1)
    return place


def owner_at(order, place):
    away = jnp.zeros_like(place)
    for n, (axis, bit) in enumerate(order):
        away = away + (((place >> (len(order) - 1 - n)) & 1) << flat_bit(axis, bit))
    return away ^ lax.axis_index(AXES)


class Term:
    def __init__(self, value):
        self.value = value


class Columns:
    def __init__(self, width, swap):
        self.order = halving_order(swap)
        self.width = width
        self.terms = []
        self.phase = 0

    def done(self):
        return self.phase == len(self.order)

    def sum(self, start, stop):
        return sum(term.value[start:stop, at : at + self.width].astype(f32) for term, at in self.terms)

    def halve(self):
        self.rows //= 2
        return self.sum(self.rows, 2 * self.rows).astype(bf16)


class Chain:
    def __init__(self, halves, columns, grouped):
        mine, other = halves
        self.columns = columns
        if not grouped:
            count = lax.axis_size(AXES)
            whole = jnp.concatenate([mine, other]).reshape(count, -1, mine.shape[1])
            parts = []
            at = 0
            for c in columns:
                parts.append(whole[:, :, at : at + c.width][owner_at(c.order, jnp.arange(count))])
                at += c.width
            mine, other = jnp.concatenate(parts, axis=2).reshape(2, -1, mine.shape[1])
        self.going = [(columns, other)]
        kept = Term(mine)
        at = 0
        for c in columns:
            c.rows = mine.shape[0]
            c.terms.append((kept, at))
            at += c.width

    def halve(self):
        groups = {}
        for c in self.columns:
            if not c.done() and all(c not in members for members, _ in self.going):
                groups.setdefault((c.order[c.phase], c.rows), []).append(c)
        for members in groups.values():
            sent = [c.halve() for c in members]
            self.going.append((members, jnp.concatenate(sent, axis=1) if len(sent) > 1 else sent[0]))

    def exchange(self):
        for members, sent in self.going:
            first = members[0]
            came = Term(partner(sent, *first.order[first.phase]))
            at = 0
            for c in members:
                c.terms.append((came, at))
                c.phase += 1
                at += c.width
        self.going = []

    def finish(self):
        while not all(c.done() for c in self.columns):
            self.halve()
            self.exchange()
        return [c.sum(0, c.rows) for c in self.columns]


def tick(token, chains, after):
    last = {id(c.terms[-1][0]): c.terms[-1][0] for chain in chains for c in chain.columns if c.phase > 0}
    if last:
        *came, _ = lax.optimization_barrier([term.value for term in last.values()] + [after])
        for term, value in zip(last.values(), came):
            term.value = value
    for chain in chains:
        chain.halve()
    sent = [value for chain in chains for _, value in chain.going]
    *sent, token = lax.optimization_barrier(sent + [token])
    for chain in chains:
        chain.going = [(members, sent.pop(0)) for members, _ in chain.going]
        chain.exchange()
    return token


W_COLS = 6528
W_CUT = 3328


def gather_kernel(
    count, inner, flag_ref, shard_ref, tile_ref, tokens_ref, w_ref, tiles_ref, u_ref,
    kept, given, send_sem, recv_sem, tile_send, tile_recv, own_sem, give_send, give_recv,
):
    me = lax.axis_index("dp") * inner + lax.axis_index("fsdp")
    height = shard_ref.shape[0]
    x, core, y = flat_bit("fsdp", 0), flat_bit("dp", 0), flat_bit("dp", 1)
    far = [flat_bit("dp", bit) for bit in range(2, log2(lax.axis_size("dp")))]
    ways = (far + [y, x, core], far + [x, y, core])
    spans = (pl.ds(0, W_CUT), pl.ds(W_CUT, W_COLS - W_CUT))

    def place(away):
        return pl.ds(pl.multiple_of(jnp.bitwise_xor(me, away) * height, height), height)

    def link(bit):
        other = jnp.bitwise_xor(me, 2**bit)
        return (other // inner, other % inner)

    def last_step(half, away):
        return max((n for n, bit in enumerate(ways[half]) if (away >> bit) & 1), default=-1)

    def send(half, away, bit):
        src = shard_ref.at[:, spans[half]] if away == 0 else w_ref.at[place(away), spans[half]]
        return pltpu.make_async_remote_copy(
            src_ref=src,
            dst_ref=w_ref.at[place(away), spans[half]],
            send_sem=send_sem.at[half, away ^ 2**bit],
            recv_sem=recv_sem.at[half, away ^ 2**bit],
            device_id=link(bit),
            device_id_type=pl.DeviceIdType.MESH,
        )

    def receive(half, away):
        block = w_ref.at[place(away), spans[half]]
        return pltpu.make_async_remote_copy(
            src_ref=block,
            dst_ref=block,
            send_sem=send_sem.at[half, away],
            recv_sem=recv_sem.at[half, away],
            device_id=link(ways[half][last_step(half, away)]),
            device_id_type=pl.DeviceIdType.MESH,
        )

    def send_on(half, away):
        sends = [send(half, away, bit) for bit in ways[half][last_step(half, away) + 1 :]]
        for one in sends:
            one.start()
        return sends

    def tile_copy(n):
        other = jnp.bitwise_xor(me, n)
        return pltpu.make_async_remote_copy(
            src_ref=tile_ref,
            dst_ref=tiles_ref.at[me],
            send_sem=tile_send.at[n],
            recv_sem=tile_recv.at[n],
            device_id=(other // inner, other % inner),
            device_id_type=pl.DeviceIdType.MESH,
        )

    def start_tile(n, _):
        tile_copy(n).start()
        return 0

    def wait_tile(n, _):
        tile_copy(n).wait()
        return 0

    started = []
    for step in range(len(ways[0])):
        for half in range(2):
            one = send(half, 0, ways[half][step])
            one.start()
            started.append(one)
    own = pltpu.make_async_copy(shard_ref, w_ref.at[place(0), :], own_sem.at[0])
    own.start()
    lax.fori_loop(1, count, start_tile, 0)
    tiles_ref[me] = tile_ref[...]

    second = jnp.broadcast_to(flag_ref[0, 0], (1, D)) == 1
    rows = kept.shape[0]

    def choose(n, _):
        r = pl.ds(pl.multiple_of(n * 64, 64), 64)
        zero, one = tokens_ref[0, r, :].astype(f32), tokens_ref[1, r, :].astype(f32)
        kept[r, :] = jnp.where(second, one, zero).astype(bf16)
        given[r, :] = jnp.where(second, zero, one).astype(bf16)
        return 0

    lax.fori_loop(0, rows // 64, choose, 0)

    blocks = [(half, away) for half in range(2) for away in range(1, count)]
    blocks.sort(key=lambda b: (b[1].bit_count(), last_step(*b), b[0]))
    tail = []
    for n, (half, away) in enumerate(blocks):
        receive(half, away).wait_recv()
        started += send_on(half, away)
        if n == 8:
            keep = pltpu.make_async_copy(kept, u_ref.at[pl.ds(0, rows), :], own_sem.at[1])
            give = pltpu.make_async_remote_copy(
                src_ref=given,
                dst_ref=u_ref.at[pl.ds(rows, rows), :],
                send_sem=give_send,
                recv_sem=give_recv,
                device_id=link(core),
                device_id_type=pl.DeviceIdType.MESH,
            )
            keep.start()
            give.start()
            tail = [keep, give]
    for one in started:
        one.wait_send()
    for one in tail:
        one.wait()
    own.wait()
    lax.fori_loop(1, count, wait_tile, 0)


def gather(flag, shard, tile, tokens):
    count = lax.axis_size(AXES)
    slot = tokens.shape[1]
    whole = pl.BlockSpec(memory_space=pltpu.VMEM)
    anywhere = pl.BlockSpec(memory_space=pl.ANY)
    dma = pltpu.SemaphoreType.DMA
    return pl.pallas_call(
        functools.partial(gather_kernel, count, lax.axis_size("fsdp")),
        out_shape=(
            jax.ShapeDtypeStruct((D, W_COLS), bf16),
            jax.ShapeDtypeStruct((count, 8, 128), f32),
            jax.ShapeDtypeStruct((2 * slot, D), bf16),
        ),
        in_specs=[pl.BlockSpec(memory_space=pltpu.SMEM), whole, whole, whole],
        out_specs=(anywhere, whole, anywhere),
        scratch_shapes=[
            pltpu.VMEM((slot, D), bf16),
            pltpu.VMEM((slot, D), bf16),
            dma((2, count)),
            dma((2, count)),
            dma((count,)),
            dma((count,)),
            dma((2,)),
            dma,
            dma,
        ],
        compiler_params=params(has_side_effects=True),
        cost_estimate=cost(1e6, 2 * D * W_COLS),
        name="gather",
    )(flag, shard, tile, tokens)


def sum_kernel(count, inner, sent_ref, out_ref, came, send_sem, recv_sem):
    me = lax.axis_index("dp") * inner + lax.axis_index("fsdp")

    def copy(n):
        other = jnp.bitwise_xor(me, n)
        return pltpu.make_async_remote_copy(
            src_ref=sent_ref.at[other],
            dst_ref=came.at[n],
            send_sem=send_sem.at[n],
            recv_sem=recv_sem.at[n],
            device_id=(other // inner, other % inner),
            device_id_type=pl.DeviceIdType.MESH,
        )

    def start(n, _):
        copy(n).start()
        return 0

    def add(n, total):
        copy(n).wait()
        return total + came[n]

    lax.fori_loop(1, count, start, 0)
    out_ref[...] = lax.fori_loop(1, count, add, sent_ref[me])


def sum_small(tiles):
    count = tiles.shape[0]
    whole = pl.BlockSpec(memory_space=pltpu.VMEM)
    return pl.pallas_call(
        functools.partial(sum_kernel, count, lax.axis_size("fsdp")),
        out_shape=jax.ShapeDtypeStruct(tiles.shape[1:], f32),
        in_specs=[whole],
        out_specs=whole,
        scratch_shapes=[
            pltpu.VMEM(tiles.shape, f32),
            pltpu.SemaphoreType.DMA((count,)),
            pltpu.SemaphoreType.DMA((count,)),
        ],
        compiler_params=pltpu.CompilerParams(has_side_effects=True),
        cost_estimate=cost(count * 1024, 8 * count * 1024),
        name="sum_small",
    )(tiles)


def on_device(
    tokens, cotangent, lengths, balance, norm_gain, in_weight, conv_weight, conv_bias,
    step_bias, decay_log, skip_weight, inner_gain, out_weight,
):
    device = lax.axis_index(AXES)
    count = lax.axis_size(AXES)
    slot = tokens.shape[1]
    rows = 2 * slot
    first_source = balance[2 * device]
    second_source = balance[2 * device + 1]
    keep_second = first_source - 2 * device == 1
    cot = cotangent.reshape(rows, D)
    lens = [lengths[first_source], lengths[second_source]]
    chunks = [(n + Q - 1) // Q for n in lens]
    grouped = D // count == H_UNIT
    h_units = jnp.arange(D // H_UNIT)
    o_units = jnp.arange(INNER // O_UNIT)
    if grouped:
        order = halving_order(False)
        each = INNER // count // O_UNIT
        h_units = kept_at(order, h_units)
        o_units = kept_at(order, o_units // each) * each + o_units % each
    meta = jnp.concatenate(
        [jnp.stack([chunks[0] + chunks[1], chunks[0], lens[0], lens[1]]), h_units * H_UNIT, o_units * O_UNIT]
    ).astype(jnp.int32)

    small = [norm_gain, conv_weight.reshape(-1), conv_bias, inner_gain]
    sizes = [v.shape[0] for v in small]
    packed = jnp.concatenate(small).astype(bf16)
    if grouped:
        tile = jnp.pad(packed.astype(f32), (0, 1024 - packed.shape[0])).reshape(8, 128)
        shard = jnp.pad(in_weight.astype(bf16), ((0, 0), (0, W_COLS - PROJ)))
        w1, packed, u = gather(keep_second.astype(jnp.int32).reshape(1, 1), shard, tile, tokens)
        packed = packed.reshape(count, -1)
    else:
        outgoing = jnp.where(keep_second, tokens[0], tokens[1])
        incoming = partner(outgoing, "dp", 0)
        u = jnp.concatenate([jnp.where(keep_second, tokens[1], tokens[0]), incoming], axis=0)
        w1 = lax.all_gather(in_weight.astype(bf16), AXES, axis=0, tiled=True)
        packed = lax.all_gather(packed[None, :], AXES, axis=0, tiled=True).astype(f32)
    cuts = [sum(sizes[:n]) for n in range(len(sizes) + 1)]
    norm_full, conv_full, bias_full, inner_full = (
        packed[:, cuts[n] : cuts[n + 1]].reshape(-1) for n in range(4)
    )
    w2_own, w1 = lax.optimization_barrier([out_weight.astype(bf16), w1])
    w2 = lax.all_gather(w2_own, AXES, axis=0, tiled=True)

    wc = jnp.concatenate([conv_full.reshape(XBC, CONV).T, bias_full[None], jnp.zeros((3, XBC), f32)])
    rate = -jnp.exp(decay_log)
    par = jnp.zeros((8, 128), f32).at[0, :HEADS].set(step_bias).at[1, :HEADS].set(rate)
    skip = jnp.repeat(skip_weight, HEADDIM)[None]
    g1 = norm_full[None]
    g2 = inner_full[None]

    proj, e, ht = project(meta, u, g1, w1)
    o, ot, y, sin, err = mixer(meta, proj, e, cot, wc, par, skip, g2)
    never = 1 << 20

    def both(width):
        return [Columns(width // 2, False), Columns(width // 2, True)]

    halves = weight_grad(meta, ot, err, 0, D, D // 2, 1 if grouped else never)
    c_out = Chain(halves, both(D), grouped)
    meta = tick(meta, [c_out], err)
    out, dy, dz, gi = gate(meta, u, err, w2, o, y, proj, g2)
    meta = tick(meta, [c_out], gi)
    halves = weight_grad(meta, ht, dz, 0, INNER, INNER // 4, 2 if grouped else never)
    c_z = Chain(halves, both(INNER), grouped)
    parts = 3
    carried = ()
    for part in range(parts):
        meta = tick(meta, [c_out, c_z] if part > 0 else [c_z], carried[2] if part > 0 else gi)
        carried = back(meta, part, parts, carried, proj, e, dy, sin, wc, par, skip)
    dx, gconv, gpar, gskip = carried
    meta = tick(meta, [c_out, c_z], gpar)
    cut = 1792
    halves = weight_grad(meta, ht, dx, 0, cut, cut // 2, never)
    c_x = Chain(halves, [Columns(cut, False)], grouped)
    meta = tick(meta, [c_z, c_x], halves[1])
    halves = weight_grad(meta, ht, dx, cut, XE - cut, cut // 2, 0 if grouped else never)
    c_x1 = Chain(halves, [Columns(XE - cut, True)], grouped)
    meta = tick(meta, [c_x, c_x1], halves[1])
    meta = tick(meta, [c_x1], c_x1.columns[0].terms[-1][0].value)
    c_x.columns += c_x1.columns
    kept_half, given_half, gn = input_grad_of(meta, u, err, g1, dz, dx, w1)
    heads = jnp.concatenate(
        [gpar[0, :HEADS], gpar[1, :HEADS] * rate, gskip.reshape(HEADS, HEADDIM).sum(axis=1)]
    )
    owned = [gconv[:CONV].T.reshape(count, -1), gconv[CONV].reshape(count, -1), gi.reshape(count, -1)]
    tiles = jnp.concatenate(owned + [jnp.broadcast_to(heads, (count, 3 * HEADS)), gn.reshape(count, -1)], axis=1)
    tiles = jnp.pad(tiles, ((0, 0), (0, 1024 - tiles.shape[1]))).reshape(count, 8, 128)
    tiles = tick(tiles, [c_out, c_z, c_x], gn)
    sums = sum_small(tiles).reshape(-1)
    grad_out = jnp.concatenate(c_out.finish(), axis=1)
    grad_in = jnp.concatenate(c_z.finish() + c_x.finish(), axis=1)[:, :PROJ]

    back_half = partner(given_half, "dp", 0)
    input_grad = jnp.stack(
        [jnp.where(keep_second, back_half, kept_half), jnp.where(keep_second, kept_half, back_half)]
    )
    ends = [sum(v.shape[1] for v in owned[:n]) for n in range(4)]
    grad_conv = sums[: ends[1]].reshape(-1, CONV)
    grad_bias = sums[ends[1] : ends[2]]
    grad_inner = sums[ends[2] : ends[3]]
    heads = sums[ends[3] : ends[3] + 3 * HEADS]
    grad_norm = sums[ends[3] + 3 * HEADS :][: sizes[0]]
    return (
        out.reshape(2, slot, D),
        input_grad,
        grad_norm,
        grad_in,
        grad_conv,
        grad_bias,
        heads[:HEADS],
        heads[HEADS : 2 * HEADS],
        heads[2 * HEADS :],
        grad_inner,
        grad_out,
    )


def solution(mesh):
    flat = P(AXES)
    rowed = P(AXES, None)
    slots = P(AXES, None, None)
    return jax.shard_map(
        on_device,
        mesh=mesh,
        in_specs=(slots, slots, P(), P(), flat, rowed, rowed, flat, P(), P(), P(), flat, rowed),
        out_specs=(slots, slots, flat, rowed, rowed, flat, P(), P(), P(), flat, rowed),
        check_vma=False,
    )
```

```python
import functools
import jax
import jax.numpy as jnp
from jax import lax
from jax.experimental import pallas as pl
from jax.experimental.pallas import tpu as pltpu
from jax.sharding import PartitionSpec as P

D = 1536
INNER = 3072
HEADS = 48
HEADDIM = 64
STATE = 128
CONV = 4
XBC = 3328
PROJ = 6448
XE = XBC + 128
Q = 128
PAIRS = HEADS // 2

f32 = jnp.float32
bf16 = jnp.bfloat16
epsilon = 1e-05
AXES = ("dp", "fsdp")


def sigmoid(v):
    return 0.5 * jnp.tanh(0.5 * v) + 0.5


def dot_nn(a, b, precision=None):
    return jnp.dot(a, b, preferred_element_type=f32, precision=precision)


def dot_nt(a, b):
    return lax.dot_general(a, b, (((1,), (1,)), ((), ())), preferred_element_type=f32)


def dot_tn(a, b):
    return lax.dot_general(a, b, (((0,), (0,)), ((), ())), preferred_element_type=f32)


def lane_iota(shape):
    return lax.broadcasted_iota(jnp.int32, shape, len(shape) - 1)


def row_iota(shape):
    return lax.broadcasted_iota(jnp.int32, shape, len(shape) - 2)


H_UNIT = 48
H_TABLE = 4
O_UNIT = 32
O_TABLE = H_TABLE + D // H_UNIT


def source_chunk(meta, k, slot_chunks):
    return jnp.where(k < meta[1], k, k - meta[1] + slot_chunks)


def live_rows(meta, k):
    inside = k < meta[1]
    return jnp.where(inside, meta[2] - k * Q, meta[3] - (k - meta[1]) * Q)


def last_live(meta, k):
    return jnp.minimum(k, meta[0] - 1)


def last_padded(meta, k):
    return jnp.minimum(k, meta[0] + lax.rem(meta[0], 2) - 1)


def for_blocks(total, blocks, body):
    for b in range(blocks):
        pl.when(total >= 2 * b + 2)(functools.partial(body, b, 2 * Q))
        pl.when(total == 2 * b + 1)(functools.partial(body, b, Q))


def cost(flops, moved, transcendentals=0):
    return pl.CostEstimate(flops=int(flops), bytes_accessed=int(moved), transcendentals=int(transcendentals))


def params(**kw):
    return pltpu.CompilerParams(vmem_limit_bytes=60 * 1024 * 1024, **kw)


def project_kernel(slot_chunks, steps, tile, meta, u_ref, g_ref, w_ref, proj_ref, e_ref, ht_ref, h_ref):
    j = pl.program_id(0)
    total = meta[0]
    chunks = 2 * slot_chunks

    @pl.when(j == 0)
    def _():
        for k in range(chunks):

            @pl.when(k < total)
            def _():
                start = pl.multiple_of(source_chunk(meta, k, slot_chunks) * Q, Q)
                x = u_ref[pl.ds(start, Q), :].astype(f32)
                scale = lax.rsqrt(jnp.mean(x * x, axis=-1, keepdims=True) + epsilon)
                normed = x * scale * g_ref[...]
                h_ref[k * Q : (k + 1) * Q, :] = normed.astype(bf16)
                turned = normed.T.astype(bf16)
                for n in range(D // H_UNIT):
                    there = pl.ds(pl.multiple_of(meta[H_TABLE + n], 16), H_UNIT)
                    ht_ref[there, k * Q : (k + 1) * Q] = turned[n * H_UNIT : (n + 1) * H_UNIT, :]

            @pl.when(k >= total)
            def _():
                ht_ref[:, k * Q : (k + 1) * Q] = jnp.zeros((D, Q), bf16)

    edge = XBC + INNER - (steps - 1) * tile

    def block(b, rows):
        r = slice(b * 2 * Q, b * 2 * Q + rows)
        acc = dot_nn(h_ref[r, :], w_ref[...])
        proj_ref[r, :] = acc.astype(bf16)

        @pl.when(j == steps - 1)
        def _():
            tail = dot_nn(h_ref[r, :], w_ref[:, edge : edge + 128])
            e_ref[r, :] = jnp.where(lane_iota(tail.shape) < HEADS, tail, 0.0)

    for_blocks(total, chunks // 2, block)


def project(meta, u, g1, w1):
    rows = u.shape[0]
    tile = 512
    steps = pl.cdiv(PROJ, tile)
    return pl.pallas_call(
        functools.partial(project_kernel, rows // Q // 2, steps, tile),
        out_shape=(
            jax.ShapeDtypeStruct((rows, PROJ), bf16),
            jax.ShapeDtypeStruct((rows, 128), f32),
            jax.ShapeDtypeStruct((D, rows), bf16),
        ),
        grid_spec=pltpu.PrefetchScalarGridSpec(
            num_scalar_prefetch=1,
            grid=(steps,),
            in_specs=[
                pl.BlockSpec((rows, D), lambda j, m: (0, 0)),
                pl.BlockSpec((1, D), lambda j, m: (0, 0)),
                pl.BlockSpec((D, tile), lambda j, m: (0, j)),
            ],
            out_specs=[
                pl.BlockSpec((rows, tile), lambda j, m: (0, j)),
                pl.BlockSpec((rows, 128), lambda j, m: (0, 0)),
                pl.BlockSpec((D, rows), lambda j, m: (0, 0)),
            ],
            scratch_shapes=[pltpu.VMEM((rows, D), bf16)],
        ),
        compiler_params=params(),
        cost_estimate=cost(2 * rows * D * PROJ, 2 * (D * PROJ + rows * PROJ)),
        name="project",
    )(meta, u, g1, w1)


def conv_tile(buf, wc_ref, lanes):
    c = wc_ref[CONV : CONV + 1, lanes]
    for tap in range(CONV):
        c = c + wc_ref[tap : tap + 1, lanes] * buf[5 + tap : 5 + tap + Q, lanes]
    return c


def step_sizes(e_ref, par_ref):
    raw = e_ref[...] + par_ref[0:1, :]
    dt = jnp.maximum(raw, 0.0) + jnp.log1p(jnp.exp(-jnp.abs(raw)))
    decay = par_ref[1:2, :]
    lower = (row_iota((Q, Q)) >= lane_iota((Q, Q))).astype(f32)
    cum = dot_nn(lower, dt * decay, precision=lax.Precision.HIGHEST)
    return raw, dt, cum


def spread_heads(cum, dt, col_ref, dtp_ref):
    low = lane_iota((Q, 128)) < HEADDIM
    for p in range(PAIRS):
        for h in (2 * p, 2 * p + 1):
            col_ref[h] = jnp.broadcast_to(cum[:, h : h + 1], (Q, 128))
        dtp_ref[p] = jnp.where(
            low,
            jnp.broadcast_to(dt[:, 2 * p : 2 * p + 1], (Q, 128)),
            jnp.broadcast_to(dt[:, 2 * p + 1 : 2 * p + 2], (Q, 128)),
        )


def split_pair(v, low):
    zero = jnp.zeros_like(v)
    return jnp.concatenate([jnp.where(low, v, zero), jnp.where(low, zero, v)], axis=0)


def mixer_kernel(
    unroll, meta, proj_ref, e_ref, cot_ref, wc_ref, par_ref, skip_ref, g_ref,
    o_ref, ot_ref, y_ref, sin_ref, err_ref,
    buf, state, col_ref, dtp_ref, row_ref, q_ref,
):
    k = pl.program_id(0)
    total = meta[0]

    @pl.when((k == total) & (lax.rem(total, 2) == 1))
    def _():
        o_ref[...] = jnp.zeros_like(o_ref)
        ot_ref[...] = jnp.zeros_like(ot_ref)
        err_ref[...] = jnp.zeros_like(err_ref)

    @pl.when(k < total)
    def _():
        live = row_iota((Q, D)) < live_rows(meta, k)
        err_ref[...] = jnp.where(live, cot_ref[...].astype(f32), 0.0).astype(bf16)
        first = (k == 0) | (k == meta[1])

        @pl.when(first)
        def _():
            buf[0:8, :] = jnp.zeros((8, XBC), f32)
            state[...] = jnp.zeros_like(state)

        @pl.when(jnp.logical_not(first))
        def _():
            buf[0:8, :] = buf[Q : Q + 8, :]

        buf[8 : 8 + Q, :] = proj_ref[:, INNER : INNER + XBC].astype(f32)
        tail_lanes = slice(INNER, XBC)
        c = conv_tile(buf, wc_ref, tail_lanes)
        act = c * sigmoid(c)
        keys = act[:, :STATE]
        queries = act[:, STATE:].astype(bf16)
        keys_t = keys.T.astype(bf16)
        scores = dot_nn(queries, keys_t)
        _, dt, cum = step_sizes(e_ref, par_ref)
        row_ref[...] = cum.T
        spread_heads(cum, dt, col_ref, dtp_ref)
        lower = row_iota((Q, Q)) >= lane_iota((Q, Q))
        low = lane_iota((Q, 128)) < HEADDIM
        scores = jnp.where(lower, scores, 0.0)

        def pair(p):
            lanes = pl.ds(pl.multiple_of(p * 128, 128), 128)
            c = conv_tile(buf, wc_ref, lanes)
            values = c * sigmoid(c)
            col0, col1 = col_ref[2 * p], col_ref[2 * p + 1]
            both = jnp.where(low, col0, col1)
            end = both[Q - 1 : Q, :]
            stepped = values * dtp_ref[p]
            parts = split_pair(stepped.astype(bf16), low)
            mix = []
            for n, col in enumerate((col0, col1)):
                decay = jnp.exp(jnp.minimum(col - row_ref[pl.ds(2 * p + n, 1), :], 0.0))
                mix.append((scores * decay).astype(bf16))
            y = dot_nn(jnp.concatenate(mix, axis=1), parts)
            before = state[:, lanes]
            before_low = before.astype(bf16)
            sin_ref[0, :, lanes] = before_low
            y = y + dot_nn(queries, before_low) * jnp.exp(both)
            y = y + skip_ref[:, lanes] * values
            state[:, lanes] = before * jnp.exp(end) + dot_nn(
                keys_t, (stepped * jnp.exp(end - both)).astype(bf16)
            )
            z = proj_ref[:, lanes].astype(f32)
            gated = y * (z * sigmoid(z))
            y_ref[:, lanes] = y.astype(bf16)
            q_ref[:, lanes] = gated
            return gated * gated

        def body(i, squares):
            for n in range(unroll):
                squares = squares + pair(i * unroll + n)
            return squares

        squares = lax.fori_loop(0, PAIRS // unroll, body, jnp.zeros((Q, 128), f32))
        scale = lax.rsqrt(jnp.sum(squares, axis=-1, keepdims=True) / INNER + epsilon)

        def finish(p, _):
            lanes = pl.ds(pl.multiple_of(p * 128, 128), 128)
            out = q_ref[:, lanes] * scale * g_ref[:, lanes]
            o_ref[:, lanes] = out.astype(bf16)
            turned = out.T.astype(bf16)
            for n in range(128 // O_UNIT):
                there = pl.ds(pl.multiple_of(meta[O_TABLE + p * (128 // O_UNIT) + n], O_UNIT), O_UNIT)
                ot_ref[there, :] = turned[n * O_UNIT : (n + 1) * O_UNIT, :]
            return 0

        lax.fori_loop(0, PAIRS, finish, 0, unroll=2)


def mixer(meta, proj, e, cot, wc, par, skip, g2):
    rows = proj.shape[0]
    chunks = rows // Q
    const = lambda k, m: (0, 0)
    live = lambda k, m: (last_live(m, k), 0)
    return pl.pallas_call(
        functools.partial(mixer_kernel, 2),
        out_shape=(
            jax.ShapeDtypeStruct((rows, INNER), bf16),
            jax.ShapeDtypeStruct((INNER, rows), bf16),
            jax.ShapeDtypeStruct((rows, INNER), bf16),
            jax.ShapeDtypeStruct((chunks, STATE, INNER), bf16),
            jax.ShapeDtypeStruct((rows, D), bf16),
        ),
        grid_spec=pltpu.PrefetchScalarGridSpec(
            num_scalar_prefetch=1,
            grid=(chunks,),
            in_specs=[
                pl.BlockSpec((Q, PROJ), live),
                pl.BlockSpec((Q, 128), live),
                pl.BlockSpec((Q, D), lambda k, m: (source_chunk(m, last_live(m, k), chunks // 2), 0)),
                pl.BlockSpec((8, XBC), const),
                pl.BlockSpec((8, 128), const),
                pl.BlockSpec((1, INNER), const),
                pl.BlockSpec((1, INNER), const),
            ],
            out_specs=[
                pl.BlockSpec((Q, INNER), lambda k, m: (last_padded(m, k), 0)),
                pl.BlockSpec((INNER, Q), lambda k, m: (0, last_padded(m, k))),
                pl.BlockSpec((Q, INNER), live),
                pl.BlockSpec((1, STATE, INNER), lambda k, m: (last_live(m, k), 0, 0)),
                pl.BlockSpec((Q, D), lambda k, m: (last_padded(m, k), 0)),
            ],
            scratch_shapes=[
                pltpu.VMEM((Q + 8, XBC), f32),
                pltpu.VMEM((STATE, INNER), f32),
                pltpu.VMEM((HEADS, Q, 128), f32),
                pltpu.VMEM((PAIRS, Q, 128), f32),
                pltpu.VMEM((128, Q), f32),
                pltpu.VMEM((Q, INNER), f32),
            ],
        ),
        compiler_params=params(),
        cost_estimate=cost(chunks * PAIRS * 8 * 2 * Q * 128 * 128, 2 * rows * (PROJ + 3 * INNER)),
        name="mixer",
    )(meta, proj, e, cot, wc, par, skip, g2)


def gate_kernel(
    slot_chunks, meta, u_ref, err_ref, w_ref, o_ref, y_ref, z_ref, g_ref,
    out_ref, dy_ref, dz_ref, gi_ref,
    do_ref,
):
    b = pl.program_id(0)
    total = meta[0]

    @pl.when(b == 0)
    def _():
        out_ref[...] = jnp.zeros_like(out_ref)
        gi_ref[...] = jnp.zeros_like(gi_ref)

    def body(rows):
        halves = rows // Q
        if halves == 1:
            dz_ref[Q:, :] = jnp.zeros((Q, INNER), bf16)
        starts = []
        for n in range(halves):
            k = 2 * b + n
            start = pl.multiple_of(source_chunk(meta, k, slot_chunks) * Q, Q)
            starts.append(start)
        branch = dot_nn(o_ref[0:rows, :], w_ref[...])
        for n in range(halves):
            live = row_iota((Q, D)) < live_rows(meta, 2 * b + n)
            here = pl.ds(starts[n], Q)
            value = u_ref[here, :].astype(f32) + branch[n * Q : (n + 1) * Q, :]
            out_ref[here, :] = jnp.where(live, value, 0.0).astype(bf16)
        do_ref[0:rows, :] = dot_nt(err_ref[0:rows, :], w_ref[...])

        def sums(p, carry):
            squares, crossed = carry
            lanes = pl.ds(pl.multiple_of(p * 128, 128), 128)
            z = z_ref[0:rows, lanes].astype(f32)
            q = y_ref[0:rows, lanes].astype(f32) * (z * sigmoid(z))
            return squares + q * q, crossed + q * g_ref[:, lanes] * do_ref[0:rows, lanes]

        zero = jnp.zeros((rows, 128), f32)
        squares, crossed = lax.fori_loop(0, PAIRS, sums, (zero, zero), unroll=2)
        scale = lax.rsqrt(jnp.sum(squares, axis=-1, keepdims=True) / INNER + epsilon)
        factor = scale * scale * scale * (jnp.sum(crossed, axis=-1, keepdims=True) / INNER)

        def back(p, _):
            lanes = pl.ds(pl.multiple_of(p * 128, 128), 128)
            z = z_ref[0:rows, lanes].astype(f32)
            y = y_ref[0:rows, lanes].astype(f32)
            s = sigmoid(z)
            gate = z * s
            q = y * gate
            do = do_ref[0:rows, lanes]
            gi_ref[:, lanes] += jnp.sum(do * q * scale, axis=0, keepdims=True)
            dq = scale * (g_ref[:, lanes] * do) - q * factor
            dy_ref[0:rows, lanes] = (dq * gate).astype(bf16)
            dz_ref[0:rows, lanes] = (dq * y * (s * (1.0 + z * (1.0 - s)))).astype(bf16)
            return 0

        lax.fori_loop(0, PAIRS, back, 0, unroll=2)

    pl.when(total >= 2 * b + 2)(functools.partial(body, 2 * Q))
    pl.when(total == 2 * b + 1)(functools.partial(body, Q))


def last_block(m, b):
    return jnp.minimum(b, (m[0] + 1) // 2 - 1)


def gate(meta, u, err, w2, o, y, proj, g2):
    rows = u.shape[0]
    blocks = rows // (2 * Q)
    const = lambda b, m: (0, 0)
    live = lambda b, m: (last_block(m, b), 0)
    once = pl.Buffered(1)
    return pl.pallas_call(
        functools.partial(gate_kernel, rows // Q // 2),
        out_shape=(
            jax.ShapeDtypeStruct((rows, D), bf16),
            jax.ShapeDtypeStruct((rows, INNER), bf16),
            jax.ShapeDtypeStruct((rows, INNER), bf16),
            jax.ShapeDtypeStruct((1, INNER), f32),
        ),
        grid_spec=pltpu.PrefetchScalarGridSpec(
            num_scalar_prefetch=1,
            grid=(blocks,),
            in_specs=[
                pl.BlockSpec((rows, D), const, pipeline_mode=once),
                pl.BlockSpec((2 * Q, D), live),
                pl.BlockSpec((INNER, D), const, pipeline_mode=once),
                pl.BlockSpec((2 * Q, INNER), live),
                pl.BlockSpec((2 * Q, INNER), live),
                pl.BlockSpec((2 * Q, INNER), live),
                pl.BlockSpec((1, INNER), const),
            ],
            out_specs=[
                pl.BlockSpec((rows, D), const),
                pl.BlockSpec((2 * Q, INNER), live),
                pl.BlockSpec((2 * Q, INNER), live),
                pl.BlockSpec((1, INNER), const),
            ],
            scratch_shapes=[pltpu.VMEM((2 * Q, INNER), f32)],
        ),
        compiler_params=params(),
        cost_estimate=cost(4 * rows * D * INNER, 2 * (D * INNER + 5 * rows * INNER)),
        name="gate",
    )(meta, u, err, w2, o, y, proj, g2)


def back_kernel(
    unroll, part, parts, meta, x_ref, prev_ref, e_ref, dy_ref, sin_ref, wc_ref, par_ref, skip_ref, *rest
):
    carried, rest = (rest[:6], rest[6:]) if part > 0 else ((), rest)
    dx_ref, gconv_ref, gpar_ref, gskip_ref = rest[:4]
    passed_on, rest = (rest[4:6], rest[6:]) if part < parts - 1 else ((), rest[4:])
    buf, dbuf, dstate, col_ref, dtp_ref, row_ref, da_ref = rest
    i = pl.program_id(0)
    total = meta[0]
    begin, end = part_span(meta, part, parts)
    k = total - begin - i

    @pl.when(i == 0)
    def _():
        da_ref[...] = jnp.zeros_like(da_ref)
        if part == 0:
            gconv_ref[...] = jnp.zeros_like(gconv_ref)
            gpar_ref[...] = jnp.zeros_like(gpar_ref)
            gskip_ref[...] = jnp.zeros_like(gskip_ref)

            @pl.when(lax.rem(total, 2) == 1)
            def _():
                dx_ref[...] = jnp.zeros_like(dx_ref)

        else:
            for to, came in zip((gconv_ref, gpar_ref, gskip_ref, dstate), carried[1:5]):
                to[...] = came[...]
            dbuf[0:8, :] = carried[5][...]

    @pl.when((i >= 1) & (i <= end - begin))
    def _():
        first = (k == 0) | (k == meta[1])
        last = (k == total - 1) | (k == meta[1] - 1)

        @pl.when(first)
        def _():
            buf[0:8, :] = jnp.zeros((8, XBC), f32)

        @pl.when(jnp.logical_not(first))
        def _():
            buf[0:8, :] = prev_ref[8:16, INNER : INNER + XBC].astype(f32)

        @pl.when(last)
        def _():
            dbuf[Q : Q + 8, :] = jnp.zeros((8, XBC), f32)
            dstate[...] = jnp.zeros_like(dstate)

        @pl.when(jnp.logical_not(last))
        def _():
            dbuf[Q : Q + 8, :] = dbuf[0:8, :]

        buf[8 : 8 + Q, :] = x_ref[:, INNER : INNER + XBC].astype(f32)
        tail_lanes = slice(INNER, XBC)
        c_tail = conv_tile(buf, wc_ref, tail_lanes)
        s_tail = sigmoid(c_tail)
        act = c_tail * s_tail
        keys = act[:, :STATE].astype(bf16)
        queries = act[:, STATE:].astype(bf16)
        queries_t = act[:, STATE:].T.astype(bf16)
        scores = dot_nn(keys, queries_t)
        raw, dt, cum = step_sizes(e_ref, par_ref)
        row_ref[...] = cum.T
        spread_heads(cum, dt, col_ref, dtp_ref)
        upper = row_iota((Q, Q)) <= lane_iota((Q, Q))
        strict = row_iota((Q, Q)) < lane_iota((Q, Q))
        after = (row_iota((Q, Q)) >= lane_iota((Q, Q))).astype(bf16)
        low = lane_iota((Q, 128)) < HEADDIM
        scores = jnp.where(upper, scores, 0.0)
        half = (lax.broadcasted_iota(jnp.int32, (128, 128), 0) >= HEADDIM).astype(jnp.int32)
        head_lane = lane_iota((128, 128))

        def conv_back(lanes, dc):
            dbuf[0:Q, lanes] = dc
            dxbc = wc_ref[CONV - 1 : CONV, lanes] * dc
            for tap in range(CONV - 1):
                dxbc = dxbc + wc_ref[tap : tap + 1, lanes] * dbuf[3 - tap : 3 - tap + Q, lanes]
            dx_ref[:, lanes] = dxbc.astype(bf16)
            for tap in range(CONV):
                gconv_ref[tap : tap + 1, lanes] += jnp.sum(dc * buf[5 + tap : 5 + tap + Q, lanes], axis=0, keepdims=True)
            gconv_ref[CONV : CONV + 1, lanes] += jnp.sum(dc, axis=0, keepdims=True)

        def pair(p, carry):
            dscores, dquery, dkey, from_start, to_end, direct, thru = carry
            lanes = pl.ds(pl.multiple_of(p * 128, 128), 128)
            c = conv_tile(buf, wc_ref, lanes)
            s = sigmoid(c)
            values = c * s
            col0, col1 = col_ref[2 * p], col_ref[2 * p + 1]
            both = jnp.where(low, col0, col1)
            end = both[Q - 1 : Q, :]
            grown = jnp.exp(both)
            rest = jnp.exp(end - both)
            dtp = dtp_ref[p]
            stepped = values * dtp
            dy_low = dy_ref[:, lanes]
            dy = dy_low.astype(f32)
            parts = split_pair(dy_low, low)
            stepped_low = stepped.astype(bf16)
            dmix = dot_nt(stepped_low, parts)
            mix = []
            for n, col in enumerate((col0, col1)):
                decay = jnp.exp(jnp.minimum(row_ref[pl.ds(2 * p + n, 1), :] - col, 0.0))
                weighted = dmix[:, n * Q : (n + 1) * Q] * decay
                dscores = dscores + weighted
                mix.append((scores * decay).astype(bf16))
                passed = dot_nn((weighted * scores).astype(bf16), after)
                da_ref[pl.ds(2 * p + n, 1), :] = jnp.sum(jnp.where(strict, passed, 0.0), axis=0, keepdims=True)
            dstepped = dot_nn(jnp.concatenate(mix, axis=1), parts)
            dafter = dstate[:, lanes]
            dafter_low = dafter.astype(bf16)
            before_low = sin_ref[0, :, lanes]
            dend = dot_nn(keys, dafter_low) * rest
            grown_dy = (dy * grown).astype(bf16)
            select = (head_lane == 2 * p + half).astype(bf16)
            across = dot_nn(queries, before_low)
            from_start = from_start + dot_nn((across * grown * dy).astype(bf16), select)
            to_end = to_end + dot_nn((stepped * dend).astype(bf16), select)
            dstepped = dstepped + dend
            direct = direct + dot_nn((values * dstepped).astype(bf16), select)
            dquery = dquery + dot_nt(grown_dy, before_low)
            dkey = dkey + dot_nt((stepped * rest).astype(bf16), dafter_low)
            kept = jnp.exp(end) * dafter
            held = jnp.sum((kept * before_low.astype(f32)).reshape(8, 16, 128), axis=0)
            thru = thru + dot_nn(held.astype(bf16), select)
            dstate[:, lanes] = kept + dot_nn(queries_t, grown_dy)
            dvalues = dstepped * dtp + skip_ref[:, lanes] * dy
            gskip_ref[:, lanes] += jnp.sum(dy * values, axis=0, keepdims=True)
            conv_back(lanes, dvalues * (s * (1.0 + c * (1.0 - s))))
            return dscores, dquery, dkey, from_start, to_end, direct, thru

        def body(n, carry):
            for m in range(unroll):
                carry = pair(n * unroll + m, carry)
            return carry

        zero = jnp.zeros((Q, 128), f32)
        start = (zero,) * 6 + (jnp.zeros((16, 128), f32),)
        carry = lax.fori_loop(0, PAIRS // unroll, body, start)
        dscores, dquery, dkey, from_start, to_end, direct, thru = carry
        dscores = jnp.where(upper, dscores, 0.0)
        dkey = dkey + dot_nn(dscores.astype(bf16), queries)
        dquery = dquery + dot_nn(dscores.T.astype(bf16), keys)
        slope = s_tail * (1.0 + c_tail * (1.0 - s_tail))
        conv_back(slice(INNER, INNER + STATE), dkey * slope[:, :STATE])
        conv_back(slice(INNER + STATE, XBC), dquery * slope[:, STATE:])

        tail_sum = (row_iota((Q, Q)) <= lane_iota((Q, Q))).astype(f32)
        head_sum = (row_iota((Q, Q)) > lane_iota((Q, Q))).astype(f32)
        da = (
            da_ref[...].T
            + dot_nn(tail_sum, from_start, precision=lax.Precision.HIGHEST)
            + dot_nn(head_sum, to_end, precision=lax.Precision.HIGHEST)
            + jnp.sum(thru, axis=0, keepdims=True)
        )
        ddt = par_ref[1:2, :] * da + direct
        de = ddt * sigmoid(raw)
        de = jnp.where(lane_iota((Q, 128)) < HEADS, de, 0.0)
        dx_ref[:, XBC:] = de.astype(bf16)
        gpar_ref[0:1, :] += jnp.sum(de, axis=0, keepdims=True)
        gpar_ref[1:2, :] += jnp.sum(dt * da, axis=0, keepdims=True)

    if passed_on:

        @pl.when(i == pl.num_programs(0) - 1)
        def _():
            passed_on[0][...] = dstate[...]
            passed_on[1][...] = dbuf[0:8, :]


def part_span(meta, part, parts):
    return (meta[0] * part + parts - 1) // parts, (meta[0] * (part + 1) + parts - 1) // parts


def back(meta, part, parts, carried, proj, e, dy, sin, wc, par, skip):
    rows = proj.shape[0]
    chunks = rows // Q
    const = lambda i, m: (0, 0)

    def chunk(i, m):
        begin, end = part_span(m, part, parts)
        return jnp.clip(m[0] - begin - jnp.clip(i, 1, jnp.maximum(end - begin, 1)), 0, m[0] - 1)

    def written(i, m):
        begin, end = part_span(m, part, parts)
        block = jnp.where(end > begin, chunk(i, m), chunks)
        return jnp.where(i == 0, last_padded(m, m[0]), block) if part == 0 else block

    here = lambda i, m: (chunk(i, m), 0)
    out_shape = [
        jax.ShapeDtypeStruct((rows + Q, XE), bf16),
        jax.ShapeDtypeStruct((8, XBC), f32),
        jax.ShapeDtypeStruct((8, 128), f32),
        jax.ShapeDtypeStruct((1, INNER), f32),
    ]
    sums = [pl.BlockSpec((8, XBC), const), pl.BlockSpec((8, 128), const), pl.BlockSpec((1, INNER), const)]
    state = [pl.BlockSpec((STATE, INNER), const), pl.BlockSpec((8, XBC), const)]
    in_specs = [
        pl.BlockSpec((Q, PROJ), here),
        pl.BlockSpec((16, PROJ), lambda i, m: (jnp.maximum(chunk(i, m) * (Q // 16) - 1, 0), 0)),
        pl.BlockSpec((Q, 128), here),
        pl.BlockSpec((Q, INNER), here),
        pl.BlockSpec((1, STATE, INNER), lambda i, m: (chunk(i, m), 0, 0)),
        pl.BlockSpec((8, XBC), const),
        pl.BlockSpec((8, 128), const),
        pl.BlockSpec((1, INNER), const),
    ]
    out_specs = [pl.BlockSpec((Q, XE), lambda i, m: (written(i, m), 0))] + sums
    if part > 0:
        in_specs += [pl.BlockSpec(memory_space=pl.ANY)] + sums + state
    if part < parts - 1:
        out_shape += [jax.ShapeDtypeStruct((STATE, INNER), f32), jax.ShapeDtypeStruct((8, XBC), f32)]
        out_specs += state
    steps = -(-chunks // parts)
    return pl.pallas_call(
        functools.partial(back_kernel, 2, part, parts),
        out_shape=out_shape,
        grid_spec=pltpu.PrefetchScalarGridSpec(
            num_scalar_prefetch=1,
            grid=(steps + 1,),
            in_specs=in_specs,
            out_specs=out_specs,
            scratch_shapes=[
                pltpu.VMEM((Q + 8, XBC), f32),
                pltpu.VMEM((Q + 8, XBC), f32),
                pltpu.VMEM((STATE, INNER), f32),
                pltpu.VMEM((HEADS, Q, 128), f32),
                pltpu.VMEM((PAIRS, Q, 128), f32),
                pltpu.VMEM((128, Q), f32),
                pltpu.VMEM((128, Q), f32),
            ],
        ),
        input_output_aliases={9: 0} if part > 0 else {},
        compiler_params=params(),
        cost_estimate=cost(steps * PAIRS * 20 * 2 * Q * 128 * 128, 2 * steps * Q * (PROJ + 3 * INNER)),
        name="back",
    )(meta, proj, proj, e, dy, sin, wc, par, skip, *carried)


def weight_kernel(rows, swap_from, meta, at_ref, b_ref, mine_ref, other_ref):
    used = (meta[0] + 1) // 2
    half = at_ref.shape[0] // 2
    part_rows = half // 4
    swap = pl.program_id(0) >= swap_from

    def part(width):
        for c, out_ref in enumerate((mine_ref, other_ref)):

            def step(m, _):
                here = pl.ds(pl.multiple_of(c * half + 2 * m * part_rows, part_rows), 2 * part_rows)
                res = dot_nn(at_ref[here, 0:width], b_ref[0:width, :]).astype(bf16)
                for n in range(2):
                    place = jnp.where(swap, 2 * n + m, 2 * m + n)
                    there = pl.ds(pl.multiple_of(place * part_rows, part_rows), part_rows)
                    out_ref[there, :] = res[n * part_rows : (n + 1) * part_rows, :]
                return 0

            lax.fori_loop(0, 2, step, 0)

    for n in range(1, rows // (2 * Q) + 1):
        pl.when(used == n)(functools.partial(part, n * 2 * Q))


def weight_grad(meta, at, b, first, width, tile, swap_from):
    height, rows = at.shape
    offset = first // tile
    half = jax.ShapeDtypeStruct((height // 2, width), bf16)
    half_spec = pl.BlockSpec((height // 2, tile), lambda j, m: (0, j))
    return pl.pallas_call(
        functools.partial(weight_kernel, rows, swap_from),
        out_shape=(half, half),
        grid_spec=pltpu.PrefetchScalarGridSpec(
            num_scalar_prefetch=1,
            grid=(pl.cdiv(width, tile),),
            in_specs=[
                pl.BlockSpec((height, rows), lambda j, m: (0, 0)),
                pl.BlockSpec((rows, tile), lambda j, m: (0, j + offset)),
            ],
            out_specs=(half_spec, half_spec),
        ),
        compiler_params=params(),
        cost_estimate=cost(2 * rows * height * width, 2 * (rows * (height + width) + height * width)),
        name="weight_grad",
    )(meta, at, b)


def input_kernel(
    slot_chunks, steps, tile, meta, u_ref, err_ref, g_ref, dz_ref, dx_ref, w_ref, out0_ref, out1_ref, gn_ref, dh_ref
):
    j = pl.program_id(0)
    total = meta[0]
    chunks = 2 * slot_chunks
    last = w_ref[:, INNER + XBC : PROJ]
    cols = pl.ds(pl.multiple_of(j * tile, tile), tile)

    def block(b, rows):
        r = slice(b * 2 * Q, b * 2 * Q + rows)
        dh_ref[r, cols] = (
            dot_nt(dz_ref[r, :], w_ref[:, 0:INNER])
            + dot_nt(dx_ref[r, 0:XBC], w_ref[:, INNER : INNER + XBC])
            + dot_nt(dx_ref[r, XBC : XBC + HEADS], last)
        )

    for_blocks(total, chunks // 2, block)

    @pl.when(j == steps - 1)
    def _():
        out0_ref[...] = jnp.zeros_like(out0_ref)
        out1_ref[...] = jnp.zeros_like(out1_ref)
        gn_ref[...] = jnp.zeros_like(gn_ref)
        for k in range(chunks):

            @pl.when(k < total)
            def _():
                start = pl.multiple_of(source_chunk(meta, k, slot_chunks) * Q, Q)
                u = u_ref[pl.ds(start, Q), :].astype(f32)
                err = err_ref[k * Q : (k + 1) * Q, :].astype(f32)
                scale = lax.rsqrt(jnp.mean(u * u, axis=-1, keepdims=True) + epsilon)
                dh = dh_ref[k * Q : (k + 1) * Q, :]
                gn_ref[...] += jnp.sum(dh * (u * scale), axis=0, keepdims=True)
                n = dh * g_ref[...]
                inner = jnp.mean(u * n, axis=-1, keepdims=True)
                du = (err + scale * n - u * (scale * scale * scale * inner)).astype(bf16)

                @pl.when(k < meta[1])
                def _():
                    out0_ref[pl.ds(start, Q), :] = du

                @pl.when(k >= meta[1])
                def _():
                    out1_ref[pl.ds(pl.multiple_of(start - slot_chunks * Q, Q), Q), :] = du


def input_grad_of(meta, u, err, g1, dz, dx, w1):
    rows = u.shape[0]
    tile = 256
    steps = D // tile
    const = lambda j, m: (0, 0)
    once = pl.Buffered(1)
    return pl.pallas_call(
        functools.partial(input_kernel, rows // Q // 2, steps, tile),
        out_shape=(
            jax.ShapeDtypeStruct((rows // 2, D), bf16),
            jax.ShapeDtypeStruct((rows // 2, D), bf16),
            jax.ShapeDtypeStruct((1, D), f32),
        ),
        grid_spec=pltpu.PrefetchScalarGridSpec(
            num_scalar_prefetch=1,
            grid=(steps,),
            in_specs=[
                pl.BlockSpec((rows, D), const, pipeline_mode=once),
                pl.BlockSpec((rows, D), const, pipeline_mode=once),
                pl.BlockSpec((1, D), const),
                pl.BlockSpec((rows, INNER), const, pipeline_mode=once),
                pl.BlockSpec((rows, XE), const, pipeline_mode=once),
                pl.BlockSpec((tile, w1.shape[1]), lambda j, m: (j, 0)),
            ],
            out_specs=[
                pl.BlockSpec((rows // 2, D), const),
                pl.BlockSpec((rows // 2, D), const),
                pl.BlockSpec((1, D), const),
            ],
            scratch_shapes=[pltpu.VMEM((rows, D), f32)],
        ),
        compiler_params=params(),
        cost_estimate=cost(2 * rows * D * PROJ, 2 * (D * PROJ + rows * PROJ)),
        name="input_grad",
    )(meta, u, err, g1, dz, dx, w1)


def partner(value, axis, bit):
    mask = 2**bit
    pairs = [(source, source ^ mask) for source in range(lax.axis_size(axis))]
    return lax.ppermute(value, axis, pairs)


def log2(size):
    return size.bit_length() - 1


def halving_order(swap):
    fsdp = [("fsdp", bit) for bit in range(log2(lax.axis_size("fsdp")))]
    near = [("dp", 1)]
    far = [("dp", bit) for bit in range(2, log2(lax.axis_size("dp")))]
    return [("dp", 0)] + (near + fsdp if swap else fsdp + near) + far


def flat_bit(axis, bit):
    return bit + (log2(lax.axis_size("fsdp")) if axis == "dp" else 0)


def kept_at(order, owner):
    away = owner ^ lax.axis_index(AXES)
    place = jnp.zeros_like(away)
    for axis, bit in order:
        place = 2 * place + ((away >> flat_bit(axis, bit)) & 1)
    return place


def owner_at(order, place):
    away = jnp.zeros_like(place)
    for n, (axis, bit) in enumerate(order):
        away = away + (((place >> (len(order) - 1 - n)) & 1) << flat_bit(axis, bit))
    return away ^ lax.axis_index(AXES)


class Term:
    def __init__(self, value):
        self.value = value


class Columns:
    def __init__(self, width, swap):
        self.order = halving_order(swap)
        self.width = width
        self.terms = []
        self.phase = 0

    def done(self):
        return self.phase == len(self.order)

    def sum(self, start, stop):
        return sum(term.value[start:stop, at : at + self.width].astype(f32) for term, at in self.terms)

    def halve(self):
        self.rows //= 2
        return self.sum(self.rows, 2 * self.rows).astype(bf16)


class Chain:
    def __init__(self, halves, columns, grouped):
        mine, other = halves
        self.columns = columns
        if not grouped:
            count = lax.axis_size(AXES)
            whole = jnp.concatenate([mine, other]).reshape(count, -1, mine.shape[1])
            parts = []
            at = 0
            for c in columns:
                parts.append(whole[:, :, at : at + c.width][owner_at(c.order, jnp.arange(count))])
                at += c.width
            mine, other = jnp.concatenate(parts, axis=2).reshape(2, -1, mine.shape[1])
        self.going = [(columns, other)]
        kept = Term(mine)
        at = 0
        for c in columns:
            c.rows = mine.shape[0]
            c.terms.append((kept, at))
            at += c.width

    def halve(self):
        groups = {}
        for c in self.columns:
            if not c.done() and all(c not in members for members, _ in self.going):
                groups.setdefault((c.order[c.phase], c.rows), []).append(c)
        for members in groups.values():
            sent = [c.halve() for c in members]
            self.going.append((members, jnp.concatenate(sent, axis=1) if len(sent) > 1 else sent[0]))

    def exchange(self):
        for members, sent in self.going:
            first = members[0]
            came = Term(partner(sent, *first.order[first.phase]))
            at = 0
            for c in members:
                c.terms.append((came, at))
                c.phase += 1
                at += c.width
        self.going = []

    def finish(self):
        while not all(c.done() for c in self.columns):
            self.halve()
            self.exchange()
        return [c.sum(0, c.rows) for c in self.columns]


def tick(token, chains, after):
    last = {id(c.terms[-1][0]): c.terms[-1][0] for chain in chains for c in chain.columns if c.phase > 0}
    if last:
        *came, _ = lax.optimization_barrier([term.value for term in last.values()] + [after])
        for term, value in zip(last.values(), came):
            term.value = value
    for chain in chains:
        chain.halve()
    sent = [value for chain in chains for _, value in chain.going]
    *sent, token = lax.optimization_barrier(sent + [token])
    for chain in chains:
        chain.going = [(members, sent.pop(0)) for members, _ in chain.going]
        chain.exchange()
    return token


W_COLS = 6528
W_CUT = 3328


def gather_kernel(
    count, inner, flag_ref, shard_ref, tile_ref, tokens_ref, w_ref, tiles_ref, u_ref,
    kept, given, send_sem, recv_sem, tile_send, tile_recv, own_sem, give_send, give_recv,
):
    me = lax.axis_index("dp") * inner + lax.axis_index("fsdp")
    height = shard_ref.shape[0]
    x, core, y = flat_bit("fsdp", 0), flat_bit("dp", 0), flat_bit("dp", 1)
    far = [flat_bit("dp", bit) for bit in range(2, log2(lax.axis_size("dp")))]
    ways = (far + [y, x, core], far + [x, y, core])
    spans = (pl.ds(0, W_CUT), pl.ds(W_CUT, W_COLS - W_CUT))

    def place(away):
        return pl.ds(pl.multiple_of(jnp.bitwise_xor(me, away) * height, height), height)

    def link(bit):
        other = jnp.bitwise_xor(me, 2**bit)
        return (other // inner, other % inner)

    def last_step(half, away):
        return max((n for n, bit in enumerate(ways[half]) if (away >> bit) & 1), default=-1)

    def send(half, away, bit):
        src = shard_ref.at[:, spans[half]] if away == 0 else w_ref.at[place(away), spans[half]]
        return pltpu.make_async_remote_copy(
            src_ref=src,
            dst_ref=w_ref.at[place(away), spans[half]],
            send_sem=send_sem.at[half, away ^ 2**bit],
            recv_sem=recv_sem.at[half, away ^ 2**bit],
            device_id=link(bit),
            device_id_type=pl.DeviceIdType.MESH,
        )

    def receive(half, away):
        block = w_ref.at[place(away), spans[half]]
        return pltpu.make_async_remote_copy(
            src_ref=block,
            dst_ref=block,
            send_sem=send_sem.at[half, away],
            recv_sem=recv_sem.at[half, away],
            device_id=link(ways[half][last_step(half, away)]),
            device_id_type=pl.DeviceIdType.MESH,
        )

    def send_on(half, away):
        sends = [send(half, away, bit) for bit in ways[half][last_step(half, away) + 1 :]]
        for one in sends:
            one.start()
        return sends

    def tile_copy(n):
        other = jnp.bitwise_xor(me, n)
        return pltpu.make_async_remote_copy(
            src_ref=tile_ref,
            dst_ref=tiles_ref.at[me],
            send_sem=tile_send.at[n],
            recv_sem=tile_recv.at[n],
            device_id=(other // inner, other % inner),
            device_id_type=pl.DeviceIdType.MESH,
        )

    def start_tile(n, _):
        tile_copy(n).start()
        return 0

    def wait_tile(n, _):
        tile_copy(n).wait()
        return 0

    started = []
    for step in range(len(ways[0])):
        for half in range(2):
            one = send(half, 0, ways[half][step])
            one.start()
            started.append(one)
    own = pltpu.make_async_copy(shard_ref, w_ref.at[place(0), :], own_sem.at[0])
    own.start()
    lax.fori_loop(1, count, start_tile, 0)
    tiles_ref[me] = tile_ref[...]

    second = jnp.broadcast_to(flag_ref[0, 0], (1, D)) == 1
    rows = kept.shape[0]

    def choose(n, _):
        r = pl.ds(pl.multiple_of(n * 64, 64), 64)
        zero, one = tokens_ref[0, r, :].astype(f32), tokens_ref[1, r, :].astype(f32)
        kept[r, :] = jnp.where(second, one, zero).astype(bf16)
        given[r, :] = jnp.where(second, zero, one).astype(bf16)
        return 0

    lax.fori_loop(0, rows // 64, choose, 0)

    blocks = [(half, away) for half in range(2) for away in range(1, count)]
    blocks.sort(key=lambda b: (b[1].bit_count(), last_step(*b), b[0]))
    tail = []
    for n, (half, away) in enumerate(blocks):
        receive(half, away).wait_recv()
        started += send_on(half, away)
        if n == 8:
            keep = pltpu.make_async_copy(kept, u_ref.at[pl.ds(0, rows), :], own_sem.at[1])
            give = pltpu.make_async_remote_copy(
                src_ref=given,
                dst_ref=u_ref.at[pl.ds(rows, rows), :],
                send_sem=give_send,
                recv_sem=give_recv,
                device_id=link(core),
                device_id_type=pl.DeviceIdType.MESH,
            )
            keep.start()
            give.start()
            tail = [keep, give]
    for one in started:
        one.wait_send()
    for one in tail:
        one.wait()
    own.wait()
    lax.fori_loop(1, count, wait_tile, 0)


def gather(flag, shard, tile, tokens):
    count = lax.axis_size(AXES)
    slot = tokens.shape[1]
    whole = pl.BlockSpec(memory_space=pltpu.VMEM)
    anywhere = pl.BlockSpec(memory_space=pl.ANY)
    dma = pltpu.SemaphoreType.DMA
    return pl.pallas_call(
        functools.partial(gather_kernel, count, lax.axis_size("fsdp")),
        out_shape=(
            jax.ShapeDtypeStruct((D, W_COLS), bf16),
            jax.ShapeDtypeStruct((count, 8, 128), f32),
            jax.ShapeDtypeStruct((2 * slot, D), bf16),
        ),
        in_specs=[pl.BlockSpec(memory_space=pltpu.SMEM), whole, whole, whole],
        out_specs=(anywhere, whole, anywhere),
        scratch_shapes=[
            pltpu.VMEM((slot, D), bf16),
            pltpu.VMEM((slot, D), bf16),
            dma((2, count)),
            dma((2, count)),
            dma((count,)),
            dma((count,)),
            dma((2,)),
            dma,
            dma,
        ],
        compiler_params=params(has_side_effects=True),
        cost_estimate=cost(1e6, 2 * D * W_COLS),
        name="gather",
    )(flag, shard, tile, tokens)


def sum_kernel(count, inner, sent_ref, out_ref, came, send_sem, recv_sem):
    me = lax.axis_index("dp") * inner + lax.axis_index("fsdp")

    def copy(n):
        other = jnp.bitwise_xor(me, n)
        return pltpu.make_async_remote_copy(
            src_ref=sent_ref.at[other],
            dst_ref=came.at[n],
            send_sem=send_sem.at[n],
            recv_sem=recv_sem.at[n],
            device_id=(other // inner, other % inner),
            device_id_type=pl.DeviceIdType.MESH,
        )

    def start(n, _):
        copy(n).start()
        return 0

    def add(n, total):
        copy(n).wait()
        return total + came[n]

    lax.fori_loop(1, count, start, 0)
    out_ref[...] = lax.fori_loop(1, count, add, sent_ref[me])


def sum_small(tiles):
    count = tiles.shape[0]
    whole = pl.BlockSpec(memory_space=pltpu.VMEM)
    return pl.pallas_call(
        functools.partial(sum_kernel, count, lax.axis_size("fsdp")),
        out_shape=jax.ShapeDtypeStruct(tiles.shape[1:], f32),
        in_specs=[whole],
        out_specs=whole,
        scratch_shapes=[
            pltpu.VMEM(tiles.shape, f32),
            pltpu.SemaphoreType.DMA((count,)),
            pltpu.SemaphoreType.DMA((count,)),
        ],
        compiler_params=pltpu.CompilerParams(has_side_effects=True),
        cost_estimate=cost(count * 1024, 8 * count * 1024),
        name="sum_small",
    )(tiles)


TILE_ROWS = 16
X_CUT = 1792
X_PIECES = tuple((which, 512 * n, width) for n in range(4) for which, width in ((0, 512 if n < 3 else 256), (1, 512 if n < 3 else 128)))


def finish_kernel(
    count, inner, m0, a0, b0, m1, a1, b1, gconv_ref, gpar_ref, par_ref, gskip_ref, gi_ref, gn_ref, given_ref,
    x_ref, tile_ref, back_ref, *scratch,
):
    sources = ((m0, a0, b0), (m1, a1, b1))
    terms, scratch = scratch[:2], scratch[2:]
    sent, scratch = [scratch[2 * n : 2 * n + 2] for n in range(3)], scratch[6:]
    came, scratch = [scratch[2 * n : 2 * n + 2] for n in range(3)], scratch[6:]
    tiles, tiles_in, load_sem, send_sem, recv_sem, tile_send, tile_recv, give_send, give_recv = scratch
    me = lax.axis_index("dp") * inner + lax.axis_index("fsdp")
    far = [flat_bit("dp", bit) for bit in (2, 3)]
    ways = ([flat_bit("dp", 1)] + far, [flat_bit("fsdp", 0)] + far)
    tall = terms[0].shape[1]

    def target(other):
        return {"device_id": (other // inner, other % inner), "device_id_type": pl.DeviceIdType.MESH}

    def load(n):
        which, at, width = X_PIECES[n]
        cols = pl.ds(at, width)
        return [
            pltpu.make_async_copy(ref.at[pl.ds(0, tall), cols], terms[which].at[i, :, cols], load_sem.at[n, i])
            for i, ref in enumerate(sources[which])
        ]

    def copy(n, phase):
        which, at, width = X_PIECES[n]
        cols = pl.ds(at, width)
        return pltpu.make_async_remote_copy(
            src_ref=sent[phase][which].at[:, cols],
            dst_ref=came[phase][which].at[:, cols],
            send_sem=send_sem.at[n, phase],
            recv_sem=recv_sem.at[n, phase],
            **target(jnp.bitwise_xor(me, 2 ** ways[which][phase])),
        )

    def total(n, phase, start, rows):
        which, at, width = X_PIECES[n]
        parts = [terms[which][i, start : start + rows, at : at + width] for i in range(3)]
        parts += [came[p][which][start : start + rows, at : at + width] for p in range(phase)]
        return sum(part.astype(f32) for part in parts)

    def go(n, phase):
        which, at, width = X_PIECES[n]
        rows = tall >> (phase + 1)
        sent[phase][which][:, at : at + width] = total(n, phase, rows, rows).astype(bf16)
        copy(n, phase).start()

    def tile_copy(n):
        other = jnp.bitwise_xor(me, n)
        return pltpu.make_async_remote_copy(
            src_ref=tiles.at[other],
            dst_ref=tiles_in.at[n],
            send_sem=tile_send.at[n],
            recv_sem=tile_recv.at[n],
            **target(other),
        )

    def start_tile(n, _):
        tile_copy(n).start()
        return 0

    def add_tile(n, value):
        tile_copy(n).wait()
        return value + tiles_in[n]

    give = pltpu.make_async_remote_copy(
        src_ref=given_ref,
        dst_ref=back_ref,
        send_sem=give_send,
        recv_sem=give_recv,
        **target(jnp.bitwise_xor(me, 2 ** flat_bit("dp", 0))),
    )
    pieces = len(X_PIECES)
    for n in range(pieces):
        for one in load(n):
            one.start()
    for n in range(pieces):
        for one in load(n):
            one.wait()
        go(n, 0)
    give.start()

    pick = lax.broadcasted_iota(jnp.int32, (INNER, 128), 0) // HEADDIM == lane_iota((INNER, 128))
    skips = dot_nn(
        jnp.broadcast_to(gskip_ref[...], (8, INNER)), pick.astype(f32), precision=lax.Precision.HIGHEST
    )
    tiles[...] = jnp.zeros_like(tiles)
    for owner in range(count):
        for row, ref in ((0, gconv_ref), (8, gi_ref), (9, gn_ref)):
            each = ref.shape[1] // count
            tiles[owner, row : row + ref.shape[0], 0:each] = ref[:, owner * each : (owner + 1) * each]
        tiles[owner, 10:11, :] = gpar_ref[0:1, :]
        tiles[owner, 11:12, :] = gpar_ref[1:2, :] * par_ref[1:2, :]
        tiles[owner, 12:13, :] = skips[0:1, :]

    lag = 2
    for n in range(pieces + 2 * lag):
        if n < pieces:
            copy(n, 0).wait_recv()
            go(n, 1)
        if n == 1:
            lax.fori_loop(1, count, start_tile, 0)
        if lag <= n < pieces + lag:
            copy(n - lag, 1).wait_recv()
            go(n - lag, 2)
        if n >= 2 * lag:
            which, at, width = X_PIECES[n - 2 * lag]
            copy(n - 2 * lag, 2).wait_recv()
            x_ref[:, which * X_CUT + at : which * X_CUT + at + width] = total(n - 2 * lag, 3, 0, tall >> 3)
    tile_ref[...] = lax.fori_loop(1, count, add_tile, tiles[me])
    for n in range(pieces):
        for phase in range(3):
            copy(n, phase).wait_send()
    give.wait()


def finish(chains, gconv, gpar, par, gskip, gi, gn, given):
    count = lax.axis_size(AXES)
    operands = [term.value for chain in chains for term, _ in chain.columns[0].terms]
    widths = [chain.columns[0].width for chain in chains]
    tall = chains[0].columns[0].rows
    dma = pltpu.SemaphoreType.DMA
    anywhere = pl.BlockSpec(memory_space=pl.ANY)
    whole = pl.BlockSpec(memory_space=pltpu.VMEM)
    halves = [pltpu.VMEM((tall >> (phase + 1), width), bf16) for phase in range(3) for width in widths]
    pieces = len(X_PIECES)
    return pl.pallas_call(
        functools.partial(finish_kernel, count, lax.axis_size("fsdp")),
        out_shape=(
            jax.ShapeDtypeStruct((tall >> 3, XE), f32),
            jax.ShapeDtypeStruct((TILE_ROWS, 128), f32),
            jax.ShapeDtypeStruct(given.shape, bf16),
        ),
        in_specs=[anywhere] * 6 + [whole] * 6 + [anywhere],
        out_specs=(whole, whole, anywhere),
        scratch_shapes=[
            *(pltpu.VMEM((3, tall, width), bf16) for width in widths),
            *halves,
            *halves,
            pltpu.VMEM((count, TILE_ROWS, 128), f32),
            pltpu.VMEM((count, TILE_ROWS, 128), f32),
            dma((pieces, 3)),
            dma((pieces, 3)),
            dma((pieces, 3)),
            dma((count,)),
            dma((count,)),
            dma,
            dma,
        ],
        compiler_params=params(has_side_effects=True),
        cost_estimate=cost(1e7, 2e7),
        name="finish",
    )(*operands, gconv, gpar, par, gskip, gi, gn, given)


def on_device(
    tokens, cotangent, lengths, balance, norm_gain, in_weight, conv_weight, conv_bias,
    step_bias, decay_log, skip_weight, inner_gain, out_weight,
):
    device = lax.axis_index(AXES)
    count = lax.axis_size(AXES)
    slot = tokens.shape[1]
    rows = 2 * slot
    first_source = balance[2 * device]
    second_source = balance[2 * device + 1]
    keep_second = first_source - 2 * device == 1
    cot = cotangent.reshape(rows, D)
    lens = [lengths[first_source], lengths[second_source]]
    chunks = [(n + Q - 1) // Q for n in lens]
    grouped = D // count == H_UNIT
    h_units = jnp.arange(D // H_UNIT)
    o_units = jnp.arange(INNER // O_UNIT)
    if grouped:
        order = halving_order(False)
        each = INNER // count // O_UNIT
        h_units = kept_at(order, h_units)
        o_units = kept_at(order, o_units // each) * each + o_units % each
    meta = jnp.concatenate(
        [jnp.stack([chunks[0] + chunks[1], chunks[0], lens[0], lens[1]]), h_units * H_UNIT, o_units * O_UNIT]
    ).astype(jnp.int32)

    small = [norm_gain, conv_weight.reshape(-1), conv_bias, inner_gain]
    sizes = [v.shape[0] for v in small]
    packed = jnp.concatenate(small).astype(bf16)
    if grouped:
        tile = jnp.pad(packed.astype(f32), (0, 1024 - packed.shape[0])).reshape(8, 128)
        shard = jnp.pad(in_weight.astype(bf16), ((0, 0), (0, W_COLS - PROJ)))
        w1, packed, u = gather(keep_second.astype(jnp.int32).reshape(1, 1), shard, tile, tokens)
        packed = packed.reshape(count, -1)
    else:
        outgoing = jnp.where(keep_second, tokens[0], tokens[1])
        incoming = partner(outgoing, "dp", 0)
        u = jnp.concatenate([jnp.where(keep_second, tokens[1], tokens[0]), incoming], axis=0)
        w1 = lax.all_gather(in_weight.astype(bf16), AXES, axis=0, tiled=True)
        packed = lax.all_gather(packed[None, :], AXES, axis=0, tiled=True).astype(f32)
    cuts = [sum(sizes[:n]) for n in range(len(sizes) + 1)]
    norm_full, conv_full, bias_full, inner_full = (
        packed[:, cuts[n] : cuts[n + 1]].reshape(-1) for n in range(4)
    )
    w2_own, w1 = lax.optimization_barrier([out_weight.astype(bf16), w1])
    w2 = lax.all_gather(w2_own, AXES, axis=0, tiled=True)

    wc = jnp.concatenate([conv_full.reshape(XBC, CONV).T, bias_full[None], jnp.zeros((3, XBC), f32)])
    rate = -jnp.exp(decay_log)
    par = jnp.zeros((8, 128), f32).at[0, :HEADS].set(step_bias).at[1, :HEADS].set(rate)
    skip = jnp.repeat(skip_weight, HEADDIM)[None]
    g1 = norm_full[None]
    g2 = inner_full[None]

    proj, e, ht = project(meta, u, g1, w1)
    o, ot, y, sin, err = mixer(meta, proj, e, cot, wc, par, skip, g2)
    never = 1 << 20

    def both(width):
        return [Columns(width // 2, False), Columns(width // 2, True)]

    halves = weight_grad(meta, ot, err, 0, D, D // 2, 1 if grouped else never)
    c_out = Chain(halves, both(D), grouped)
    meta = tick(meta, [c_out], err)
    out, dy, dz, gi = gate(meta, u, err, w2, o, y, proj, g2)
    meta = tick(meta, [c_out], gi)
    halves = weight_grad(meta, ht, dz, 0, INNER, INNER // 4, 2 if grouped else never)
    c_z = Chain(halves, both(INNER), grouped)
    parts = 3
    carried = ()
    for part in range(parts):
        meta = tick(meta, [c_out, c_z] if part > 0 else [c_z], carried[2] if part > 0 else gi)
        carried = back(meta, part, parts, carried, proj, e, dy, sin, wc, par, skip)
    dx, gconv, gpar, gskip = carried
    meta = tick(meta, [c_out, c_z], gpar)
    cut = X_CUT
    halves = weight_grad(meta, ht, dx, 0, cut, cut // 2, never)
    c_x = Chain(halves, [Columns(cut, False)], grouped)
    meta = tick(meta, [c_z, c_x], halves[1])
    halves = weight_grad(meta, ht, dx, cut, XE - cut, cut // 2, 0 if grouped else never)
    c_x1 = Chain(halves, [Columns(XE - cut, True)], grouped)
    meta = tick(meta, [c_x, c_x1], halves[1])
    meta = tick(meta, [c_x1], c_x1.columns[0].terms[-1][0].value)
    kept_half, given_half, gn = input_grad_of(meta, u, err, g1, dz, dx, w1)
    conv_each = XBC // count
    if grouped:
        late = [chain.columns[0].terms[-1][0] for chain in (c_out, c_z)]
        *came, gn = lax.optimization_barrier([term.value for term in late] + [gn])
        for term, value in zip(late, came):
            term.value = value
        grad_x, tile, back_half = finish([c_x, c_x1], gconv, gpar, par, gskip, gi, gn, given_half)
        grad_x = [grad_x]
        grad_conv, grad_bias = tile[:CONV, :conv_each].T, tile[CONV, :conv_each]
        grad_inner, grad_norm = tile[8, : sizes[3]], tile[9, : sizes[0]]
        heads = [tile[10 + n, :HEADS] for n in range(3)]
    else:
        back_half = partner(given_half, "dp", 0)
        heads = jnp.concatenate(
            [gpar[0, :HEADS], gpar[1, :HEADS] * rate, gskip.reshape(HEADS, HEADDIM).sum(axis=1)]
        )
        owned = [gconv[:CONV].T.reshape(count, -1), gconv[CONV].reshape(count, -1), gi.reshape(count, -1)]
        tiles = jnp.concatenate(owned + [jnp.broadcast_to(heads, (count, 3 * HEADS)), gn.reshape(count, -1)], axis=1)
        tiles = jnp.pad(tiles, ((0, 0), (0, 1024 - tiles.shape[1]))).reshape(count, 8, 128)
        sums = sum_small(tiles).reshape(-1)
        grad_x = c_x.finish() + c_x1.finish()
        ends = [sum(v.shape[1] for v in owned[:n]) for n in range(4)]
        grad_conv = sums[: ends[1]].reshape(-1, CONV)
        grad_bias = sums[ends[1] : ends[2]]
        grad_inner = sums[ends[2] : ends[3]]
        heads = sums[ends[3] : ends[3] + 3 * HEADS].reshape(3, HEADS)
        grad_norm = sums[ends[3] + 3 * HEADS :][: sizes[0]]
    grad_out = jnp.concatenate(c_out.finish(), axis=1)
    grad_in = jnp.concatenate(c_z.finish() + grad_x, axis=1)[:, :PROJ]
    swapped = [jnp.stack([back_half, kept_half]), jnp.stack([kept_half, back_half])]
    input_grad = jnp.where(keep_second, *swapped)
    return (
        out.reshape(2, slot, D),
        input_grad,
        grad_norm,
        grad_in,
        grad_conv,
        grad_bias,
        heads[0],
        heads[1],
        heads[2],
        grad_inner,
        grad_out,
    )


def solution(mesh):
    flat = P(AXES)
    rowed = P(AXES, None)
    slots = P(AXES, None, None)
    return jax.shard_map(
        on_device,
        mesh=mesh,
        in_specs=(slots, slots, P(), P(), flat, rowed, rowed, flat, P(), P(), P(), flat, rowed),
        out_specs=(slots, slots, flat, rowed, rowed, flat, P(), P(), P(), flat, rowed),
        check_vma=False,
    )
```

```python
import functools
import jax
import jax.numpy as jnp
from jax import lax
from jax.experimental import pallas as pl
from jax.experimental.pallas import tpu as pltpu
from jax.sharding import PartitionSpec as P

D = 1536
INNER = 3072
HEADS = 48
HEADDIM = 64
STATE = 128
CONV = 4
XBC = 3328
PROJ = 6448
XE = XBC + 128
Q = 128
PAIRS = HEADS // 2

f32 = jnp.float32
bf16 = jnp.bfloat16
epsilon = 1e-05
AXES = ("dp", "fsdp")


def sigmoid(v):
    return 0.5 * jnp.tanh(0.5 * v) + 0.5


def dot_nn(a, b, precision=None):
    return jnp.dot(a, b, preferred_element_type=f32, precision=precision)


def dot_nt(a, b):
    return lax.dot_general(a, b, (((1,), (1,)), ((), ())), preferred_element_type=f32)


def dot_tn(a, b):
    return lax.dot_general(a, b, (((0,), (0,)), ((), ())), preferred_element_type=f32)


def lane_iota(shape):
    return lax.broadcasted_iota(jnp.int32, shape, len(shape) - 1)


def row_iota(shape):
    return lax.broadcasted_iota(jnp.int32, shape, len(shape) - 2)


H_UNIT = 48
O_UNIT = 32


def is_grouped():
    return D // lax.axis_size(AXES) == H_UNIT


def unit_row(unit, size, per_owner):
    if is_grouped():
        owner = unit // per_owner
        unit = kept_at(halving_order(False), owner) * per_owner + (unit - owner * per_owner)
    return pl.multiple_of(unit * size, 16)


def source_chunk(meta, k, slot_chunks):
    return jnp.where(k < meta[1], k, k - meta[1] + slot_chunks)


def live_rows(meta, k):
    inside = k < meta[1]
    return jnp.where(inside, meta[2] - k * Q, meta[3] - (k - meta[1]) * Q)


def last_live(meta, k):
    return jnp.minimum(k, meta[0] - 1)


def last_padded(meta, k):
    return jnp.minimum(k, meta[0] + lax.rem(meta[0], 2) - 1)


def for_blocks(total, blocks, body):
    for b in range(blocks):
        pl.when(total >= 2 * b + 2)(functools.partial(body, b, 2 * Q))
        pl.when(total == 2 * b + 1)(functools.partial(body, b, Q))


def cost(flops, moved, transcendentals=0):
    return pl.CostEstimate(flops=int(flops), bytes_accessed=int(moved), transcendentals=int(transcendentals))


def params(**kw):
    return pltpu.CompilerParams(vmem_limit_bytes=60 * 1024 * 1024, **kw)


def project_kernel(slot_chunks, steps, tile, meta, u_ref, g_ref, w_ref, proj_ref, e_ref, ht_ref, h_ref):
    j = pl.program_id(0)
    total = meta[0]
    chunks = 2 * slot_chunks

    @pl.when(j == 0)
    def _():
        for k in range(chunks):

            @pl.when(k < total)
            def _():
                start = pl.multiple_of(source_chunk(meta, k, slot_chunks) * Q, Q)
                x = u_ref[pl.ds(start, Q), :].astype(f32)
                scale = lax.rsqrt(jnp.mean(x * x, axis=-1, keepdims=True) + epsilon)
                normed = x * scale * g_ref[...]
                h_ref[k * Q : (k + 1) * Q, :] = normed.astype(bf16)
                turned = normed.T.astype(bf16)
                for n in range(D // H_UNIT):
                    there = pl.ds(unit_row(jnp.int32(n), H_UNIT, 1), H_UNIT)
                    ht_ref[there, k * Q : (k + 1) * Q] = turned[n * H_UNIT : (n + 1) * H_UNIT, :]

            @pl.when(k >= total)
            def _():
                ht_ref[:, k * Q : (k + 1) * Q] = jnp.zeros((D, Q), bf16)

    edge = XBC + INNER - (steps - 1) * tile

    def block(b, rows):
        r = slice(b * 2 * Q, b * 2 * Q + rows)
        acc = dot_nn(h_ref[r, :], w_ref[...])
        proj_ref[r, :] = acc.astype(bf16)

        @pl.when(j == steps - 1)
        def _():
            tail = dot_nn(h_ref[r, :], w_ref[:, edge : edge + 128])
            e_ref[r, :] = jnp.where(lane_iota(tail.shape) < HEADS, tail, 0.0)

    for_blocks(total, chunks // 2, block)


def project(meta, u, g1, w1):
    rows = u.shape[0]
    tile = 512
    steps = pl.cdiv(PROJ, tile)
    return pl.pallas_call(
        functools.partial(project_kernel, rows // Q // 2, steps, tile),
        out_shape=(
            jax.ShapeDtypeStruct((rows, PROJ), bf16),
            jax.ShapeDtypeStruct((rows, 128), f32),
            jax.ShapeDtypeStruct((D, rows), bf16),
        ),
        grid_spec=pltpu.PrefetchScalarGridSpec(
            num_scalar_prefetch=1,
            grid=(steps,),
            in_specs=[
                pl.BlockSpec((rows, D), lambda j, m: (0, 0)),
                pl.BlockSpec((1, D), lambda j, m: (0, 0)),
                pl.BlockSpec((D, tile), lambda j, m: (0, j)),
            ],
            out_specs=[
                pl.BlockSpec((rows, tile), lambda j, m: (0, j)),
                pl.BlockSpec((rows, 128), lambda j, m: (0, 0)),
                pl.BlockSpec((D, rows), lambda j, m: (0, 0)),
            ],
            scratch_shapes=[pltpu.VMEM((rows, D), bf16)],
        ),
        compiler_params=params(),
        cost_estimate=cost(2 * rows * D * PROJ, 2 * (D * PROJ + rows * PROJ)),
        name="project",
    )(meta, u, g1, w1)


def conv_tile(buf, wc_ref, lanes):
    c = wc_ref[CONV : CONV + 1, lanes]
    for tap in range(CONV):
        c = c + wc_ref[tap : tap + 1, lanes] * buf[5 + tap : 5 + tap + Q, lanes]
    return c


def step_sizes(e_ref, par_ref):
    raw = e_ref[...] + par_ref[0:1, :]
    dt = jnp.maximum(raw, 0.0) + jnp.log1p(jnp.exp(-jnp.abs(raw)))
    decay = par_ref[1:2, :]
    lower = (row_iota((Q, Q)) >= lane_iota((Q, Q))).astype(f32)
    cum = dot_nn(lower, dt * decay, precision=lax.Precision.HIGHEST)
    return raw, dt, cum


def spread_heads(cum, dt, col_ref, dtp_ref):
    low = lane_iota((Q, 128)) < HEADDIM
    for p in range(PAIRS):
        for h in (2 * p, 2 * p + 1):
            col_ref[h] = jnp.broadcast_to(cum[:, h : h + 1], (Q, 128))
        dtp_ref[p] = jnp.where(
            low,
            jnp.broadcast_to(dt[:, 2 * p : 2 * p + 1], (Q, 128)),
            jnp.broadcast_to(dt[:, 2 * p + 1 : 2 * p + 2], (Q, 128)),
        )


def split_pair(v, low):
    zero = jnp.zeros_like(v)
    return jnp.concatenate([jnp.where(low, v, zero), jnp.where(low, zero, v)], axis=0)


def mixer_kernel(
    unroll, meta, proj_ref, e_ref, cot_ref, wc_ref, par_ref, skip_ref, g_ref,
    o_ref, ot_ref, y_ref, sin_ref, err_ref,
    buf, state, col_ref, dtp_ref, row_ref, q_ref,
):
    k = pl.program_id(0)
    total = meta[0]

    @pl.when((k == total) & (lax.rem(total, 2) == 1))
    def _():
        o_ref[...] = jnp.zeros_like(o_ref)
        ot_ref[...] = jnp.zeros_like(ot_ref)
        err_ref[...] = jnp.zeros_like(err_ref)

    @pl.when(k < total)
    def _():
        live = row_iota((Q, D)) < live_rows(meta, k)
        err_ref[...] = jnp.where(live, cot_ref[...].astype(f32), 0.0).astype(bf16)
        first = (k == 0) | (k == meta[1])

        @pl.when(first)
        def _():
            buf[0:8, :] = jnp.zeros((8, XBC), f32)
            state[...] = jnp.zeros_like(state)

        @pl.when(jnp.logical_not(first))
        def _():
            buf[0:8, :] = buf[Q : Q + 8, :]

        buf[8 : 8 + Q, :] = proj_ref[:, INNER : INNER + XBC].astype(f32)
        tail_lanes = slice(INNER, XBC)
        c = conv_tile(buf, wc_ref, tail_lanes)
        act = c * sigmoid(c)
        keys = act[:, :STATE]
        queries = act[:, STATE:].astype(bf16)
        keys_t = keys.T.astype(bf16)
        scores = dot_nn(queries, keys_t)
        _, dt, cum = step_sizes(e_ref, par_ref)
        row_ref[...] = cum.T
        spread_heads(cum, dt, col_ref, dtp_ref)
        lower = row_iota((Q, Q)) >= lane_iota((Q, Q))
        low = lane_iota((Q, 128)) < HEADDIM
        scores = jnp.where(lower, scores, 0.0)

        def pair(p):
            lanes = pl.ds(pl.multiple_of(p * 128, 128), 128)
            c = conv_tile(buf, wc_ref, lanes)
            values = c * sigmoid(c)
            col0, col1 = col_ref[2 * p], col_ref[2 * p + 1]
            both = jnp.where(low, col0, col1)
            end = both[Q - 1 : Q, :]
            stepped = values * dtp_ref[p]
            parts = split_pair(stepped.astype(bf16), low)
            mix = []
            for n, col in enumerate((col0, col1)):
                decay = jnp.exp(jnp.minimum(col - row_ref[pl.ds(2 * p + n, 1), :], 0.0))
                mix.append((scores * decay).astype(bf16))
            y = dot_nn(jnp.concatenate(mix, axis=1), parts)
            before = state[:, lanes]
            before_low = before.astype(bf16)
            sin_ref[0, :, lanes] = before_low
            y = y + dot_nn(queries, before_low) * jnp.exp(both)
            y = y + skip_ref[:, lanes] * values
            state[:, lanes] = before * jnp.exp(end) + dot_nn(
                keys_t, (stepped * jnp.exp(end - both)).astype(bf16)
            )
            z = proj_ref[:, lanes].astype(f32)
            gated = y * (z * sigmoid(z))
            y_ref[:, lanes] = y.astype(bf16)
            q_ref[:, lanes] = gated
            return gated * gated

        def body(i, squares):
            for n in range(unroll):
                squares = squares + pair(i * unroll + n)
            return squares

        squares = lax.fori_loop(0, PAIRS // unroll, body, jnp.zeros((Q, 128), f32))
        scale = lax.rsqrt(jnp.sum(squares, axis=-1, keepdims=True) / INNER + epsilon)

        def finish(p, _):
            lanes = pl.ds(pl.multiple_of(p * 128, 128), 128)
            out = q_ref[:, lanes] * scale * g_ref[:, lanes]
            o_ref[:, lanes] = out.astype(bf16)
            turned = out.T.astype(bf16)
            for n in range(128 // O_UNIT):
                there = pl.ds(unit_row(p * (128 // O_UNIT) + n, O_UNIT, 3), O_UNIT)
                ot_ref[there, :] = turned[n * O_UNIT : (n + 1) * O_UNIT, :]
            return 0

        lax.fori_loop(0, PAIRS, finish, 0, unroll=2)


def mixer(meta, proj, e, cot, wc, par, skip, g2):
    rows = proj.shape[0]
    chunks = rows // Q
    const = lambda k, m: (0, 0)
    live = lambda k, m: (last_live(m, k), 0)
    return pl.pallas_call(
        functools.partial(mixer_kernel, 2),
        out_shape=(
            jax.ShapeDtypeStruct((rows, INNER), bf16),
            jax.ShapeDtypeStruct((INNER, rows), bf16),
            jax.ShapeDtypeStruct((rows, INNER), bf16),
            jax.ShapeDtypeStruct((chunks, STATE, INNER), bf16),
            jax.ShapeDtypeStruct((rows, D), bf16),
        ),
        grid_spec=pltpu.PrefetchScalarGridSpec(
            num_scalar_prefetch=1,
            grid=(chunks,),
            in_specs=[
                pl.BlockSpec((Q, PROJ), live),
                pl.BlockSpec((Q, 128), live),
                pl.BlockSpec((Q, D), lambda k, m: (source_chunk(m, last_live(m, k), chunks // 2), 0)),
                pl.BlockSpec((8, XBC), const),
                pl.BlockSpec((8, 128), const),
                pl.BlockSpec((1, INNER), const),
                pl.BlockSpec((1, INNER), const),
            ],
            out_specs=[
                pl.BlockSpec((Q, INNER), lambda k, m: (last_padded(m, k), 0)),
                pl.BlockSpec((INNER, Q), lambda k, m: (0, last_padded(m, k))),
                pl.BlockSpec((Q, INNER), live),
                pl.BlockSpec((1, STATE, INNER), lambda k, m: (last_live(m, k), 0, 0)),
                pl.BlockSpec((Q, D), lambda k, m: (last_padded(m, k), 0)),
            ],
            scratch_shapes=[
                pltpu.VMEM((Q + 8, XBC), f32),
                pltpu.VMEM((STATE, INNER), f32),
                pltpu.VMEM((HEADS, Q, 128), f32),
                pltpu.VMEM((PAIRS, Q, 128), f32),
                pltpu.VMEM((128, Q), f32),
                pltpu.VMEM((Q, INNER), f32),
            ],
        ),
        compiler_params=params(),
        cost_estimate=cost(chunks * PAIRS * 8 * 2 * Q * 128 * 128, 2 * rows * (PROJ + 3 * INNER)),
        name="mixer",
    )(meta, proj, e, cot, wc, par, skip, g2)


def gate_kernel(
    slot_chunks, meta, u_ref, err_ref, w_ref, o_ref, y_ref, z_ref, g_ref,
    out_ref, dy_ref, dz_ref, gi_ref,
    do_ref,
):
    b = pl.program_id(0)
    total = meta[0]

    @pl.when(b == 0)
    def _():
        out_ref[...] = jnp.zeros_like(out_ref)
        gi_ref[...] = jnp.zeros_like(gi_ref)

    def body(rows):
        halves = rows // Q
        if halves == 1:
            dz_ref[Q:, :] = jnp.zeros((Q, INNER), bf16)
        starts = []
        for n in range(halves):
            k = 2 * b + n
            start = pl.multiple_of(source_chunk(meta, k, slot_chunks) * Q, Q)
            starts.append(start)
        branch = dot_nn(o_ref[0:rows, :], w_ref[...])
        for n in range(halves):
            live = row_iota((Q, D)) < live_rows(meta, 2 * b + n)
            here = pl.ds(starts[n], Q)
            value = u_ref[here, :].astype(f32) + branch[n * Q : (n + 1) * Q, :]
            out_ref[here, :] = jnp.where(live, value, 0.0).astype(bf16)
        do_ref[0:rows, :] = dot_nt(err_ref[0:rows, :], w_ref[...])

        def sums(p, carry):
            squares, crossed = carry
            lanes = pl.ds(pl.multiple_of(p * 128, 128), 128)
            z = z_ref[0:rows, lanes].astype(f32)
            q = y_ref[0:rows, lanes].astype(f32) * (z * sigmoid(z))
            return squares + q * q, crossed + q * g_ref[:, lanes] * do_ref[0:rows, lanes]

        zero = jnp.zeros((rows, 128), f32)
        squares, crossed = lax.fori_loop(0, PAIRS, sums, (zero, zero), unroll=2)
        scale = lax.rsqrt(jnp.sum(squares, axis=-1, keepdims=True) / INNER + epsilon)
        factor = scale * scale * scale * (jnp.sum(crossed, axis=-1, keepdims=True) / INNER)

        def back(p, _):
            lanes = pl.ds(pl.multiple_of(p * 128, 128), 128)
            z = z_ref[0:rows, lanes].astype(f32)
            y = y_ref[0:rows, lanes].astype(f32)
            s = sigmoid(z)
            gate = z * s
            q = y * gate
            do = do_ref[0:rows, lanes]
            gi_ref[:, lanes] += jnp.sum(do * q * scale, axis=0, keepdims=True)
            dq = scale * (g_ref[:, lanes] * do) - q * factor
            dy_ref[0:rows, lanes] = (dq * gate).astype(bf16)
            dz_ref[0:rows, lanes] = (dq * y * (s * (1.0 + z * (1.0 - s)))).astype(bf16)
            return 0

        lax.fori_loop(0, PAIRS, back, 0, unroll=2)

    pl.when(total >= 2 * b + 2)(functools.partial(body, 2 * Q))
    pl.when(total == 2 * b + 1)(functools.partial(body, Q))


def last_block(m, b):
    return jnp.minimum(b, (m[0] + 1) // 2 - 1)


def gate(meta, u, err, w2, o, y, proj, g2):
    rows = u.shape[0]
    blocks = rows // (2 * Q)
    const = lambda b, m: (0, 0)
    live = lambda b, m: (last_block(m, b), 0)
    once = pl.Buffered(1)
    return pl.pallas_call(
        functools.partial(gate_kernel, rows // Q // 2),
        out_shape=(
            jax.ShapeDtypeStruct((rows, D), bf16),
            jax.ShapeDtypeStruct((rows, INNER), bf16),
            jax.ShapeDtypeStruct((rows, INNER), bf16),
            jax.ShapeDtypeStruct((1, INNER), f32),
        ),
        grid_spec=pltpu.PrefetchScalarGridSpec(
            num_scalar_prefetch=1,
            grid=(blocks,),
            in_specs=[
                pl.BlockSpec((rows, D), const, pipeline_mode=once),
                pl.BlockSpec((2 * Q, D), live),
                pl.BlockSpec((INNER, D), const, pipeline_mode=once),
                pl.BlockSpec((2 * Q, INNER), live),
                pl.BlockSpec((2 * Q, INNER), live),
                pl.BlockSpec((2 * Q, INNER), live),
                pl.BlockSpec((1, INNER), const),
            ],
            out_specs=[
                pl.BlockSpec((rows, D), const),
                pl.BlockSpec((2 * Q, INNER), live),
                pl.BlockSpec((2 * Q, INNER), live),
                pl.BlockSpec((1, INNER), const),
            ],
            scratch_shapes=[pltpu.VMEM((2 * Q, INNER), f32)],
        ),
        compiler_params=params(),
        cost_estimate=cost(4 * rows * D * INNER, 2 * (D * INNER + 5 * rows * INNER)),
        name="gate",
    )(meta, u, err, w2, o, y, proj, g2)


def back_kernel(
    unroll, part, parts, meta, x_ref, prev_ref, e_ref, dy_ref, sin_ref, wc_ref, par_ref, skip_ref, *rest
):
    carried, rest = (rest[:6], rest[6:]) if part > 0 else ((), rest)
    dx_ref, gconv_ref, gpar_ref, gskip_ref = rest[:4]
    passed_on, rest = (rest[4:6], rest[6:]) if part < parts - 1 else ((), rest[4:])
    buf, dbuf, dstate, col_ref, dtp_ref, row_ref, da_ref = rest
    i = pl.program_id(0)
    total = meta[0]
    begin, end = part_span(meta, part, parts)
    k = total - begin - i

    @pl.when(i == 0)
    def _():
        da_ref[...] = jnp.zeros_like(da_ref)
        if part == 0:
            gconv_ref[...] = jnp.zeros_like(gconv_ref)
            gpar_ref[...] = jnp.zeros_like(gpar_ref)
            gskip_ref[...] = jnp.zeros_like(gskip_ref)

            @pl.when(lax.rem(total, 2) == 1)
            def _():
                dx_ref[...] = jnp.zeros_like(dx_ref)

        else:
            for to, came in zip((gconv_ref, gpar_ref, gskip_ref, dstate), carried[1:5]):
                to[...] = came[...]
            dbuf[0:8, :] = carried[5][...]

    @pl.when((i >= 1) & (i <= end - begin))
    def _():
        first = (k == 0) | (k == meta[1])
        last = (k == total - 1) | (k == meta[1] - 1)

        @pl.when(first)
        def _():
            buf[0:8, :] = jnp.zeros((8, XBC), f32)

        @pl.when(jnp.logical_not(first))
        def _():
            buf[0:8, :] = prev_ref[8:16, INNER : INNER + XBC].astype(f32)

        @pl.when(last)
        def _():
            dbuf[Q : Q + 8, :] = jnp.zeros((8, XBC), f32)
            dstate[...] = jnp.zeros_like(dstate)

        @pl.when(jnp.logical_not(last))
        def _():
            dbuf[Q : Q + 8, :] = dbuf[0:8, :]

        buf[8 : 8 + Q, :] = x_ref[:, INNER : INNER + XBC].astype(f32)
        tail_lanes = slice(INNER, XBC)
        c_tail = conv_tile(buf, wc_ref, tail_lanes)
        s_tail = sigmoid(c_tail)
        act = c_tail * s_tail
        keys = act[:, :STATE].astype(bf16)
        queries = act[:, STATE:].astype(bf16)
        queries_t = act[:, STATE:].T.astype(bf16)
        scores = dot_nn(keys, queries_t)
        raw, dt, cum = step_sizes(e_ref, par_ref)
        row_ref[...] = cum.T
        spread_heads(cum, dt, col_ref, dtp_ref)
        upper = row_iota((Q, Q)) <= lane_iota((Q, Q))
        strict = row_iota((Q, Q)) < lane_iota((Q, Q))
        after = (row_iota((Q, Q)) >= lane_iota((Q, Q))).astype(bf16)
        low = lane_iota((Q, 128)) < HEADDIM
        scores = jnp.where(upper, scores, 0.0)
        half = (lax.broadcasted_iota(jnp.int32, (128, 128), 0) >= HEADDIM).astype(jnp.int32)
        head_lane = lane_iota((128, 128))

        def conv_back(lanes, dc):
            dbuf[0:Q, lanes] = dc
            dxbc = wc_ref[CONV - 1 : CONV, lanes] * dc
            for tap in range(CONV - 1):
                dxbc = dxbc + wc_ref[tap : tap + 1, lanes] * dbuf[3 - tap : 3 - tap + Q, lanes]
            dx_ref[:, lanes] = dxbc.astype(bf16)
            for tap in range(CONV):
                gconv_ref[tap : tap + 1, lanes] += jnp.sum(dc * buf[5 + tap : 5 + tap + Q, lanes], axis=0, keepdims=True)
            gconv_ref[CONV : CONV + 1, lanes] += jnp.sum(dc, axis=0, keepdims=True)

        def pair(p, carry):
            dscores, dquery, dkey, from_start, to_end, direct, thru = carry
            lanes = pl.ds(pl.multiple_of(p * 128, 128), 128)
            c = conv_tile(buf, wc_ref, lanes)
            s = sigmoid(c)
            values = c * s
            col0, col1 = col_ref[2 * p], col_ref[2 * p + 1]
            both = jnp.where(low, col0, col1)
            end = both[Q - 1 : Q, :]
            grown = jnp.exp(both)
            rest = jnp.exp(end - both)
            dtp = dtp_ref[p]
            stepped = values * dtp
            dy_low = dy_ref[:, lanes]
            dy = dy_low.astype(f32)
            parts = split_pair(dy_low, low)
            stepped_low = stepped.astype(bf16)
            dmix = dot_nt(stepped_low, parts)
            mix = []
            for n, col in enumerate((col0, col1)):
                decay = jnp.exp(jnp.minimum(row_ref[pl.ds(2 * p + n, 1), :] - col, 0.0))
                weighted = dmix[:, n * Q : (n + 1) * Q] * decay
                dscores = dscores + weighted
                mix.append((scores * decay).astype(bf16))
                passed = dot_nn((weighted * scores).astype(bf16), after)
                da_ref[pl.ds(2 * p + n, 1), :] = jnp.sum(jnp.where(strict, passed, 0.0), axis=0, keepdims=True)
            dstepped = dot_nn(jnp.concatenate(mix, axis=1), parts)
            dafter = dstate[:, lanes]
            dafter_low = dafter.astype(bf16)
            before_low = sin_ref[0, :, lanes]
            dend = dot_nn(keys, dafter_low) * rest
            grown_dy = (dy * grown).astype(bf16)
            select = (head_lane == 2 * p + half).astype(bf16)
            across = dot_nn(queries, before_low)
            from_start = from_start + dot_nn((across * grown * dy).astype(bf16), select)
            to_end = to_end + dot_nn((stepped * dend).astype(bf16), select)
            dstepped = dstepped + dend
            direct = direct + dot_nn((values * dstepped).astype(bf16), select)
            dquery = dquery + dot_nt(grown_dy, before_low)
            dkey = dkey + dot_nt((stepped * rest).astype(bf16), dafter_low)
            kept = jnp.exp(end) * dafter
            held = jnp.sum((kept * before_low.astype(f32)).reshape(8, 16, 128), axis=0)
            thru = thru + dot_nn(held.astype(bf16), select)
            dstate[:, lanes] = kept + dot_nn(queries_t, grown_dy)
            dvalues = dstepped * dtp + skip_ref[:, lanes] * dy
            gskip_ref[:, lanes] += jnp.sum(dy * values, axis=0, keepdims=True)
            conv_back(lanes, dvalues * (s * (1.0 + c * (1.0 - s))))
            return dscores, dquery, dkey, from_start, to_end, direct, thru

        def body(n, carry):
            for m in range(unroll):
                carry = pair(n * unroll + m, carry)
            return carry

        zero = jnp.zeros((Q, 128), f32)
        start = (zero,) * 6 + (jnp.zeros((16, 128), f32),)
        carry = lax.fori_loop(0, PAIRS // unroll, body, start)
        dscores, dquery, dkey, from_start, to_end, direct, thru = carry
        dscores = jnp.where(upper, dscores, 0.0)
        dkey = dkey + dot_nn(dscores.astype(bf16), queries)
        dquery = dquery + dot_nn(dscores.T.astype(bf16), keys)
        slope = s_tail * (1.0 + c_tail * (1.0 - s_tail))
        conv_back(slice(INNER, INNER + STATE), dkey * slope[:, :STATE])
        conv_back(slice(INNER + STATE, XBC), dquery * slope[:, STATE:])

        tail_sum = (row_iota((Q, Q)) <= lane_iota((Q, Q))).astype(f32)
        head_sum = (row_iota((Q, Q)) > lane_iota((Q, Q))).astype(f32)
        da = (
            da_ref[...].T
            + dot_nn(tail_sum, from_start, precision=lax.Precision.HIGHEST)
            + dot_nn(head_sum, to_end, precision=lax.Precision.HIGHEST)
            + jnp.sum(thru, axis=0, keepdims=True)
        )
        ddt = par_ref[1:2, :] * da + direct
        de = ddt * sigmoid(raw)
        de = jnp.where(lane_iota((Q, 128)) < HEADS, de, 0.0)
        dx_ref[:, XBC:] = de.astype(bf16)
        gpar_ref[0:1, :] += jnp.sum(de, axis=0, keepdims=True)
        gpar_ref[1:2, :] += jnp.sum(dt * da, axis=0, keepdims=True)

    if passed_on:

        @pl.when(i == pl.num_programs(0) - 1)
        def _():
            passed_on[0][...] = dstate[...]
            passed_on[1][...] = dbuf[0:8, :]


def part_span(meta, part, parts):
    return (meta[0] * part + parts - 1) // parts, (meta[0] * (part + 1) + parts - 1) // parts


def back(meta, part, parts, carried, proj, e, dy, sin, wc, par, skip):
    rows = proj.shape[0]
    chunks = rows // Q
    const = lambda i, m: (0, 0)

    def chunk(i, m):
        begin, end = part_span(m, part, parts)
        return jnp.clip(m[0] - begin - jnp.clip(i, 1, jnp.maximum(end - begin, 1)), 0, m[0] - 1)

    def written(i, m):
        begin, end = part_span(m, part, parts)
        block = jnp.where(end > begin, chunk(i, m), chunks)
        return jnp.where(i == 0, last_padded(m, m[0]), block) if part == 0 else block

    here = lambda i, m: (chunk(i, m), 0)
    out_shape = [
        jax.ShapeDtypeStruct((rows + Q, XE), bf16),
        jax.ShapeDtypeStruct((8, XBC), f32),
        jax.ShapeDtypeStruct((8, 128), f32),
        jax.ShapeDtypeStruct((1, INNER), f32),
    ]
    sums = [pl.BlockSpec((8, XBC), const), pl.BlockSpec((8, 128), const), pl.BlockSpec((1, INNER), const)]
    state = [pl.BlockSpec((STATE, INNER), const), pl.BlockSpec((8, XBC), const)]
    in_specs = [
        pl.BlockSpec((Q, PROJ), here),
        pl.BlockSpec((16, PROJ), lambda i, m: (jnp.maximum(chunk(i, m) * (Q // 16) - 1, 0), 0)),
        pl.BlockSpec((Q, 128), here),
        pl.BlockSpec((Q, INNER), here),
        pl.BlockSpec((1, STATE, INNER), lambda i, m: (chunk(i, m), 0, 0)),
        pl.BlockSpec((8, XBC), const),
        pl.BlockSpec((8, 128), const),
        pl.BlockSpec((1, INNER), const),
    ]
    out_specs = [pl.BlockSpec((Q, XE), lambda i, m: (written(i, m), 0))] + sums
    if part > 0:
        in_specs += [pl.BlockSpec(memory_space=pl.ANY)] + sums + state
    if part < parts - 1:
        out_shape += [jax.ShapeDtypeStruct((STATE, INNER), f32), jax.ShapeDtypeStruct((8, XBC), f32)]
        out_specs += state
    steps = -(-chunks // parts)
    return pl.pallas_call(
        functools.partial(back_kernel, 2, part, parts),
        out_shape=out_shape,
        grid_spec=pltpu.PrefetchScalarGridSpec(
            num_scalar_prefetch=1,
            grid=(steps + 1,),
            in_specs=in_specs,
            out_specs=out_specs,
            scratch_shapes=[
                pltpu.VMEM((Q + 8, XBC), f32),
                pltpu.VMEM((Q + 8, XBC), f32),
                pltpu.VMEM((STATE, INNER), f32),
                pltpu.VMEM((HEADS, Q, 128), f32),
                pltpu.VMEM((PAIRS, Q, 128), f32),
                pltpu.VMEM((128, Q), f32),
                pltpu.VMEM((128, Q), f32),
            ],
        ),
        input_output_aliases={9: 0} if part > 0 else {},
        compiler_params=params(),
        cost_estimate=cost(steps * PAIRS * 20 * 2 * Q * 128 * 128, 2 * steps * Q * (PROJ + 3 * INNER)),
        name="back",
    )(meta, proj, proj, e, dy, sin, wc, par, skip, *carried)


def weight_kernel(rows, swap_from, meta, at_ref, b_ref, mine_ref, other_ref):
    used = (meta[0] + 1) // 2
    half = at_ref.shape[0] // 2
    part_rows = half // 4
    swap = pl.program_id(0) >= swap_from

    def part(width):
        for c, out_ref in enumerate((mine_ref, other_ref)):

            def step(m, _):
                here = pl.ds(pl.multiple_of(c * half + 2 * m * part_rows, part_rows), 2 * part_rows)
                res = dot_nn(at_ref[here, 0:width], b_ref[0:width, :]).astype(bf16)
                for n in range(2):
                    place = jnp.where(swap, 2 * n + m, 2 * m + n)
                    there = pl.ds(pl.multiple_of(place * part_rows, part_rows), part_rows)
                    out_ref[there, :] = res[n * part_rows : (n + 1) * part_rows, :]
                return 0

            lax.fori_loop(0, 2, step, 0)

    for n in range(1, rows // (2 * Q) + 1):
        pl.when(used == n)(functools.partial(part, n * 2 * Q))


def weight_grad(meta, at, b, first, width, tile, swap_from):
    height, rows = at.shape
    offset = first // tile
    half = jax.ShapeDtypeStruct((height // 2, width), bf16)
    half_spec = pl.BlockSpec((height // 2, tile), lambda j, m: (0, j))
    return pl.pallas_call(
        functools.partial(weight_kernel, rows, swap_from),
        out_shape=(half, half),
        grid_spec=pltpu.PrefetchScalarGridSpec(
            num_scalar_prefetch=1,
            grid=(pl.cdiv(width, tile),),
            in_specs=[
                pl.BlockSpec((height, rows), lambda j, m: (0, 0)),
                pl.BlockSpec((rows, tile), lambda j, m: (0, j + offset)),
            ],
            out_specs=(half_spec, half_spec),
        ),
        compiler_params=params(),
        cost_estimate=cost(2 * rows * height * width, 2 * (rows * (height + width) + height * width)),
        name="weight_grad",
    )(meta, at, b)


def input_kernel(
    slot_chunks, steps, tile, meta, u_ref, err_ref, g_ref, dz_ref, dx_ref, w_ref, out0_ref, out1_ref, gn_ref, dh_ref
):
    j = pl.program_id(0)
    total = meta[0]
    chunks = 2 * slot_chunks
    last = w_ref[:, INNER + XBC : PROJ]
    cols = pl.ds(pl.multiple_of(j * tile, tile), tile)

    def block(b, rows):
        r = slice(b * 2 * Q, b * 2 * Q + rows)
        dh_ref[r, cols] = (
            dot_nt(dz_ref[r, :], w_ref[:, 0:INNER])
            + dot_nt(dx_ref[r, 0:XBC], w_ref[:, INNER : INNER + XBC])
            + dot_nt(dx_ref[r, XBC : XBC + HEADS], last)
        )

    for_blocks(total, chunks // 2, block)

    @pl.when(j == steps - 1)
    def _():
        out0_ref[...] = jnp.zeros_like(out0_ref)
        out1_ref[...] = jnp.zeros_like(out1_ref)
        gn_ref[...] = jnp.zeros_like(gn_ref)
        for k in range(chunks):

            @pl.when(k < total)
            def _():
                start = pl.multiple_of(source_chunk(meta, k, slot_chunks) * Q, Q)
                u = u_ref[pl.ds(start, Q), :].astype(f32)
                err = err_ref[k * Q : (k + 1) * Q, :].astype(f32)
                scale = lax.rsqrt(jnp.mean(u * u, axis=-1, keepdims=True) + epsilon)
                dh = dh_ref[k * Q : (k + 1) * Q, :]
                gn_ref[...] += jnp.sum(dh * (u * scale), axis=0, keepdims=True)
                n = dh * g_ref[...]
                inner = jnp.mean(u * n, axis=-1, keepdims=True)
                du = (err + scale * n - u * (scale * scale * scale * inner)).astype(bf16)

                @pl.when(k < meta[1])
                def _():
                    out0_ref[pl.ds(start, Q), :] = du

                @pl.when(k >= meta[1])
                def _():
                    out1_ref[pl.ds(pl.multiple_of(start - slot_chunks * Q, Q), Q), :] = du


def input_grad_of(meta, u, err, g1, dz, dx, w1):
    rows = u.shape[0]
    tile = 256
    steps = D // tile
    const = lambda j, m: (0, 0)
    once = pl.Buffered(1)
    return pl.pallas_call(
        functools.partial(input_kernel, rows // Q // 2, steps, tile),
        out_shape=(
            jax.ShapeDtypeStruct((rows // 2, D), bf16),
            jax.ShapeDtypeStruct((rows // 2, D), bf16),
            jax.ShapeDtypeStruct((1, D), f32),
        ),
        grid_spec=pltpu.PrefetchScalarGridSpec(
            num_scalar_prefetch=1,
            grid=(steps,),
            in_specs=[
                pl.BlockSpec((rows, D), const, pipeline_mode=once),
                pl.BlockSpec((rows, D), const, pipeline_mode=once),
                pl.BlockSpec((1, D), const),
                pl.BlockSpec((rows, INNER), const, pipeline_mode=once),
                pl.BlockSpec((rows, XE), const, pipeline_mode=once),
                pl.BlockSpec((tile, w1.shape[1]), lambda j, m: (j, 0)),
            ],
            out_specs=[
                pl.BlockSpec((rows // 2, D), const),
                pl.BlockSpec((rows // 2, D), const),
                pl.BlockSpec((1, D), const),
            ],
            scratch_shapes=[pltpu.VMEM((rows, D), f32)],
        ),
        compiler_params=params(),
        cost_estimate=cost(2 * rows * D * PROJ, 2 * (D * PROJ + rows * PROJ)),
        name="input_grad",
    )(meta, u, err, g1, dz, dx, w1)


def partner(value, axis, bit):
    mask = 2**bit
    pairs = [(source, source ^ mask) for source in range(lax.axis_size(axis))]
    return lax.ppermute(value, axis, pairs)


def log2(size):
    return size.bit_length() - 1


def halving_order(swap):
    fsdp = [("fsdp", bit) for bit in range(log2(lax.axis_size("fsdp")))]
    near = [("dp", 1)]
    far = [("dp", bit) for bit in range(2, log2(lax.axis_size("dp")))]
    return [("dp", 0)] + (near + fsdp if swap else fsdp + near) + far


def flat_bit(axis, bit):
    return bit + (log2(lax.axis_size("fsdp")) if axis == "dp" else 0)


def kept_at(order, owner):
    away = owner ^ lax.axis_index(AXES)
    place = jnp.zeros_like(away)
    for axis, bit in order:
        place = 2 * place + ((away >> flat_bit(axis, bit)) & 1)
    return place


def owner_at(order, place):
    away = jnp.zeros_like(place)
    for n, (axis, bit) in enumerate(order):
        away = away + (((place >> (len(order) - 1 - n)) & 1) << flat_bit(axis, bit))
    return away ^ lax.axis_index(AXES)


class Term:
    def __init__(self, value):
        self.value = value


class Columns:
    def __init__(self, width, swap):
        self.order = halving_order(swap)
        self.width = width
        self.terms = []
        self.phase = 0

    def done(self):
        return self.phase == len(self.order)

    def sum(self, start, stop):
        return sum(term.value[start:stop, at : at + self.width].astype(f32) for term, at in self.terms)

    def halve(self):
        self.rows //= 2
        return self.sum(self.rows, 2 * self.rows).astype(bf16)


class Chain:
    def __init__(self, halves, columns, grouped):
        mine, other = halves
        self.columns = columns
        if not grouped:
            count = lax.axis_size(AXES)
            whole = jnp.concatenate([mine, other]).reshape(count, -1, mine.shape[1])
            parts = []
            at = 0
            for c in columns:
                parts.append(whole[:, :, at : at + c.width][owner_at(c.order, jnp.arange(count))])
                at += c.width
            mine, other = jnp.concatenate(parts, axis=2).reshape(2, -1, mine.shape[1])
        self.going = [(columns, other)]
        kept = Term(mine)
        at = 0
        for c in columns:
            c.rows = mine.shape[0]
            c.terms.append((kept, at))
            at += c.width

    def halve(self):
        groups = {}
        for c in self.columns:
            if not c.done() and all(c not in members for members, _ in self.going):
                groups.setdefault((c.order[c.phase], c.rows), []).append(c)
        for members in groups.values():
            sent = [c.halve() for c in members]
            self.going.append((members, jnp.concatenate(sent, axis=1) if len(sent) > 1 else sent[0]))

    def exchange(self):
        for members, sent in self.going:
            first = members[0]
            came = Term(partner(sent, *first.order[first.phase]))
            at = 0
            for c in members:
                c.terms.append((came, at))
                c.phase += 1
                at += c.width
        self.going = []

    def finish(self):
        while not all(c.done() for c in self.columns):
            self.halve()
            self.exchange()
        return [c.sum(0, c.rows) for c in self.columns]


def tick(token, chains, after):
    last = {id(c.terms[-1][0]): c.terms[-1][0] for chain in chains for c in chain.columns if c.phase > 0}
    if last:
        *came, _ = lax.optimization_barrier([term.value for term in last.values()] + [after])
        for term, value in zip(last.values(), came):
            term.value = value
    for chain in chains:
        chain.halve()
    sent = [value for chain in chains for _, value in chain.going]
    *sent, token = lax.optimization_barrier(sent + [token])
    for chain in chains:
        chain.going = [(members, sent.pop(0)) for members, _ in chain.going]
        chain.exchange()
    return token


W_COLS = 6528
W_SPANS = ((0, 2944), (2944, 2944), (5888, 640))


def gather_kernel(
    count, inner, flag_ref, own_ref, norm_ref, conv_ref, bias_ref, inner_ref, tokens_ref,
    w_ref, wc_ref, g1_ref, g2_ref, u_ref,
    shard_ref, tile_ref, tiles_ref, kept, given,
    send_sem, recv_sem, tile_send, tile_recv, own_sem, give_send, give_recv,
):
    me = lax.axis_index("dp") * inner + lax.axis_index("fsdp")
    height = shard_ref.shape[0]
    x, core, y = flat_bit("fsdp", 0), flat_bit("dp", 0), flat_bit("dp", 1)
    far = [flat_bit("dp", bit) for bit in range(2, log2(lax.axis_size("dp")))]
    ways = (far + [y, x, core], far + [x, y, core], [x, y] + far[::-1] + [core])
    spans = [pl.ds(at, width) for at, width in W_SPANS]
    groups = range(len(spans))

    full = PROJ // 128 * 128
    shard_ref[:, 0:full] = own_ref[:, 0:full].astype(bf16)
    shard_ref[:, full:] = jnp.zeros((height, W_COLS - full), bf16)
    shard_ref[:, full:PROJ] = own_ref[:, full:].astype(bf16)
    tile_ref[...] = jnp.zeros_like(tile_ref)
    for row, ref in ((0, conv_ref), (4, bias_ref), (5, inner_ref), (6, norm_ref)):
        tile_ref[row : row + ref.shape[0], 0 : ref.shape[1]] = ref[...].astype(bf16).astype(f32)

    def place(away):
        return pl.ds(pl.multiple_of(jnp.bitwise_xor(me, away) * height, height), height)

    def link(bit):
        other = jnp.bitwise_xor(me, 2**bit)
        return (other // inner, other % inner)

    def last_step(half, away):
        return max((n for n, bit in enumerate(ways[half]) if (away >> bit) & 1), default=-1)

    def send(half, away, bit):
        src = shard_ref.at[:, spans[half]] if away == 0 else w_ref.at[place(away), spans[half]]
        return pltpu.make_async_remote_copy(
            src_ref=src,
            dst_ref=w_ref.at[place(away), spans[half]],
            send_sem=send_sem.at[half, away ^ 2**bit],
            recv_sem=recv_sem.at[half, away ^ 2**bit],
            device_id=link(bit),
            device_id_type=pl.DeviceIdType.MESH,
        )

    def receive(half, away):
        block = w_ref.at[place(away), spans[half]]
        return pltpu.make_async_remote_copy(
            src_ref=block,
            dst_ref=block,
            send_sem=send_sem.at[half, away],
            recv_sem=recv_sem.at[half, away],
            device_id=link(ways[half][last_step(half, away)]),
            device_id_type=pl.DeviceIdType.MESH,
        )

    def send_on(half, away):
        sends = [send(half, away, bit) for bit in ways[half][last_step(half, away) + 1 :]]
        for one in sends:
            one.start()
        return sends

    def tile_copy(n):
        other = jnp.bitwise_xor(me, n)
        return pltpu.make_async_remote_copy(
            src_ref=tile_ref,
            dst_ref=tiles_ref.at[me],
            send_sem=tile_send.at[n],
            recv_sem=tile_recv.at[n],
            device_id=(other // inner, other % inner),
            device_id_type=pl.DeviceIdType.MESH,
        )

    def start_tile(n, _):
        tile_copy(n).start()
        return 0

    def wait_tile(n, _):
        tile_copy(n).wait()
        return 0

    started = []
    for step in range(len(ways[0])):
        for half in groups:
            one = send(half, 0, ways[half][step])
            one.start()
            started.append(one)
    own = pltpu.make_async_copy(shard_ref, w_ref.at[place(0), :], own_sem.at[0])
    own.start()

    second = jnp.broadcast_to(flag_ref[0, 0], (1, D)) == 1
    rows = kept.shape[0]

    def choose(n, _):
        r = pl.ds(pl.multiple_of(n * 64, 64), 64)
        zero, one = tokens_ref[0, r, :].astype(f32), tokens_ref[1, r, :].astype(f32)
        kept[r, :] = jnp.where(second, one, zero).astype(bf16)
        given[r, :] = jnp.where(second, zero, one).astype(bf16)
        return 0

    lax.fori_loop(0, rows // 64, choose, 0)
    lax.fori_loop(1, count, start_tile, 0)
    tiles_ref[me] = tile_ref[...]

    blocks = [(half, away) for half in groups for away in range(1, count)]
    blocks.sort(key=lambda b: (b[1].bit_count(), last_step(*b), b[0]))
    tail = []
    for n, (half, away) in enumerate(blocks):
        receive(half, away).wait_recv()
        started += send_on(half, away)
        if n == 8:
            keep = pltpu.make_async_copy(kept, u_ref.at[pl.ds(0, rows), :], own_sem.at[1])
            give = pltpu.make_async_remote_copy(
                src_ref=given,
                dst_ref=u_ref.at[pl.ds(rows, rows), :],
                send_sem=give_send,
                recv_sem=give_recv,
                device_id=link(core),
                device_id_type=pl.DeviceIdType.MESH,
            )
            keep.start()
            give.start()
            tail = [keep, give]
        if n == 40:
            lax.fori_loop(1, count, wait_tile, 0)
            wc_ref[...] = jnp.zeros_like(wc_ref)
            for owner in range(count):
                for ref, row, tall in ((wc_ref, 0, 5), (g2_ref, 5, 1), (g1_ref, 6, 1)):
                    each = ref.shape[1] // count
                    ref[0:tall, owner * each : (owner + 1) * each] = tiles_ref[owner, row : row + tall, 0:each]
    for one in started:
        one.wait_send()
    for one in tail:
        one.wait()
    own.wait()


def gather(flag, own, norm, conv, bias, inner, tokens):
    count = lax.axis_size(AXES)
    slot = tokens.shape[1]
    whole = pl.BlockSpec(memory_space=pltpu.VMEM)
    anywhere = pl.BlockSpec(memory_space=pl.ANY)
    dma = pltpu.SemaphoreType.DMA
    return pl.pallas_call(
        functools.partial(gather_kernel, count, lax.axis_size("fsdp")),
        out_shape=(
            jax.ShapeDtypeStruct((D, W_COLS), bf16),
            jax.ShapeDtypeStruct((8, XBC), f32),
            jax.ShapeDtypeStruct((1, D), f32),
            jax.ShapeDtypeStruct((1, INNER), f32),
            jax.ShapeDtypeStruct((2 * slot, D), bf16),
        ),
        in_specs=[pl.BlockSpec(memory_space=pltpu.SMEM)] + [whole] * 6,
        out_specs=(anywhere, whole, whole, whole, anywhere),
        scratch_shapes=[
            pltpu.VMEM((own.shape[0], W_COLS), bf16),
            pltpu.VMEM((8, 128), f32),
            pltpu.VMEM((count, 8, 128), f32),
            pltpu.VMEM((slot, D), bf16),
            pltpu.VMEM((slot, D), bf16),
            dma((len(W_SPANS), count)),
            dma((len(W_SPANS), count)),
            dma((count,)),
            dma((count,)),
            dma((2,)),
            dma,
            dma,
        ],
        compiler_params=params(has_side_effects=True),
        cost_estimate=cost(1e6, 2 * D * W_COLS),
        name="gather",
    )(flag, own, norm, conv, bias, inner, tokens)


def sum_kernel(count, inner, sent_ref, out_ref, came, send_sem, recv_sem):
    me = lax.axis_index("dp") * inner + lax.axis_index("fsdp")

    def copy(n):
        other = jnp.bitwise_xor(me, n)
        return pltpu.make_async_remote_copy(
            src_ref=sent_ref.at[other],
            dst_ref=came.at[n],
            send_sem=send_sem.at[n],
            recv_sem=recv_sem.at[n],
            device_id=(other // inner, other % inner),
            device_id_type=pl.DeviceIdType.MESH,
        )

    def start(n, _):
        copy(n).start()
        return 0

    def add(n, total):
        copy(n).wait()
        return total + came[n]

    lax.fori_loop(1, count, start, 0)
    out_ref[...] = lax.fori_loop(1, count, add, sent_ref[me])


def sum_small(tiles):
    count = tiles.shape[0]
    whole = pl.BlockSpec(memory_space=pltpu.VMEM)
    return pl.pallas_call(
        functools.partial(sum_kernel, count, lax.axis_size("fsdp")),
        out_shape=jax.ShapeDtypeStruct(tiles.shape[1:], f32),
        in_specs=[whole],
        out_specs=whole,
        scratch_shapes=[
            pltpu.VMEM(tiles.shape, f32),
            pltpu.SemaphoreType.DMA((count,)),
            pltpu.SemaphoreType.DMA((count,)),
        ],
        compiler_params=pltpu.CompilerParams(has_side_effects=True),
        cost_estimate=cost(count * 1024, 8 * count * 1024),
        name="sum_small",
    )(tiles)


TILE_ROWS = 16
X_CUT = 1792
X_PIECES = tuple((which, 512 * n, width) for n in range(4) for which, width in ((0, 512 if n < 3 else 256), (1, 512 if n < 3 else 128)))


def finish_kernel(
    count, inner, m0, a0, b0, m1, a1, b1, gconv_ref, gpar_ref, par_ref, gskip_ref, gi_ref, gn_ref, given_ref,
    x_ref, tile_ref, back_ref, *scratch,
):
    sources = ((m0, a0, b0), (m1, a1, b1))
    terms, scratch = scratch[:2], scratch[2:]
    sent, scratch = [scratch[2 * n : 2 * n + 2] for n in range(3)], scratch[6:]
    came, scratch = [scratch[2 * n : 2 * n + 2] for n in range(3)], scratch[6:]
    tiles, tiles_in, load_sem, send_sem, recv_sem, tile_send, tile_recv, give_send, give_recv = scratch
    me = lax.axis_index("dp") * inner + lax.axis_index("fsdp")
    far = [flat_bit("dp", bit) for bit in (2, 3)]
    ways = ([flat_bit("dp", 1)] + far, [flat_bit("fsdp", 0)] + far)
    tall = terms[0].shape[1]

    def target(other):
        return {"device_id": (other // inner, other % inner), "device_id_type": pl.DeviceIdType.MESH}

    def load(n):
        which, at, width = X_PIECES[n]
        cols = pl.ds(at, width)
        return [
            pltpu.make_async_copy(ref.at[pl.ds(0, tall), cols], terms[which].at[i, :, cols], load_sem.at[n, i])
            for i, ref in enumerate(sources[which])
        ]

    def copy(n, phase):
        which, at, width = X_PIECES[n]
        cols = pl.ds(at, width)
        return pltpu.make_async_remote_copy(
            src_ref=sent[phase][which].at[:, cols],
            dst_ref=came[phase][which].at[:, cols],
            send_sem=send_sem.at[n, phase],
            recv_sem=recv_sem.at[n, phase],
            **target(jnp.bitwise_xor(me, 2 ** ways[which][phase])),
        )

    def total(n, phase, start, rows):
        which, at, width = X_PIECES[n]
        parts = [terms[which][i, start : start + rows, at : at + width] for i in range(3)]
        parts += [came[p][which][start : start + rows, at : at + width] for p in range(phase)]
        return sum(part.astype(f32) for part in parts)

    def go(n, phase):
        which, at, width = X_PIECES[n]
        rows = tall >> (phase + 1)
        sent[phase][which][:, at : at + width] = total(n, phase, rows, rows).astype(bf16)
        copy(n, phase).start()

    def tile_copy(n):
        other = jnp.bitwise_xor(me, n)
        return pltpu.make_async_remote_copy(
            src_ref=tiles.at[other],
            dst_ref=tiles_in.at[n],
            send_sem=tile_send.at[n],
            recv_sem=tile_recv.at[n],
            **target(other),
        )

    def start_tile(n, _):
        tile_copy(n).start()
        return 0

    def add_tile(n, value):
        tile_copy(n).wait()
        return value + tiles_in[n]

    give = pltpu.make_async_remote_copy(
        src_ref=given_ref,
        dst_ref=back_ref,
        send_sem=give_send,
        recv_sem=give_recv,
        **target(jnp.bitwise_xor(me, 2 ** flat_bit("dp", 0))),
    )
    pieces = len(X_PIECES)
    for n in range(pieces):
        for one in load(n):
            one.start()
    for n in range(pieces):
        for one in load(n):
            one.wait()
        go(n, 0)
    give.start()

    pick = lax.broadcasted_iota(jnp.int32, (INNER, 128), 0) // HEADDIM == lane_iota((INNER, 128))
    skips = dot_nn(
        jnp.broadcast_to(gskip_ref[...], (8, INNER)), pick.astype(f32), precision=lax.Precision.HIGHEST
    )
    tiles[...] = jnp.zeros_like(tiles)
    for owner in range(count):
        for row, ref in ((0, gconv_ref), (8, gi_ref), (9, gn_ref)):
            each = ref.shape[1] // count
            tiles[owner, row : row + ref.shape[0], 0:each] = ref[:, owner * each : (owner + 1) * each]
        tiles[owner, 10:11, :] = gpar_ref[0:1, :]
        tiles[owner, 11:12, :] = gpar_ref[1:2, :] * par_ref[1:2, :]
        tiles[owner, 12:13, :] = skips[0:1, :]

    lag = 2
    for n in range(pieces + 2 * lag):
        if n < pieces:
            copy(n, 0).wait_recv()
            go(n, 1)
        if n == 1:
            lax.fori_loop(1, count, start_tile, 0)
        if lag <= n < pieces + lag:
            copy(n - lag, 1).wait_recv()
            go(n - lag, 2)
        if n >= 2 * lag:
            which, at, width = X_PIECES[n - 2 * lag]
            copy(n - 2 * lag, 2).wait_recv()
            x_ref[:, which * X_CUT + at : which * X_CUT + at + width] = total(n - 2 * lag, 3, 0, tall >> 3)
    tile_ref[...] = lax.fori_loop(1, count, add_tile, tiles[me])
    for n in range(pieces):
        for phase in range(3):
            copy(n, phase).wait_send()
    give.wait()


def finish(chains, gconv, gpar, par, gskip, gi, gn, given):
    count = lax.axis_size(AXES)
    operands = [term.value for chain in chains for term, _ in chain.columns[0].terms]
    widths = [chain.columns[0].width for chain in chains]
    tall = chains[0].columns[0].rows
    dma = pltpu.SemaphoreType.DMA
    anywhere = pl.BlockSpec(memory_space=pl.ANY)
    whole = pl.BlockSpec(memory_space=pltpu.VMEM)
    halves = [pltpu.VMEM((tall >> (phase + 1), width), bf16) for phase in range(3) for width in widths]
    pieces = len(X_PIECES)
    return pl.pallas_call(
        functools.partial(finish_kernel, count, lax.axis_size("fsdp")),
        out_shape=(
            jax.ShapeDtypeStruct((tall >> 3, XE), f32),
            jax.ShapeDtypeStruct((TILE_ROWS, 128), f32),
            jax.ShapeDtypeStruct(given.shape, bf16),
        ),
        in_specs=[anywhere] * 6 + [whole] * 6 + [anywhere],
        out_specs=(whole, whole, anywhere),
        scratch_shapes=[
            *(pltpu.VMEM((3, tall, width), bf16) for width in widths),
            *halves,
            *halves,
            pltpu.VMEM((count, TILE_ROWS, 128), f32),
            pltpu.VMEM((count, TILE_ROWS, 128), f32),
            dma((pieces, 3)),
            dma((pieces, 3)),
            dma((pieces, 3)),
            dma((count,)),
            dma((count,)),
            dma,
            dma,
        ],
        compiler_params=params(has_side_effects=True),
        cost_estimate=cost(1e7, 2e7),
        name="finish",
    )(*operands, gconv, gpar, par, gskip, gi, gn, given)


def on_device(
    tokens, cotangent, lengths, balance, norm_gain, in_weight, conv_weight, conv_bias,
    step_bias, decay_log, skip_weight, inner_gain, out_weight,
):
    device = lax.axis_index(AXES)
    count = lax.axis_size(AXES)
    slot = tokens.shape[1]
    rows = 2 * slot
    first_source = balance[2 * device]
    second_source = balance[2 * device + 1]
    keep_second = first_source - 2 * device == 1
    cot = cotangent.reshape(rows, D)
    lens = [lengths[first_source], lengths[second_source]]
    chunks = [(n + Q - 1) // Q for n in lens]
    grouped = is_grouped()
    meta = jnp.stack([chunks[0] + chunks[1], chunks[0], lens[0], lens[1]]).astype(jnp.int32)

    sizes = [v.shape[0] for v in (norm_gain, inner_gain)]
    if grouped:
        flag = keep_second.astype(jnp.int32).reshape(1, 1)
        w1, wc, g1, g2, u = gather(
            flag, in_weight, norm_gain[None], conv_weight.T, conv_bias[None], inner_gain[None], tokens
        )
    else:
        outgoing = jnp.where(keep_second, tokens[0], tokens[1])
        incoming = partner(outgoing, "dp", 0)
        u = jnp.concatenate([jnp.where(keep_second, tokens[1], tokens[0]), incoming], axis=0)
        w1 = lax.all_gather(in_weight.astype(bf16), AXES, axis=0, tiled=True)
        small = [norm_gain, inner_gain, conv_bias, conv_weight.reshape(-1)]
        packed = jnp.concatenate(small).astype(bf16)
        packed = lax.all_gather(packed[None, :], AXES, axis=0, tiled=True).astype(f32)
        cuts = [sum(v.shape[0] for v in small[:n]) for n in range(5)]
        g1, g2, bias, taps = (packed[:, cuts[n] : cuts[n + 1]].reshape(1, -1) for n in range(4))
        wc = jnp.concatenate([taps.reshape(XBC, CONV).T, bias, jnp.zeros((3, XBC), f32)])
    w2_own, w1 = lax.optimization_barrier([out_weight.astype(bf16), w1])
    w2 = lax.all_gather(w2_own, AXES, axis=0, tiled=True)

    rate = -jnp.exp(decay_log)
    par = jnp.zeros((8, 128), f32).at[0, :HEADS].set(step_bias).at[1, :HEADS].set(rate)
    skip = jnp.repeat(skip_weight, HEADDIM)[None]

    proj, e, ht = project(meta, u, g1, w1)
    o, ot, y, sin, err = mixer(meta, proj, e, cot, wc, par, skip, g2)
    never = 1 << 20

    def both(width):
        return [Columns(width // 2, False), Columns(width // 2, True)]

    halves = weight_grad(meta, ot, err, 0, D, D // 2, 1 if grouped else never)
    c_out = Chain(halves, both(D), grouped)
    meta = tick(meta, [c_out], err)
    out, dy, dz, gi = gate(meta, u, err, w2, o, y, proj, g2)
    meta = tick(meta, [c_out], gi)
    halves = weight_grad(meta, ht, dz, 0, INNER, INNER // 4, 2 if grouped else never)
    c_z = Chain(halves, both(INNER), grouped)
    parts = 3
    carried = ()
    for part in range(parts):
        meta = tick(meta, [c_out, c_z] if part > 0 else [c_z], carried[2] if part > 0 else gi)
        carried = back(meta, part, parts, carried, proj, e, dy, sin, wc, par, skip)
    dx, gconv, gpar, gskip = carried
    meta = tick(meta, [c_out, c_z], gpar)
    cut = X_CUT
    halves = weight_grad(meta, ht, dx, 0, cut, cut // 2, never)
    c_x = Chain(halves, [Columns(cut, False)], grouped)
    meta = tick(meta, [c_z, c_x], halves[1])
    halves = weight_grad(meta, ht, dx, cut, XE - cut, cut // 2, 0 if grouped else never)
    c_x1 = Chain(halves, [Columns(XE - cut, True)], grouped)
    meta = tick(meta, [c_x, c_x1], halves[1])
    meta = tick(meta, [c_x1], c_x1.columns[0].terms[-1][0].value)
    kept_half, given_half, gn = input_grad_of(meta, u, err, g1, dz, dx, w1)
    conv_each = XBC // count
    if grouped:
        late = [chain.columns[0].terms[-1][0] for chain in (c_out, c_z)]
        *came, gn = lax.optimization_barrier([term.value for term in late] + [gn])
        for term, value in zip(late, came):
            term.value = value
        grad_x, tile, back_half = finish([c_x, c_x1], gconv, gpar, par, gskip, gi, gn, given_half)
        grad_x = [grad_x]
        grad_conv, grad_bias = tile[:CONV, :conv_each].T, tile[CONV, :conv_each]
        grad_inner, grad_norm = tile[8, : sizes[1]], tile[9, : sizes[0]]
        heads = [tile[10 + n, :HEADS] for n in range(3)]
    else:
        back_half = partner(given_half, "dp", 0)
        heads = jnp.concatenate(
            [gpar[0, :HEADS], gpar[1, :HEADS] * rate, gskip.reshape(HEADS, HEADDIM).sum(axis=1)]
        )
        owned = [gconv[:CONV].T.reshape(count, -1), gconv[CONV].reshape(count, -1), gi.reshape(count, -1)]
        tiles = jnp.concatenate(owned + [jnp.broadcast_to(heads, (count, 3 * HEADS)), gn.reshape(count, -1)], axis=1)
        tiles = jnp.pad(tiles, ((0, 0), (0, 1024 - tiles.shape[1]))).reshape(count, 8, 128)
        sums = sum_small(tiles).reshape(-1)
        grad_x = c_x.finish() + c_x1.finish()
        ends = [sum(v.shape[1] for v in owned[:n]) for n in range(4)]
        grad_conv = sums[: ends[1]].reshape(-1, CONV)
        grad_bias = sums[ends[1] : ends[2]]
        grad_inner = sums[ends[2] : ends[3]]
        heads = sums[ends[3] : ends[3] + 3 * HEADS].reshape(3, HEADS)
        grad_norm = sums[ends[3] + 3 * HEADS :][: sizes[0]]
    grad_out = jnp.concatenate(c_out.finish(), axis=1)
    grad_in = jnp.concatenate(c_z.finish() + grad_x, axis=1)[:, :PROJ]
    swapped = [jnp.stack([back_half, kept_half]), jnp.stack([kept_half, back_half])]
    input_grad = jnp.where(keep_second, *swapped)
    return (
        out.reshape(2, slot, D),
        input_grad,
        grad_norm,
        grad_in,
        grad_conv,
        grad_bias,
        heads[0],
        heads[1],
        heads[2],
        grad_inner,
        grad_out,
    )


def solution(mesh):
    flat = P(AXES)
    rowed = P(AXES, None)
    slots = P(AXES, None, None)
    return jax.shard_map(
        on_device,
        mesh=mesh,
        in_specs=(slots, slots, P(), P(), flat, rowed, rowed, flat, P(), P(), P(), flat, rowed),
        out_specs=(slots, slots, flat, rowed, rowed, flat, P(), P(), P(), flat, rowed),
        check_vma=False,
    )
```

```python
import functools
import jax
import jax.numpy as jnp
from jax import lax
from jax.experimental import pallas as pl
from jax.experimental.pallas import tpu as pltpu
from jax.sharding import PartitionSpec as P

D = 1536
INNER = 3072
HEADS = 48
HEADDIM = 64
STATE = 128
CONV = 4
XBC = 3328
PROJ = 6448
XE = XBC + 128
Q = 128
PAIRS = HEADS // 2

f32 = jnp.float32
bf16 = jnp.bfloat16
epsilon = 1e-05
LOG2E = 1.4426950408889634
AXES = ("dp", "fsdp")


def sigmoid(v):
    return 0.5 * jnp.tanh(0.5 * v) + 0.5


def dot_nn(a, b, precision=None):
    return jnp.dot(a, b, preferred_element_type=f32, precision=precision)


def dot_nt(a, b):
    return lax.dot_general(a, b, (((1,), (1,)), ((), ())), preferred_element_type=f32)


def dot_tn(a, b):
    return lax.dot_general(a, b, (((0,), (0,)), ((), ())), preferred_element_type=f32)


def lane_iota(shape):
    return lax.broadcasted_iota(jnp.int32, shape, len(shape) - 1)


def row_iota(shape):
    return lax.broadcasted_iota(jnp.int32, shape, len(shape) - 2)


H_UNIT = 48
O_UNIT = 32


def is_grouped():
    return D // lax.axis_size(AXES) == H_UNIT


def unit_row(unit, size, per_owner):
    if is_grouped():
        owner = unit // per_owner
        unit = kept_at(halving_order(False), owner) * per_owner + (unit - owner * per_owner)
    return pl.multiple_of(unit * size, 16)


def source_chunk(meta, k, slot_chunks):
    return jnp.where(k < meta[1], k, k - meta[1] + slot_chunks)


def live_rows(meta, k):
    inside = k < meta[1]
    return jnp.where(inside, meta[2] - k * Q, meta[3] - (k - meta[1]) * Q)


def last_live(meta, k):
    return jnp.minimum(k, meta[0] - 1)


def last_padded(meta, k):
    return jnp.minimum(k, meta[0] + lax.rem(meta[0], 2) - 1)


def for_live(total, chunks, body):
    for n in range(2, chunks + 1):
        pl.when(total == n)(functools.partial(body, n * Q))


def cost(flops, moved, transcendentals=0):
    return pl.CostEstimate(flops=int(flops), bytes_accessed=int(moved), transcendentals=int(transcendentals))


def params(**kw):
    return pltpu.CompilerParams(vmem_limit_bytes=60 * 1024 * 1024, **kw)


def project_kernel(slot_chunks, steps, tile, meta, u_ref, g_ref, w_ref, proj_ref, e_ref, ht_ref, h_ref):
    j = pl.program_id(0)
    total = meta[0]
    chunks = 2 * slot_chunks

    @pl.when(j == 0)
    def _():
        for k in range(chunks):

            @pl.when(k < total)
            def _():
                start = pl.multiple_of(source_chunk(meta, k, slot_chunks) * Q, Q)
                x = u_ref[pl.ds(start, Q), :].astype(f32)
                scale = lax.rsqrt(jnp.mean(x * x, axis=-1, keepdims=True) + epsilon)
                normed = x * scale * g_ref[...]
                h_ref[k * Q : (k + 1) * Q, :] = normed.astype(bf16)
                turned = normed.T.astype(bf16)
                for n in range(D // H_UNIT):
                    there = pl.ds(unit_row(jnp.int32(n), H_UNIT, 1), H_UNIT)
                    ht_ref[there, k * Q : (k + 1) * Q] = turned[n * H_UNIT : (n + 1) * H_UNIT, :]

            @pl.when(k >= total)
            def _():
                ht_ref[:, k * Q : (k + 1) * Q] = jnp.zeros((D, Q), bf16)

    edge = XBC + INNER - (steps - 1) * tile

    def live(rows):
        def part(n, _):
            cols = pl.ds(pl.multiple_of(n * 256, 256), 256)
            proj_ref[0:rows, cols] = dot_nn(h_ref[0:rows, :], w_ref[:, cols]).astype(bf16)
            return 0

        lax.fori_loop(0, tile // 256, part, 0)

    for_live(total, chunks, live)

    @pl.when(j == steps - 1)
    def _():
        def steps_of(k, _):
            r = pl.ds(pl.multiple_of(k * Q, Q), Q)
            tail = dot_nn(h_ref[r, :], w_ref[:, edge : edge + 128])
            e_ref[r, :] = jnp.where(lane_iota(tail.shape) < HEADS, tail, 0.0)
            return 0

        lax.fori_loop(0, total, steps_of, 0)


def project(meta, u, g1, w1):
    rows = u.shape[0]
    tile = 512
    steps = pl.cdiv(PROJ, tile)
    return pl.pallas_call(
        functools.partial(project_kernel, rows // Q // 2, steps, tile),
        out_shape=(
            jax.ShapeDtypeStruct((rows, PROJ), bf16),
            jax.ShapeDtypeStruct((rows, 128), f32),
            jax.ShapeDtypeStruct((D, rows), bf16),
        ),
        grid_spec=pltpu.PrefetchScalarGridSpec(
            num_scalar_prefetch=1,
            grid=(steps,),
            in_specs=[
                pl.BlockSpec((rows, D), lambda j, m: (0, 0)),
                pl.BlockSpec((1, D), lambda j, m: (0, 0)),
                pl.BlockSpec((D, tile), lambda j, m: (0, j)),
            ],
            out_specs=[
                pl.BlockSpec((rows, tile), lambda j, m: (0, j)),
                pl.BlockSpec((rows, 128), lambda j, m: (0, 0)),
                pl.BlockSpec((D, rows), lambda j, m: (0, 0)),
            ],
            scratch_shapes=[pltpu.VMEM((rows, D), bf16)],
        ),
        compiler_params=params(),
        cost_estimate=cost(2 * rows * D * PROJ, 2 * (D * PROJ + rows * PROJ)),
        name="project",
    )(meta, u, g1, w1)


def conv_tile(buf, wc_ref, lanes):
    c = wc_ref[CONV : CONV + 1, lanes]
    for tap in range(CONV):
        c = c + wc_ref[tap : tap + 1, lanes] * buf[5 + tap : 5 + tap + Q, lanes]
    return c


def step_sizes(e_ref, par_ref):
    raw = e_ref[...] + par_ref[0:1, :]
    dt = jnp.maximum(raw, 0.0) + jnp.log1p(jnp.exp(-jnp.abs(raw)))
    decay = par_ref[1:2, :]
    lower = (row_iota((Q, Q)) >= lane_iota((Q, Q))).astype(f32)
    cum = dot_nn(lower, dt * (decay * LOG2E), precision=lax.Precision.HIGHEST)
    return raw, dt, cum


def head_column(values, n):
    return jnp.broadcast_to(values[:, n : n + 1], (Q, 128))


def head_pair(values, n):
    index = n + (lane_iota((Q, 128)) >= HEADDIM).astype(jnp.int32)
    return jnp.take_along_axis(values, index, axis=1, mode="promise_in_bounds")


def next_heads(ref, values, used):
    ref[...] = pltpu.roll(values, 128 - used, 1)


def split_pair(v, low):
    zero = jnp.zeros_like(v)
    return jnp.concatenate([jnp.where(low, v, zero), jnp.where(low, zero, v)], axis=0)


def mixer_kernel(
    unroll, meta, proj_ref, e_ref, cot_ref, wc_ref, par_ref, skip_ref, g_ref,
    o_ref, ot_ref, y_ref, sin_ref, err_ref,
    buf, state, cum_ref, dts_ref, row_ref, q_ref,
):
    k = pl.program_id(0)
    total = meta[0]

    @pl.when((k == total) & (lax.rem(total, 2) == 1))
    def _():
        o_ref[...] = jnp.zeros_like(o_ref)
        ot_ref[...] = jnp.zeros_like(ot_ref)
        err_ref[...] = jnp.zeros_like(err_ref)

    @pl.when(k < total)
    def _():
        live = row_iota((Q, D)) < live_rows(meta, k)
        err_ref[...] = jnp.where(live, cot_ref[...].astype(f32), 0.0).astype(bf16)
        first = (k == 0) | (k == meta[1])

        @pl.when(first)
        def _():
            buf[0:8, :] = jnp.zeros((8, XBC), f32)
            state[...] = jnp.zeros_like(state)

        @pl.when(jnp.logical_not(first))
        def _():
            buf[0:8, :] = buf[Q : Q + 8, :]

        buf[8 : 8 + Q, :] = proj_ref[:, INNER : INNER + XBC].astype(f32)
        tail_lanes = slice(INNER, XBC)
        c = conv_tile(buf, wc_ref, tail_lanes)
        act = c * sigmoid(c)
        keys = act[:, :STATE]
        queries = act[:, STATE:].astype(bf16)
        keys_t = keys.T.astype(bf16)
        scores = dot_nn(queries, keys_t)
        _, dt, cum = step_sizes(e_ref, par_ref)
        row_ref[...] = cum.T
        cum_ref[...] = cum
        dts_ref[...] = dt
        lower = row_iota((Q, Q)) >= lane_iota((Q, Q))
        low = lane_iota((Q, 128)) < HEADDIM
        scores = jnp.where(lower, scores, 0.0)

        def pair(p, cums, dts, at):
            lanes = pl.ds(pl.multiple_of(p * 128, 128), 128)
            c = conv_tile(buf, wc_ref, lanes)
            values = c * sigmoid(c)
            col0, col1 = head_column(cums, at), head_column(cums, at + 1)
            both = head_pair(cums, at)
            end = both[Q - 1 : Q, :]
            stepped = values * head_pair(dts, at)
            parts = split_pair(stepped.astype(bf16), low)
            mix = []
            for n, col in enumerate((col0, col1)):
                decay = jnp.exp2(jnp.minimum(col - row_ref[pl.ds(2 * p + n, 1), :], 0.0))
                mix.append((scores * decay).astype(bf16))
            y = dot_nn(jnp.concatenate(mix, axis=1), parts)
            before = state[:, lanes]
            before_low = before.astype(bf16)
            sin_ref[0, :, lanes] = before_low
            y = y + dot_nn(queries, before_low) * jnp.exp2(both)
            y = y + skip_ref[:, lanes] * values
            state[:, lanes] = before * jnp.exp2(end) + dot_nn(
                keys_t, (stepped * jnp.exp2(end - both)).astype(bf16)
            )
            z = proj_ref[:, lanes].astype(f32)
            gated = y * (z * sigmoid(z))
            y_ref[:, lanes] = y.astype(bf16)
            q_ref[:, lanes] = gated
            return gated * gated

        def body(i, squares):
            cums, dts = cum_ref[...], dts_ref[...]
            for n in range(unroll):
                squares = squares + pair(i * unroll + n, cums, dts, 2 * n)
            next_heads(cum_ref, cums, 2 * unroll)
            next_heads(dts_ref, dts, 2 * unroll)
            return squares

        squares = lax.fori_loop(0, PAIRS // unroll, body, jnp.zeros((Q, 128), f32))
        scale = lax.rsqrt(jnp.sum(squares, axis=-1, keepdims=True) / INNER + epsilon)

        def finish(p, _):
            lanes = pl.ds(pl.multiple_of(p * 128, 128), 128)
            out = q_ref[:, lanes] * scale * g_ref[:, lanes]
            o_ref[:, lanes] = out.astype(bf16)
            turned = out.T.astype(bf16)
            for n in range(128 // O_UNIT):
                there = pl.ds(unit_row(p * (128 // O_UNIT) + n, O_UNIT, 3), O_UNIT)
                ot_ref[there, :] = turned[n * O_UNIT : (n + 1) * O_UNIT, :]
            return 0

        lax.fori_loop(0, PAIRS, finish, 0, unroll=2)


def mixer(meta, proj, e, cot, wc, par, skip, g2):
    rows = proj.shape[0]
    chunks = rows // Q
    const = lambda k, m: (0, 0)
    live = lambda k, m: (last_live(m, k), 0)
    return pl.pallas_call(
        functools.partial(mixer_kernel, 2),
        out_shape=(
            jax.ShapeDtypeStruct((rows, INNER), bf16),
            jax.ShapeDtypeStruct((INNER, rows), bf16),
            jax.ShapeDtypeStruct((rows, INNER), bf16),
            jax.ShapeDtypeStruct((chunks, STATE, INNER), bf16),
            jax.ShapeDtypeStruct((rows, D), bf16),
        ),
        grid_spec=pltpu.PrefetchScalarGridSpec(
            num_scalar_prefetch=1,
            grid=(chunks,),
            in_specs=[
                pl.BlockSpec((Q, PROJ), live),
                pl.BlockSpec((Q, 128), live),
                pl.BlockSpec((Q, D), lambda k, m: (source_chunk(m, last_live(m, k), chunks // 2), 0)),
                pl.BlockSpec((8, XBC), const),
                pl.BlockSpec((8, 128), const),
                pl.BlockSpec((1, INNER), const),
                pl.BlockSpec((1, INNER), const),
            ],
            out_specs=[
                pl.BlockSpec((Q, INNER), lambda k, m: (last_padded(m, k), 0)),
                pl.BlockSpec((INNER, Q), lambda k, m: (0, last_padded(m, k))),
                pl.BlockSpec((Q, INNER), live),
                pl.BlockSpec((1, STATE, INNER), lambda k, m: (last_live(m, k), 0, 0)),
                pl.BlockSpec((Q, D), lambda k, m: (last_padded(m, k), 0)),
            ],
            scratch_shapes=[
                pltpu.VMEM((Q + 8, XBC), f32),
                pltpu.VMEM((STATE, INNER), f32),
                pltpu.VMEM((Q, 128), f32),
                pltpu.VMEM((Q, 128), f32),
                pltpu.VMEM((128, Q), f32),
                pltpu.VMEM((Q, INNER), f32),
            ],
        ),
        compiler_params=params(),
        cost_estimate=cost(chunks * PAIRS * 8 * 2 * Q * 128 * 128, 2 * rows * (PROJ + 3 * INNER)),
        name="mixer",
    )(meta, proj, e, cot, wc, par, skip, g2)


def gate_kernel(
    slot_chunks, meta, u_ref, err_ref, w_ref, o_ref, y_ref, z_ref, g_ref,
    out_ref, dy_ref, dz_ref, gi_ref,
    do_ref,
):
    b = pl.program_id(0)
    total = meta[0]

    @pl.when(b == 0)
    def _():
        out_ref[...] = jnp.zeros_like(out_ref)
        gi_ref[...] = jnp.zeros_like(gi_ref)

    def body(rows):
        halves = rows // Q
        if halves == 1:
            dz_ref[Q:, :] = jnp.zeros((Q, INNER), bf16)
        starts = []
        for n in range(halves):
            k = 2 * b + n
            start = pl.multiple_of(source_chunk(meta, k, slot_chunks) * Q, Q)
            starts.append(start)
        branch = dot_nn(o_ref[0:rows, :], w_ref[...])
        for n in range(halves):
            live = row_iota((Q, D)) < live_rows(meta, 2 * b + n)
            here = pl.ds(starts[n], Q)
            value = u_ref[here, :].astype(f32) + branch[n * Q : (n + 1) * Q, :]
            out_ref[here, :] = jnp.where(live, value, 0.0).astype(bf16)
        do_ref[0:rows, :] = dot_nt(err_ref[0:rows, :], w_ref[...])

        def sums(p, carry):
            squares, crossed = carry
            lanes = pl.ds(pl.multiple_of(p * 128, 128), 128)
            z = z_ref[0:rows, lanes].astype(f32)
            q = y_ref[0:rows, lanes].astype(f32) * (z * sigmoid(z))
            return squares + q * q, crossed + q * g_ref[:, lanes] * do_ref[0:rows, lanes]

        zero = jnp.zeros((rows, 128), f32)
        squares, crossed = lax.fori_loop(0, PAIRS, sums, (zero, zero), unroll=2)
        scale = lax.rsqrt(jnp.sum(squares, axis=-1, keepdims=True) / INNER + epsilon)
        factor = scale * scale * scale * (jnp.sum(crossed, axis=-1, keepdims=True) / INNER)

        def back(p, _):
            lanes = pl.ds(pl.multiple_of(p * 128, 128), 128)
            z = z_ref[0:rows, lanes].astype(f32)
            y = y_ref[0:rows, lanes].astype(f32)
            s = sigmoid(z)
            gate = z * s
            q = y * gate
            do = do_ref[0:rows, lanes]
            gi_ref[:, lanes] += jnp.sum(do * q * scale, axis=0, keepdims=True)
            dq = scale * (g_ref[:, lanes] * do) - q * factor
            dy_ref[0:rows, lanes] = (dq * gate).astype(bf16)
            dz_ref[0:rows, lanes] = (dq * y * (s * (1.0 + z * (1.0 - s)))).astype(bf16)
            return 0

        lax.fori_loop(0, PAIRS, back, 0, unroll=2)

    pl.when(total >= 2 * b + 2)(functools.partial(body, 2 * Q))
    pl.when(total == 2 * b + 1)(functools.partial(body, Q))


def last_block(m, b):
    return jnp.minimum(b, (m[0] + 1) // 2 - 1)


def gate(meta, u, err, w2, o, y, proj, g2):
    rows = u.shape[0]
    blocks = rows // (2 * Q)
    const = lambda b, m: (0, 0)
    live = lambda b, m: (last_block(m, b), 0)
    once = pl.Buffered(1)
    return pl.pallas_call(
        functools.partial(gate_kernel, rows // Q // 2),
        out_shape=(
            jax.ShapeDtypeStruct((rows, D), bf16),
            jax.ShapeDtypeStruct((rows, INNER), bf16),
            jax.ShapeDtypeStruct((rows, INNER), bf16),
            jax.ShapeDtypeStruct((1, INNER), f32),
        ),
        grid_spec=pltpu.PrefetchScalarGridSpec(
            num_scalar_prefetch=1,
            grid=(blocks,),
            in_specs=[
                pl.BlockSpec((rows, D), const, pipeline_mode=once),
                pl.BlockSpec((2 * Q, D), live),
                pl.BlockSpec((INNER, D), const, pipeline_mode=once),
                pl.BlockSpec((2 * Q, INNER), live),
                pl.BlockSpec((2 * Q, INNER), live),
                pl.BlockSpec((2 * Q, INNER), live),
                pl.BlockSpec((1, INNER), const),
            ],
            out_specs=[
                pl.BlockSpec((rows, D), const),
                pl.BlockSpec((2 * Q, INNER), live),
                pl.BlockSpec((2 * Q, INNER), live),
                pl.BlockSpec((1, INNER), const),
            ],
            scratch_shapes=[pltpu.VMEM((2 * Q, INNER), f32)],
        ),
        compiler_params=params(),
        cost_estimate=cost(4 * rows * D * INNER, 2 * (D * INNER + 5 * rows * INNER)),
        name="gate",
    )(meta, u, err, w2, o, y, proj, g2)


def back_kernel(
    unroll, part, parts, meta, x_ref, prev_ref, e_ref, dy_ref, sin_ref, wc_ref, par_ref, skip_ref, *rest
):
    carried, rest = (rest[:6], rest[6:]) if part > 0 else ((), rest)
    dx_ref, gconv_ref, gpar_ref, gskip_ref = rest[:4]
    passed_on, rest = (rest[4:6], rest[6:]) if part < parts - 1 else ((), rest[4:])
    buf, dbuf, dstate, cum_ref, dts_ref, row_ref, da_ref = rest
    i = pl.program_id(0)
    total = meta[0]
    begin, end = part_span(meta, part, parts)
    k = total - begin - i

    @pl.when(i == 0)
    def _():
        da_ref[...] = jnp.zeros_like(da_ref)
        if part == 0:
            gconv_ref[...] = jnp.zeros_like(gconv_ref)
            gpar_ref[...] = jnp.zeros_like(gpar_ref)
            gskip_ref[...] = jnp.zeros_like(gskip_ref)

            @pl.when(lax.rem(total, 2) == 1)
            def _():
                dx_ref[...] = jnp.zeros_like(dx_ref)

        else:
            for to, came in zip((gconv_ref, gpar_ref, gskip_ref, dstate), carried[1:5]):
                to[...] = came[...]
            dbuf[0:8, :] = carried[5][...]

    @pl.when((i >= 1) & (i <= end - begin))
    def _():
        first = (k == 0) | (k == meta[1])
        last = (k == total - 1) | (k == meta[1] - 1)

        @pl.when(first)
        def _():
            buf[0:8, :] = jnp.zeros((8, XBC), f32)

        @pl.when(jnp.logical_not(first))
        def _():
            buf[0:8, :] = prev_ref[8:16, INNER : INNER + XBC].astype(f32)

        @pl.when(last)
        def _():
            dbuf[Q : Q + 8, :] = jnp.zeros((8, XBC), f32)
            dstate[...] = jnp.zeros_like(dstate)

        @pl.when(jnp.logical_not(last))
        def _():
            dbuf[Q : Q + 8, :] = dbuf[0:8, :]

        buf[8 : 8 + Q, :] = x_ref[:, INNER : INNER + XBC].astype(f32)
        tail_lanes = slice(INNER, XBC)
        c_tail = conv_tile(buf, wc_ref, tail_lanes)
        s_tail = sigmoid(c_tail)
        act = c_tail * s_tail
        keys = act[:, :STATE].astype(bf16)
        queries = act[:, STATE:].astype(bf16)
        queries_t = act[:, STATE:].T.astype(bf16)
        scores = dot_nn(keys, queries_t)
        raw, dt, cum = step_sizes(e_ref, par_ref)
        row_ref[...] = cum.T
        cum_ref[...] = cum
        dts_ref[...] = dt
        upper = row_iota((Q, Q)) <= lane_iota((Q, Q))
        strict = row_iota((Q, Q)) < lane_iota((Q, Q))
        after = (row_iota((Q, Q)) >= lane_iota((Q, Q))).astype(bf16)
        low = lane_iota((Q, 128)) < HEADDIM
        scores = jnp.where(upper, scores, 0.0)
        half = (lax.broadcasted_iota(jnp.int32, (128, 128), 0) >= HEADDIM).astype(jnp.int32)
        head_lane = lane_iota((128, 128))

        def conv_back(lanes, dc):
            dbuf[0:Q, lanes] = dc
            dxbc = wc_ref[CONV - 1 : CONV, lanes] * dc
            for tap in range(CONV - 1):
                dxbc = dxbc + wc_ref[tap : tap + 1, lanes] * dbuf[3 - tap : 3 - tap + Q, lanes]
            dx_ref[:, lanes] = dxbc.astype(bf16)
            for tap in range(CONV):
                gconv_ref[tap : tap + 1, lanes] += jnp.sum(dc * buf[5 + tap : 5 + tap + Q, lanes], axis=0, keepdims=True)
            gconv_ref[CONV : CONV + 1, lanes] += jnp.sum(dc, axis=0, keepdims=True)

        def pair(p, cums, dts, at, carry):
            dscores, dquery, dkey, from_start, to_end, direct, thru = carry
            lanes = pl.ds(pl.multiple_of(p * 128, 128), 128)
            c = conv_tile(buf, wc_ref, lanes)
            s = sigmoid(c)
            values = c * s
            col0, col1 = head_column(cums, at), head_column(cums, at + 1)
            both = head_pair(cums, at)
            end = both[Q - 1 : Q, :]
            grown = jnp.exp2(both)
            rest = jnp.exp2(end - both)
            dtp = head_pair(dts, at)
            stepped = values * dtp
            dy_low = dy_ref[:, lanes]
            dy = dy_low.astype(f32)
            parts = split_pair(dy_low, low)
            stepped_low = stepped.astype(bf16)
            dmix = dot_nt(stepped_low, parts)
            mix = []
            for n, col in enumerate((col0, col1)):
                decay = jnp.exp2(jnp.minimum(row_ref[pl.ds(2 * p + n, 1), :] - col, 0.0))
                weighted = dmix[:, n * Q : (n + 1) * Q] * decay
                dscores = dscores + weighted
                mix.append((scores * decay).astype(bf16))
                passed = dot_nn((weighted * scores).astype(bf16), after)
                da_ref[pl.ds(2 * p + n, 1), :] = jnp.sum(jnp.where(strict, passed, 0.0), axis=0, keepdims=True)
            dstepped = dot_nn(jnp.concatenate(mix, axis=1), parts)
            dafter = dstate[:, lanes]
            dafter_low = dafter.astype(bf16)
            before_low = sin_ref[0, :, lanes]
            dend = dot_nn(keys, dafter_low) * rest
            grown_dy = (dy * grown).astype(bf16)
            select = (head_lane == 2 * p + half).astype(bf16)
            across = dot_nn(queries, before_low)
            from_start = from_start + dot_nn((across * grown * dy).astype(bf16), select)
            to_end = to_end + dot_nn((stepped * dend).astype(bf16), select)
            dstepped = dstepped + dend
            direct = direct + dot_nn((values * dstepped).astype(bf16), select)
            dquery = dquery + dot_nt(grown_dy, before_low)
            dkey = dkey + dot_nt((stepped * rest).astype(bf16), dafter_low)
            kept = jnp.exp2(end) * dafter
            held = jnp.sum((kept * before_low.astype(f32)).reshape(8, 16, 128), axis=0)
            thru = thru + dot_nn(held.astype(bf16), select)
            dstate[:, lanes] = kept + dot_nn(queries_t, grown_dy)
            dvalues = dstepped * dtp + skip_ref[:, lanes] * dy
            gskip_ref[:, lanes] += jnp.sum(dy * values, axis=0, keepdims=True)
            conv_back(lanes, dvalues * (s * (1.0 + c * (1.0 - s))))
            return dscores, dquery, dkey, from_start, to_end, direct, thru

        def body(n, carry):
            cums, dts = cum_ref[...], dts_ref[...]
            for m in range(unroll):
                carry = pair(n * unroll + m, cums, dts, 2 * m, carry)
            next_heads(cum_ref, cums, 2 * unroll)
            next_heads(dts_ref, dts, 2 * unroll)
            return carry

        zero = jnp.zeros((Q, 128), f32)
        start = (zero,) * 6 + (jnp.zeros((16, 128), f32),)
        carry = lax.fori_loop(0, PAIRS // unroll, body, start)
        dscores, dquery, dkey, from_start, to_end, direct, thru = carry
        dscores = jnp.where(upper, dscores, 0.0)
        dkey = dkey + dot_nn(dscores.astype(bf16), queries)
        dquery = dquery + dot_nn(dscores.T.astype(bf16), keys)
        slope = s_tail * (1.0 + c_tail * (1.0 - s_tail))
        conv_back(slice(INNER, INNER + STATE), dkey * slope[:, :STATE])
        conv_back(slice(INNER + STATE, XBC), dquery * slope[:, STATE:])

        tail_sum = (row_iota((Q, Q)) <= lane_iota((Q, Q))).astype(f32)
        head_sum = (row_iota((Q, Q)) > lane_iota((Q, Q))).astype(f32)
        da = (
            da_ref[...].T
            + dot_nn(tail_sum, from_start, precision=lax.Precision.HIGHEST)
            + dot_nn(head_sum, to_end, precision=lax.Precision.HIGHEST)
            + jnp.sum(thru, axis=0, keepdims=True)
        )
        ddt = par_ref[1:2, :] * da + direct
        de = ddt * sigmoid(raw)
        de = jnp.where(lane_iota((Q, 128)) < HEADS, de, 0.0)
        dx_ref[:, XBC:] = de.astype(bf16)
        gpar_ref[0:1, :] += jnp.sum(de, axis=0, keepdims=True)
        gpar_ref[1:2, :] += jnp.sum(dt * da, axis=0, keepdims=True)

    if passed_on:

        @pl.when(i == pl.num_programs(0) - 1)
        def _():
            passed_on[0][...] = dstate[...]
            passed_on[1][...] = dbuf[0:8, :]


def part_span(meta, part, parts):
    return (meta[0] * part + parts - 1) // parts, (meta[0] * (part + 1) + parts - 1) // parts


def back(meta, part, parts, carried, proj, e, dy, sin, wc, par, skip):
    rows = proj.shape[0]
    chunks = rows // Q
    const = lambda i, m: (0, 0)

    def chunk(i, m):
        begin, end = part_span(m, part, parts)
        return jnp.clip(m[0] - begin - jnp.clip(i, 1, jnp.maximum(end - begin, 1)), 0, m[0] - 1)

    def written(i, m):
        begin, end = part_span(m, part, parts)
        block = jnp.where(end > begin, chunk(i, m), chunks)
        return jnp.where(i == 0, last_padded(m, m[0]), block) if part == 0 else block

    here = lambda i, m: (chunk(i, m), 0)
    out_shape = [
        jax.ShapeDtypeStruct((rows + Q, XE), bf16),
        jax.ShapeDtypeStruct((8, XBC), f32),
        jax.ShapeDtypeStruct((8, 128), f32),
        jax.ShapeDtypeStruct((1, INNER), f32),
    ]
    sums = [pl.BlockSpec((8, XBC), const), pl.BlockSpec((8, 128), const), pl.BlockSpec((1, INNER), const)]
    state = [pl.BlockSpec((STATE, INNER), const), pl.BlockSpec((8, XBC), const)]
    in_specs = [
        pl.BlockSpec((Q, PROJ), here),
        pl.BlockSpec((16, PROJ), lambda i, m: (jnp.maximum(chunk(i, m) * (Q // 16) - 1, 0), 0)),
        pl.BlockSpec((Q, 128), here),
        pl.BlockSpec((Q, INNER), here),
        pl.BlockSpec((1, STATE, INNER), lambda i, m: (chunk(i, m), 0, 0)),
        pl.BlockSpec((8, XBC), const),
        pl.BlockSpec((8, 128), const),
        pl.BlockSpec((1, INNER), const),
    ]
    out_specs = [pl.BlockSpec((Q, XE), lambda i, m: (written(i, m), 0))] + sums
    if part > 0:
        in_specs += [pl.BlockSpec(memory_space=pl.ANY)] + sums + state
    if part < parts - 1:
        out_shape += [jax.ShapeDtypeStruct((STATE, INNER), f32), jax.ShapeDtypeStruct((8, XBC), f32)]
        out_specs += state
    steps = -(-chunks // parts)
    return pl.pallas_call(
        functools.partial(back_kernel, 2, part, parts),
        out_shape=out_shape,
        grid_spec=pltpu.PrefetchScalarGridSpec(
            num_scalar_prefetch=1,
            grid=(steps + 1,),
            in_specs=in_specs,
            out_specs=out_specs,
            scratch_shapes=[
                pltpu.VMEM((Q + 8, XBC), f32),
                pltpu.VMEM((Q + 8, XBC), f32),
                pltpu.VMEM((STATE, INNER), f32),
                pltpu.VMEM((Q, 128), f32),
                pltpu.VMEM((Q, 128), f32),
                pltpu.VMEM((128, Q), f32),
                pltpu.VMEM((128, Q), f32),
            ],
        ),
        input_output_aliases={9: 0} if part > 0 else {},
        compiler_params=params(),
        cost_estimate=cost(steps * PAIRS * 20 * 2 * Q * 128 * 128, 2 * steps * Q * (PROJ + 3 * INNER)),
        name="back",
    )(meta, proj, proj, e, dy, sin, wc, par, skip, *carried)


def weight_kernel(rows, swap_from, meta, at_ref, b_ref, mine_ref, other_ref):
    used = (meta[0] + 1) // 2
    half = at_ref.shape[0] // 2
    part_rows = half // 4
    swap = pl.program_id(0) >= swap_from

    def part(width):
        for c, out_ref in enumerate((mine_ref, other_ref)):

            def step(m, _):
                here = pl.ds(pl.multiple_of(c * half + 2 * m * part_rows, part_rows), 2 * part_rows)
                res = dot_nn(at_ref[here, 0:width], b_ref[0:width, :]).astype(bf16)
                for n in range(2):
                    place = jnp.where(swap, 2 * n + m, 2 * m + n)
                    there = pl.ds(pl.multiple_of(place * part_rows, part_rows), part_rows)
                    out_ref[there, :] = res[n * part_rows : (n + 1) * part_rows, :]
                return 0

            lax.fori_loop(0, 2, step, 0)

    for n in range(1, rows // (2 * Q) + 1):
        pl.when(used == n)(functools.partial(part, n * 2 * Q))


def weight_grad(meta, at, b, first, width, tile, swap_from):
    height, rows = at.shape
    offset = first // tile
    half = jax.ShapeDtypeStruct((height // 2, width), bf16)
    half_spec = pl.BlockSpec((height // 2, tile), lambda j, m: (0, j))
    return pl.pallas_call(
        functools.partial(weight_kernel, rows, swap_from),
        out_shape=(half, half),
        grid_spec=pltpu.PrefetchScalarGridSpec(
            num_scalar_prefetch=1,
            grid=(pl.cdiv(width, tile),),
            in_specs=[
                pl.BlockSpec((height, rows), lambda j, m: (0, 0)),
                pl.BlockSpec((rows, tile), lambda j, m: (0, j + offset)),
            ],
            out_specs=(half_spec, half_spec),
        ),
        compiler_params=params(),
        cost_estimate=cost(2 * rows * height * width, 2 * (rows * (height + width) + height * width)),
        name="weight_grad",
    )(meta, at, b)


def input_kernel(
    slot_chunks, steps, tile, meta, u_ref, err_ref, g_ref, dz_ref, dx_ref, w_ref, out0_ref, out1_ref, gn_ref, dh_ref
):
    j = pl.program_id(0)
    total = meta[0]
    chunks = 2 * slot_chunks
    last = w_ref[:, INNER + XBC : PROJ]
    cols = pl.ds(pl.multiple_of(j * tile, tile), tile)

    def live(rows):
        dh_ref[0:rows, cols] = (
            dot_nt(dz_ref[0:rows, :], w_ref[:, 0:INNER])
            + dot_nt(dx_ref[0:rows, 0:XBC], w_ref[:, INNER : INNER + XBC])
            + dot_nt(dx_ref[0:rows, XBC : XBC + HEADS], last)
        )

    for_live(total, chunks, live)

    @pl.when(j == steps - 1)
    def _():
        out0_ref[...] = jnp.zeros_like(out0_ref)
        out1_ref[...] = jnp.zeros_like(out1_ref)
        gn_ref[...] = jnp.zeros_like(gn_ref)
        for k in range(chunks):

            @pl.when(k < total)
            def _():
                start = pl.multiple_of(source_chunk(meta, k, slot_chunks) * Q, Q)
                u = u_ref[pl.ds(start, Q), :].astype(f32)
                err = err_ref[k * Q : (k + 1) * Q, :].astype(f32)
                scale = lax.rsqrt(jnp.mean(u * u, axis=-1, keepdims=True) + epsilon)
                dh = dh_ref[k * Q : (k + 1) * Q, :]
                gn_ref[...] += jnp.sum(dh * (u * scale), axis=0, keepdims=True)
                n = dh * g_ref[...]
                inner = jnp.mean(u * n, axis=-1, keepdims=True)
                du = (err + scale * n - u * (scale * scale * scale * inner)).astype(bf16)

                @pl.when(k < meta[1])
                def _():
                    out0_ref[pl.ds(start, Q), :] = du

                @pl.when(k >= meta[1])
                def _():
                    out1_ref[pl.ds(pl.multiple_of(start - slot_chunks * Q, Q), Q), :] = du


def input_grad_of(meta, u, err, g1, dz, dx, w1):
    rows = u.shape[0]
    tile = 256
    steps = D // tile
    const = lambda j, m: (0, 0)
    once = pl.Buffered(1)
    return pl.pallas_call(
        functools.partial(input_kernel, rows // Q // 2, steps, tile),
        out_shape=(
            jax.ShapeDtypeStruct((rows // 2, D), bf16),
            jax.ShapeDtypeStruct((rows // 2, D), bf16),
            jax.ShapeDtypeStruct((1, D), f32),
        ),
        grid_spec=pltpu.PrefetchScalarGridSpec(
            num_scalar_prefetch=1,
            grid=(steps,),
            in_specs=[
                pl.BlockSpec((rows, D), const, pipeline_mode=once),
                pl.BlockSpec((rows, D), const, pipeline_mode=once),
                pl.BlockSpec((1, D), const),
                pl.BlockSpec((rows, INNER), const, pipeline_mode=once),
                pl.BlockSpec((rows, XE), const, pipeline_mode=once),
                pl.BlockSpec((tile, w1.shape[1]), lambda j, m: (j, 0)),
            ],
            out_specs=[
                pl.BlockSpec((rows // 2, D), const),
                pl.BlockSpec((rows // 2, D), const),
                pl.BlockSpec((1, D), const),
            ],
            scratch_shapes=[pltpu.VMEM((rows, D), f32)],
        ),
        compiler_params=params(),
        cost_estimate=cost(2 * rows * D * PROJ, 2 * (D * PROJ + rows * PROJ)),
        name="input_grad",
    )(meta, u, err, g1, dz, dx, w1)


def partner(value, axis, bit):
    mask = 2**bit
    pairs = [(source, source ^ mask) for source in range(lax.axis_size(axis))]
    return lax.ppermute(value, axis, pairs)


def log2(size):
    return size.bit_length() - 1


def halving_order(swap):
    fsdp = [("fsdp", bit) for bit in range(log2(lax.axis_size("fsdp")))]
    near = [("dp", 1)]
    far = [("dp", bit) for bit in range(2, log2(lax.axis_size("dp")))]
    return [("dp", 0)] + (near + fsdp if swap else fsdp + near) + far


def flat_bit(axis, bit):
    return bit + (log2(lax.axis_size("fsdp")) if axis == "dp" else 0)


def kept_at(order, owner):
    away = owner ^ lax.axis_index(AXES)
    place = jnp.zeros_like(away)
    for axis, bit in order:
        place = 2 * place + ((away >> flat_bit(axis, bit)) & 1)
    return place


def owner_at(order, place):
    away = jnp.zeros_like(place)
    for n, (axis, bit) in enumerate(order):
        away = away + (((place >> (len(order) - 1 - n)) & 1) << flat_bit(axis, bit))
    return away ^ lax.axis_index(AXES)


class Term:
    def __init__(self, value):
        self.value = value


class Columns:
    def __init__(self, width, swap):
        self.order = halving_order(swap)
        self.width = width
        self.terms = []
        self.phase = 0

    def done(self):
        return self.phase == len(self.order)

    def sum(self, start, stop):
        return sum(term.value[start:stop, at : at + self.width].astype(f32) for term, at in self.terms)

    def halve(self):
        self.rows //= 2
        return self.sum(self.rows, 2 * self.rows).astype(bf16)


class Chain:
    def __init__(self, halves, columns, grouped):
        mine, other = halves
        self.columns = columns
        if not grouped:
            count = lax.axis_size(AXES)
            whole = jnp.concatenate([mine, other]).reshape(count, -1, mine.shape[1])
            parts = []
            at = 0
            for c in columns:
                parts.append(whole[:, :, at : at + c.width][owner_at(c.order, jnp.arange(count))])
                at += c.width
            mine, other = jnp.concatenate(parts, axis=2).reshape(2, -1, mine.shape[1])
        self.going = [(columns, other)]
        kept = Term(mine)
        at = 0
        for c in columns:
            c.rows = mine.shape[0]
            c.terms.append((kept, at))
            at += c.width

    def halve(self):
        groups = {}
        for c in self.columns:
            if not c.done() and all(c not in members for members, _ in self.going):
                groups.setdefault((c.order[c.phase], c.rows), []).append(c)
        for members in groups.values():
            sent = [c.halve() for c in members]
            self.going.append((members, jnp.concatenate(sent, axis=1) if len(sent) > 1 else sent[0]))

    def exchange(self):
        for members, sent in self.going:
            first = members[0]
            came = Term(partner(sent, *first.order[first.phase]))
            at = 0
            for c in members:
                c.terms.append((came, at))
                c.phase += 1
                at += c.width
        self.going = []

    def finish(self):
        while not all(c.done() for c in self.columns):
            self.halve()
            self.exchange()
        return [c.sum(0, c.rows) for c in self.columns]


def tick(token, chains, after):
    last = {id(c.terms[-1][0]): c.terms[-1][0] for chain in chains for c in chain.columns if c.phase > 0}
    if last:
        *came, _ = lax.optimization_barrier([term.value for term in last.values()] + [after])
        for term, value in zip(last.values(), came):
            term.value = value
    for chain in chains:
        chain.halve()
    sent = [value for chain in chains for _, value in chain.going]
    *sent, token = lax.optimization_barrier(sent + [token])
    for chain in chains:
        chain.going = [(members, sent.pop(0)) for members, _ in chain.going]
        chain.exchange()
    return token


W_COLS = 6528
W_SPANS = ((0, 2944), (2944, 2944), (5888, 640))


def gather_kernel(
    count, inner, flag_ref, own_ref, norm_ref, conv_ref, bias_ref, inner_ref, tokens_ref,
    w_ref, wc_ref, g1_ref, g2_ref, u_ref,
    shard_ref, tile_ref, tiles_ref, kept, given,
    send_sem, recv_sem, tile_send, tile_recv, own_sem, give_send, give_recv,
):
    me = lax.axis_index("dp") * inner + lax.axis_index("fsdp")
    height = shard_ref.shape[0]
    x, core, y = flat_bit("fsdp", 0), flat_bit("dp", 0), flat_bit("dp", 1)
    far = [flat_bit("dp", bit) for bit in range(2, log2(lax.axis_size("dp")))]
    ways = (far + [y, x, core], far + [x, y, core], [x, y] + far[::-1] + [core])
    spans = [pl.ds(at, width) for at, width in W_SPANS]
    groups = range(len(spans))

    full = PROJ // 128 * 128
    shard_ref[:, 0:full] = own_ref[:, 0:full].astype(bf16)
    shard_ref[:, full:] = jnp.zeros((height, W_COLS - full), bf16)
    shard_ref[:, full:PROJ] = own_ref[:, full:].astype(bf16)
    tile_ref[...] = jnp.zeros_like(tile_ref)
    for row, ref in ((0, conv_ref), (4, bias_ref), (5, inner_ref), (6, norm_ref)):
        tile_ref[row : row + ref.shape[0], 0 : ref.shape[1]] = ref[...].astype(bf16).astype(f32)

    def place(away):
        return pl.ds(pl.multiple_of(jnp.bitwise_xor(me, away) * height, height), height)

    def link(bit):
        other = jnp.bitwise_xor(me, 2**bit)
        return (other // inner, other % inner)

    def last_step(half, away):
        return max((n for n, bit in enumerate(ways[half]) if (away >> bit) & 1), default=-1)

    def send(half, away, bit):
        src = shard_ref.at[:, spans[half]] if away == 0 else w_ref.at[place(away), spans[half]]
        return pltpu.make_async_remote_copy(
            src_ref=src,
            dst_ref=w_ref.at[place(away), spans[half]],
            send_sem=send_sem.at[half, away ^ 2**bit],
            recv_sem=recv_sem.at[half, away ^ 2**bit],
            device_id=link(bit),
            device_id_type=pl.DeviceIdType.MESH,
        )

    def receive(half, away):
        block = w_ref.at[place(away), spans[half]]
        return pltpu.make_async_remote_copy(
            src_ref=block,
            dst_ref=block,
            send_sem=send_sem.at[half, away],
            recv_sem=recv_sem.at[half, away],
            device_id=link(ways[half][last_step(half, away)]),
            device_id_type=pl.DeviceIdType.MESH,
        )

    def send_on(half, away):
        sends = [send(half, away, bit) for bit in ways[half][last_step(half, away) + 1 :]]
        for one in sends:
            one.start()
        return sends

    def tile_copy(n):
        other = jnp.bitwise_xor(me, n)
        return pltpu.make_async_remote_copy(
            src_ref=tile_ref,
            dst_ref=tiles_ref.at[me],
            send_sem=tile_send.at[n],
            recv_sem=tile_recv.at[n],
            device_id=(other // inner, other % inner),
            device_id_type=pl.DeviceIdType.MESH,
        )

    def start_tile(n, _):
        tile_copy(n).start()
        return 0

    def wait_tile(n, _):
        tile_copy(n).wait()
        return 0

    started = []
    for step in range(len(ways[0])):
        for half in groups:
            one = send(half, 0, ways[half][step])
            one.start()
            started.append(one)
    own = pltpu.make_async_copy(shard_ref, w_ref.at[place(0), :], own_sem.at[0])
    own.start()

    second = jnp.broadcast_to(flag_ref[0, 0], (1, D)) == 1
    rows = kept.shape[0]

    def choose(n, _):
        r = pl.ds(pl.multiple_of(n * 64, 64), 64)
        zero, one = tokens_ref[0, r, :].astype(f32), tokens_ref[1, r, :].astype(f32)
        kept[r, :] = jnp.where(second, one, zero).astype(bf16)
        given[r, :] = jnp.where(second, zero, one).astype(bf16)
        return 0

    lax.fori_loop(0, rows // 64, choose, 0)
    lax.fori_loop(1, count, start_tile, 0)
    tiles_ref[me] = tile_ref[...]

    blocks = [(half, away) for half in groups for away in range(1, count)]
    blocks.sort(key=lambda b: (b[1].bit_count(), last_step(*b), b[0]))
    tail = []
    for n, (half, away) in enumerate(blocks):
        receive(half, away).wait_recv()
        started += send_on(half, away)
        if n == 8:
            keep = pltpu.make_async_copy(kept, u_ref.at[pl.ds(0, rows), :], own_sem.at[1])
            give = pltpu.make_async_remote_copy(
                src_ref=given,
                dst_ref=u_ref.at[pl.ds(rows, rows), :],
                send_sem=give_send,
                recv_sem=give_recv,
                device_id=link(core),
                device_id_type=pl.DeviceIdType.MESH,
            )
            keep.start()
            give.start()
            tail = [keep, give]
        if n == 40:
            lax.fori_loop(1, count, wait_tile, 0)
            wc_ref[...] = jnp.zeros_like(wc_ref)
            for owner in range(count):
                for ref, row, tall in ((wc_ref, 0, 5), (g2_ref, 5, 1), (g1_ref, 6, 1)):
                    each = ref.shape[1] // count
                    ref[0:tall, owner * each : (owner + 1) * each] = tiles_ref[owner, row : row + tall, 0:each]
    for one in started:
        one.wait_send()
    for one in tail:
        one.wait()
    own.wait()


def gather(flag, own, norm, conv, bias, inner, tokens):
    count = lax.axis_size(AXES)
    slot = tokens.shape[1]
    whole = pl.BlockSpec(memory_space=pltpu.VMEM)
    anywhere = pl.BlockSpec(memory_space=pl.ANY)
    dma = pltpu.SemaphoreType.DMA
    return pl.pallas_call(
        functools.partial(gather_kernel, count, lax.axis_size("fsdp")),
        out_shape=(
            jax.ShapeDtypeStruct((D, W_COLS), bf16),
            jax.ShapeDtypeStruct((8, XBC), f32),
            jax.ShapeDtypeStruct((1, D), f32),
            jax.ShapeDtypeStruct((1, INNER), f32),
            jax.ShapeDtypeStruct((2 * slot, D), bf16),
        ),
        in_specs=[pl.BlockSpec(memory_space=pltpu.SMEM)] + [whole] * 6,
        out_specs=(anywhere, whole, whole, whole, anywhere),
        scratch_shapes=[
            pltpu.VMEM((own.shape[0], W_COLS), bf16),
            pltpu.VMEM((8, 128), f32),
            pltpu.VMEM((count, 8, 128), f32),
            pltpu.VMEM((slot, D), bf16),
            pltpu.VMEM((slot, D), bf16),
            dma((len(W_SPANS), count)),
            dma((len(W_SPANS), count)),
            dma((count,)),
            dma((count,)),
            dma((2,)),
            dma,
            dma,
        ],
        compiler_params=params(has_side_effects=True),
        cost_estimate=cost(1e6, 2 * D * W_COLS),
        name="gather",
    )(flag, own, norm, conv, bias, inner, tokens)


def sum_kernel(count, inner, sent_ref, out_ref, came, send_sem, recv_sem):
    me = lax.axis_index("dp") * inner + lax.axis_index("fsdp")

    def copy(n):
        other = jnp.bitwise_xor(me, n)
        return pltpu.make_async_remote_copy(
            src_ref=sent_ref.at[other],
            dst_ref=came.at[n],
            send_sem=send_sem.at[n],
            recv_sem=recv_sem.at[n],
            device_id=(other // inner, other % inner),
            device_id_type=pl.DeviceIdType.MESH,
        )

    def start(n, _):
        copy(n).start()
        return 0

    def add(n, total):
        copy(n).wait()
        return total + came[n]

    lax.fori_loop(1, count, start, 0)
    out_ref[...] = lax.fori_loop(1, count, add, sent_ref[me])


def sum_small(tiles):
    count = tiles.shape[0]
    whole = pl.BlockSpec(memory_space=pltpu.VMEM)
    return pl.pallas_call(
        functools.partial(sum_kernel, count, lax.axis_size("fsdp")),
        out_shape=jax.ShapeDtypeStruct(tiles.shape[1:], f32),
        in_specs=[whole],
        out_specs=whole,
        scratch_shapes=[
            pltpu.VMEM(tiles.shape, f32),
            pltpu.SemaphoreType.DMA((count,)),
            pltpu.SemaphoreType.DMA((count,)),
        ],
        compiler_params=pltpu.CompilerParams(has_side_effects=True),
        cost_estimate=cost(count * 1024, 8 * count * 1024),
        name="sum_small",
    )(tiles)


TILE_ROWS = 16
X_CUT = 1792
X_PIECES = tuple((which, 512 * n, width) for n in range(4) for which, width in ((0, 512 if n < 3 else 256), (1, 512 if n < 3 else 128)))


def finish_kernel(
    count, inner, m0, a0, b0, m1, a1, b1, gconv_ref, gpar_ref, par_ref, gskip_ref, gi_ref, gn_ref, given_ref,
    x_ref, tile_ref, back_ref, *scratch,
):
    sources = ((m0, a0, b0), (m1, a1, b1))
    terms, scratch = scratch[:2], scratch[2:]
    sent, scratch = [scratch[2 * n : 2 * n + 2] for n in range(3)], scratch[6:]
    came, scratch = [scratch[2 * n : 2 * n + 2] for n in range(3)], scratch[6:]
    tiles, tiles_in, load_sem, send_sem, recv_sem, tile_send, tile_recv, give_send, give_recv = scratch
    me = lax.axis_index("dp") * inner + lax.axis_index("fsdp")
    far = [flat_bit("dp", bit) for bit in (2, 3)]
    ways = ([flat_bit("dp", 1)] + far, [flat_bit("fsdp", 0)] + far)
    tall = terms[0].shape[1]

    def target(other):
        return {"device_id": (other // inner, other % inner), "device_id_type": pl.DeviceIdType.MESH}

    def load(n):
        which, at, width = X_PIECES[n]
        cols = pl.ds(at, width)
        return [
            pltpu.make_async_copy(ref.at[pl.ds(0, tall), cols], terms[which].at[i, :, cols], load_sem.at[n, i])
            for i, ref in enumerate(sources[which])
        ]

    def copy(n, phase):
        which, at, width = X_PIECES[n]
        cols = pl.ds(at, width)
        return pltpu.make_async_remote_copy(
            src_ref=sent[phase][which].at[:, cols],
            dst_ref=came[phase][which].at[:, cols],
            send_sem=send_sem.at[n, phase],
            recv_sem=recv_sem.at[n, phase],
            **target(jnp.bitwise_xor(me, 2 ** ways[which][phase])),
        )

    def total(n, phase, start, rows):
        which, at, width = X_PIECES[n]
        parts = [terms[which][i, start : start + rows, at : at + width] for i in range(3)]
        parts += [came[p][which][start : start + rows, at : at + width] for p in range(phase)]
        return sum(part.astype(f32) for part in parts)

    def go(n, phase):
        which, at, width = X_PIECES[n]
        rows = tall >> (phase + 1)
        sent[phase][which][:, at : at + width] = total(n, phase, rows, rows).astype(bf16)
        copy(n, phase).start()

    def tile_copy(n):
        other = jnp.bitwise_xor(me, n)
        return pltpu.make_async_remote_copy(
            src_ref=tiles.at[other],
            dst_ref=tiles_in.at[n],
            send_sem=tile_send.at[n],
            recv_sem=tile_recv.at[n],
            **target(other),
        )

    def start_tile(n, _):
        tile_copy(n).start()
        return 0

    def add_tile(n, value):
        tile_copy(n).wait()
        return value + tiles_in[n]

    give = pltpu.make_async_remote_copy(
        src_ref=given_ref,
        dst_ref=back_ref,
        send_sem=give_send,
        recv_sem=give_recv,
        **target(jnp.bitwise_xor(me, 2 ** flat_bit("dp", 0))),
    )
    pieces = len(X_PIECES)
    for n in range(pieces):
        for one in load(n):
            one.start()
    for n in range(pieces):
        for one in load(n):
            one.wait()
        go(n, 0)
    give.start()

    pick = lax.broadcasted_iota(jnp.int32, (INNER, 128), 0) // HEADDIM == lane_iota((INNER, 128))
    skips = dot_nn(
        jnp.broadcast_to(gskip_ref[...], (8, INNER)), pick.astype(f32), precision=lax.Precision.HIGHEST
    )
    tiles[...] = jnp.zeros_like(tiles)
    for owner in range(count):
        for row, ref in ((0, gconv_ref), (8, gi_ref), (9, gn_ref)):
            each = ref.shape[1] // count
            tiles[owner, row : row + ref.shape[0], 0:each] = ref[:, owner * each : (owner + 1) * each]
        tiles[owner, 10:11, :] = gpar_ref[0:1, :]
        tiles[owner, 11:12, :] = gpar_ref[1:2, :] * par_ref[1:2, :]
        tiles[owner, 12:13, :] = skips[0:1, :]

    lag = 2
    for n in range(pieces + 2 * lag):
        if n < pieces:
            copy(n, 0).wait_recv()
            go(n, 1)
        if n == 1:
            lax.fori_loop(1, count, start_tile, 0)
        if lag <= n < pieces + lag:
            copy(n - lag, 1).wait_recv()
            go(n - lag, 2)
        if n >= 2 * lag:
            which, at, width = X_PIECES[n - 2 * lag]
            copy(n - 2 * lag, 2).wait_recv()
            x_ref[:, which * X_CUT + at : which * X_CUT + at + width] = total(n - 2 * lag, 3, 0, tall >> 3)
    tile_ref[...] = lax.fori_loop(1, count, add_tile, tiles[me])
    for n in range(pieces):
        for phase in range(3):
            copy(n, phase).wait_send()
    give.wait()


def finish(chains, gconv, gpar, par, gskip, gi, gn, given):
    count = lax.axis_size(AXES)
    operands = [term.value for chain in chains for term, _ in chain.columns[0].terms]
    widths = [chain.columns[0].width for chain in chains]
    tall = chains[0].columns[0].rows
    dma = pltpu.SemaphoreType.DMA
    anywhere = pl.BlockSpec(memory_space=pl.ANY)
    whole = pl.BlockSpec(memory_space=pltpu.VMEM)
    halves = [pltpu.VMEM((tall >> (phase + 1), width), bf16) for phase in range(3) for width in widths]
    pieces = len(X_PIECES)
    return pl.pallas_call(
        functools.partial(finish_kernel, count, lax.axis_size("fsdp")),
        out_shape=(
            jax.ShapeDtypeStruct((tall >> 3, XE), f32),
            jax.ShapeDtypeStruct((TILE_ROWS, 128), f32),
            jax.ShapeDtypeStruct(given.shape, bf16),
        ),
        in_specs=[anywhere] * 6 + [whole] * 6 + [anywhere],
        out_specs=(whole, whole, anywhere),
        scratch_shapes=[
            *(pltpu.VMEM((3, tall, width), bf16) for width in widths),
            *halves,
            *halves,
            pltpu.VMEM((count, TILE_ROWS, 128), f32),
            pltpu.VMEM((count, TILE_ROWS, 128), f32),
            dma((pieces, 3)),
            dma((pieces, 3)),
            dma((pieces, 3)),
            dma((count,)),
            dma((count,)),
            dma,
            dma,
        ],
        compiler_params=params(has_side_effects=True),
        cost_estimate=cost(1e7, 2e7),
        name="finish",
    )(*operands, gconv, gpar, par, gskip, gi, gn, given)


def on_device(
    tokens, cotangent, lengths, balance, norm_gain, in_weight, conv_weight, conv_bias,
    step_bias, decay_log, skip_weight, inner_gain, out_weight,
):
    device = lax.axis_index(AXES)
    count = lax.axis_size(AXES)
    slot = tokens.shape[1]
    rows = 2 * slot
    first_source = balance[2 * device]
    second_source = balance[2 * device + 1]
    keep_second = first_source - 2 * device == 1
    cot = cotangent.reshape(rows, D)
    lens = [lengths[first_source], lengths[second_source]]
    chunks = [(n + Q - 1) // Q for n in lens]
    grouped = is_grouped()
    meta = jnp.stack([chunks[0] + chunks[1], chunks[0], lens[0], lens[1]]).astype(jnp.int32)

    sizes = [v.shape[0] for v in (norm_gain, inner_gain)]
    if grouped:
        flag = keep_second.astype(jnp.int32).reshape(1, 1)
        w1, wc, g1, g2, u = gather(
            flag, in_weight, norm_gain[None], conv_weight.T, conv_bias[None], inner_gain[None], tokens
        )
    else:
        outgoing = jnp.where(keep_second, tokens[0], tokens[1])
        incoming = partner(outgoing, "dp", 0)
        u = jnp.concatenate([jnp.where(keep_second, tokens[1], tokens[0]), incoming], axis=0)
        w1 = lax.all_gather(in_weight.astype(bf16), AXES, axis=0, tiled=True)
        small = [norm_gain, inner_gain, conv_bias, conv_weight.reshape(-1)]
        packed = jnp.concatenate(small).astype(bf16)
        packed = lax.all_gather(packed[None, :], AXES, axis=0, tiled=True).astype(f32)
        cuts = [sum(v.shape[0] for v in small[:n]) for n in range(5)]
        g1, g2, bias, taps = (packed[:, cuts[n] : cuts[n + 1]].reshape(1, -1) for n in range(4))
        wc = jnp.concatenate([taps.reshape(XBC, CONV).T, bias, jnp.zeros((3, XBC), f32)])
    w2_own, w1 = lax.optimization_barrier([out_weight.astype(bf16), w1])
    w2 = lax.all_gather(w2_own, AXES, axis=0, tiled=True)

    rate = -jnp.exp(decay_log)
    par = jnp.zeros((8, 128), f32).at[0, :HEADS].set(step_bias).at[1, :HEADS].set(rate)
    skip = jnp.repeat(skip_weight, HEADDIM)[None]

    proj, e, ht = project(meta, u, g1, w1)
    o, ot, y, sin, err = mixer(meta, proj, e, cot, wc, par, skip, g2)
    never = 1 << 20

    def both(width):
        return [Columns(width // 2, False), Columns(width // 2, True)]

    halves = weight_grad(meta, ot, err, 0, D, D // 2, 1 if grouped else never)
    c_out = Chain(halves, both(D), grouped)
    meta = tick(meta, [c_out], err)
    out, dy, dz, gi = gate(meta, u, err, w2, o, y, proj, g2)
    meta = tick(meta, [c_out], gi)
    halves = weight_grad(meta, ht, dz, 0, INNER, INNER // 4, 2 if grouped else never)
    c_z = Chain(halves, both(INNER), grouped)
    parts = 3
    carried = ()
    for part in range(parts):
        meta = tick(meta, [c_out, c_z] if part > 0 else [c_z], carried[2] if part > 0 else gi)
        carried = back(meta, part, parts, carried, proj, e, dy, sin, wc, par, skip)
    dx, gconv, gpar, gskip = carried
    meta = tick(meta, [c_out, c_z], gpar)
    cut = X_CUT
    halves = weight_grad(meta, ht, dx, 0, cut, cut // 2, never)
    c_x = Chain(halves, [Columns(cut, False)], grouped)
    meta = tick(meta, [c_z, c_x], halves[1])
    halves = weight_grad(meta, ht, dx, cut, XE - cut, cut // 2, 0 if grouped else never)
    c_x1 = Chain(halves, [Columns(XE - cut, True)], grouped)
    meta = tick(meta, [c_x, c_x1], halves[1])
    meta = tick(meta, [c_x1], c_x1.columns[0].terms[-1][0].value)
    kept_half, given_half, gn = input_grad_of(meta, u, err, g1, dz, dx, w1)
    conv_each = XBC // count
    if grouped:
        late = [chain.columns[0].terms[-1][0] for chain in (c_out, c_z)]
        *came, gn = lax.optimization_barrier([term.value for term in late] + [gn])
        for term, value in zip(late, came):
            term.value = value
        grad_x, tile, back_half = finish([c_x, c_x1], gconv, gpar, par, gskip, gi, gn, given_half)
        grad_x = [grad_x]
        grad_conv, grad_bias = tile[:CONV, :conv_each].T, tile[CONV, :conv_each]
        grad_inner, grad_norm = tile[8, : sizes[1]], tile[9, : sizes[0]]
        heads = [tile[10 + n, :HEADS] for n in range(3)]
    else:
        back_half = partner(given_half, "dp", 0)
        heads = jnp.concatenate(
            [gpar[0, :HEADS], gpar[1, :HEADS] * rate, gskip.reshape(HEADS, HEADDIM).sum(axis=1)]
        )
        owned = [gconv[:CONV].T.reshape(count, -1), gconv[CONV].reshape(count, -1), gi.reshape(count, -1)]
        tiles = jnp.concatenate(owned + [jnp.broadcast_to(heads, (count, 3 * HEADS)), gn.reshape(count, -1)], axis=1)
        tiles = jnp.pad(tiles, ((0, 0), (0, 1024 - tiles.shape[1]))).reshape(count, 8, 128)
        sums = sum_small(tiles).reshape(-1)
        grad_x = c_x.finish() + c_x1.finish()
        ends = [sum(v.shape[1] for v in owned[:n]) for n in range(4)]
        grad_conv = sums[: ends[1]].reshape(-1, CONV)
        grad_bias = sums[ends[1] : ends[2]]
        grad_inner = sums[ends[2] : ends[3]]
        heads = sums[ends[3] : ends[3] + 3 * HEADS].reshape(3, HEADS)
        grad_norm = sums[ends[3] + 3 * HEADS :][: sizes[0]]
    grad_out = jnp.concatenate(c_out.finish(), axis=1)
    grad_in = jnp.concatenate(c_z.finish() + grad_x, axis=1)[:, :PROJ]
    swapped = [jnp.stack([back_half, kept_half]), jnp.stack([kept_half, back_half])]
    input_grad = jnp.where(keep_second, *swapped)
    return (
        out.reshape(2, slot, D),
        input_grad,
        grad_norm,
        grad_in,
        grad_conv,
        grad_bias,
        heads[0],
        heads[1],
        heads[2],
        grad_inner,
        grad_out,
    )


def solution(mesh):
    flat = P(AXES)
    rowed = P(AXES, None)
    slots = P(AXES, None, None)
    return jax.shard_map(
        on_device,
        mesh=mesh,
        in_specs=(slots, slots, P(), P(), flat, rowed, rowed, flat, P(), P(), P(), flat, rowed),
        out_specs=(slots, slots, flat, rowed, rowed, flat, P(), P(), P(), flat, rowed),
        check_vma=False,
    )
```

```python
import functools
import jax
import jax.numpy as jnp
from jax import lax
from jax.experimental import pallas as pl
from jax.experimental.pallas import tpu as pltpu
from jax.sharding import PartitionSpec as P

D = 1536
INNER = 3072
HEADS = 48
HEADDIM = 64
STATE = 128
CONV = 4
XBC = 3328
PROJ = 6448
XE = XBC + 128
Q = 128
PAIRS = HEADS // 2

f32 = jnp.float32
bf16 = jnp.bfloat16
epsilon = 1e-05
LOG2E = 1.4426950408889634
AXES = ("dp", "fsdp")


def sigmoid(v):
    return 0.5 * jnp.tanh(0.5 * v) + 0.5


def dot_nn(a, b, precision=None):
    return jnp.dot(a, b, preferred_element_type=f32, precision=precision)


def dot_nt(a, b):
    return lax.dot_general(a, b, (((1,), (1,)), ((), ())), preferred_element_type=f32)


def dot_tn(a, b):
    return lax.dot_general(a, b, (((0,), (0,)), ((), ())), preferred_element_type=f32)


def lane_iota(shape):
    return lax.broadcasted_iota(jnp.int32, shape, len(shape) - 1)


def row_iota(shape):
    return lax.broadcasted_iota(jnp.int32, shape, len(shape) - 2)


H_UNIT = 48
O_UNIT = 32


def is_grouped():
    return D // lax.axis_size(AXES) == H_UNIT


def unit_row(unit, size, per_owner):
    if is_grouped():
        owner = unit // per_owner
        unit = kept_at(halving_order(False), owner) * per_owner + (unit - owner * per_owner)
    return pl.multiple_of(unit * size, 16)


def source_chunk(meta, k, slot_chunks):
    return jnp.where(k < meta[1], k, k - meta[1] + slot_chunks)


def live_rows(meta, k):
    inside = k < meta[1]
    return jnp.where(inside, meta[2] - k * Q, meta[3] - (k - meta[1]) * Q)


def last_live(meta, k):
    return jnp.minimum(k, meta[0] - 1)


def last_padded(meta, k):
    return jnp.minimum(k, meta[0] + lax.rem(meta[0], 2) - 1)


def for_live(total, chunks, body):
    for n in range(2, chunks + 1):
        pl.when(total == n)(functools.partial(body, n * Q))


def cost(flops, moved, transcendentals=0):
    return pl.CostEstimate(flops=int(flops), bytes_accessed=int(moved), transcendentals=int(transcendentals))


def params(**kw):
    return pltpu.CompilerParams(vmem_limit_bytes=60 * 1024 * 1024, **kw)


def project_kernel(slot_chunks, steps, tile, meta, u_ref, g_ref, w_ref, proj_ref, e_ref, ht_ref, h_ref):
    j = pl.program_id(0)
    total = meta[0]
    chunks = 2 * slot_chunks

    @pl.when(j == 0)
    def _():
        for k in range(chunks):

            @pl.when(k < total)
            def _():
                start = pl.multiple_of(source_chunk(meta, k, slot_chunks) * Q, Q)
                x = u_ref[pl.ds(start, Q), :].astype(f32)
                scale = lax.rsqrt(jnp.mean(x * x, axis=-1, keepdims=True) + epsilon)
                normed = x * scale * g_ref[...]
                h_ref[k * Q : (k + 1) * Q, :] = normed.astype(bf16)
                turned = normed.T.astype(bf16)
                for n in range(D // H_UNIT):
                    there = pl.ds(unit_row(jnp.int32(n), H_UNIT, 1), H_UNIT)
                    ht_ref[there, k * Q : (k + 1) * Q] = turned[n * H_UNIT : (n + 1) * H_UNIT, :]

            @pl.when(k >= total)
            def _():
                ht_ref[:, k * Q : (k + 1) * Q] = jnp.zeros((D, Q), bf16)

    edge = XBC + INNER - (steps - 1) * tile

    def live(rows):
        def part(n, _):
            cols = pl.ds(pl.multiple_of(n * 256, 256), 256)
            proj_ref[0:rows, cols] = dot_nn(h_ref[0:rows, :], w_ref[:, cols]).astype(bf16)
            return 0

        lax.fori_loop(0, tile // 256, part, 0)

    for_live(total, chunks, live)

    @pl.when(j == steps - 1)
    def _():
        def steps_of(k, _):
            r = pl.ds(pl.multiple_of(k * Q, Q), Q)
            tail = dot_nn(h_ref[r, :], w_ref[:, edge : edge + 128])
            e_ref[r, :] = jnp.where(lane_iota(tail.shape) < HEADS, tail, 0.0)
            return 0

        lax.fori_loop(0, total, steps_of, 0)


def project(meta, u, g1, w1):
    rows = u.shape[0]
    tile = 512
    steps = pl.cdiv(PROJ, tile)
    return pl.pallas_call(
        functools.partial(project_kernel, rows // Q // 2, steps, tile),
        out_shape=(
            jax.ShapeDtypeStruct((rows, PROJ), bf16),
            jax.ShapeDtypeStruct((rows, 128), f32),
            jax.ShapeDtypeStruct((D, rows), bf16),
        ),
        grid_spec=pltpu.PrefetchScalarGridSpec(
            num_scalar_prefetch=1,
            grid=(steps,),
            in_specs=[
                pl.BlockSpec((rows, D), lambda j, m: (0, 0)),
                pl.BlockSpec((1, D), lambda j, m: (0, 0)),
                pl.BlockSpec((D, tile), lambda j, m: (0, j)),
            ],
            out_specs=[
                pl.BlockSpec((rows, tile), lambda j, m: (0, j)),
                pl.BlockSpec((rows, 128), lambda j, m: (0, 0)),
                pl.BlockSpec((D, rows), lambda j, m: (0, 0)),
            ],
            scratch_shapes=[pltpu.VMEM((rows, D), bf16)],
        ),
        compiler_params=params(),
        cost_estimate=cost(2 * rows * D * PROJ, 2 * (D * PROJ + rows * PROJ)),
        name="project",
    )(meta, u, g1, w1)


def conv_tile(buf, wc_ref, lanes):
    c = wc_ref[CONV : CONV + 1, lanes]
    for tap in range(CONV):
        c = c + wc_ref[tap : tap + 1, lanes] * buf[5 + tap : 5 + tap + Q, lanes]
    return c


def step_sizes(e_ref, par_ref):
    raw = e_ref[...] + par_ref[0:1, :]
    dt = jnp.maximum(raw, 0.0) + jnp.log1p(jnp.exp(-jnp.abs(raw)))
    decay = par_ref[1:2, :]
    lower = (row_iota((Q, Q)) >= lane_iota((Q, Q))).astype(f32)
    cum = dot_nn(lower, dt * (decay * LOG2E), precision=lax.Precision.HIGHEST)
    return raw, dt, cum


def head_column(values, n):
    return jnp.broadcast_to(values[:, n : n + 1], (Q, 128))


def head_pair(values, n):
    index = n + (lane_iota((Q, 128)) >= HEADDIM).astype(jnp.int32)
    return jnp.take_along_axis(values, index, axis=1, mode="promise_in_bounds")


def next_heads(ref, values, used):
    ref[...] = pltpu.roll(values, 128 - used, 1)


def split_pair(v, low):
    zero = jnp.zeros_like(v)
    return jnp.concatenate([jnp.where(low, v, zero), jnp.where(low, zero, v)], axis=0)


def mixer_kernel(
    unroll, meta, proj_ref, e_ref, cot_ref, wc_ref, par_ref, skip_ref, g_ref,
    o_ref, ot_ref, y_ref, sin_ref, err_ref,
    buf, state, cum_ref, dts_ref, row_ref, q_ref,
):
    k = pl.program_id(0)
    total = meta[0]

    @pl.when((k == total) & (lax.rem(total, 2) == 1))
    def _():
        o_ref[...] = jnp.zeros_like(o_ref)
        ot_ref[...] = jnp.zeros_like(ot_ref)
        err_ref[...] = jnp.zeros_like(err_ref)

    @pl.when(k < total)
    def _():
        live = row_iota((Q, D)) < live_rows(meta, k)
        err_ref[...] = jnp.where(live, cot_ref[...].astype(f32), 0.0).astype(bf16)
        first = (k == 0) | (k == meta[1])

        @pl.when(first)
        def _():
            buf[0:8, :] = jnp.zeros((8, XBC), f32)
            state[...] = jnp.zeros_like(state)

        @pl.when(jnp.logical_not(first))
        def _():
            buf[0:8, :] = buf[Q : Q + 8, :]

        buf[8 : 8 + Q, :] = proj_ref[:, INNER : INNER + XBC].astype(f32)
        tail_lanes = slice(INNER, XBC)
        c = conv_tile(buf, wc_ref, tail_lanes)
        act = c * sigmoid(c)
        keys = act[:, :STATE]
        queries = act[:, STATE:].astype(bf16)
        keys_t = keys.T.astype(bf16)
        scores = dot_nn(queries, keys_t)
        _, dt, cum = step_sizes(e_ref, par_ref)
        row_ref[...] = cum.T
        cum_ref[...] = cum
        dts_ref[...] = dt
        lower = row_iota((Q, Q)) >= lane_iota((Q, Q))
        low = lane_iota((Q, 128)) < HEADDIM
        scores = jnp.where(lower, scores, 0.0)

        def pair(p, cums, dts, at):
            lanes = pl.ds(pl.multiple_of(p * 128, 128), 128)
            c = conv_tile(buf, wc_ref, lanes)
            values = c * sigmoid(c)
            col0, col1 = head_column(cums, at), head_column(cums, at + 1)
            both = head_pair(cums, at)
            end = both[Q - 1 : Q, :]
            stepped = values * head_pair(dts, at)
            parts = split_pair(stepped.astype(bf16), low)
            mix = []
            for n, col in enumerate((col0, col1)):
                decay = jnp.exp2(jnp.minimum(col - row_ref[pl.ds(2 * p + n, 1), :], 0.0))
                mix.append((scores * decay).astype(bf16))
            y = dot_nn(jnp.concatenate(mix, axis=1), parts)
            before = state[:, lanes]
            before_low = before.astype(bf16)
            sin_ref[0, :, lanes] = before_low
            y = y + dot_nn(queries, before_low) * jnp.exp2(both)
            y = y + skip_ref[:, lanes] * values
            state[:, lanes] = before * jnp.exp2(end) + dot_nn(
                keys_t, (stepped * jnp.exp2(end - both)).astype(bf16)
            )
            z = proj_ref[:, lanes].astype(f32)
            gated = y * (z * sigmoid(z))
            y_ref[:, lanes] = y.astype(bf16)
            q_ref[:, lanes] = gated
            return gated * gated

        def body(i, squares):
            cums, dts = cum_ref[...], dts_ref[...]
            for n in range(unroll):
                squares = squares + pair(i * unroll + n, cums, dts, 2 * n)
            next_heads(cum_ref, cums, 2 * unroll)
            next_heads(dts_ref, dts, 2 * unroll)
            return squares

        squares = lax.fori_loop(0, PAIRS // unroll, body, jnp.zeros((Q, 128), f32))
        scale = lax.rsqrt(jnp.sum(squares, axis=-1, keepdims=True) / INNER + epsilon)

        def finish(p, _):
            lanes = pl.ds(pl.multiple_of(p * 128, 128), 128)
            out = q_ref[:, lanes] * scale * g_ref[:, lanes]
            o_ref[:, lanes] = out.astype(bf16)
            turned = out.T.astype(bf16)
            for n in range(128 // O_UNIT):
                there = pl.ds(unit_row(p * (128 // O_UNIT) + n, O_UNIT, 3), O_UNIT)
                ot_ref[there, :] = turned[n * O_UNIT : (n + 1) * O_UNIT, :]
            return 0

        lax.fori_loop(0, PAIRS, finish, 0, unroll=2)


def mixer(meta, proj, e, cot, wc, par, skip, g2):
    rows = proj.shape[0]
    chunks = rows // Q
    const = lambda k, m: (0, 0)
    live = lambda k, m: (last_live(m, k), 0)
    return pl.pallas_call(
        functools.partial(mixer_kernel, 4),
        out_shape=(
            jax.ShapeDtypeStruct((rows, INNER), bf16),
            jax.ShapeDtypeStruct((INNER, rows), bf16),
            jax.ShapeDtypeStruct((rows, INNER), bf16),
            jax.ShapeDtypeStruct((chunks, STATE, INNER), bf16),
            jax.ShapeDtypeStruct((rows, D), bf16),
        ),
        grid_spec=pltpu.PrefetchScalarGridSpec(
            num_scalar_prefetch=1,
            grid=(chunks,),
            in_specs=[
                pl.BlockSpec((Q, PROJ), live),
                pl.BlockSpec((Q, 128), live),
                pl.BlockSpec((Q, D), lambda k, m: (source_chunk(m, last_live(m, k), chunks // 2), 0)),
                pl.BlockSpec((8, XBC), const),
                pl.BlockSpec((8, 128), const),
                pl.BlockSpec((1, INNER), const),
                pl.BlockSpec((1, INNER), const),
            ],
            out_specs=[
                pl.BlockSpec((Q, INNER), lambda k, m: (last_padded(m, k), 0)),
                pl.BlockSpec((INNER, Q), lambda k, m: (0, last_padded(m, k))),
                pl.BlockSpec((Q, INNER), live),
                pl.BlockSpec((1, STATE, INNER), lambda k, m: (last_live(m, k), 0, 0)),
                pl.BlockSpec((Q, D), lambda k, m: (last_padded(m, k), 0)),
            ],
            scratch_shapes=[
                pltpu.VMEM((Q + 8, XBC), f32),
                pltpu.VMEM((STATE, INNER), f32),
                pltpu.VMEM((Q, 128), f32),
                pltpu.VMEM((Q, 128), f32),
                pltpu.VMEM((128, Q), f32),
                pltpu.VMEM((Q, INNER), f32),
            ],
        ),
        compiler_params=params(),
        cost_estimate=cost(chunks * PAIRS * 8 * 2 * Q * 128 * 128, 2 * rows * (PROJ + 3 * INNER)),
        name="mixer",
    )(meta, proj, e, cot, wc, par, skip, g2)


def gate_kernel(
    slot_chunks, meta, u_ref, err_ref, w_ref, o_ref, y_ref, z_ref, g_ref,
    out_ref, dy_ref, dz_ref, gi_ref,
    do_ref,
):
    b = pl.program_id(0)
    total = meta[0]

    @pl.when(b == 0)
    def _():
        out_ref[...] = jnp.zeros_like(out_ref)
        gi_ref[...] = jnp.zeros_like(gi_ref)

    def body(rows):
        halves = rows // Q
        if halves == 1:
            dz_ref[Q:, :] = jnp.zeros((Q, INNER), bf16)
        starts = []
        for n in range(halves):
            k = 2 * b + n
            start = pl.multiple_of(source_chunk(meta, k, slot_chunks) * Q, Q)
            starts.append(start)
        branch = dot_nn(o_ref[0:rows, :], w_ref[...])
        for n in range(halves):
            live = row_iota((Q, D)) < live_rows(meta, 2 * b + n)
            here = pl.ds(starts[n], Q)
            value = u_ref[here, :].astype(f32) + branch[n * Q : (n + 1) * Q, :]
            out_ref[here, :] = jnp.where(live, value, 0.0).astype(bf16)
        do_ref[0:rows, :] = dot_nt(err_ref[0:rows, :], w_ref[...])

        def sums(p, carry):
            squares, crossed = carry
            lanes = pl.ds(pl.multiple_of(p * 128, 128), 128)
            z = z_ref[0:rows, lanes].astype(f32)
            q = y_ref[0:rows, lanes].astype(f32) * (z * sigmoid(z))
            return squares + q * q, crossed + q * g_ref[:, lanes] * do_ref[0:rows, lanes]

        zero = jnp.zeros((rows, 128), f32)
        squares, crossed = lax.fori_loop(0, PAIRS, sums, (zero, zero), unroll=2)
        scale = lax.rsqrt(jnp.sum(squares, axis=-1, keepdims=True) / INNER + epsilon)
        factor = scale * scale * scale * (jnp.sum(crossed, axis=-1, keepdims=True) / INNER)

        def back(p, _):
            lanes = pl.ds(pl.multiple_of(p * 128, 128), 128)
            z = z_ref[0:rows, lanes].astype(f32)
            y = y_ref[0:rows, lanes].astype(f32)
            s = sigmoid(z)
            gate = z * s
            q = y * gate
            do = do_ref[0:rows, lanes]
            gi_ref[:, lanes] += jnp.sum(do * q * scale, axis=0, keepdims=True)
            dq = scale * (g_ref[:, lanes] * do) - q * factor
            dy_ref[0:rows, lanes] = (dq * gate).astype(bf16)
            dz_ref[0:rows, lanes] = (dq * y * (s * (1.0 + z * (1.0 - s)))).astype(bf16)
            return 0

        lax.fori_loop(0, PAIRS, back, 0, unroll=2)

    pl.when(total >= 2 * b + 2)(functools.partial(body, 2 * Q))
    pl.when(total == 2 * b + 1)(functools.partial(body, Q))


def last_block(m, b):
    return jnp.minimum(b, (m[0] + 1) // 2 - 1)


def gate(meta, u, err, w2, o, y, proj, g2):
    rows = u.shape[0]
    blocks = rows // (2 * Q)
    const = lambda b, m: (0, 0)
    live = lambda b, m: (last_block(m, b), 0)
    once = pl.Buffered(1)
    return pl.pallas_call(
        functools.partial(gate_kernel, rows // Q // 2),
        out_shape=(
            jax.ShapeDtypeStruct((rows, D), bf16),
            jax.ShapeDtypeStruct((rows, INNER), bf16),
            jax.ShapeDtypeStruct((rows, INNER), bf16),
            jax.ShapeDtypeStruct((1, INNER), f32),
        ),
        grid_spec=pltpu.PrefetchScalarGridSpec(
            num_scalar_prefetch=1,
            grid=(blocks,),
            in_specs=[
                pl.BlockSpec((rows, D), const, pipeline_mode=once),
                pl.BlockSpec((2 * Q, D), live),
                pl.BlockSpec((INNER, D), const, pipeline_mode=once),
                pl.BlockSpec((2 * Q, INNER), live),
                pl.BlockSpec((2 * Q, INNER), live),
                pl.BlockSpec((2 * Q, INNER), live),
                pl.BlockSpec((1, INNER), const),
            ],
            out_specs=[
                pl.BlockSpec((rows, D), const),
                pl.BlockSpec((2 * Q, INNER), live),
                pl.BlockSpec((2 * Q, INNER), live),
                pl.BlockSpec((1, INNER), const),
            ],
            scratch_shapes=[pltpu.VMEM((2 * Q, INNER), f32)],
        ),
        compiler_params=params(),
        cost_estimate=cost(4 * rows * D * INNER, 2 * (D * INNER + 5 * rows * INNER)),
        name="gate",
    )(meta, u, err, w2, o, y, proj, g2)


def back_kernel(
    unroll, part, parts, meta, x_ref, prev_ref, e_ref, dy_ref, sin_ref, wc_ref, par_ref, skip_ref, *rest
):
    carried, rest = (rest[:6], rest[6:]) if part > 0 else ((), rest)
    dx_ref, gconv_ref, gpar_ref, gskip_ref = rest[:4]
    passed_on, rest = (rest[4:6], rest[6:]) if part < parts - 1 else ((), rest[4:])
    buf, dbuf, dstate, cum_ref, dts_ref, row_ref, da_ref = rest
    i = pl.program_id(0)
    total = meta[0]
    begin, end = part_span(meta, part, parts)
    k = total - begin - i

    @pl.when(i == 0)
    def _():
        da_ref[...] = jnp.zeros_like(da_ref)
        if part == 0:
            gconv_ref[...] = jnp.zeros_like(gconv_ref)
            gpar_ref[...] = jnp.zeros_like(gpar_ref)
            gskip_ref[...] = jnp.zeros_like(gskip_ref)

            @pl.when(lax.rem(total, 2) == 1)
            def _():
                dx_ref[...] = jnp.zeros_like(dx_ref)

        else:
            for to, came in zip((gconv_ref, gpar_ref, gskip_ref, dstate), carried[1:5]):
                to[...] = came[...]
            dbuf[0:8, :] = carried[5][...]

    @pl.when((i >= 1) & (i <= end - begin))
    def _():
        first = (k == 0) | (k == meta[1])
        last = (k == total - 1) | (k == meta[1] - 1)

        @pl.when(first)
        def _():
            buf[0:8, :] = jnp.zeros((8, XBC), f32)

        @pl.when(jnp.logical_not(first))
        def _():
            buf[0:8, :] = prev_ref[8:16, INNER : INNER + XBC].astype(f32)

        @pl.when(last)
        def _():
            dbuf[Q : Q + 8, :] = jnp.zeros((8, XBC), f32)
            dstate[...] = jnp.zeros_like(dstate)

        @pl.when(jnp.logical_not(last))
        def _():
            dbuf[Q : Q + 8, :] = dbuf[0:8, :]

        buf[8 : 8 + Q, :] = x_ref[:, INNER : INNER + XBC].astype(f32)
        tail_lanes = slice(INNER, XBC)
        c_tail = conv_tile(buf, wc_ref, tail_lanes)
        s_tail = sigmoid(c_tail)
        act = c_tail * s_tail
        keys = act[:, :STATE].astype(bf16)
        queries = act[:, STATE:].astype(bf16)
        queries_t = act[:, STATE:].T.astype(bf16)
        scores = dot_nn(keys, queries_t)
        raw, dt, cum = step_sizes(e_ref, par_ref)
        row_ref[...] = cum.T
        cum_ref[...] = cum
        dts_ref[...] = dt
        upper = row_iota((Q, Q)) <= lane_iota((Q, Q))
        strict = row_iota((Q, Q)) < lane_iota((Q, Q))
        after = (row_iota((Q, Q)) >= lane_iota((Q, Q))).astype(bf16)
        low = lane_iota((Q, 128)) < HEADDIM
        scores = jnp.where(upper, scores, 0.0)
        half = (lax.broadcasted_iota(jnp.int32, (128, 128), 0) >= HEADDIM).astype(jnp.int32)
        head_lane = lane_iota((128, 128))

        def conv_back(lanes, dc):
            dbuf[0:Q, lanes] = dc
            dxbc = wc_ref[CONV - 1 : CONV, lanes] * dc
            for tap in range(CONV - 1):
                dxbc = dxbc + wc_ref[tap : tap + 1, lanes] * dbuf[3 - tap : 3 - tap + Q, lanes]
            dx_ref[:, lanes] = dxbc.astype(bf16)
            for tap in range(CONV):
                gconv_ref[tap : tap + 1, lanes] += jnp.sum(dc * buf[5 + tap : 5 + tap + Q, lanes], axis=0, keepdims=True)
            gconv_ref[CONV : CONV + 1, lanes] += jnp.sum(dc, axis=0, keepdims=True)

        def pair(p, cums, dts, at, carry):
            dscores, dquery, dkey, from_start, to_end, direct, thru = carry
            lanes = pl.ds(pl.multiple_of(p * 128, 128), 128)
            c = conv_tile(buf, wc_ref, lanes)
            s = sigmoid(c)
            values = c * s
            col0, col1 = head_column(cums, at), head_column(cums, at + 1)
            both = head_pair(cums, at)
            end = both[Q - 1 : Q, :]
            grown = jnp.exp2(both)
            rest = jnp.exp2(end - both)
            dtp = head_pair(dts, at)
            stepped = values * dtp
            dy_low = dy_ref[:, lanes]
            dy = dy_low.astype(f32)
            parts = split_pair(dy_low, low)
            stepped_low = stepped.astype(bf16)
            dmix = dot_nt(stepped_low, parts)
            mix = []
            for n, col in enumerate((col0, col1)):
                decay = jnp.exp2(jnp.minimum(row_ref[pl.ds(2 * p + n, 1), :] - col, 0.0))
                weighted = dmix[:, n * Q : (n + 1) * Q] * decay
                dscores = dscores + weighted
                mix.append((scores * decay).astype(bf16))
                passed = dot_nn((weighted * scores).astype(bf16), after)
                da_ref[pl.ds(2 * p + n, 1), :] = jnp.sum(jnp.where(strict, passed, 0.0), axis=0, keepdims=True)
            dstepped = dot_nn(jnp.concatenate(mix, axis=1), parts)
            dafter = dstate[:, lanes]
            dafter_low = dafter.astype(bf16)
            before_low = sin_ref[0, :, lanes]
            dend = dot_nn(keys, dafter_low) * rest
            grown_dy = (dy * grown).astype(bf16)
            select = (head_lane == 2 * p + half).astype(bf16)
            across = dot_nn(queries, before_low)
            from_start = from_start + dot_nn((across * grown * dy).astype(bf16), select)
            to_end = to_end + dot_nn((stepped * dend).astype(bf16), select)
            dstepped = dstepped + dend
            direct = direct + dot_nn((values * dstepped).astype(bf16), select)
            dquery = dquery + dot_nt(grown_dy, before_low)
            dkey = dkey + dot_nt((stepped * rest).astype(bf16), dafter_low)
            kept = jnp.exp2(end) * dafter
            held = jnp.sum((kept * before_low.astype(f32)).reshape(8, 16, 128), axis=0)
            thru = thru + dot_nn(held.astype(bf16), select)
            dstate[:, lanes] = kept + dot_nn(queries_t, grown_dy)
            dvalues = dstepped * dtp + skip_ref[:, lanes] * dy
            gskip_ref[:, lanes] += jnp.sum(dy * values, axis=0, keepdims=True)
            conv_back(lanes, dvalues * (s + values * (1.0 - s)))
            return dscores, dquery, dkey, from_start, to_end, direct, thru

        def body(n, carry):
            cums, dts = cum_ref[...], dts_ref[...]
            for m in range(unroll):
                carry = pair(n * unroll + m, cums, dts, 2 * m, carry)
            next_heads(cum_ref, cums, 2 * unroll)
            next_heads(dts_ref, dts, 2 * unroll)
            return carry

        zero = jnp.zeros((Q, 128), f32)
        start = (zero,) * 6 + (jnp.zeros((16, 128), f32),)
        carry = lax.fori_loop(0, PAIRS // unroll, body, start)
        dscores, dquery, dkey, from_start, to_end, direct, thru = carry
        dscores = jnp.where(upper, dscores, 0.0)
        dkey = dkey + dot_nn(dscores.astype(bf16), queries)
        dquery = dquery + dot_nn(dscores.T.astype(bf16), keys)
        slope = s_tail * (1.0 + c_tail * (1.0 - s_tail))
        conv_back(slice(INNER, INNER + STATE), dkey * slope[:, :STATE])
        conv_back(slice(INNER + STATE, XBC), dquery * slope[:, STATE:])

        tail_sum = (row_iota((Q, Q)) <= lane_iota((Q, Q))).astype(f32)
        head_sum = (row_iota((Q, Q)) > lane_iota((Q, Q))).astype(f32)
        da = (
            da_ref[...].T
            + dot_nn(tail_sum, from_start, precision=lax.Precision.HIGHEST)
            + dot_nn(head_sum, to_end, precision=lax.Precision.HIGHEST)
            + jnp.sum(thru, axis=0, keepdims=True)
        )
        ddt = par_ref[1:2, :] * da + direct
        de = ddt * sigmoid(raw)
        de = jnp.where(lane_iota((Q, 128)) < HEADS, de, 0.0)
        dx_ref[:, XBC:] = de.astype(bf16)
        gpar_ref[0:1, :] += jnp.sum(de, axis=0, keepdims=True)
        gpar_ref[1:2, :] += jnp.sum(dt * da, axis=0, keepdims=True)

    if passed_on:

        @pl.when(i == pl.num_programs(0) - 1)
        def _():
            passed_on[0][...] = dstate[...]
            passed_on[1][...] = dbuf[0:8, :]


def part_span(meta, part, parts):
    return (meta[0] * part + parts - 1) // parts, (meta[0] * (part + 1) + parts - 1) // parts


def back(meta, part, parts, carried, proj, e, dy, sin, wc, par, skip):
    rows = proj.shape[0]
    chunks = rows // Q
    const = lambda i, m: (0, 0)

    def chunk(i, m):
        begin, end = part_span(m, part, parts)
        return jnp.clip(m[0] - begin - jnp.clip(i, 1, jnp.maximum(end - begin, 1)), 0, m[0] - 1)

    def written(i, m):
        begin, end = part_span(m, part, parts)
        block = jnp.where(end > begin, chunk(i, m), chunks)
        return jnp.where(i == 0, last_padded(m, m[0]), block) if part == 0 else block

    here = lambda i, m: (chunk(i, m), 0)
    out_shape = [
        jax.ShapeDtypeStruct((rows + Q, XE), bf16),
        jax.ShapeDtypeStruct((8, XBC), f32),
        jax.ShapeDtypeStruct((8, 128), f32),
        jax.ShapeDtypeStruct((1, INNER), f32),
    ]
    sums = [pl.BlockSpec((8, XBC), const), pl.BlockSpec((8, 128), const), pl.BlockSpec((1, INNER), const)]
    state = [pl.BlockSpec((STATE, INNER), const), pl.BlockSpec((8, XBC), const)]
    in_specs = [
        pl.BlockSpec((Q, PROJ), here),
        pl.BlockSpec((16, PROJ), lambda i, m: (jnp.maximum(chunk(i, m) * (Q // 16) - 1, 0), 0)),
        pl.BlockSpec((Q, 128), here),
        pl.BlockSpec((Q, INNER), here),
        pl.BlockSpec((1, STATE, INNER), lambda i, m: (chunk(i, m), 0, 0)),
        pl.BlockSpec((8, XBC), const),
        pl.BlockSpec((8, 128), const),
        pl.BlockSpec((1, INNER), const),
    ]
    out_specs = [pl.BlockSpec((Q, XE), lambda i, m: (written(i, m), 0))] + sums
    if part > 0:
        in_specs += [pl.BlockSpec(memory_space=pl.ANY)] + sums + state
    if part < parts - 1:
        out_shape += [jax.ShapeDtypeStruct((STATE, INNER), f32), jax.ShapeDtypeStruct((8, XBC), f32)]
        out_specs += state
    steps = -(-chunks // parts)
    return pl.pallas_call(
        functools.partial(back_kernel, 6, part, parts),
        out_shape=out_shape,
        grid_spec=pltpu.PrefetchScalarGridSpec(
            num_scalar_prefetch=1,
            grid=(steps + 1,),
            in_specs=in_specs,
            out_specs=out_specs,
            scratch_shapes=[
                pltpu.VMEM((Q + 8, XBC), f32),
                pltpu.VMEM((Q + 8, XBC), f32),
                pltpu.VMEM((STATE, INNER), f32),
                pltpu.VMEM((Q, 128), f32),
                pltpu.VMEM((Q, 128), f32),
                pltpu.VMEM((128, Q), f32),
                pltpu.VMEM((128, Q), f32),
            ],
        ),
        input_output_aliases={9: 0} if part > 0 else {},
        compiler_params=params(),
        cost_estimate=cost(steps * PAIRS * 20 * 2 * Q * 128 * 128, 2 * steps * Q * (PROJ + 3 * INNER)),
        name="back",
    )(meta, proj, proj, e, dy, sin, wc, par, skip, *carried)


def weight_kernel(rows, swap_from, meta, at_ref, b_ref, mine_ref, other_ref):
    used = (meta[0] + 1) // 2
    half = at_ref.shape[0] // 2
    part_rows = half // 4
    swap = pl.program_id(0) >= swap_from

    def part(width):
        for c, out_ref in enumerate((mine_ref, other_ref)):

            def step(m, _):
                here = pl.ds(pl.multiple_of(c * half + 2 * m * part_rows, part_rows), 2 * part_rows)
                res = dot_nn(at_ref[here, 0:width], b_ref[0:width, :]).astype(bf16)
                for n in range(2):
                    place = jnp.where(swap, 2 * n + m, 2 * m + n)
                    there = pl.ds(pl.multiple_of(place * part_rows, part_rows), part_rows)
                    out_ref[there, :] = res[n * part_rows : (n + 1) * part_rows, :]
                return 0

            lax.fori_loop(0, 2, step, 0)

    for n in range(1, rows // (2 * Q) + 1):
        pl.when(used == n)(functools.partial(part, n * 2 * Q))


def weight_grad(meta, at, b, first, width, tile, swap_from):
    height, rows = at.shape
    offset = first // tile
    half = jax.ShapeDtypeStruct((height // 2, width), bf16)
    half_spec = pl.BlockSpec((height // 2, tile), lambda j, m: (0, j))
    return pl.pallas_call(
        functools.partial(weight_kernel, rows, swap_from),
        out_shape=(half, half),
        grid_spec=pltpu.PrefetchScalarGridSpec(
            num_scalar_prefetch=1,
            grid=(pl.cdiv(width, tile),),
            in_specs=[
                pl.BlockSpec((height, rows), lambda j, m: (0, 0)),
                pl.BlockSpec((rows, tile), lambda j, m: (0, j + offset)),
            ],
            out_specs=(half_spec, half_spec),
        ),
        compiler_params=params(),
        cost_estimate=cost(2 * rows * height * width, 2 * (rows * (height + width) + height * width)),
        name="weight_grad",
    )(meta, at, b)


def input_kernel(
    slot_chunks, steps, tile, meta, u_ref, err_ref, g_ref, dz_ref, dx_ref, w_ref, out0_ref, out1_ref, gn_ref, dh_ref
):
    j = pl.program_id(0)
    total = meta[0]
    chunks = 2 * slot_chunks
    last = w_ref[:, INNER + XBC : PROJ]
    cols = pl.ds(pl.multiple_of(j * tile, tile), tile)

    def live(rows):
        dh_ref[0:rows, cols] = (
            dot_nt(dz_ref[0:rows, :], w_ref[:, 0:INNER])
            + dot_nt(dx_ref[0:rows, 0:XBC], w_ref[:, INNER : INNER + XBC])
            + dot_nt(dx_ref[0:rows, XBC : XBC + HEADS], last)
        )

    for_live(total, chunks, live)

    @pl.when(j == steps - 1)
    def _():
        out0_ref[...] = jnp.zeros_like(out0_ref)
        out1_ref[...] = jnp.zeros_like(out1_ref)
        gn_ref[...] = jnp.zeros_like(gn_ref)
        for k in range(chunks):

            @pl.when(k < total)
            def _():
                start = pl.multiple_of(source_chunk(meta, k, slot_chunks) * Q, Q)
                u = u_ref[pl.ds(start, Q), :].astype(f32)
                err = err_ref[k * Q : (k + 1) * Q, :].astype(f32)
                scale = lax.rsqrt(jnp.mean(u * u, axis=-1, keepdims=True) + epsilon)
                dh = dh_ref[k * Q : (k + 1) * Q, :]
                gn_ref[...] += jnp.sum(dh * (u * scale), axis=0, keepdims=True)
                n = dh * g_ref[...]
                inner = jnp.mean(u * n, axis=-1, keepdims=True)
                du = (err + scale * n - u * (scale * scale * scale * inner)).astype(bf16)

                @pl.when(k < meta[1])
                def _():
                    out0_ref[pl.ds(start, Q), :] = du

                @pl.when(k >= meta[1])
                def _():
                    out1_ref[pl.ds(pl.multiple_of(start - slot_chunks * Q, Q), Q), :] = du


def input_grad_of(meta, u, err, g1, dz, dx, w1):
    rows = u.shape[0]
    tile = 256
    steps = D // tile
    const = lambda j, m: (0, 0)
    once = pl.Buffered(1)
    return pl.pallas_call(
        functools.partial(input_kernel, rows // Q // 2, steps, tile),
        out_shape=(
            jax.ShapeDtypeStruct((rows // 2, D), bf16),
            jax.ShapeDtypeStruct((rows // 2, D), bf16),
            jax.ShapeDtypeStruct((1, D), f32),
        ),
        grid_spec=pltpu.PrefetchScalarGridSpec(
            num_scalar_prefetch=1,
            grid=(steps,),
            in_specs=[
                pl.BlockSpec((rows, D), const, pipeline_mode=once),
                pl.BlockSpec((rows, D), const, pipeline_mode=once),
                pl.BlockSpec((1, D), const),
                pl.BlockSpec((rows, INNER), const, pipeline_mode=once),
                pl.BlockSpec((rows, XE), const, pipeline_mode=once),
                pl.BlockSpec((tile, w1.shape[1]), lambda j, m: (j, 0)),
            ],
            out_specs=[
                pl.BlockSpec((rows // 2, D), const),
                pl.BlockSpec((rows // 2, D), const),
                pl.BlockSpec((1, D), const),
            ],
            scratch_shapes=[pltpu.VMEM((rows, D), f32)],
        ),
        compiler_params=params(),
        cost_estimate=cost(2 * rows * D * PROJ, 2 * (D * PROJ + rows * PROJ)),
        name="input_grad",
    )(meta, u, err, g1, dz, dx, w1)


def partner(value, axis, bit):
    mask = 2**bit
    pairs = [(source, source ^ mask) for source in range(lax.axis_size(axis))]
    return lax.ppermute(value, axis, pairs)


def log2(size):
    return size.bit_length() - 1


def halving_order(swap):
    fsdp = [("fsdp", bit) for bit in range(log2(lax.axis_size("fsdp")))]
    near = [("dp", 1)]
    far = [("dp", bit) for bit in range(2, log2(lax.axis_size("dp")))]
    return [("dp", 0)] + (near + fsdp if swap else fsdp + near) + far


def flat_bit(axis, bit):
    return bit + (log2(lax.axis_size("fsdp")) if axis == "dp" else 0)


def kept_at(order, owner):
    away = owner ^ lax.axis_index(AXES)
    place = jnp.zeros_like(away)
    for axis, bit in order:
        place = 2 * place + ((away >> flat_bit(axis, bit)) & 1)
    return place


def owner_at(order, place):
    away = jnp.zeros_like(place)
    for n, (axis, bit) in enumerate(order):
        away = away + (((place >> (len(order) - 1 - n)) & 1) << flat_bit(axis, bit))
    return away ^ lax.axis_index(AXES)


class Term:
    def __init__(self, value):
        self.value = value


class Columns:
    def __init__(self, width, swap):
        self.order = halving_order(swap)
        self.width = width
        self.terms = []
        self.phase = 0

    def done(self):
        return self.phase == len(self.order)

    def sum(self, start, stop):
        return sum(term.value[start:stop, at : at + self.width].astype(f32) for term, at in self.terms)

    def halve(self):
        self.rows //= 2
        return self.sum(self.rows, 2 * self.rows).astype(bf16)


class Chain:
    def __init__(self, halves, columns, grouped):
        mine, other = halves
        self.columns = columns
        if not grouped:
            count = lax.axis_size(AXES)
            whole = jnp.concatenate([mine, other]).reshape(count, -1, mine.shape[1])
            parts = []
            at = 0
            for c in columns:
                parts.append(whole[:, :, at : at + c.width][owner_at(c.order, jnp.arange(count))])
                at += c.width
            mine, other = jnp.concatenate(parts, axis=2).reshape(2, -1, mine.shape[1])
        self.going = [(columns, other)]
        kept = Term(mine)
        at = 0
        for c in columns:
            c.rows = mine.shape[0]
            c.terms.append((kept, at))
            at += c.width

    def halve(self):
        groups = {}
        for c in self.columns:
            if not c.done() and all(c not in members for members, _ in self.going):
                groups.setdefault((c.order[c.phase], c.rows), []).append(c)
        for members in groups.values():
            sent = [c.halve() for c in members]
            self.going.append((members, jnp.concatenate(sent, axis=1) if len(sent) > 1 else sent[0]))

    def exchange(self):
        for members, sent in self.going:
            first = members[0]
            came = Term(partner(sent, *first.order[first.phase]))
            at = 0
            for c in members:
                c.terms.append((came, at))
                c.phase += 1
                at += c.width
        self.going = []

    def finish(self):
        while not all(c.done() for c in self.columns):
            self.halve()
            self.exchange()
        return [c.sum(0, c.rows) for c in self.columns]


def tick(token, chains, after):
    last = {id(c.terms[-1][0]): c.terms[-1][0] for chain in chains for c in chain.columns if c.phase > 0}
    if last:
        *came, _ = lax.optimization_barrier([term.value for term in last.values()] + [after])
        for term, value in zip(last.values(), came):
            term.value = value
    for chain in chains:
        chain.halve()
    sent = [value for chain in chains for _, value in chain.going]
    *sent, token = lax.optimization_barrier(sent + [token])
    for chain in chains:
        chain.going = [(members, sent.pop(0)) for members, _ in chain.going]
        chain.exchange()
    return token


W_COLS = 6528
W_SPANS = ((0, 2944), (2944, 2944), (5888, 640))


def gather_kernel(
    count, inner, flag_ref, own_ref, norm_ref, conv_ref, bias_ref, inner_ref, tokens_ref,
    w_ref, wc_ref, g1_ref, g2_ref, u_ref,
    shard_ref, tile_ref, tiles_ref, kept, given,
    send_sem, recv_sem, tile_send, tile_recv, own_sem, give_send, give_recv,
):
    me = lax.axis_index("dp") * inner + lax.axis_index("fsdp")
    height = shard_ref.shape[0]
    x, core, y = flat_bit("fsdp", 0), flat_bit("dp", 0), flat_bit("dp", 1)
    far = [flat_bit("dp", bit) for bit in range(2, log2(lax.axis_size("dp")))]
    ways = (far + [y, x, core], far + [x, y, core], [x, y] + far[::-1] + [core])
    spans = [pl.ds(at, width) for at, width in W_SPANS]
    groups = range(len(spans))

    full = PROJ // 128 * 128
    shard_ref[:, 0:full] = own_ref[:, 0:full].astype(bf16)
    shard_ref[:, full:] = jnp.zeros((height, W_COLS - full), bf16)
    shard_ref[:, full:PROJ] = own_ref[:, full:].astype(bf16)
    tile_ref[...] = jnp.zeros_like(tile_ref)
    for row, ref in ((0, conv_ref), (4, bias_ref), (5, inner_ref), (6, norm_ref)):
        tile_ref[row : row + ref.shape[0], 0 : ref.shape[1]] = ref[...].astype(bf16).astype(f32)

    def place(away):
        return pl.ds(pl.multiple_of(jnp.bitwise_xor(me, away) * height, height), height)

    def link(bit):
        other = jnp.bitwise_xor(me, 2**bit)
        return (other // inner, other % inner)

    def last_step(half, away):
        return max((n for n, bit in enumerate(ways[half]) if (away >> bit) & 1), default=-1)

    def send(half, away, bit):
        src = shard_ref.at[:, spans[half]] if away == 0 else w_ref.at[place(away), spans[half]]
        return pltpu.make_async_remote_copy(
            src_ref=src,
            dst_ref=w_ref.at[place(away), spans[half]],
            send_sem=send_sem.at[half, away ^ 2**bit],
            recv_sem=recv_sem.at[half, away ^ 2**bit],
            device_id=link(bit),
            device_id_type=pl.DeviceIdType.MESH,
        )

    def receive(half, away):
        block = w_ref.at[place(away), spans[half]]
        return pltpu.make_async_remote_copy(
            src_ref=block,
            dst_ref=block,
            send_sem=send_sem.at[half, away],
            recv_sem=recv_sem.at[half, away],
            device_id=link(ways[half][last_step(half, away)]),
            device_id_type=pl.DeviceIdType.MESH,
        )

    def send_on(half, away):
        sends = [send(half, away, bit) for bit in ways[half][last_step(half, away) + 1 :]]
        for one in sends:
            one.start()
        return sends

    def tile_copy(n):
        other = jnp.bitwise_xor(me, n)
        return pltpu.make_async_remote_copy(
            src_ref=tile_ref,
            dst_ref=tiles_ref.at[me],
            send_sem=tile_send.at[n],
            recv_sem=tile_recv.at[n],
            device_id=(other // inner, other % inner),
            device_id_type=pl.DeviceIdType.MESH,
        )

    def start_tile(n, _):
        tile_copy(n).start()
        return 0

    def wait_tile(n, _):
        tile_copy(n).wait()
        return 0

    started = []
    for step in range(len(ways[0])):
        for half in groups:
            one = send(half, 0, ways[half][step])
            one.start()
            started.append(one)
    own = pltpu.make_async_copy(shard_ref, w_ref.at[place(0), :], own_sem.at[0])
    own.start()

    second = jnp.broadcast_to(flag_ref[0, 0], (1, D)) == 1
    rows = kept.shape[0]

    def choose(n, _):
        r = pl.ds(pl.multiple_of(n * 64, 64), 64)
        zero, one = tokens_ref[0, r, :].astype(f32), tokens_ref[1, r, :].astype(f32)
        kept[r, :] = jnp.where(second, one, zero).astype(bf16)
        given[r, :] = jnp.where(second, zero, one).astype(bf16)
        return 0

    lax.fori_loop(0, rows // 64, choose, 0)
    lax.fori_loop(1, count, start_tile, 0)
    tiles_ref[me] = tile_ref[...]

    blocks = [(half, away) for half in groups for away in range(1, count)]
    blocks.sort(key=lambda b: (b[1].bit_count(), last_step(*b), b[0]))
    tail = []
    for n, (half, away) in enumerate(blocks):
        receive(half, away).wait_recv()
        started += send_on(half, away)
        if n == 8:
            keep = pltpu.make_async_copy(kept, u_ref.at[pl.ds(0, rows), :], own_sem.at[1])
            give = pltpu.make_async_remote_copy(
                src_ref=given,
                dst_ref=u_ref.at[pl.ds(rows, rows), :],
                send_sem=give_send,
                recv_sem=give_recv,
                device_id=link(core),
                device_id_type=pl.DeviceIdType.MESH,
            )
            keep.start()
            give.start()
            tail = [keep, give]
        if n == 40:
            lax.fori_loop(1, count, wait_tile, 0)
            wc_ref[...] = jnp.zeros_like(wc_ref)
            for owner in range(count):
                for ref, row, tall in ((wc_ref, 0, 5), (g2_ref, 5, 1), (g1_ref, 6, 1)):
                    each = ref.shape[1] // count
                    ref[0:tall, owner * each : (owner + 1) * each] = tiles_ref[owner, row : row + tall, 0:each]
    for one in started:
        one.wait_send()
    for one in tail:
        one.wait()
    own.wait()


def gather(flag, own, norm, conv, bias, inner, tokens):
    count = lax.axis_size(AXES)
    slot = tokens.shape[1]
    whole = pl.BlockSpec(memory_space=pltpu.VMEM)
    anywhere = pl.BlockSpec(memory_space=pl.ANY)
    dma = pltpu.SemaphoreType.DMA
    return pl.pallas_call(
        functools.partial(gather_kernel, count, lax.axis_size("fsdp")),
        out_shape=(
            jax.ShapeDtypeStruct((D, W_COLS), bf16),
            jax.ShapeDtypeStruct((8, XBC), f32),
            jax.ShapeDtypeStruct((1, D), f32),
            jax.ShapeDtypeStruct((1, INNER), f32),
            jax.ShapeDtypeStruct((2 * slot, D), bf16),
        ),
        in_specs=[pl.BlockSpec(memory_space=pltpu.SMEM)] + [whole] * 6,
        out_specs=(anywhere, whole, whole, whole, anywhere),
        scratch_shapes=[
            pltpu.VMEM((own.shape[0], W_COLS), bf16),
            pltpu.VMEM((8, 128), f32),
            pltpu.VMEM((count, 8, 128), f32),
            pltpu.VMEM((slot, D), bf16),
            pltpu.VMEM((slot, D), bf16),
            dma((len(W_SPANS), count)),
            dma((len(W_SPANS), count)),
            dma((count,)),
            dma((count,)),
            dma((2,)),
            dma,
            dma,
        ],
        compiler_params=params(has_side_effects=True),
        cost_estimate=cost(1e6, 2 * D * W_COLS),
        name="gather",
    )(flag, own, norm, conv, bias, inner, tokens)


def sum_kernel(count, inner, sent_ref, out_ref, came, send_sem, recv_sem):
    me = lax.axis_index("dp") * inner + lax.axis_index("fsdp")

    def copy(n):
        other = jnp.bitwise_xor(me, n)
        return pltpu.make_async_remote_copy(
            src_ref=sent_ref.at[other],
            dst_ref=came.at[n],
            send_sem=send_sem.at[n],
            recv_sem=recv_sem.at[n],
            device_id=(other // inner, other % inner),
            device_id_type=pl.DeviceIdType.MESH,
        )

    def start(n, _):
        copy(n).start()
        return 0

    def add(n, total):
        copy(n).wait()
        return total + came[n]

    lax.fori_loop(1, count, start, 0)
    out_ref[...] = lax.fori_loop(1, count, add, sent_ref[me])


def sum_small(tiles):
    count = tiles.shape[0]
    whole = pl.BlockSpec(memory_space=pltpu.VMEM)
    return pl.pallas_call(
        functools.partial(sum_kernel, count, lax.axis_size("fsdp")),
        out_shape=jax.ShapeDtypeStruct(tiles.shape[1:], f32),
        in_specs=[whole],
        out_specs=whole,
        scratch_shapes=[
            pltpu.VMEM(tiles.shape, f32),
            pltpu.SemaphoreType.DMA((count,)),
            pltpu.SemaphoreType.DMA((count,)),
        ],
        compiler_params=pltpu.CompilerParams(has_side_effects=True),
        cost_estimate=cost(count * 1024, 8 * count * 1024),
        name="sum_small",
    )(tiles)


TILE_ROWS = 16
X_CUT = 1792
X_PIECES = tuple((which, 512 * n, width) for n in range(4) for which, width in ((0, 512 if n < 3 else 256), (1, 512 if n < 3 else 128)))


def finish_kernel(
    count, inner, m0, a0, b0, m1, a1, b1, gconv_ref, gpar_ref, par_ref, gskip_ref, gi_ref, gn_ref, given_ref,
    x_ref, tile_ref, back_ref, *scratch,
):
    sources = ((m0, a0, b0), (m1, a1, b1))
    terms, scratch = scratch[:2], scratch[2:]
    sent, scratch = [scratch[2 * n : 2 * n + 2] for n in range(3)], scratch[6:]
    came, scratch = [scratch[2 * n : 2 * n + 2] for n in range(3)], scratch[6:]
    tiles, tiles_in, load_sem, send_sem, recv_sem, tile_send, tile_recv, give_send, give_recv = scratch
    me = lax.axis_index("dp") * inner + lax.axis_index("fsdp")
    far = [flat_bit("dp", bit) for bit in (2, 3)]
    ways = ([flat_bit("dp", 1)] + far, [flat_bit("fsdp", 0)] + far)
    tall = terms[0].shape[1]

    def target(other):
        return {"device_id": (other // inner, other % inner), "device_id_type": pl.DeviceIdType.MESH}

    def load(n):
        which, at, width = X_PIECES[n]
        cols = pl.ds(at, width)
        return [
            pltpu.make_async_copy(ref.at[pl.ds(0, tall), cols], terms[which].at[i, :, cols], load_sem.at[n, i])
            for i, ref in enumerate(sources[which])
        ]

    def copy(n, phase):
        which, at, width = X_PIECES[n]
        cols = pl.ds(at, width)
        return pltpu.make_async_remote_copy(
            src_ref=sent[phase][which].at[:, cols],
            dst_ref=came[phase][which].at[:, cols],
            send_sem=send_sem.at[n, phase],
            recv_sem=recv_sem.at[n, phase],
            **target(jnp.bitwise_xor(me, 2 ** ways[which][phase])),
        )

    def total(n, phase, start, rows):
        which, at, width = X_PIECES[n]
        parts = [terms[which][i, start : start + rows, at : at + width] for i in range(3)]
        parts += [came[p][which][start : start + rows, at : at + width] for p in range(phase)]
        return sum(part.astype(f32) for part in parts)

    def go(n, phase):
        which, at, width = X_PIECES[n]
        rows = tall >> (phase + 1)
        sent[phase][which][:, at : at + width] = total(n, phase, rows, rows).astype(bf16)
        copy(n, phase).start()

    def tile_copy(n):
        other = jnp.bitwise_xor(me, n)
        return pltpu.make_async_remote_copy(
            src_ref=tiles.at[other],
            dst_ref=tiles_in.at[n],
            send_sem=tile_send.at[n],
            recv_sem=tile_recv.at[n],
            **target(other),
        )

    def start_tile(n, _):
        tile_copy(n).start()
        return 0

    def add_tile(n, value):
        tile_copy(n).wait()
        return value + tiles_in[n]

    give = pltpu.make_async_remote_copy(
        src_ref=given_ref,
        dst_ref=back_ref,
        send_sem=give_send,
        recv_sem=give_recv,
        **target(jnp.bitwise_xor(me, 2 ** flat_bit("dp", 0))),
    )
    pieces = len(X_PIECES)
    for n in range(pieces):
        for one in load(n):
            one.start()
    for n in range(pieces):
        for one in load(n):
            one.wait()
        go(n, 0)
    give.start()

    pick = lax.broadcasted_iota(jnp.int32, (INNER, 128), 0) // HEADDIM == lane_iota((INNER, 128))
    skips = dot_nn(
        jnp.broadcast_to(gskip_ref[...], (8, INNER)), pick.astype(f32), precision=lax.Precision.HIGHEST
    )
    tiles[...] = jnp.zeros_like(tiles)
    for owner in range(count):
        for row, ref in ((0, gconv_ref), (8, gi_ref), (9, gn_ref)):
            each = ref.shape[1] // count
            tiles[owner, row : row + ref.shape[0], 0:each] = ref[:, owner * each : (owner + 1) * each]
        tiles[owner, 10:11, :] = gpar_ref[0:1, :]
        tiles[owner, 11:12, :] = gpar_ref[1:2, :] * par_ref[1:2, :]
        tiles[owner, 12:13, :] = skips[0:1, :]

    lag = 2
    for n in range(pieces + 2 * lag):
        if n < pieces:
            copy(n, 0).wait_recv()
            go(n, 1)
        if n == 1:
            lax.fori_loop(1, count, start_tile, 0)
        if lag <= n < pieces + lag:
            copy(n - lag, 1).wait_recv()
            go(n - lag, 2)
        if n >= 2 * lag:
            which, at, width = X_PIECES[n - 2 * lag]
            copy(n - 2 * lag, 2).wait_recv()
            x_ref[:, which * X_CUT + at : which * X_CUT + at + width] = total(n - 2 * lag, 3, 0, tall >> 3)
    tile_ref[...] = lax.fori_loop(1, count, add_tile, tiles[me])
    for n in range(pieces):
        for phase in range(3):
            copy(n, phase).wait_send()
    give.wait()


def finish(chains, gconv, gpar, par, gskip, gi, gn, given):
    count = lax.axis_size(AXES)
    operands = [term.value for chain in chains for term, _ in chain.columns[0].terms]
    widths = [chain.columns[0].width for chain in chains]
    tall = chains[0].columns[0].rows
    dma = pltpu.SemaphoreType.DMA
    anywhere = pl.BlockSpec(memory_space=pl.ANY)
    whole = pl.BlockSpec(memory_space=pltpu.VMEM)
    halves = [pltpu.VMEM((tall >> (phase + 1), width), bf16) for phase in range(3) for width in widths]
    pieces = len(X_PIECES)
    return pl.pallas_call(
        functools.partial(finish_kernel, count, lax.axis_size("fsdp")),
        out_shape=(
            jax.ShapeDtypeStruct((tall >> 3, XE), f32),
            jax.ShapeDtypeStruct((TILE_ROWS, 128), f32),
            jax.ShapeDtypeStruct(given.shape, bf16),
        ),
        in_specs=[anywhere] * 6 + [whole] * 6 + [anywhere],
        out_specs=(whole, whole, anywhere),
        scratch_shapes=[
            *(pltpu.VMEM((3, tall, width), bf16) for width in widths),
            *halves,
            *halves,
            pltpu.VMEM((count, TILE_ROWS, 128), f32),
            pltpu.VMEM((count, TILE_ROWS, 128), f32),
            dma((pieces, 3)),
            dma((pieces, 3)),
            dma((pieces, 3)),
            dma((count,)),
            dma((count,)),
            dma,
            dma,
        ],
        compiler_params=params(has_side_effects=True),
        cost_estimate=cost(1e7, 2e7),
        name="finish",
    )(*operands, gconv, gpar, par, gskip, gi, gn, given)


def on_device(
    tokens, cotangent, lengths, balance, norm_gain, in_weight, conv_weight, conv_bias,
    step_bias, decay_log, skip_weight, inner_gain, out_weight,
):
    device = lax.axis_index(AXES)
    count = lax.axis_size(AXES)
    slot = tokens.shape[1]
    rows = 2 * slot
    first_source = balance[2 * device]
    second_source = balance[2 * device + 1]
    keep_second = first_source - 2 * device == 1
    cot = cotangent.reshape(rows, D)
    lens = [lengths[first_source], lengths[second_source]]
    chunks = [(n + Q - 1) // Q for n in lens]
    grouped = is_grouped()
    meta = jnp.stack([chunks[0] + chunks[1], chunks[0], lens[0], lens[1]]).astype(jnp.int32)

    sizes = [v.shape[0] for v in (norm_gain, inner_gain)]
    if grouped:
        flag = keep_second.astype(jnp.int32).reshape(1, 1)
        w1, wc, g1, g2, u = gather(
            flag, in_weight, norm_gain[None], conv_weight.T, conv_bias[None], inner_gain[None], tokens
        )
    else:
        outgoing = jnp.where(keep_second, tokens[0], tokens[1])
        incoming = partner(outgoing, "dp", 0)
        u = jnp.concatenate([jnp.where(keep_second, tokens[1], tokens[0]), incoming], axis=0)
        w1 = lax.all_gather(in_weight.astype(bf16), AXES, axis=0, tiled=True)
        small = [norm_gain, inner_gain, conv_bias, conv_weight.reshape(-1)]
        packed = jnp.concatenate(small).astype(bf16)
        packed = lax.all_gather(packed[None, :], AXES, axis=0, tiled=True).astype(f32)
        cuts = [sum(v.shape[0] for v in small[:n]) for n in range(5)]
        g1, g2, bias, taps = (packed[:, cuts[n] : cuts[n + 1]].reshape(1, -1) for n in range(4))
        wc = jnp.concatenate([taps.reshape(XBC, CONV).T, bias, jnp.zeros((3, XBC), f32)])
    w2_own, w1 = lax.optimization_barrier([out_weight.astype(bf16), w1])
    w2 = lax.all_gather(w2_own, AXES, axis=0, tiled=True)

    rate = -jnp.exp(decay_log)
    par = jnp.zeros((8, 128), f32).at[0, :HEADS].set(step_bias).at[1, :HEADS].set(rate)
    skip = jnp.repeat(skip_weight, HEADDIM)[None]

    proj, e, ht = project(meta, u, g1, w1)
    o, ot, y, sin, err = mixer(meta, proj, e, cot, wc, par, skip, g2)
    never = 1 << 20

    def both(width):
        return [Columns(width // 2, False), Columns(width // 2, True)]

    halves = weight_grad(meta, ot, err, 0, D, D // 2, 1 if grouped else never)
    c_out = Chain(halves, both(D), grouped)
    meta = tick(meta, [c_out], err)
    out, dy, dz, gi = gate(meta, u, err, w2, o, y, proj, g2)
    meta = tick(meta, [c_out], gi)
    halves = weight_grad(meta, ht, dz, 0, INNER, INNER // 4, 2 if grouped else never)
    c_z = Chain(halves, both(INNER), grouped)
    parts = 3
    carried = ()
    for part in range(parts):
        meta = tick(meta, [c_out, c_z] if part > 0 else [c_z], carried[2] if part > 0 else gi)
        carried = back(meta, part, parts, carried, proj, e, dy, sin, wc, par, skip)
    dx, gconv, gpar, gskip = carried
    meta = tick(meta, [c_out, c_z], gpar)
    cut = X_CUT
    halves = weight_grad(meta, ht, dx, 0, cut, cut // 2, never)
    c_x = Chain(halves, [Columns(cut, False)], grouped)
    meta = tick(meta, [c_z, c_x], halves[1])
    halves = weight_grad(meta, ht, dx, cut, XE - cut, cut // 2, 0 if grouped else never)
    c_x1 = Chain(halves, [Columns(XE - cut, True)], grouped)
    meta = tick(meta, [c_x, c_x1], halves[1])
    meta = tick(meta, [c_x1], c_x1.columns[0].terms[-1][0].value)
    kept_half, given_half, gn = input_grad_of(meta, u, err, g1, dz, dx, w1)
    conv_each = XBC // count
    if grouped:
        late = [chain.columns[0].terms[-1][0] for chain in (c_out, c_z)]
        *came, gn = lax.optimization_barrier([term.value for term in late] + [gn])
        for term, value in zip(late, came):
            term.value = value
        grad_x, tile, back_half = finish([c_x, c_x1], gconv, gpar, par, gskip, gi, gn, given_half)
        grad_x = [grad_x]
        grad_conv, grad_bias = tile[:CONV, :conv_each].T, tile[CONV, :conv_each]
        grad_inner, grad_norm = tile[8, : sizes[1]], tile[9, : sizes[0]]
        heads = [tile[10 + n, :HEADS] for n in range(3)]
    else:
        back_half = partner(given_half, "dp", 0)
        heads = jnp.concatenate(
            [gpar[0, :HEADS], gpar[1, :HEADS] * rate, gskip.reshape(HEADS, HEADDIM).sum(axis=1)]
        )
        owned = [gconv[:CONV].T.reshape(count, -1), gconv[CONV].reshape(count, -1), gi.reshape(count, -1)]
        tiles = jnp.concatenate(owned + [jnp.broadcast_to(heads, (count, 3 * HEADS)), gn.reshape(count, -1)], axis=1)
        tiles = jnp.pad(tiles, ((0, 0), (0, 1024 - tiles.shape[1]))).reshape(count, 8, 128)
        sums = sum_small(tiles).reshape(-1)
        grad_x = c_x.finish() + c_x1.finish()
        ends = [sum(v.shape[1] for v in owned[:n]) for n in range(4)]
        grad_conv = sums[: ends[1]].reshape(-1, CONV)
        grad_bias = sums[ends[1] : ends[2]]
        grad_inner = sums[ends[2] : ends[3]]
        heads = sums[ends[3] : ends[3] + 3 * HEADS].reshape(3, HEADS)
        grad_norm = sums[ends[3] + 3 * HEADS :][: sizes[0]]
    grad_out = jnp.concatenate(c_out.finish(), axis=1)
    grad_in = jnp.concatenate(c_z.finish() + grad_x, axis=1)[:, :PROJ]
    swapped = [jnp.stack([back_half, kept_half]), jnp.stack([kept_half, back_half])]
    input_grad = jnp.where(keep_second, *swapped)
    return (
        out.reshape(2, slot, D),
        input_grad,
        grad_norm,
        grad_in,
        grad_conv,
        grad_bias,
        heads[0],
        heads[1],
        heads[2],
        grad_inner,
        grad_out,
    )


def solution(mesh):
    flat = P(AXES)
    rowed = P(AXES, None)
    slots = P(AXES, None, None)
    return jax.shard_map(
        on_device,
        mesh=mesh,
        in_specs=(slots, slots, P(), P(), flat, rowed, rowed, flat, P(), P(), P(), flat, rowed),
        out_specs=(slots, slots, flat, rowed, rowed, flat, P(), P(), P(), flat, rowed),
        check_vma=False,
    )
```

```python
import functools
import jax
import jax.numpy as jnp
from jax import lax
from jax.experimental import pallas as pl
from jax.experimental.pallas import tpu as pltpu
from jax.sharding import PartitionSpec as P

D = 1536
INNER = 3072
HEADS = 48
HEADDIM = 64
STATE = 128
CONV = 4
XBC = 3328
PROJ = 6448
XE = XBC + 128
Q = 128
PAIRS = HEADS // 2

f32 = jnp.float32
bf16 = jnp.bfloat16
epsilon = 1e-05
LOG2E = 1.4426950408889634
AXES = ("dp", "fsdp")


def sigmoid(v):
    return 0.5 * jnp.tanh(0.5 * v) + 0.5


def dot_nn(a, b, precision=None):
    return jnp.dot(a, b, preferred_element_type=f32, precision=precision)


def dot_nt(a, b):
    return lax.dot_general(a, b, (((1,), (1,)), ((), ())), preferred_element_type=f32)


def dot_tn(a, b):
    return lax.dot_general(a, b, (((0,), (0,)), ((), ())), preferred_element_type=f32)


def lane_iota(shape):
    return lax.broadcasted_iota(jnp.int32, shape, len(shape) - 1)


def row_iota(shape):
    return lax.broadcasted_iota(jnp.int32, shape, len(shape) - 2)


H_UNIT = 48
O_UNIT = 32


def is_grouped():
    return D // lax.axis_size(AXES) == H_UNIT


def unit_row(unit, size, per_owner):
    if is_grouped():
        owner = unit // per_owner
        unit = kept_at(halving_order(False), owner) * per_owner + (unit - owner * per_owner)
    return pl.multiple_of(unit * size, 16)


def source_chunk(meta, k, slot_chunks):
    return jnp.where(k < meta[1], k, k - meta[1] + slot_chunks)


def live_rows(meta, k):
    inside = k < meta[1]
    return jnp.where(inside, meta[2] - k * Q, meta[3] - (k - meta[1]) * Q)


def last_live(meta, k):
    return jnp.minimum(k, meta[0] - 1)


def last_padded(meta, k):
    return jnp.minimum(k, meta[0] + lax.rem(meta[0], 2) - 1)


def for_live(total, chunks, body):
    for n in range(2, chunks + 1):
        pl.when(total == n)(functools.partial(body, n * Q))


def cost(flops, moved, transcendentals=0):
    return pl.CostEstimate(flops=int(flops), bytes_accessed=int(moved), transcendentals=int(transcendentals))


def params(**kw):
    return pltpu.CompilerParams(vmem_limit_bytes=60 * 1024 * 1024, **kw)


def project_kernel(slot_chunks, steps, tile, meta, u_ref, g_ref, w_ref, proj_ref, e_ref, ht_ref, h_ref):
    j = pl.program_id(0)
    total = meta[0]
    chunks = 2 * slot_chunks

    @pl.when(j == 0)
    def _():
        for k in range(chunks):

            @pl.when(k < total)
            def _():
                start = pl.multiple_of(source_chunk(meta, k, slot_chunks) * Q, Q)
                x = u_ref[pl.ds(start, Q), :].astype(f32)
                scale = lax.rsqrt(jnp.mean(x * x, axis=-1, keepdims=True) + epsilon)
                normed = x * scale * g_ref[...]
                h_ref[k * Q : (k + 1) * Q, :] = normed.astype(bf16)
                turned = normed.T.astype(bf16)
                for n in range(D // H_UNIT):
                    there = pl.ds(unit_row(jnp.int32(n), H_UNIT, 1), H_UNIT)
                    ht_ref[there, k * Q : (k + 1) * Q] = turned[n * H_UNIT : (n + 1) * H_UNIT, :]

            @pl.when(k >= total)
            def _():
                ht_ref[:, k * Q : (k + 1) * Q] = jnp.zeros((D, Q), bf16)

    edge = XBC + INNER - (steps - 1) * tile

    def live(rows):
        def part(n, _):
            cols = pl.ds(pl.multiple_of(n * 256, 256), 256)
            proj_ref[0:rows, cols] = dot_nn(h_ref[0:rows, :], w_ref[:, cols]).astype(bf16)
            return 0

        lax.fori_loop(0, tile // 256, part, 0)

    for_live(total, chunks, live)

    @pl.when(j == steps - 1)
    def _():
        def steps_of(k, _):
            r = pl.ds(pl.multiple_of(k * Q, Q), Q)
            tail = dot_nn(h_ref[r, :], w_ref[:, edge : edge + 128])
            e_ref[r, :] = jnp.where(lane_iota(tail.shape) < HEADS, tail, 0.0)
            return 0

        lax.fori_loop(0, total, steps_of, 0)


def project(meta, u, g1, w1):
    rows = u.shape[0]
    tile = 512
    steps = pl.cdiv(PROJ, tile)
    return pl.pallas_call(
        functools.partial(project_kernel, rows // Q // 2, steps, tile),
        out_shape=(
            jax.ShapeDtypeStruct((rows, PROJ), bf16),
            jax.ShapeDtypeStruct((rows, 128), f32),
            jax.ShapeDtypeStruct((D, rows), bf16),
        ),
        grid_spec=pltpu.PrefetchScalarGridSpec(
            num_scalar_prefetch=1,
            grid=(steps,),
            in_specs=[
                pl.BlockSpec((rows, D), lambda j, m: (0, 0)),
                pl.BlockSpec((1, D), lambda j, m: (0, 0)),
                pl.BlockSpec((D, tile), lambda j, m: (0, j)),
            ],
            out_specs=[
                pl.BlockSpec((rows, tile), lambda j, m: (0, j)),
                pl.BlockSpec((rows, 128), lambda j, m: (0, 0)),
                pl.BlockSpec((D, rows), lambda j, m: (0, 0)),
            ],
            scratch_shapes=[pltpu.VMEM((rows, D), bf16)],
        ),
        compiler_params=params(),
        cost_estimate=cost(2 * rows * D * PROJ, 2 * (D * PROJ + rows * PROJ)),
        name="project",
    )(meta, u, g1, w1)


def conv_tile(buf, wc_ref, lanes):
    c = wc_ref[CONV : CONV + 1, lanes]
    for tap in range(CONV):
        c = c + wc_ref[tap : tap + 1, lanes] * buf[5 + tap : 5 + tap + Q, lanes]
    return c


def step_sizes(e_ref, par_ref):
    raw = e_ref[...] + par_ref[0:1, :]
    dt = jnp.maximum(raw, 0.0) + jnp.log1p(jnp.exp(-jnp.abs(raw)))
    decay = par_ref[1:2, :]
    lower = (row_iota((Q, Q)) >= lane_iota((Q, Q))).astype(f32)
    cum = dot_nn(lower, dt * (decay * LOG2E), precision=lax.Precision.HIGHEST)
    return raw, dt, cum


def head_column(values, n):
    return jnp.broadcast_to(values[:, n : n + 1], (Q, 128))


def head_pair(values, n):
    index = n + (lane_iota((Q, 128)) >= HEADDIM).astype(jnp.int32)
    return jnp.take_along_axis(values, index, axis=1, mode="promise_in_bounds")


def next_heads(ref, values, used):
    ref[...] = pltpu.roll(values, 128 - used, 1)


def split_pair(v, low):
    zero = jnp.zeros_like(v)
    return jnp.concatenate([jnp.where(low, v, zero), jnp.where(low, zero, v)], axis=0)


def mixer_kernel(
    unroll, meta, proj_ref, e_ref, cot_ref, wc_ref, par_ref, skip_ref, g_ref,
    o_ref, ot_ref, y_ref, sin_ref, err_ref,
    buf, state, cum_ref, dts_ref, row_ref, q_ref,
):
    k = pl.program_id(0)
    total = meta[0]

    @pl.when((k == total) & (lax.rem(total, 2) == 1))
    def _():
        o_ref[...] = jnp.zeros_like(o_ref)
        ot_ref[...] = jnp.zeros_like(ot_ref)
        err_ref[...] = jnp.zeros_like(err_ref)

    @pl.when(k < total)
    def _():
        live = row_iota((Q, D)) < live_rows(meta, k)
        err_ref[...] = jnp.where(live, cot_ref[...].astype(f32), 0.0).astype(bf16)
        first = (k == 0) | (k == meta[1])

        @pl.when(first)
        def _():
            buf[0:8, :] = jnp.zeros((8, XBC), f32)
            state[...] = jnp.zeros_like(state)

        @pl.when(jnp.logical_not(first))
        def _():
            buf[0:8, :] = buf[Q : Q + 8, :]

        buf[8 : 8 + Q, :] = proj_ref[:, INNER : INNER + XBC].astype(f32)
        tail_lanes = slice(INNER, XBC)
        c = conv_tile(buf, wc_ref, tail_lanes)
        act = c * sigmoid(c)
        keys = act[:, :STATE]
        queries = act[:, STATE:].astype(bf16)
        keys_t = keys.T.astype(bf16)
        scores = dot_nn(queries, keys_t)
        _, dt, cum = step_sizes(e_ref, par_ref)
        row_ref[...] = cum.T
        cum_ref[...] = cum
        dts_ref[...] = dt
        lower = row_iota((Q, Q)) >= lane_iota((Q, Q))
        low = lane_iota((Q, 128)) < HEADDIM
        scores = jnp.where(lower, scores, 0.0)

        def pair(p, cums, dts, at):
            lanes = pl.ds(pl.multiple_of(p * 128, 128), 128)
            c = conv_tile(buf, wc_ref, lanes)
            values = c * sigmoid(c)
            col0, col1 = head_column(cums, at), head_column(cums, at + 1)
            both = head_pair(cums, at)
            end = both[Q - 1 : Q, :]
            stepped = values * head_pair(dts, at)
            parts = split_pair(stepped.astype(bf16), low)
            mix = []
            for n, col in enumerate((col0, col1)):
                decay = jnp.exp2(jnp.minimum(col - row_ref[pl.ds(2 * p + n, 1), :], 0.0))
                mix.append((scores * decay).astype(bf16))
            y = dot_nn(jnp.concatenate(mix, axis=1), parts)
            before = state[:, lanes]
            before_low = before.astype(bf16)
            sin_ref[0, :, lanes] = before_low
            y = y + dot_nn(queries, before_low) * jnp.exp2(both)
            y = y + skip_ref[:, lanes] * values
            state[:, lanes] = before * jnp.exp2(end) + dot_nn(
                keys_t, (stepped * jnp.exp2(end - both)).astype(bf16)
            )
            z = proj_ref[:, lanes].astype(f32)
            gated = y * (z * sigmoid(z))
            y_ref[:, lanes] = y.astype(bf16)
            q_ref[:, lanes] = gated
            return gated * gated

        def body(i, squares):
            cums, dts = cum_ref[...], dts_ref[...]
            for n in range(unroll):
                squares = squares + pair(i * unroll + n, cums, dts, 2 * n)
            next_heads(cum_ref, cums, 2 * unroll)
            next_heads(dts_ref, dts, 2 * unroll)
            return squares

        squares = lax.fori_loop(0, PAIRS // unroll, body, jnp.zeros((Q, 128), f32))
        scale = lax.rsqrt(jnp.sum(squares, axis=-1, keepdims=True) / INNER + epsilon)

        def finish(p, _):
            lanes = pl.ds(pl.multiple_of(p * 128, 128), 128)
            out = q_ref[:, lanes] * scale * g_ref[:, lanes]
            o_ref[:, lanes] = out.astype(bf16)
            turned = out.T.astype(bf16)
            for n in range(128 // O_UNIT):
                there = pl.ds(unit_row(p * (128 // O_UNIT) + n, O_UNIT, 3), O_UNIT)
                ot_ref[there, :] = turned[n * O_UNIT : (n + 1) * O_UNIT, :]
            return 0

        lax.fori_loop(0, PAIRS, finish, 0, unroll=6)


def mixer(meta, proj, e, cot, wc, par, skip, g2):
    rows = proj.shape[0]
    chunks = rows // Q
    const = lambda k, m: (0, 0)
    live = lambda k, m: (last_live(m, k), 0)
    return pl.pallas_call(
        functools.partial(mixer_kernel, 4),
        out_shape=(
            jax.ShapeDtypeStruct((rows, INNER), bf16),
            jax.ShapeDtypeStruct((INNER, rows), bf16),
            jax.ShapeDtypeStruct((rows, INNER), bf16),
            jax.ShapeDtypeStruct((chunks, STATE, INNER), bf16),
            jax.ShapeDtypeStruct((rows, D), bf16),
        ),
        grid_spec=pltpu.PrefetchScalarGridSpec(
            num_scalar_prefetch=1,
            grid=(chunks,),
            in_specs=[
                pl.BlockSpec((Q, PROJ), live),
                pl.BlockSpec((Q, 128), live),
                pl.BlockSpec((Q, D), lambda k, m: (source_chunk(m, last_live(m, k), chunks // 2), 0)),
                pl.BlockSpec((8, XBC), const),
                pl.BlockSpec((8, 128), const),
                pl.BlockSpec((1, INNER), const),
                pl.BlockSpec((1, INNER), const),
            ],
            out_specs=[
                pl.BlockSpec((Q, INNER), lambda k, m: (last_padded(m, k), 0)),
                pl.BlockSpec((INNER, Q), lambda k, m: (0, last_padded(m, k))),
                pl.BlockSpec((Q, INNER), live),
                pl.BlockSpec((1, STATE, INNER), lambda k, m: (last_live(m, k), 0, 0)),
                pl.BlockSpec((Q, D), lambda k, m: (last_padded(m, k), 0)),
            ],
            scratch_shapes=[
                pltpu.VMEM((Q + 8, XBC), f32),
                pltpu.VMEM((STATE, INNER), f32),
                pltpu.VMEM((Q, 128), f32),
                pltpu.VMEM((Q, 128), f32),
                pltpu.VMEM((128, Q), f32),
                pltpu.VMEM((Q, INNER), f32),
            ],
        ),
        compiler_params=params(),
        cost_estimate=cost(chunks * PAIRS * 8 * 2 * Q * 128 * 128, 2 * rows * (PROJ + 3 * INNER)),
        name="mixer",
    )(meta, proj, e, cot, wc, par, skip, g2)


def gate_kernel(
    slot_chunks, meta, u_ref, err_ref, w_ref, o_ref, y_ref, z_ref, g_ref,
    out_ref, dy_ref, dz_ref, gi_ref,
    do_ref,
):
    b = pl.program_id(0)
    total = meta[0]

    @pl.when(b == 0)
    def _():
        out_ref[...] = jnp.zeros_like(out_ref)
        gi_ref[...] = jnp.zeros_like(gi_ref)

    def body(rows):
        halves = rows // Q
        if halves == 1:
            dz_ref[Q:, :] = jnp.zeros((Q, INNER), bf16)
        starts = []
        for n in range(halves):
            k = 2 * b + n
            start = pl.multiple_of(source_chunk(meta, k, slot_chunks) * Q, Q)
            starts.append(start)
        branch = dot_nn(o_ref[0:rows, :], w_ref[...])
        for n in range(halves):
            live = row_iota((Q, D)) < live_rows(meta, 2 * b + n)
            here = pl.ds(starts[n], Q)
            value = u_ref[here, :].astype(f32) + branch[n * Q : (n + 1) * Q, :]
            out_ref[here, :] = jnp.where(live, value, 0.0).astype(bf16)
        do_ref[0:rows, :] = dot_nt(err_ref[0:rows, :], w_ref[...])

        def sums(p, carry):
            squares, crossed = carry
            lanes = pl.ds(pl.multiple_of(p * 128, 128), 128)
            z = z_ref[0:rows, lanes].astype(f32)
            q = y_ref[0:rows, lanes].astype(f32) * (z * sigmoid(z))
            return squares + q * q, crossed + q * g_ref[:, lanes] * do_ref[0:rows, lanes]

        zero = jnp.zeros((rows, 128), f32)
        squares, crossed = lax.fori_loop(0, PAIRS, sums, (zero, zero), unroll=1)
        scale = lax.rsqrt(jnp.sum(squares, axis=-1, keepdims=True) / INNER + epsilon)
        factor = scale * scale * scale * (jnp.sum(crossed, axis=-1, keepdims=True) / INNER)

        def back(p, _):
            lanes = pl.ds(pl.multiple_of(p * 128, 128), 128)
            z = z_ref[0:rows, lanes].astype(f32)
            y = y_ref[0:rows, lanes].astype(f32)
            s = sigmoid(z)
            gate = z * s
            q = y * gate
            do = do_ref[0:rows, lanes]
            gi_ref[:, lanes] += jnp.sum(do * q * scale, axis=0, keepdims=True)
            dq = scale * (g_ref[:, lanes] * do) - q * factor
            dy_ref[0:rows, lanes] = (dq * gate).astype(bf16)
            dz_ref[0:rows, lanes] = (dq * y * (s * (1.0 + z * (1.0 - s)))).astype(bf16)
            return 0

        lax.fori_loop(0, PAIRS, back, 0, unroll=1)

    pl.when(total >= 2 * b + 2)(functools.partial(body, 2 * Q))
    pl.when(total == 2 * b + 1)(functools.partial(body, Q))


def last_block(m, b):
    return jnp.minimum(b, (m[0] + 1) // 2 - 1)


def gate(meta, u, err, w2, o, y, proj, g2):
    rows = u.shape[0]
    blocks = rows // (2 * Q)
    const = lambda b, m: (0, 0)
    live = lambda b, m: (last_block(m, b), 0)
    once = pl.Buffered(1)
    return pl.pallas_call(
        functools.partial(gate_kernel, rows // Q // 2),
        out_shape=(
            jax.ShapeDtypeStruct((rows, D), bf16),
            jax.ShapeDtypeStruct((rows, INNER), bf16),
            jax.ShapeDtypeStruct((rows, INNER), bf16),
            jax.ShapeDtypeStruct((1, INNER), f32),
        ),
        grid_spec=pltpu.PrefetchScalarGridSpec(
            num_scalar_prefetch=1,
            grid=(blocks,),
            in_specs=[
                pl.BlockSpec((rows, D), const, pipeline_mode=once),
                pl.BlockSpec((2 * Q, D), live),
                pl.BlockSpec((INNER, D), const, pipeline_mode=once),
                pl.BlockSpec((2 * Q, INNER), live),
                pl.BlockSpec((2 * Q, INNER), live),
                pl.BlockSpec((2 * Q, INNER), live),
                pl.BlockSpec((1, INNER), const),
            ],
            out_specs=[
                pl.BlockSpec((rows, D), const),
                pl.BlockSpec((2 * Q, INNER), live),
                pl.BlockSpec((2 * Q, INNER), live),
                pl.BlockSpec((1, INNER), const),
            ],
            scratch_shapes=[pltpu.VMEM((2 * Q, INNER), f32)],
        ),
        compiler_params=params(),
        cost_estimate=cost(4 * rows * D * INNER, 2 * (D * INNER + 5 * rows * INNER)),
        name="gate",
    )(meta, u, err, w2, o, y, proj, g2)


def back_kernel(
    unroll, part, parts, meta, x_ref, prev_ref, e_ref, dy_ref, sin_ref, wc_ref, par_ref, skip_ref, *rest
):
    carried, rest = (rest[:6], rest[6:]) if part > 0 else ((), rest)
    dx_ref, gconv_ref, gpar_ref, gskip_ref = rest[:4]
    passed_on, rest = (rest[4:6], rest[6:]) if part < parts - 1 else ((), rest[4:])
    buf, dbuf, dstate, cum_ref, dts_ref, row_ref, da_ref = rest
    i = pl.program_id(0)
    total = meta[0]
    begin, end = part_span(meta, part, parts)
    k = total - begin - i

    @pl.when(i == 0)
    def _():
        da_ref[...] = jnp.zeros_like(da_ref)
        if part == 0:
            gconv_ref[...] = jnp.zeros_like(gconv_ref)
            gpar_ref[...] = jnp.zeros_like(gpar_ref)
            gskip_ref[...] = jnp.zeros_like(gskip_ref)

            @pl.when(lax.rem(total, 2) == 1)
            def _():
                dx_ref[...] = jnp.zeros_like(dx_ref)

        else:
            for to, came in zip((gconv_ref, gpar_ref, gskip_ref, dstate), carried[1:5]):
                to[...] = came[...]
            dbuf[0:8, :] = carried[5][...]

    @pl.when((i >= 1) & (i <= end - begin))
    def _():
        first = (k == 0) | (k == meta[1])
        last = (k == total - 1) | (k == meta[1] - 1)

        @pl.when(first)
        def _():
            buf[0:8, :] = jnp.zeros((8, XBC), f32)

        @pl.when(jnp.logical_not(first))
        def _():
            buf[0:8, :] = prev_ref[8:16, INNER : INNER + XBC].astype(f32)

        @pl.when(last)
        def _():
            dbuf[Q : Q + 8, :] = jnp.zeros((8, XBC), f32)
            dstate[...] = jnp.zeros_like(dstate)

        @pl.when(jnp.logical_not(last))
        def _():
            dbuf[Q : Q + 8, :] = dbuf[0:8, :]

        buf[8 : 8 + Q, :] = x_ref[:, INNER : INNER + XBC].astype(f32)
        tail_lanes = slice(INNER, XBC)
        c_tail = conv_tile(buf, wc_ref, tail_lanes)
        s_tail = sigmoid(c_tail)
        act = c_tail * s_tail
        keys = act[:, :STATE].astype(bf16)
        queries = act[:, STATE:].astype(bf16)
        queries_t = act[:, STATE:].T.astype(bf16)
        scores = dot_nn(keys, queries_t)
        raw, dt, cum = step_sizes(e_ref, par_ref)
        row_ref[...] = cum.T
        cum_ref[...] = cum
        dts_ref[...] = dt
        upper = row_iota((Q, Q)) <= lane_iota((Q, Q))
        strict = row_iota((Q, Q)) < lane_iota((Q, Q))
        after = (row_iota((Q, Q)) >= lane_iota((Q, Q))).astype(bf16)
        low = lane_iota((Q, 128)) < HEADDIM
        scores = jnp.where(upper, scores, 0.0)
        half = (lax.broadcasted_iota(jnp.int32, (128, 128), 0) >= HEADDIM).astype(jnp.int32)
        head_lane = lane_iota((128, 128))

        def conv_back(lanes, dc):
            dbuf[0:Q, lanes] = dc
            dxbc = wc_ref[CONV - 1 : CONV, lanes] * dc
            for tap in range(CONV - 1):
                dxbc = dxbc + wc_ref[tap : tap + 1, lanes] * dbuf[3 - tap : 3 - tap + Q, lanes]
            dx_ref[:, lanes] = dxbc.astype(bf16)
            for tap in range(CONV):
                gconv_ref[tap : tap + 1, lanes] += jnp.sum(dc * buf[5 + tap : 5 + tap + Q, lanes], axis=0, keepdims=True)
            gconv_ref[CONV : CONV + 1, lanes] += jnp.sum(dc, axis=0, keepdims=True)

        def pair(p, cums, dts, at, carry):
            dscores, dquery, dkey, from_start, to_end, direct, thru = carry
            lanes = pl.ds(pl.multiple_of(p * 128, 128), 128)
            c = conv_tile(buf, wc_ref, lanes)
            s = sigmoid(c)
            values = c * s
            col0, col1 = head_column(cums, at), head_column(cums, at + 1)
            both = head_pair(cums, at)
            end = both[Q - 1 : Q, :]
            grown = jnp.exp2(both)
            rest = jnp.exp2(end - both)
            dtp = head_pair(dts, at)
            stepped = values * dtp
            dy_low = dy_ref[:, lanes]
            dy = dy_low.astype(f32)
            parts = split_pair(dy_low, low)
            stepped_low = stepped.astype(bf16)
            dmix = dot_nt(stepped_low, parts)
            mix = []
            for n, col in enumerate((col0, col1)):
                decay = jnp.exp2(jnp.minimum(row_ref[pl.ds(2 * p + n, 1), :] - col, 0.0))
                weighted = dmix[:, n * Q : (n + 1) * Q] * decay
                dscores = dscores + weighted
                mix.append((scores * decay).astype(bf16))
                passed = dot_nn((weighted * scores).astype(bf16), after)
                da_ref[pl.ds(2 * p + n, 1), :] = jnp.sum(jnp.where(strict, passed, 0.0), axis=0, keepdims=True)
            dstepped = dot_nn(jnp.concatenate(mix, axis=1), parts)
            dafter = dstate[:, lanes]
            dafter_low = dafter.astype(bf16)
            before_low = sin_ref[0, :, lanes]
            dend = dot_nn(keys, dafter_low) * rest
            grown_dy = (dy * grown).astype(bf16)
            select = (head_lane == 2 * p + half).astype(bf16)
            across = dot_nn(queries, before_low)
            from_start = from_start + dot_nn((across * grown * dy).astype(bf16), select)
            to_end = to_end + dot_nn((stepped * dend).astype(bf16), select)
            dstepped = dstepped + dend
            direct = direct + dot_nn((values * dstepped).astype(bf16), select)
            dquery = dquery + dot_nt(grown_dy, before_low)
            dkey = dkey + dot_nt((stepped * rest).astype(bf16), dafter_low)
            kept = jnp.exp2(end) * dafter
            held = jnp.sum((kept * before_low.astype(f32)).reshape(8, 16, 128), axis=0)
            thru = thru + dot_nn(held.astype(bf16), select)
            dstate[:, lanes] = kept + dot_nn(queries_t, grown_dy)
            dvalues = dstepped * dtp + skip_ref[:, lanes] * dy
            gskip_ref[:, lanes] += jnp.sum(dy * values, axis=0, keepdims=True)
            conv_back(lanes, dvalues * (s + values * (1.0 - s)))
            return dscores, dquery, dkey, from_start, to_end, direct, thru

        def body(n, carry):
            cums, dts = cum_ref[...], dts_ref[...]
            for m in range(unroll):
                carry = pair(n * unroll + m, cums, dts, 2 * m, carry)
            next_heads(cum_ref, cums, 2 * unroll)
            next_heads(dts_ref, dts, 2 * unroll)
            return carry

        zero = jnp.zeros((Q, 128), f32)
        start = (zero,) * 6 + (jnp.zeros((16, 128), f32),)
        carry = lax.fori_loop(0, PAIRS // unroll, body, start)
        dscores, dquery, dkey, from_start, to_end, direct, thru = carry
        dscores = jnp.where(upper, dscores, 0.0)
        dkey = dkey + dot_nn(dscores.astype(bf16), queries)
        dquery = dquery + dot_nn(dscores.T.astype(bf16), keys)
        slope = s_tail * (1.0 + c_tail * (1.0 - s_tail))
        conv_back(slice(INNER, INNER + STATE), dkey * slope[:, :STATE])
        conv_back(slice(INNER + STATE, XBC), dquery * slope[:, STATE:])

        tail_sum = (row_iota((Q, Q)) <= lane_iota((Q, Q))).astype(f32)
        head_sum = (row_iota((Q, Q)) > lane_iota((Q, Q))).astype(f32)
        da = (
            da_ref[...].T
            + dot_nn(tail_sum, from_start, precision=lax.Precision.HIGHEST)
            + dot_nn(head_sum, to_end, precision=lax.Precision.HIGHEST)
            + jnp.sum(thru, axis=0, keepdims=True)
        )
        ddt = par_ref[1:2, :] * da + direct
        de = ddt * sigmoid(raw)
        de = jnp.where(lane_iota((Q, 128)) < HEADS, de, 0.0)
        dx_ref[:, XBC:] = de.astype(bf16)
        gpar_ref[0:1, :] += jnp.sum(de, axis=0, keepdims=True)
        gpar_ref[1:2, :] += jnp.sum(dt * da, axis=0, keepdims=True)

    if passed_on:

        @pl.when(i == pl.num_programs(0) - 1)
        def _():
            passed_on[0][...] = dstate[...]
            passed_on[1][...] = dbuf[0:8, :]


def part_span(meta, part, parts):
    return (meta[0] * part + parts - 1) // parts, (meta[0] * (part + 1) + parts - 1) // parts


def back(meta, part, parts, carried, proj, e, dy, sin, wc, par, skip):
    rows = proj.shape[0]
    chunks = rows // Q
    const = lambda i, m: (0, 0)

    def chunk(i, m):
        begin, end = part_span(m, part, parts)
        return jnp.clip(m[0] - begin - jnp.clip(i, 1, jnp.maximum(end - begin, 1)), 0, m[0] - 1)

    def written(i, m):
        begin, end = part_span(m, part, parts)
        block = jnp.where(end > begin, chunk(i, m), chunks)
        return jnp.where(i == 0, last_padded(m, m[0]), block) if part == 0 else block

    here = lambda i, m: (chunk(i, m), 0)
    out_shape = [
        jax.ShapeDtypeStruct((rows + Q, XE), bf16),
        jax.ShapeDtypeStruct((8, XBC), f32),
        jax.ShapeDtypeStruct((8, 128), f32),
        jax.ShapeDtypeStruct((1, INNER), f32),
    ]
    sums = [pl.BlockSpec((8, XBC), const), pl.BlockSpec((8, 128), const), pl.BlockSpec((1, INNER), const)]
    state = [pl.BlockSpec((STATE, INNER), const), pl.BlockSpec((8, XBC), const)]
    in_specs = [
        pl.BlockSpec((Q, PROJ), here),
        pl.BlockSpec((16, PROJ), lambda i, m: (jnp.maximum(chunk(i, m) * (Q // 16) - 1, 0), 0)),
        pl.BlockSpec((Q, 128), here),
        pl.BlockSpec((Q, INNER), here),
        pl.BlockSpec((1, STATE, INNER), lambda i, m: (chunk(i, m), 0, 0)),
        pl.BlockSpec((8, XBC), const),
        pl.BlockSpec((8, 128), const),
        pl.BlockSpec((1, INNER), const),
    ]
    out_specs = [pl.BlockSpec((Q, XE), lambda i, m: (written(i, m), 0))] + sums
    if part > 0:
        in_specs += [pl.BlockSpec(memory_space=pl.ANY)] + sums + state
    if part < parts - 1:
        out_shape += [jax.ShapeDtypeStruct((STATE, INNER), f32), jax.ShapeDtypeStruct((8, XBC), f32)]
        out_specs += state
    steps = -(-chunks // parts)
    return pl.pallas_call(
        functools.partial(back_kernel, 6, part, parts),
        out_shape=out_shape,
        grid_spec=pltpu.PrefetchScalarGridSpec(
            num_scalar_prefetch=1,
            grid=(steps + 1,),
            in_specs=in_specs,
            out_specs=out_specs,
            scratch_shapes=[
                pltpu.VMEM((Q + 8, XBC), f32),
                pltpu.VMEM((Q + 8, XBC), f32),
                pltpu.VMEM((STATE, INNER), f32),
                pltpu.VMEM((Q, 128), f32),
                pltpu.VMEM((Q, 128), f32),
                pltpu.VMEM((128, Q), f32),
                pltpu.VMEM((128, Q), f32),
            ],
        ),
        input_output_aliases={9: 0} if part > 0 else {},
        compiler_params=params(),
        cost_estimate=cost(steps * PAIRS * 20 * 2 * Q * 128 * 128, 2 * steps * Q * (PROJ + 3 * INNER)),
        name="back",
    )(meta, proj, proj, e, dy, sin, wc, par, skip, *carried)


def weight_kernel(rows, swap_from, meta, at_ref, b_ref, mine_ref, other_ref):
    used = (meta[0] + 1) // 2
    half = at_ref.shape[0] // 2
    part_rows = half // 4
    swap = pl.program_id(0) >= swap_from

    def part(width):
        for c, out_ref in enumerate((mine_ref, other_ref)):

            def step(m, _):
                here = pl.ds(pl.multiple_of(c * half + 2 * m * part_rows, part_rows), 2 * part_rows)
                res = dot_nn(at_ref[here, 0:width], b_ref[0:width, :]).astype(bf16)
                for n in range(2):
                    place = jnp.where(swap, 2 * n + m, 2 * m + n)
                    there = pl.ds(pl.multiple_of(place * part_rows, part_rows), part_rows)
                    out_ref[there, :] = res[n * part_rows : (n + 1) * part_rows, :]
                return 0

            lax.fori_loop(0, 2, step, 0)

    for n in range(1, rows // (2 * Q) + 1):
        pl.when(used == n)(functools.partial(part, n * 2 * Q))


def weight_grad(meta, at, b, first, width, tile, swap_from):
    height, rows = at.shape
    offset = first // tile
    half = jax.ShapeDtypeStruct((height // 2, width), bf16)
    half_spec = pl.BlockSpec((height // 2, tile), lambda j, m: (0, j))
    return pl.pallas_call(
        functools.partial(weight_kernel, rows, swap_from),
        out_shape=(half, half),
        grid_spec=pltpu.PrefetchScalarGridSpec(
            num_scalar_prefetch=1,
            grid=(pl.cdiv(width, tile),),
            in_specs=[
                pl.BlockSpec((height, rows), lambda j, m: (0, 0)),
                pl.BlockSpec((rows, tile), lambda j, m: (0, j + offset)),
            ],
            out_specs=(half_spec, half_spec),
        ),
        compiler_params=params(),
        cost_estimate=cost(2 * rows * height * width, 2 * (rows * (height + width) + height * width)),
        name="weight_grad",
    )(meta, at, b)


def input_kernel(
    slot_chunks, steps, tile, meta, u_ref, err_ref, g_ref, dz_ref, dx_ref, w_ref, out0_ref, out1_ref, gn_ref, dh_ref
):
    j = pl.program_id(0)
    total = meta[0]
    chunks = 2 * slot_chunks
    last = w_ref[:, INNER + XBC : PROJ]
    cols = pl.ds(pl.multiple_of(j * tile, tile), tile)

    def live(rows):
        dh_ref[0:rows, cols] = (
            dot_nt(dz_ref[0:rows, :], w_ref[:, 0:INNER])
            + dot_nt(dx_ref[0:rows, 0:XBC], w_ref[:, INNER : INNER + XBC])
            + dot_nt(dx_ref[0:rows, XBC : XBC + HEADS], last)
        )

    for_live(total, chunks, live)

    @pl.when(j == steps - 1)
    def _():
        out0_ref[...] = jnp.zeros_like(out0_ref)
        out1_ref[...] = jnp.zeros_like(out1_ref)
        gn_ref[...] = jnp.zeros_like(gn_ref)
        for k in range(chunks):

            @pl.when(k < total)
            def _():
                start = pl.multiple_of(source_chunk(meta, k, slot_chunks) * Q, Q)
                u = u_ref[pl.ds(start, Q), :].astype(f32)
                err = err_ref[k * Q : (k + 1) * Q, :].astype(f32)
                scale = lax.rsqrt(jnp.mean(u * u, axis=-1, keepdims=True) + epsilon)
                dh = dh_ref[k * Q : (k + 1) * Q, :]
                gn_ref[...] += jnp.sum(dh * (u * scale), axis=0, keepdims=True)
                n = dh * g_ref[...]
                inner = jnp.mean(u * n, axis=-1, keepdims=True)
                du = (err + scale * n - u * (scale * scale * scale * inner)).astype(bf16)

                @pl.when(k < meta[1])
                def _():
                    out0_ref[pl.ds(start, Q), :] = du

                @pl.when(k >= meta[1])
                def _():
                    out1_ref[pl.ds(pl.multiple_of(start - slot_chunks * Q, Q), Q), :] = du


def input_grad_of(meta, u, err, g1, dz, dx, w1):
    rows = u.shape[0]
    tile = 256
    steps = D // tile
    const = lambda j, m: (0, 0)
    once = pl.Buffered(1)
    return pl.pallas_call(
        functools.partial(input_kernel, rows // Q // 2, steps, tile),
        out_shape=(
            jax.ShapeDtypeStruct((rows // 2, D), bf16),
            jax.ShapeDtypeStruct((rows // 2, D), bf16),
            jax.ShapeDtypeStruct((1, D), f32),
        ),
        grid_spec=pltpu.PrefetchScalarGridSpec(
            num_scalar_prefetch=1,
            grid=(steps,),
            in_specs=[
                pl.BlockSpec((rows, D), const, pipeline_mode=once),
                pl.BlockSpec((rows, D), const, pipeline_mode=once),
                pl.BlockSpec((1, D), const),
                pl.BlockSpec((rows, INNER), const, pipeline_mode=once),
                pl.BlockSpec((rows, XE), const, pipeline_mode=once),
                pl.BlockSpec((tile, w1.shape[1]), lambda j, m: (j, 0)),
            ],
            out_specs=[
                pl.BlockSpec((rows // 2, D), const),
                pl.BlockSpec((rows // 2, D), const),
                pl.BlockSpec((1, D), const),
            ],
            scratch_shapes=[pltpu.VMEM((rows, D), f32)],
        ),
        compiler_params=params(),
        cost_estimate=cost(2 * rows * D * PROJ, 2 * (D * PROJ + rows * PROJ)),
        name="input_grad",
    )(meta, u, err, g1, dz, dx, w1)


def partner(value, axis, bit):
    mask = 2**bit
    pairs = [(source, source ^ mask) for source in range(lax.axis_size(axis))]
    return lax.ppermute(value, axis, pairs)


def log2(size):
    return size.bit_length() - 1


def halving_order(swap):
    fsdp = [("fsdp", bit) for bit in range(log2(lax.axis_size("fsdp")))]
    near = [("dp", 1)]
    far = [("dp", bit) for bit in range(2, log2(lax.axis_size("dp")))]
    return [("dp", 0)] + (near + fsdp if swap else fsdp + near) + far


def flat_bit(axis, bit):
    return bit + (log2(lax.axis_size("fsdp")) if axis == "dp" else 0)


def kept_at(order, owner):
    away = owner ^ lax.axis_index(AXES)
    place = jnp.zeros_like(away)
    for axis, bit in order:
        place = 2 * place + ((away >> flat_bit(axis, bit)) & 1)
    return place


def owner_at(order, place):
    away = jnp.zeros_like(place)
    for n, (axis, bit) in enumerate(order):
        away = away + (((place >> (len(order) - 1 - n)) & 1) << flat_bit(axis, bit))
    return away ^ lax.axis_index(AXES)


class Term:
    def __init__(self, value):
        self.value = value


class Columns:
    def __init__(self, width, swap):
        self.order = halving_order(swap)
        self.width = width
        self.terms = []
        self.phase = 0

    def done(self):
        return self.phase == len(self.order)

    def sum(self, start, stop):
        return sum(term.value[start:stop, at : at + self.width].astype(f32) for term, at in self.terms)

    def halve(self):
        self.rows //= 2
        return self.sum(self.rows, 2 * self.rows).astype(bf16)


class Chain:
    def __init__(self, halves, columns, grouped):
        mine, other = halves
        self.columns = columns
        if not grouped:
            count = lax.axis_size(AXES)
            whole = jnp.concatenate([mine, other]).reshape(count, -1, mine.shape[1])
            parts = []
            at = 0
            for c in columns:
                parts.append(whole[:, :, at : at + c.width][owner_at(c.order, jnp.arange(count))])
                at += c.width
            mine, other = jnp.concatenate(parts, axis=2).reshape(2, -1, mine.shape[1])
        self.going = [(columns, other)]
        kept = Term(mine)
        at = 0
        for c in columns:
            c.rows = mine.shape[0]
            c.terms.append((kept, at))
            at += c.width

    def halve(self):
        groups = {}
        for c in self.columns:
            if not c.done() and all(c not in members for members, _ in self.going):
                groups.setdefault((c.order[c.phase], c.rows), []).append(c)
        for members in groups.values():
            sent = [c.halve() for c in members]
            self.going.append((members, jnp.concatenate(sent, axis=1) if len(sent) > 1 else sent[0]))

    def exchange(self):
        for members, sent in self.going:
            first = members[0]
            came = Term(partner(sent, *first.order[first.phase]))
            at = 0
            for c in members:
                c.terms.append((came, at))
                c.phase += 1
                at += c.width
        self.going = []

    def finish(self):
        while not all(c.done() for c in self.columns):
            self.halve()
            self.exchange()
        return [c.sum(0, c.rows) for c in self.columns]


def tick(token, chains, after):
    last = {id(c.terms[-1][0]): c.terms[-1][0] for chain in chains for c in chain.columns if c.phase > 0}
    if last:
        *came, _ = lax.optimization_barrier([term.value for term in last.values()] + [after])
        for term, value in zip(last.values(), came):
            term.value = value
    for chain in chains:
        chain.halve()
    sent = [value for chain in chains for _, value in chain.going]
    *sent, token = lax.optimization_barrier(sent + [token])
    for chain in chains:
        chain.going = [(members, sent.pop(0)) for members, _ in chain.going]
        chain.exchange()
    return token


W_COLS = 6528
W_SPANS = ((0, 2944), (2944, 2944), (5888, 640))


def gather_kernel(
    count, inner, flag_ref, own_ref, norm_ref, conv_ref, bias_ref, inner_ref, tokens_ref,
    w_ref, wc_ref, g1_ref, g2_ref, u_ref,
    shard_ref, tile_ref, tiles_ref, kept, given,
    send_sem, recv_sem, tile_send, tile_recv, own_sem, give_send, give_recv,
):
    me = lax.axis_index("dp") * inner + lax.axis_index("fsdp")
    height = shard_ref.shape[0]
    x, core, y = flat_bit("fsdp", 0), flat_bit("dp", 0), flat_bit("dp", 1)
    far = [flat_bit("dp", bit) for bit in range(2, log2(lax.axis_size("dp")))]
    ways = (far + [y, x, core], far + [x, y, core], [x, y] + far[::-1] + [core])
    spans = [pl.ds(at, width) for at, width in W_SPANS]
    groups = range(len(spans))

    full = PROJ // 128 * 128
    shard_ref[:, 0:full] = own_ref[:, 0:full].astype(bf16)
    shard_ref[:, full:] = jnp.zeros((height, W_COLS - full), bf16)
    shard_ref[:, full:PROJ] = own_ref[:, full:].astype(bf16)
    tile_ref[...] = jnp.zeros_like(tile_ref)
    for row, ref in ((0, conv_ref), (4, bias_ref), (5, inner_ref), (6, norm_ref)):
        tile_ref[row : row + ref.shape[0], 0 : ref.shape[1]] = ref[...].astype(bf16).astype(f32)

    def place(away):
        return pl.ds(pl.multiple_of(jnp.bitwise_xor(me, away) * height, height), height)

    def link(bit):
        other = jnp.bitwise_xor(me, 2**bit)
        return (other // inner, other % inner)

    def last_step(half, away):
        return max((n for n, bit in enumerate(ways[half]) if (away >> bit) & 1), default=-1)

    def send(half, away, bit):
        src = shard_ref.at[:, spans[half]] if away == 0 else w_ref.at[place(away), spans[half]]
        return pltpu.make_async_remote_copy(
            src_ref=src,
            dst_ref=w_ref.at[place(away), spans[half]],
            send_sem=send_sem.at[half, away ^ 2**bit],
            recv_sem=recv_sem.at[half, away ^ 2**bit],
            device_id=link(bit),
            device_id_type=pl.DeviceIdType.MESH,
        )

    def receive(half, away):
        block = w_ref.at[place(away), spans[half]]
        return pltpu.make_async_remote_copy(
            src_ref=block,
            dst_ref=block,
            send_sem=send_sem.at[half, away],
            recv_sem=recv_sem.at[half, away],
            device_id=link(ways[half][last_step(half, away)]),
            device_id_type=pl.DeviceIdType.MESH,
        )

    def send_on(half, away):
        sends = [send(half, away, bit) for bit in ways[half][last_step(half, away) + 1 :]]
        for one in sends:
            one.start()
        return sends

    def tile_copy(n):
        other = jnp.bitwise_xor(me, n)
        return pltpu.make_async_remote_copy(
            src_ref=tile_ref,
            dst_ref=tiles_ref.at[me],
            send_sem=tile_send.at[n],
            recv_sem=tile_recv.at[n],
            device_id=(other // inner, other % inner),
            device_id_type=pl.DeviceIdType.MESH,
        )

    def start_tile(n, _):
        tile_copy(n).start()
        return 0

    def wait_tile(n, _):
        tile_copy(n).wait()
        return 0

    started = []
    for step in range(len(ways[0])):
        for half in groups:
            one = send(half, 0, ways[half][step])
            one.start()
            started.append(one)
    own = pltpu.make_async_copy(shard_ref, w_ref.at[place(0), :], own_sem.at[0])
    own.start()

    second = jnp.broadcast_to(flag_ref[0, 0], (1, D)) == 1
    rows = kept.shape[0]

    def choose(n, _):
        r = pl.ds(pl.multiple_of(n * 64, 64), 64)
        zero, one = tokens_ref[0, r, :].astype(f32), tokens_ref[1, r, :].astype(f32)
        kept[r, :] = jnp.where(second, one, zero).astype(bf16)
        given[r, :] = jnp.where(second, zero, one).astype(bf16)
        return 0

    lax.fori_loop(0, rows // 64, choose, 0)
    lax.fori_loop(1, count, start_tile, 0)
    tiles_ref[me] = tile_ref[...]

    blocks = [(half, away) for half in groups for away in range(1, count)]
    blocks.sort(key=lambda b: (b[1].bit_count(), last_step(*b), b[0]))
    tail = []
    for n, (half, away) in enumerate(blocks):
        receive(half, away).wait_recv()
        started += send_on(half, away)
        if n == 8:
            keep = pltpu.make_async_copy(kept, u_ref.at[pl.ds(0, rows), :], own_sem.at[1])
            give = pltpu.make_async_remote_copy(
                src_ref=given,
                dst_ref=u_ref.at[pl.ds(rows, rows), :],
                send_sem=give_send,
                recv_sem=give_recv,
                device_id=link(core),
                device_id_type=pl.DeviceIdType.MESH,
            )
            keep.start()
            give.start()
            tail = [keep, give]
        if n == 40:
            lax.fori_loop(1, count, wait_tile, 0)
            wc_ref[...] = jnp.zeros_like(wc_ref)
            for owner in range(count):
                for ref, row, tall in ((wc_ref, 0, 5), (g2_ref, 5, 1), (g1_ref, 6, 1)):
                    each = ref.shape[1] // count
                    ref[0:tall, owner * each : (owner + 1) * each] = tiles_ref[owner, row : row + tall, 0:each]
    for one in started:
        one.wait_send()
    for one in tail:
        one.wait()
    own.wait()


def gather(flag, own, norm, conv, bias, inner, tokens):
    count = lax.axis_size(AXES)
    slot = tokens.shape[1]
    whole = pl.BlockSpec(memory_space=pltpu.VMEM)
    anywhere = pl.BlockSpec(memory_space=pl.ANY)
    dma = pltpu.SemaphoreType.DMA
    return pl.pallas_call(
        functools.partial(gather_kernel, count, lax.axis_size("fsdp")),
        out_shape=(
            jax.ShapeDtypeStruct((D, W_COLS), bf16),
            jax.ShapeDtypeStruct((8, XBC), f32),
            jax.ShapeDtypeStruct((1, D), f32),
            jax.ShapeDtypeStruct((1, INNER), f32),
            jax.ShapeDtypeStruct((2 * slot, D), bf16),
        ),
        in_specs=[pl.BlockSpec(memory_space=pltpu.SMEM)] + [whole] * 6,
        out_specs=(anywhere, whole, whole, whole, anywhere),
        scratch_shapes=[
            pltpu.VMEM((own.shape[0], W_COLS), bf16),
            pltpu.VMEM((8, 128), f32),
            pltpu.VMEM((count, 8, 128), f32),
            pltpu.VMEM((slot, D), bf16),
            pltpu.VMEM((slot, D), bf16),
            dma((len(W_SPANS), count)),
            dma((len(W_SPANS), count)),
            dma((count,)),
            dma((count,)),
            dma((2,)),
            dma,
            dma,
        ],
        compiler_params=params(has_side_effects=True),
        cost_estimate=cost(1e6, 2 * D * W_COLS),
        name="gather",
    )(flag, own, norm, conv, bias, inner, tokens)


def sum_kernel(count, inner, sent_ref, out_ref, came, send_sem, recv_sem):
    me = lax.axis_index("dp") * inner + lax.axis_index("fsdp")

    def copy(n):
        other = jnp.bitwise_xor(me, n)
        return pltpu.make_async_remote_copy(
            src_ref=sent_ref.at[other],
            dst_ref=came.at[n],
            send_sem=send_sem.at[n],
            recv_sem=recv_sem.at[n],
            device_id=(other // inner, other % inner),
            device_id_type=pl.DeviceIdType.MESH,
        )

    def start(n, _):
        copy(n).start()
        return 0

    def add(n, total):
        copy(n).wait()
        return total + came[n]

    lax.fori_loop(1, count, start, 0)
    out_ref[...] = lax.fori_loop(1, count, add, sent_ref[me])


def sum_small(tiles):
    count = tiles.shape[0]
    whole = pl.BlockSpec(memory_space=pltpu.VMEM)
    return pl.pallas_call(
        functools.partial(sum_kernel, count, lax.axis_size("fsdp")),
        out_shape=jax.ShapeDtypeStruct(tiles.shape[1:], f32),
        in_specs=[whole],
        out_specs=whole,
        scratch_shapes=[
            pltpu.VMEM(tiles.shape, f32),
            pltpu.SemaphoreType.DMA((count,)),
            pltpu.SemaphoreType.DMA((count,)),
        ],
        compiler_params=pltpu.CompilerParams(has_side_effects=True),
        cost_estimate=cost(count * 1024, 8 * count * 1024),
        name="sum_small",
    )(tiles)


TILE_ROWS = 16
X_CUT = 1792
X_PIECES = tuple((which, 512 * n, width) for n in range(4) for which, width in ((0, 512 if n < 3 else 256), (1, 512 if n < 3 else 128)))


def finish_kernel(
    count, inner, m0, a0, b0, m1, a1, b1, gconv_ref, gpar_ref, par_ref, gskip_ref, gi_ref, gn_ref, given_ref,
    x_ref, tile_ref, back_ref, *scratch,
):
    sources = ((m0, a0, b0), (m1, a1, b1))
    terms, scratch = scratch[:2], scratch[2:]
    sent, scratch = [scratch[2 * n : 2 * n + 2] for n in range(3)], scratch[6:]
    came, scratch = [scratch[2 * n : 2 * n + 2] for n in range(3)], scratch[6:]
    tiles, tiles_in, load_sem, send_sem, recv_sem, tile_send, tile_recv, give_send, give_recv = scratch
    me = lax.axis_index("dp") * inner + lax.axis_index("fsdp")
    far = [flat_bit("dp", bit) for bit in (2, 3)]
    ways = ([flat_bit("dp", 1)] + far, [flat_bit("fsdp", 0)] + far)
    tall = terms[0].shape[1]

    def target(other):
        return {"device_id": (other // inner, other % inner), "device_id_type": pl.DeviceIdType.MESH}

    def load(n):
        which, at, width = X_PIECES[n]
        cols = pl.ds(at, width)
        return [
            pltpu.make_async_copy(ref.at[pl.ds(0, tall), cols], terms[which].at[i, :, cols], load_sem.at[n, i])
            for i, ref in enumerate(sources[which])
        ]

    def copy(n, phase):
        which, at, width = X_PIECES[n]
        cols = pl.ds(at, width)
        return pltpu.make_async_remote_copy(
            src_ref=sent[phase][which].at[:, cols],
            dst_ref=came[phase][which].at[:, cols],
            send_sem=send_sem.at[n, phase],
            recv_sem=recv_sem.at[n, phase],
            **target(jnp.bitwise_xor(me, 2 ** ways[which][phase])),
        )

    def total(n, phase, start, rows):
        which, at, width = X_PIECES[n]
        parts = [terms[which][i, start : start + rows, at : at + width] for i in range(3)]
        parts += [came[p][which][start : start + rows, at : at + width] for p in range(phase)]
        return sum(part.astype(f32) for part in parts)

    def go(n, phase):
        which, at, width = X_PIECES[n]
        rows = tall >> (phase + 1)
        sent[phase][which][:, at : at + width] = total(n, phase, rows, rows).astype(bf16)
        copy(n, phase).start()

    def tile_copy(n):
        other = jnp.bitwise_xor(me, n)
        return pltpu.make_async_remote_copy(
            src_ref=tiles.at[other],
            dst_ref=tiles_in.at[n],
            send_sem=tile_send.at[n],
            recv_sem=tile_recv.at[n],
            **target(other),
        )

    def start_tile(n, _):
        tile_copy(n).start()
        return 0

    def add_tile(n, value):
        tile_copy(n).wait()
        return value + tiles_in[n]

    give = pltpu.make_async_remote_copy(
        src_ref=given_ref,
        dst_ref=back_ref,
        send_sem=give_send,
        recv_sem=give_recv,
        **target(jnp.bitwise_xor(me, 2 ** flat_bit("dp", 0))),
    )
    pieces = len(X_PIECES)
    for n in range(pieces):
        for one in load(n):
            one.start()
    for n in range(pieces):
        for one in load(n):
            one.wait()
        go(n, 0)
    give.start()

    pick = lax.broadcasted_iota(jnp.int32, (INNER, 128), 0) // HEADDIM == lane_iota((INNER, 128))
    skips = dot_nn(
        jnp.broadcast_to(gskip_ref[...], (8, INNER)), pick.astype(f32), precision=lax.Precision.HIGHEST
    )
    tiles[...] = jnp.zeros_like(tiles)
    for owner in range(count):
        for row, ref in ((0, gconv_ref), (8, gi_ref), (9, gn_ref)):
            each = ref.shape[1] // count
            tiles[owner, row : row + ref.shape[0], 0:each] = ref[:, owner * each : (owner + 1) * each]
        tiles[owner, 10:11, :] = gpar_ref[0:1, :]
        tiles[owner, 11:12, :] = gpar_ref[1:2, :] * par_ref[1:2, :]
        tiles[owner, 12:13, :] = skips[0:1, :]

    lag = 2
    for n in range(pieces + 2 * lag):
        if n < pieces:
            copy(n, 0).wait_recv()
            go(n, 1)
        if n == 1:
            lax.fori_loop(1, count, start_tile, 0)
        if lag <= n < pieces + lag:
            copy(n - lag, 1).wait_recv()
            go(n - lag, 2)
        if n >= 2 * lag:
            which, at, width = X_PIECES[n - 2 * lag]
            copy(n - 2 * lag, 2).wait_recv()
            x_ref[:, which * X_CUT + at : which * X_CUT + at + width] = total(n - 2 * lag, 3, 0, tall >> 3)
    tile_ref[...] = lax.fori_loop(1, count, add_tile, tiles[me])
    for n in range(pieces):
        for phase in range(3):
            copy(n, phase).wait_send()
    give.wait()


def finish(chains, gconv, gpar, par, gskip, gi, gn, given):
    count = lax.axis_size(AXES)
    operands = [term.value for chain in chains for term, _ in chain.columns[0].terms]
    widths = [chain.columns[0].width for chain in chains]
    tall = chains[0].columns[0].rows
    dma = pltpu.SemaphoreType.DMA
    anywhere = pl.BlockSpec(memory_space=pl.ANY)
    whole = pl.BlockSpec(memory_space=pltpu.VMEM)
    halves = [pltpu.VMEM((tall >> (phase + 1), width), bf16) for phase in range(3) for width in widths]
    pieces = len(X_PIECES)
    return pl.pallas_call(
        functools.partial(finish_kernel, count, lax.axis_size("fsdp")),
        out_shape=(
            jax.ShapeDtypeStruct((tall >> 3, XE), f32),
            jax.ShapeDtypeStruct((TILE_ROWS, 128), f32),
            jax.ShapeDtypeStruct(given.shape, bf16),
        ),
        in_specs=[anywhere] * 6 + [whole] * 6 + [anywhere],
        out_specs=(whole, whole, anywhere),
        scratch_shapes=[
            *(pltpu.VMEM((3, tall, width), bf16) for width in widths),
            *halves,
            *halves,
            pltpu.VMEM((count, TILE_ROWS, 128), f32),
            pltpu.VMEM((count, TILE_ROWS, 128), f32),
            dma((pieces, 3)),
            dma((pieces, 3)),
            dma((pieces, 3)),
            dma((count,)),
            dma((count,)),
            dma,
            dma,
        ],
        compiler_params=params(has_side_effects=True),
        cost_estimate=cost(1e7, 2e7),
        name="finish",
    )(*operands, gconv, gpar, par, gskip, gi, gn, given)


def on_device(
    tokens, cotangent, lengths, balance, norm_gain, in_weight, conv_weight, conv_bias,
    step_bias, decay_log, skip_weight, inner_gain, out_weight,
):
    device = lax.axis_index(AXES)
    count = lax.axis_size(AXES)
    slot = tokens.shape[1]
    rows = 2 * slot
    first_source = balance[2 * device]
    second_source = balance[2 * device + 1]
    keep_second = first_source - 2 * device == 1
    cot = cotangent.reshape(rows, D)
    lens = [lengths[first_source], lengths[second_source]]
    chunks = [(n + Q - 1) // Q for n in lens]
    grouped = is_grouped()
    meta = jnp.stack([chunks[0] + chunks[1], chunks[0], lens[0], lens[1]]).astype(jnp.int32)

    sizes = [v.shape[0] for v in (norm_gain, inner_gain)]
    if grouped:
        flag = keep_second.astype(jnp.int32).reshape(1, 1)
        w1, wc, g1, g2, u = gather(
            flag, in_weight, norm_gain[None], conv_weight.T, conv_bias[None], inner_gain[None], tokens
        )
    else:
        outgoing = jnp.where(keep_second, tokens[0], tokens[1])
        incoming = partner(outgoing, "dp", 0)
        u = jnp.concatenate([jnp.where(keep_second, tokens[1], tokens[0]), incoming], axis=0)
        w1 = lax.all_gather(in_weight.astype(bf16), AXES, axis=0, tiled=True)
        small = [norm_gain, inner_gain, conv_bias, conv_weight.reshape(-1)]
        packed = jnp.concatenate(small).astype(bf16)
        packed = lax.all_gather(packed[None, :], AXES, axis=0, tiled=True).astype(f32)
        cuts = [sum(v.shape[0] for v in small[:n]) for n in range(5)]
        g1, g2, bias, taps = (packed[:, cuts[n] : cuts[n + 1]].reshape(1, -1) for n in range(4))
        wc = jnp.concatenate([taps.reshape(XBC, CONV).T, bias, jnp.zeros((3, XBC), f32)])
    w2_own, w1 = lax.optimization_barrier([out_weight.astype(bf16), w1])
    w2 = lax.all_gather(w2_own, AXES, axis=0, tiled=True)

    rate = -jnp.exp(decay_log)
    par = jnp.zeros((8, 128), f32).at[0, :HEADS].set(step_bias).at[1, :HEADS].set(rate)
    skip = jnp.repeat(skip_weight, HEADDIM)[None]

    proj, e, ht = project(meta, u, g1, w1)
    o, ot, y, sin, err = mixer(meta, proj, e, cot, wc, par, skip, g2)
    never = 1 << 20

    def both(width):
        return [Columns(width // 2, False), Columns(width // 2, True)]

    halves = weight_grad(meta, ot, err, 0, D, D // 2, 1 if grouped else never)
    c_out = Chain(halves, both(D), grouped)
    meta = tick(meta, [c_out], err)
    out, dy, dz, gi = gate(meta, u, err, w2, o, y, proj, g2)
    meta = tick(meta, [c_out], gi)
    halves = weight_grad(meta, ht, dz, 0, INNER, INNER // 4, 2 if grouped else never)
    c_z = Chain(halves, both(INNER), grouped)
    parts = 3
    carried = ()
    for part in range(parts):
        meta = tick(meta, [c_out, c_z] if part > 0 else [c_z], carried[2] if part > 0 else gi)
        carried = back(meta, part, parts, carried, proj, e, dy, sin, wc, par, skip)
    dx, gconv, gpar, gskip = carried
    meta = tick(meta, [c_out, c_z], gpar)
    cut = X_CUT
    halves = weight_grad(meta, ht, dx, 0, cut, cut // 2, never)
    c_x = Chain(halves, [Columns(cut, False)], grouped)
    meta = tick(meta, [c_z, c_x], halves[1])
    halves = weight_grad(meta, ht, dx, cut, XE - cut, cut // 2, 0 if grouped else never)
    c_x1 = Chain(halves, [Columns(XE - cut, True)], grouped)
    meta = tick(meta, [c_x, c_x1], halves[1])
    meta = tick(meta, [c_x1], c_x1.columns[0].terms[-1][0].value)
    kept_half, given_half, gn = input_grad_of(meta, u, err, g1, dz, dx, w1)
    conv_each = XBC // count
    if grouped:
        late = [chain.columns[0].terms[-1][0] for chain in (c_out, c_z)]
        *came, gn = lax.optimization_barrier([term.value for term in late] + [gn])
        for term, value in zip(late, came):
            term.value = value
        grad_x, tile, back_half = finish([c_x, c_x1], gconv, gpar, par, gskip, gi, gn, given_half)
        grad_x = [grad_x]
        grad_conv, grad_bias = tile[:CONV, :conv_each].T, tile[CONV, :conv_each]
        grad_inner, grad_norm = tile[8, : sizes[1]], tile[9, : sizes[0]]
        heads = [tile[10 + n, :HEADS] for n in range(3)]
    else:
        back_half = partner(given_half, "dp", 0)
        heads = jnp.concatenate(
            [gpar[0, :HEADS], gpar[1, :HEADS] * rate, gskip.reshape(HEADS, HEADDIM).sum(axis=1)]
        )
        owned = [gconv[:CONV].T.reshape(count, -1), gconv[CONV].reshape(count, -1), gi.reshape(count, -1)]
        tiles = jnp.concatenate(owned + [jnp.broadcast_to(heads, (count, 3 * HEADS)), gn.reshape(count, -1)], axis=1)
        tiles = jnp.pad(tiles, ((0, 0), (0, 1024 - tiles.shape[1]))).reshape(count, 8, 128)
        sums = sum_small(tiles).reshape(-1)
        grad_x = c_x.finish() + c_x1.finish()
        ends = [sum(v.shape[1] for v in owned[:n]) for n in range(4)]
        grad_conv = sums[: ends[1]].reshape(-1, CONV)
        grad_bias = sums[ends[1] : ends[2]]
        grad_inner = sums[ends[2] : ends[3]]
        heads = sums[ends[3] : ends[3] + 3 * HEADS].reshape(3, HEADS)
        grad_norm = sums[ends[3] + 3 * HEADS :][: sizes[0]]
    grad_out = jnp.concatenate(c_out.finish(), axis=1)
    grad_in = jnp.concatenate(c_z.finish() + grad_x, axis=1)[:, :PROJ]
    swapped = [jnp.stack([back_half, kept_half]), jnp.stack([kept_half, back_half])]
    input_grad = jnp.where(keep_second, *swapped)
    return (
        out.reshape(2, slot, D),
        input_grad,
        grad_norm,
        grad_in,
        grad_conv,
        grad_bias,
        heads[0],
        heads[1],
        heads[2],
        grad_inner,
        grad_out,
    )


def solution(mesh):
    flat = P(AXES)
    rowed = P(AXES, None)
    slots = P(AXES, None, None)
    return jax.shard_map(
        on_device,
        mesh=mesh,
        in_specs=(slots, slots, P(), P(), flat, rowed, rowed, flat, P(), P(), P(), flat, rowed),
        out_specs=(slots, slots, flat, rowed, rowed, flat, P(), P(), P(), flat, rowed),
        check_vma=False,
    )
```

```python
import functools
import jax
import jax.numpy as jnp
from jax import lax
from jax.experimental import pallas as pl
from jax.experimental.pallas import tpu as pltpu
from jax.sharding import PartitionSpec as P

D = 1536
INNER = 3072
HEADS = 48
HEADDIM = 64
STATE = 128
CONV = 4
XBC = 3328
PROJ = 6448
XE = XBC + 128
Q = 128
PAIRS = HEADS // 2

f32 = jnp.float32
bf16 = jnp.bfloat16
epsilon = 1e-05
LOG2E = 1.4426950408889634
AXES = ("dp", "fsdp")


def sigmoid(v):
    return 0.5 * jnp.tanh(0.5 * v) + 0.5


def dot_nn(a, b, precision=None):
    return jnp.dot(a, b, preferred_element_type=f32, precision=precision)


def dot_nt(a, b):
    return lax.dot_general(a, b, (((1,), (1,)), ((), ())), preferred_element_type=f32)


def dot_tn(a, b):
    return lax.dot_general(a, b, (((0,), (0,)), ((), ())), preferred_element_type=f32)


def lane_iota(shape):
    return lax.broadcasted_iota(jnp.int32, shape, len(shape) - 1)


def row_iota(shape):
    return lax.broadcasted_iota(jnp.int32, shape, len(shape) - 2)


H_UNIT = 48
O_UNIT = 32


def is_grouped():
    return D // lax.axis_size(AXES) == H_UNIT


def unit_row(unit, size, per_owner):
    if is_grouped():
        owner = unit // per_owner
        unit = kept_at(halving_order(False), owner) * per_owner + (unit - owner * per_owner)
    return pl.multiple_of(unit * size, 16)


def source_chunk(meta, k, slot_chunks):
    return jnp.where(k < meta[1], k, k - meta[1] + slot_chunks)


def live_rows(meta, k):
    inside = k < meta[1]
    return jnp.where(inside, meta[2] - k * Q, meta[3] - (k - meta[1]) * Q)


def last_live(meta, k):
    return jnp.minimum(k, meta[0] - 1)


def last_padded(meta, k):
    return jnp.minimum(k, meta[0] + lax.rem(meta[0], 2) - 1)


def for_live(total, chunks, body):
    for n in range(2, chunks + 1):
        pl.when(total == n)(functools.partial(body, n * Q))


def cost(flops, moved, transcendentals=0):
    return pl.CostEstimate(flops=int(flops), bytes_accessed=int(moved), transcendentals=int(transcendentals))


def params(**kw):
    return pltpu.CompilerParams(vmem_limit_bytes=60 * 1024 * 1024, **kw)


def project_kernel(slot_chunks, steps, tile, meta, u_ref, g_ref, w_ref, proj_ref, e_ref, ht_ref, h_ref):
    j = pl.program_id(0)
    total = meta[0]
    chunks = 2 * slot_chunks

    @pl.when(j == 0)
    def _():
        for k in range(chunks):

            @pl.when(k < total)
            def _():
                start = pl.multiple_of(source_chunk(meta, k, slot_chunks) * Q, Q)
                x = u_ref[pl.ds(start, Q), :].astype(f32)
                scale = lax.rsqrt(jnp.mean(x * x, axis=-1, keepdims=True) + epsilon)
                normed = x * scale * g_ref[...]
                h_ref[k * Q : (k + 1) * Q, :] = normed.astype(bf16)
                turned = normed.T.astype(bf16)
                for n in range(D // H_UNIT):
                    there = pl.ds(unit_row(jnp.int32(n), H_UNIT, 1), H_UNIT)
                    ht_ref[there, k * Q : (k + 1) * Q] = turned[n * H_UNIT : (n + 1) * H_UNIT, :]

            @pl.when(k >= total)
            def _():
                ht_ref[:, k * Q : (k + 1) * Q] = jnp.zeros((D, Q), bf16)

    edge = XBC + INNER - (steps - 1) * tile

    def live(rows):
        def part(n, _):
            cols = pl.ds(pl.multiple_of(n * 256, 256), 256)
            proj_ref[0:rows, cols] = dot_nn(h_ref[0:rows, :], w_ref[:, cols]).astype(bf16)
            return 0

        lax.fori_loop(0, tile // 256, part, 0)

    for_live(total, chunks, live)

    @pl.when(j == steps - 1)
    def _():
        def steps_of(k, _):
            r = pl.ds(pl.multiple_of(k * Q, Q), Q)
            tail = dot_nn(h_ref[r, :], w_ref[:, edge : edge + 128])
            e_ref[r, :] = jnp.where(lane_iota(tail.shape) < HEADS, tail, 0.0)
            return 0

        lax.fori_loop(0, total, steps_of, 0)


def project(meta, u, g1, w1):
    rows = u.shape[0]
    tile = 512
    steps = pl.cdiv(PROJ, tile)
    return pl.pallas_call(
        functools.partial(project_kernel, rows // Q // 2, steps, tile),
        out_shape=(
            jax.ShapeDtypeStruct((rows, PROJ), bf16),
            jax.ShapeDtypeStruct((rows, 128), f32),
            jax.ShapeDtypeStruct((D, rows), bf16),
        ),
        grid_spec=pltpu.PrefetchScalarGridSpec(
            num_scalar_prefetch=1,
            grid=(steps,),
            in_specs=[
                pl.BlockSpec((rows, D), lambda j, m: (0, 0)),
                pl.BlockSpec((1, D), lambda j, m: (0, 0)),
                pl.BlockSpec((D, tile), lambda j, m: (0, j)),
            ],
            out_specs=[
                pl.BlockSpec((rows, tile), lambda j, m: (0, j)),
                pl.BlockSpec((rows, 128), lambda j, m: (0, 0)),
                pl.BlockSpec((D, rows), lambda j, m: (0, 0)),
            ],
            scratch_shapes=[pltpu.VMEM((rows, D), bf16)],
        ),
        compiler_params=params(),
        cost_estimate=cost(2 * rows * D * PROJ, 2 * (D * PROJ + rows * PROJ)),
        name="project",
    )(meta, u, g1, w1)


def conv_tile(buf, wc_ref, lanes):
    c = wc_ref[CONV : CONV + 1, lanes]
    for tap in range(CONV):
        c = c + wc_ref[tap : tap + 1, lanes] * buf[5 + tap : 5 + tap + Q, lanes]
    return c


def step_sizes(e_ref, par_ref):
    raw = e_ref[...] + par_ref[0:1, :]
    dt = jnp.maximum(raw, 0.0) + jnp.log1p(jnp.exp(-jnp.abs(raw)))
    decay = par_ref[1:2, :]
    lower = (row_iota((Q, Q)) >= lane_iota((Q, Q))).astype(f32)
    cum = dot_nn(lower, dt * (decay * LOG2E), precision=lax.Precision.HIGHEST)
    return raw, dt, cum


def head_column(values, n):
    return jnp.broadcast_to(values[:, n : n + 1], (Q, 128))


def head_pair(values, n):
    index = n + (lane_iota((Q, 128)) >= HEADDIM).astype(jnp.int32)
    return jnp.take_along_axis(values, index, axis=1, mode="promise_in_bounds")


def next_heads(ref, values, used):
    ref[...] = pltpu.roll(values, 128 - used, 1)


def split_pair(v, low):
    zero = jnp.zeros_like(v)
    return jnp.concatenate([jnp.where(low, v, zero), jnp.where(low, zero, v)], axis=0)


def mixer_kernel(
    unroll, meta, proj_ref, e_ref, cot_ref, wc_ref, par_ref, skip_ref, g_ref,
    o_ref, ot_ref, y_ref, sin_ref, err_ref,
    buf, state, cum_ref, dts_ref, row_ref, q_ref, place_ref,
):
    k = pl.program_id(0)
    total = meta[0]

    @pl.when(k == 0)
    def _():
        def fill(n, _):
            place_ref[n] = unit_row(n, O_UNIT, 3)
            return 0

        lax.fori_loop(0, INNER // O_UNIT, fill, 0)

    @pl.when((k == total) & (lax.rem(total, 2) == 1))
    def _():
        o_ref[...] = jnp.zeros_like(o_ref)
        ot_ref[...] = jnp.zeros_like(ot_ref)
        err_ref[...] = jnp.zeros_like(err_ref)

    @pl.when(k < total)
    def _():
        live = row_iota((Q, D)) < live_rows(meta, k)
        err_ref[...] = jnp.where(live, cot_ref[...].astype(f32), 0.0).astype(bf16)
        first = (k == 0) | (k == meta[1])

        @pl.when(first)
        def _():
            buf[0:8, :] = jnp.zeros((8, XBC), f32)
            state[...] = jnp.zeros_like(state)

        @pl.when(jnp.logical_not(first))
        def _():
            buf[0:8, :] = buf[Q : Q + 8, :]

        buf[8 : 8 + Q, :] = proj_ref[:, INNER : INNER + XBC].astype(f32)
        tail_lanes = slice(INNER, XBC)
        c = conv_tile(buf, wc_ref, tail_lanes)
        act = c * sigmoid(c)
        keys = act[:, :STATE]
        queries = act[:, STATE:].astype(bf16)
        keys_t = keys.T.astype(bf16)
        scores = dot_nn(queries, keys_t)
        _, dt, cum = step_sizes(e_ref, par_ref)
        row_ref[...] = cum.T
        cum_ref[...] = cum
        dts_ref[...] = dt
        lower = row_iota((Q, Q)) >= lane_iota((Q, Q))
        low = lane_iota((Q, 128)) < HEADDIM
        scores = jnp.where(lower, scores, 0.0)

        def pair(p, cums, dts, at):
            lanes = pl.ds(pl.multiple_of(p * 128, 128), 128)
            c = conv_tile(buf, wc_ref, lanes)
            values = c * sigmoid(c)
            col0, col1 = head_column(cums, at), head_column(cums, at + 1)
            both = head_pair(cums, at)
            end = both[Q - 1 : Q, :]
            stepped = values * head_pair(dts, at)
            parts = split_pair(stepped.astype(bf16), low)
            mix = []
            for n, col in enumerate((col0, col1)):
                decay = jnp.exp2(jnp.minimum(col - row_ref[pl.ds(2 * p + n, 1), :], 0.0))
                mix.append((scores * decay).astype(bf16))
            y = dot_nn(jnp.concatenate(mix, axis=1), parts)
            before = state[:, lanes]
            before_low = before.astype(bf16)
            sin_ref[0, :, lanes] = before_low
            y = y + dot_nn(queries, before_low) * jnp.exp2(both)
            y = y + skip_ref[:, lanes] * values
            state[:, lanes] = before * jnp.exp2(end) + dot_nn(
                keys_t, (stepped * jnp.exp2(end - both)).astype(bf16)
            )
            z = proj_ref[:, lanes].astype(f32)
            gated = y * (z * sigmoid(z))
            y_ref[:, lanes] = y.astype(bf16)
            q_ref[:, lanes] = gated
            return gated * gated

        def body(i, squares):
            cums, dts = cum_ref[...], dts_ref[...]
            for n in range(unroll):
                squares = squares + pair(i * unroll + n, cums, dts, 2 * n)
            next_heads(cum_ref, cums, 2 * unroll)
            next_heads(dts_ref, dts, 2 * unroll)
            return squares

        squares = lax.fori_loop(0, PAIRS // unroll, body, jnp.zeros((Q, 128), f32))
        scale = lax.rsqrt(jnp.sum(squares, axis=-1, keepdims=True) / INNER + epsilon)

        def finish(p, _):
            lanes = pl.ds(pl.multiple_of(p * 128, 128), 128)
            out = q_ref[:, lanes] * scale * g_ref[:, lanes]
            o_ref[:, lanes] = out.astype(bf16)
            turned = out.T.astype(bf16)
            for n in range(128 // O_UNIT):
                there = pl.ds(pl.multiple_of(place_ref[p * (128 // O_UNIT) + n], O_UNIT), O_UNIT)
                ot_ref[there, :] = turned[n * O_UNIT : (n + 1) * O_UNIT, :]
            return 0

        lax.fori_loop(0, PAIRS, finish, 0, unroll=6)


def mixer(meta, proj, e, cot, wc, par, skip, g2):
    rows = proj.shape[0]
    chunks = rows // Q
    const = lambda k, m: (0, 0)
    live = lambda k, m: (last_live(m, k), 0)
    return pl.pallas_call(
        functools.partial(mixer_kernel, 4),
        out_shape=(
            jax.ShapeDtypeStruct((rows, INNER), bf16),
            jax.ShapeDtypeStruct((INNER, rows), bf16),
            jax.ShapeDtypeStruct((rows, INNER), bf16),
            jax.ShapeDtypeStruct((chunks, STATE, INNER), bf16),
            jax.ShapeDtypeStruct((rows, D), bf16),
        ),
        grid_spec=pltpu.PrefetchScalarGridSpec(
            num_scalar_prefetch=1,
            grid=(chunks,),
            in_specs=[
                pl.BlockSpec((Q, PROJ), live),
                pl.BlockSpec((Q, 128), live),
                pl.BlockSpec((Q, D), lambda k, m: (source_chunk(m, last_live(m, k), chunks // 2), 0)),
                pl.BlockSpec((8, XBC), const),
                pl.BlockSpec((8, 128), const),
                pl.BlockSpec((1, INNER), const),
                pl.BlockSpec((1, INNER), const),
            ],
            out_specs=[
                pl.BlockSpec((Q, INNER), lambda k, m: (last_padded(m, k), 0)),
                pl.BlockSpec((INNER, Q), lambda k, m: (0, last_padded(m, k))),
                pl.BlockSpec((Q, INNER), live),
                pl.BlockSpec((1, STATE, INNER), lambda k, m: (last_live(m, k), 0, 0)),
                pl.BlockSpec((Q, D), lambda k, m: (last_padded(m, k), 0)),
            ],
            scratch_shapes=[
                pltpu.VMEM((Q + 8, XBC), f32),
                pltpu.VMEM((STATE, INNER), f32),
                pltpu.VMEM((Q, 128), f32),
                pltpu.VMEM((Q, 128), f32),
                pltpu.VMEM((128, Q), f32),
                pltpu.VMEM((Q, INNER), f32),
                pltpu.SMEM((INNER // O_UNIT,), jnp.int32),
            ],
        ),
        compiler_params=params(),
        cost_estimate=cost(chunks * PAIRS * 8 * 2 * Q * 128 * 128, 2 * rows * (PROJ + 3 * INNER)),
        name="mixer",
    )(meta, proj, e, cot, wc, par, skip, g2)


def gate_kernel(
    slot_chunks, meta, u_ref, err_ref, w_ref, o_ref, y_ref, z_ref, g_ref,
    out_ref, dy_ref, dz_ref, gi_ref,
    do_ref,
):
    b = pl.program_id(0)
    total = meta[0]

    @pl.when(b == 0)
    def _():
        out_ref[...] = jnp.zeros_like(out_ref)
        gi_ref[...] = jnp.zeros_like(gi_ref)

    def body(rows):
        halves = rows // Q
        if halves == 1:
            dz_ref[Q:, :] = jnp.zeros((Q, INNER), bf16)
        starts = []
        for n in range(halves):
            k = 2 * b + n
            start = pl.multiple_of(source_chunk(meta, k, slot_chunks) * Q, Q)
            starts.append(start)
        branch = dot_nn(o_ref[0:rows, :], w_ref[...])
        for n in range(halves):
            live = row_iota((Q, D)) < live_rows(meta, 2 * b + n)
            here = pl.ds(starts[n], Q)
            value = u_ref[here, :].astype(f32) + branch[n * Q : (n + 1) * Q, :]
            out_ref[here, :] = jnp.where(live, value, 0.0).astype(bf16)
        do_ref[0:rows, :] = dot_nt(err_ref[0:rows, :], w_ref[...])

        def sums(p, carry):
            squares, crossed = carry
            lanes = pl.ds(pl.multiple_of(p * 128, 128), 128)
            z = z_ref[0:rows, lanes].astype(f32)
            q = y_ref[0:rows, lanes].astype(f32) * (z * sigmoid(z))
            return squares + q * q, crossed + q * g_ref[:, lanes] * do_ref[0:rows, lanes]

        zero = jnp.zeros((rows, 128), f32)
        squares, crossed = lax.fori_loop(0, PAIRS, sums, (zero, zero), unroll=1)
        scale = lax.rsqrt(jnp.sum(squares, axis=-1, keepdims=True) / INNER + epsilon)
        factor = scale * scale * scale * (jnp.sum(crossed, axis=-1, keepdims=True) / INNER)

        def back(p, _):
            lanes = pl.ds(pl.multiple_of(p * 128, 128), 128)
            z = z_ref[0:rows, lanes].astype(f32)
            y = y_ref[0:rows, lanes].astype(f32)
            s = sigmoid(z)
            gate = z * s
            q = y * gate
            do = do_ref[0:rows, lanes]
            gi_ref[:, lanes] += jnp.sum(do * q * scale, axis=0, keepdims=True)
            dq = scale * (g_ref[:, lanes] * do) - q * factor
            dy_ref[0:rows, lanes] = (dq * gate).astype(bf16)
            dz_ref[0:rows, lanes] = (dq * y * (s * (1.0 + z * (1.0 - s)))).astype(bf16)
            return 0

        lax.fori_loop(0, PAIRS, back, 0, unroll=1)

    pl.when(total >= 2 * b + 2)(functools.partial(body, 2 * Q))
    pl.when(total == 2 * b + 1)(functools.partial(body, Q))


def last_block(m, b):
    return jnp.minimum(b, (m[0] + 1) // 2 - 1)


def gate(meta, u, err, w2, o, y, proj, g2):
    rows = u.shape[0]
    blocks = rows // (2 * Q)
    const = lambda b, m: (0, 0)
    live = lambda b, m: (last_block(m, b), 0)
    once = pl.Buffered(1)
    return pl.pallas_call(
        functools.partial(gate_kernel, rows // Q // 2),
        out_shape=(
            jax.ShapeDtypeStruct((rows, D), bf16),
            jax.ShapeDtypeStruct((rows, INNER), bf16),
            jax.ShapeDtypeStruct((rows, INNER), bf16),
            jax.ShapeDtypeStruct((1, INNER), f32),
        ),
        grid_spec=pltpu.PrefetchScalarGridSpec(
            num_scalar_prefetch=1,
            grid=(blocks,),
            in_specs=[
                pl.BlockSpec((rows, D), const, pipeline_mode=once),
                pl.BlockSpec((2 * Q, D), live),
                pl.BlockSpec((INNER, D), const, pipeline_mode=once),
                pl.BlockSpec((2 * Q, INNER), live),
                pl.BlockSpec((2 * Q, INNER), live),
                pl.BlockSpec((2 * Q, INNER), live),
                pl.BlockSpec((1, INNER), const),
            ],
            out_specs=[
                pl.BlockSpec((rows, D), const),
                pl.BlockSpec((2 * Q, INNER), live),
                pl.BlockSpec((2 * Q, INNER), live),
                pl.BlockSpec((1, INNER), const),
            ],
            scratch_shapes=[pltpu.VMEM((2 * Q, INNER), f32)],
        ),
        compiler_params=params(),
        cost_estimate=cost(4 * rows * D * INNER, 2 * (D * INNER + 5 * rows * INNER)),
        name="gate",
    )(meta, u, err, w2, o, y, proj, g2)


def back_kernel(
    unroll, part, parts, meta, x_ref, prev_ref, e_ref, dy_ref, sin_ref, wc_ref, par_ref, skip_ref, *rest
):
    carried, rest = (rest[:6], rest[6:]) if part > 0 else ((), rest)
    dx_ref, gconv_ref, gpar_ref, gskip_ref = rest[:4]
    passed_on, rest = (rest[4:6], rest[6:]) if part < parts - 1 else ((), rest[4:])
    buf, dbuf, dstate, cum_ref, dts_ref, row_ref, da_ref = rest
    i = pl.program_id(0)
    total = meta[0]
    begin, end = part_span(meta, part, parts)
    k = total - begin - i

    @pl.when(i == 0)
    def _():
        da_ref[...] = jnp.zeros_like(da_ref)
        if part == 0:
            gconv_ref[...] = jnp.zeros_like(gconv_ref)
            gpar_ref[...] = jnp.zeros_like(gpar_ref)
            gskip_ref[...] = jnp.zeros_like(gskip_ref)

            @pl.when(lax.rem(total, 2) == 1)
            def _():
                dx_ref[...] = jnp.zeros_like(dx_ref)

        else:
            for to, came in zip((gconv_ref, gpar_ref, gskip_ref, dstate), carried[1:5]):
                to[...] = came[...]
            dbuf[0:8, :] = carried[5][...]

    @pl.when((i >= 1) & (i <= end - begin))
    def _():
        first = (k == 0) | (k == meta[1])
        last = (k == total - 1) | (k == meta[1] - 1)

        @pl.when(first)
        def _():
            buf[0:8, :] = jnp.zeros((8, XBC), f32)

        @pl.when(jnp.logical_not(first))
        def _():
            buf[0:8, :] = prev_ref[8:16, INNER : INNER + XBC].astype(f32)

        @pl.when(last)
        def _():
            dbuf[Q : Q + 8, :] = jnp.zeros((8, XBC), f32)
            dstate[...] = jnp.zeros_like(dstate)

        @pl.when(jnp.logical_not(last))
        def _():
            dbuf[Q : Q + 8, :] = dbuf[0:8, :]

        buf[8 : 8 + Q, :] = x_ref[:, INNER : INNER + XBC].astype(f32)
        tail_lanes = slice(INNER, XBC)
        c_tail = conv_tile(buf, wc_ref, tail_lanes)
        s_tail = sigmoid(c_tail)
        act = c_tail * s_tail
        keys = act[:, :STATE].astype(bf16)
        queries = act[:, STATE:].astype(bf16)
        queries_t = act[:, STATE:].T.astype(bf16)
        scores = dot_nn(keys, queries_t)
        raw, dt, cum = step_sizes(e_ref, par_ref)
        row_ref[...] = cum.T
        cum_ref[...] = cum
        dts_ref[...] = dt
        upper = row_iota((Q, Q)) <= lane_iota((Q, Q))
        strict = row_iota((Q, Q)) < lane_iota((Q, Q))
        after = (row_iota((Q, Q)) >= lane_iota((Q, Q))).astype(bf16)
        low = lane_iota((Q, 128)) < HEADDIM
        scores = jnp.where(upper, scores, 0.0)
        half = (lax.broadcasted_iota(jnp.int32, (128, 128), 0) >= HEADDIM).astype(jnp.int32)
        head_lane = lane_iota((128, 128))

        def conv_back(lanes, dc):
            dbuf[0:Q, lanes] = dc
            dxbc = wc_ref[CONV - 1 : CONV, lanes] * dc
            for tap in range(CONV - 1):
                dxbc = dxbc + wc_ref[tap : tap + 1, lanes] * dbuf[3 - tap : 3 - tap + Q, lanes]
            dx_ref[:, lanes] = dxbc.astype(bf16)
            for tap in range(CONV):
                gconv_ref[tap : tap + 1, lanes] += jnp.sum(dc * buf[5 + tap : 5 + tap + Q, lanes], axis=0, keepdims=True)
            gconv_ref[CONV : CONV + 1, lanes] += jnp.sum(dc, axis=0, keepdims=True)

        def pair(p, cums, dts, at, carry):
            dscores, dquery, dkey, from_start, to_end, direct, thru = carry
            lanes = pl.ds(pl.multiple_of(p * 128, 128), 128)
            c = conv_tile(buf, wc_ref, lanes)
            s = sigmoid(c)
            values = c * s
            col0, col1 = head_column(cums, at), head_column(cums, at + 1)
            both = head_pair(cums, at)
            end = both[Q - 1 : Q, :]
            grown = jnp.exp2(both)
            rest = jnp.exp2(end - both)
            dtp = head_pair(dts, at)
            stepped = values * dtp
            dy_low = dy_ref[:, lanes]
            dy = dy_low.astype(f32)
            parts = split_pair(dy_low, low)
            stepped_low = stepped.astype(bf16)
            dmix = dot_nt(stepped_low, parts)
            mix = []
            for n, col in enumerate((col0, col1)):
                decay = jnp.exp2(jnp.minimum(row_ref[pl.ds(2 * p + n, 1), :] - col, 0.0))
                weighted = dmix[:, n * Q : (n + 1) * Q] * decay
                dscores = dscores + weighted
                mix.append((scores * decay).astype(bf16))
                passed = dot_nn((weighted * scores).astype(bf16), after)
                da_ref[pl.ds(2 * p + n, 1), :] = jnp.sum(jnp.where(strict, passed, 0.0), axis=0, keepdims=True)
            dstepped = dot_nn(jnp.concatenate(mix, axis=1), parts)
            dafter = dstate[:, lanes]
            dafter_low = dafter.astype(bf16)
            before_low = sin_ref[0, :, lanes]
            dend = dot_nn(keys, dafter_low) * rest
            grown_dy = (dy * grown).astype(bf16)
            select = (head_lane == 2 * p + half).astype(bf16)
            across = dot_nn(queries, before_low)
            from_start = from_start + dot_nn((across * grown * dy).astype(bf16), select)
            to_end = to_end + dot_nn((stepped * dend).astype(bf16), select)
            dstepped = dstepped + dend
            direct = direct + dot_nn((values * dstepped).astype(bf16), select)
            dquery = dquery + dot_nt(grown_dy, before_low)
            dkey = dkey + dot_nt((stepped * rest).astype(bf16), dafter_low)
            kept = jnp.exp2(end) * dafter
            held = jnp.sum((kept * before_low.astype(f32)).reshape(8, 16, 128), axis=0)
            thru = thru + dot_nn(held.astype(bf16), select)
            dstate[:, lanes] = kept + dot_nn(queries_t, grown_dy)
            dvalues = dstepped * dtp + skip_ref[:, lanes] * dy
            gskip_ref[:, lanes] += jnp.sum(dy * values, axis=0, keepdims=True)
            conv_back(lanes, dvalues * (s + values * (1.0 - s)))
            return dscores, dquery, dkey, from_start, to_end, direct, thru

        def body(n, carry):
            cums, dts = cum_ref[...], dts_ref[...]
            for m in range(unroll):
                carry = pair(n * unroll + m, cums, dts, 2 * m, carry)
            next_heads(cum_ref, cums, 2 * unroll)
            next_heads(dts_ref, dts, 2 * unroll)
            return carry

        zero = jnp.zeros((Q, 128), f32)
        start = (zero,) * 6 + (jnp.zeros((16, 128), f32),)
        carry = lax.fori_loop(0, PAIRS // unroll, body, start)
        dscores, dquery, dkey, from_start, to_end, direct, thru = carry
        dscores = jnp.where(upper, dscores, 0.0)
        dkey = dkey + dot_nn(dscores.astype(bf16), queries)
        dquery = dquery + dot_nn(dscores.T.astype(bf16), keys)
        slope = s_tail * (1.0 + c_tail * (1.0 - s_tail))
        conv_back(slice(INNER, INNER + STATE), dkey * slope[:, :STATE])
        conv_back(slice(INNER + STATE, XBC), dquery * slope[:, STATE:])

        tail_sum = (row_iota((Q, Q)) <= lane_iota((Q, Q))).astype(f32)
        head_sum = (row_iota((Q, Q)) > lane_iota((Q, Q))).astype(f32)
        da = (
            da_ref[...].T
            + dot_nn(tail_sum, from_start, precision=lax.Precision.HIGHEST)
            + dot_nn(head_sum, to_end, precision=lax.Precision.HIGHEST)
            + jnp.sum(thru, axis=0, keepdims=True)
        )
        ddt = par_ref[1:2, :] * da + direct
        de = ddt * sigmoid(raw)
        de = jnp.where(lane_iota((Q, 128)) < HEADS, de, 0.0)
        dx_ref[:, XBC:] = de.astype(bf16)
        gpar_ref[0:1, :] += jnp.sum(de, axis=0, keepdims=True)
        gpar_ref[1:2, :] += jnp.sum(dt * da, axis=0, keepdims=True)

    if passed_on:

        @pl.when(i == pl.num_programs(0) - 1)
        def _():
            passed_on[0][...] = dstate[...]
            passed_on[1][...] = dbuf[0:8, :]


def part_span(meta, part, parts):
    return (meta[0] * part + parts - 1) // parts, (meta[0] * (part + 1) + parts - 1) // parts


def back(meta, part, parts, carried, proj, e, dy, sin, wc, par, skip):
    rows = proj.shape[0]
    chunks = rows // Q
    const = lambda i, m: (0, 0)

    def chunk(i, m):
        begin, end = part_span(m, part, parts)
        return jnp.clip(m[0] - begin - jnp.clip(i, 1, jnp.maximum(end - begin, 1)), 0, m[0] - 1)

    def written(i, m):
        begin, end = part_span(m, part, parts)
        block = jnp.where(end > begin, chunk(i, m), chunks)
        return jnp.where(i == 0, last_padded(m, m[0]), block) if part == 0 else block

    here = lambda i, m: (chunk(i, m), 0)
    out_shape = [
        jax.ShapeDtypeStruct((rows + Q, XE), bf16),
        jax.ShapeDtypeStruct((8, XBC), f32),
        jax.ShapeDtypeStruct((8, 128), f32),
        jax.ShapeDtypeStruct((1, INNER), f32),
    ]
    sums = [pl.BlockSpec((8, XBC), const), pl.BlockSpec((8, 128), const), pl.BlockSpec((1, INNER), const)]
    state = [pl.BlockSpec((STATE, INNER), const), pl.BlockSpec((8, XBC), const)]
    in_specs = [
        pl.BlockSpec((Q, PROJ), here),
        pl.BlockSpec((16, PROJ), lambda i, m: (jnp.maximum(chunk(i, m) * (Q // 16) - 1, 0), 0)),
        pl.BlockSpec((Q, 128), here),
        pl.BlockSpec((Q, INNER), here),
        pl.BlockSpec((1, STATE, INNER), lambda i, m: (chunk(i, m), 0, 0)),
        pl.BlockSpec((8, XBC), const),
        pl.BlockSpec((8, 128), const),
        pl.BlockSpec((1, INNER), const),
    ]
    out_specs = [pl.BlockSpec((Q, XE), lambda i, m: (written(i, m), 0))] + sums
    if part > 0:
        in_specs += [pl.BlockSpec(memory_space=pl.ANY)] + sums + state
    if part < parts - 1:
        out_shape += [jax.ShapeDtypeStruct((STATE, INNER), f32), jax.ShapeDtypeStruct((8, XBC), f32)]
        out_specs += state
    steps = -(-chunks // parts)
    return pl.pallas_call(
        functools.partial(back_kernel, 6, part, parts),
        out_shape=out_shape,
        grid_spec=pltpu.PrefetchScalarGridSpec(
            num_scalar_prefetch=1,
            grid=(steps + 1,),
            in_specs=in_specs,
            out_specs=out_specs,
            scratch_shapes=[
                pltpu.VMEM((Q + 8, XBC), f32),
                pltpu.VMEM((Q + 8, XBC), f32),
                pltpu.VMEM((STATE, INNER), f32),
                pltpu.VMEM((Q, 128), f32),
                pltpu.VMEM((Q, 128), f32),
                pltpu.VMEM((128, Q), f32),
                pltpu.VMEM((128, Q), f32),
            ],
        ),
        input_output_aliases={9: 0} if part > 0 else {},
        compiler_params=params(),
        cost_estimate=cost(steps * PAIRS * 20 * 2 * Q * 128 * 128, 2 * steps * Q * (PROJ + 3 * INNER)),
        name="back",
    )(meta, proj, proj, e, dy, sin, wc, par, skip, *carried)


def weight_kernel(rows, swap_from, meta, at_ref, b_ref, mine_ref, other_ref):
    used = (meta[0] + 1) // 2
    half = at_ref.shape[0] // 2
    part_rows = half // 4
    swap = pl.program_id(0) >= swap_from

    def part(width):
        for c, out_ref in enumerate((mine_ref, other_ref)):

            def step(m, _):
                here = pl.ds(pl.multiple_of(c * half + 2 * m * part_rows, part_rows), 2 * part_rows)
                res = dot_nn(at_ref[here, 0:width], b_ref[0:width, :]).astype(bf16)
                for n in range(2):
                    place = jnp.where(swap, 2 * n + m, 2 * m + n)
                    there = pl.ds(pl.multiple_of(place * part_rows, part_rows), part_rows)
                    out_ref[there, :] = res[n * part_rows : (n + 1) * part_rows, :]
                return 0

            lax.fori_loop(0, 2, step, 0)

    for n in range(1, rows // (2 * Q) + 1):
        pl.when(used == n)(functools.partial(part, n * 2 * Q))


def weight_grad(meta, at, b, first, width, tile, swap_from):
    height, rows = at.shape
    offset = first // tile
    half = jax.ShapeDtypeStruct((height // 2, width), bf16)
    half_spec = pl.BlockSpec((height // 2, tile), lambda j, m: (0, j))
    return pl.pallas_call(
        functools.partial(weight_kernel, rows, swap_from),
        out_shape=(half, half),
        grid_spec=pltpu.PrefetchScalarGridSpec(
            num_scalar_prefetch=1,
            grid=(pl.cdiv(width, tile),),
            in_specs=[
                pl.BlockSpec((height, rows), lambda j, m: (0, 0)),
                pl.BlockSpec((rows, tile), lambda j, m: (0, j + offset)),
            ],
            out_specs=(half_spec, half_spec),
        ),
        compiler_params=params(),
        cost_estimate=cost(2 * rows * height * width, 2 * (rows * (height + width) + height * width)),
        name="weight_grad",
    )(meta, at, b)


def input_kernel(
    slot_chunks, steps, tile, meta, u_ref, err_ref, g_ref, dz_ref, dx_ref, w_ref, out0_ref, out1_ref, gn_ref, dh_ref
):
    j = pl.program_id(0)
    total = meta[0]
    chunks = 2 * slot_chunks
    last = w_ref[:, INNER + XBC : PROJ]
    cols = pl.ds(pl.multiple_of(j * tile, tile), tile)

    def live(rows):
        dh_ref[0:rows, cols] = (
            dot_nt(dz_ref[0:rows, :], w_ref[:, 0:INNER])
            + dot_nt(dx_ref[0:rows, 0:XBC], w_ref[:, INNER : INNER + XBC])
            + dot_nt(dx_ref[0:rows, XBC : XBC + HEADS], last)
        )

    for_live(total, chunks, live)

    @pl.when(j == steps - 1)
    def _():
        out0_ref[...] = jnp.zeros_like(out0_ref)
        out1_ref[...] = jnp.zeros_like(out1_ref)
        gn_ref[...] = jnp.zeros_like(gn_ref)
        for k in range(chunks):

            @pl.when(k < total)
            def _():
                start = pl.multiple_of(source_chunk(meta, k, slot_chunks) * Q, Q)
                u = u_ref[pl.ds(start, Q), :].astype(f32)
                err = err_ref[k * Q : (k + 1) * Q, :].astype(f32)
                scale = lax.rsqrt(jnp.mean(u * u, axis=-1, keepdims=True) + epsilon)
                dh = dh_ref[k * Q : (k + 1) * Q, :]
                gn_ref[...] += jnp.sum(dh * (u * scale), axis=0, keepdims=True)
                n = dh * g_ref[...]
                inner = jnp.mean(u * n, axis=-1, keepdims=True)
                du = (err + scale * n - u * (scale * scale * scale * inner)).astype(bf16)

                @pl.when(k < meta[1])
                def _():
                    out0_ref[pl.ds(start, Q), :] = du

                @pl.when(k >= meta[1])
                def _():
                    out1_ref[pl.ds(pl.multiple_of(start - slot_chunks * Q, Q), Q), :] = du


def input_grad_of(meta, u, err, g1, dz, dx, w1):
    rows = u.shape[0]
    tile = 256
    steps = D // tile
    const = lambda j, m: (0, 0)
    once = pl.Buffered(1)
    return pl.pallas_call(
        functools.partial(input_kernel, rows // Q // 2, steps, tile),
        out_shape=(
            jax.ShapeDtypeStruct((rows // 2, D), bf16),
            jax.ShapeDtypeStruct((rows // 2, D), bf16),
            jax.ShapeDtypeStruct((1, D), f32),
        ),
        grid_spec=pltpu.PrefetchScalarGridSpec(
            num_scalar_prefetch=1,
            grid=(steps,),
            in_specs=[
                pl.BlockSpec((rows, D), const, pipeline_mode=once),
                pl.BlockSpec((rows, D), const, pipeline_mode=once),
                pl.BlockSpec((1, D), const),
                pl.BlockSpec((rows, INNER), const, pipeline_mode=once),
                pl.BlockSpec((rows, XE), const, pipeline_mode=once),
                pl.BlockSpec((tile, w1.shape[1]), lambda j, m: (j, 0)),
            ],
            out_specs=[
                pl.BlockSpec((rows // 2, D), const),
                pl.BlockSpec((rows // 2, D), const),
                pl.BlockSpec((1, D), const),
            ],
            scratch_shapes=[pltpu.VMEM((rows, D), f32)],
        ),
        compiler_params=params(),
        cost_estimate=cost(2 * rows * D * PROJ, 2 * (D * PROJ + rows * PROJ)),
        name="input_grad",
    )(meta, u, err, g1, dz, dx, w1)


def partner(value, axis, bit):
    mask = 2**bit
    pairs = [(source, source ^ mask) for source in range(lax.axis_size(axis))]
    return lax.ppermute(value, axis, pairs)


def log2(size):
    return size.bit_length() - 1


def halving_order(swap):
    fsdp = [("fsdp", bit) for bit in range(log2(lax.axis_size("fsdp")))]
    near = [("dp", 1)]
    far = [("dp", bit) for bit in range(2, log2(lax.axis_size("dp")))]
    return [("dp", 0)] + (near + fsdp if swap else fsdp + near) + far


def flat_bit(axis, bit):
    return bit + (log2(lax.axis_size("fsdp")) if axis == "dp" else 0)


def kept_at(order, owner):
    away = owner ^ lax.axis_index(AXES)
    place = jnp.zeros_like(away)
    for axis, bit in order:
        place = 2 * place + ((away >> flat_bit(axis, bit)) & 1)
    return place


def owner_at(order, place):
    away = jnp.zeros_like(place)
    for n, (axis, bit) in enumerate(order):
        away = away + (((place >> (len(order) - 1 - n)) & 1) << flat_bit(axis, bit))
    return away ^ lax.axis_index(AXES)


class Term:
    def __init__(self, value):
        self.value = value


class Columns:
    def __init__(self, width, swap):
        self.order = halving_order(swap)
        self.width = width
        self.terms = []
        self.phase = 0

    def done(self):
        return self.phase == len(self.order)

    def sum(self, start, stop):
        return sum(term.value[start:stop, at : at + self.width].astype(f32) for term, at in self.terms)

    def halve(self):
        self.rows //= 2
        return self.sum(self.rows, 2 * self.rows).astype(bf16)


class Chain:
    def __init__(self, halves, columns, grouped):
        mine, other = halves
        self.columns = columns
        if not grouped:
            count = lax.axis_size(AXES)
            whole = jnp.concatenate([mine, other]).reshape(count, -1, mine.shape[1])
            parts = []
            at = 0
            for c in columns:
                parts.append(whole[:, :, at : at + c.width][owner_at(c.order, jnp.arange(count))])
                at += c.width
            mine, other = jnp.concatenate(parts, axis=2).reshape(2, -1, mine.shape[1])
        self.going = [(columns, other)]
        kept = Term(mine)
        at = 0
        for c in columns:
            c.rows = mine.shape[0]
            c.terms.append((kept, at))
            at += c.width

    def halve(self):
        groups = {}
        for c in self.columns:
            if not c.done() and all(c not in members for members, _ in self.going):
                groups.setdefault((c.order[c.phase], c.rows), []).append(c)
        for members in groups.values():
            sent = [c.halve() for c in members]
            self.going.append((members, jnp.concatenate(sent, axis=1) if len(sent) > 1 else sent[0]))

    def exchange(self):
        for members, sent in self.going:
            first = members[0]
            came = Term(partner(sent, *first.order[first.phase]))
            at = 0
            for c in members:
                c.terms.append((came, at))
                c.phase += 1
                at += c.width
        self.going = []

    def finish(self):
        while not all(c.done() for c in self.columns):
            self.halve()
            self.exchange()
        return [c.sum(0, c.rows) for c in self.columns]


def tick(token, chains, after):
    last = {id(c.terms[-1][0]): c.terms[-1][0] for chain in chains for c in chain.columns if c.phase > 0}
    if last:
        *came, _ = lax.optimization_barrier([term.value for term in last.values()] + [after])
        for term, value in zip(last.values(), came):
            term.value = value
    for chain in chains:
        chain.halve()
    sent = [value for chain in chains for _, value in chain.going]
    *sent, token = lax.optimization_barrier(sent + [token])
    for chain in chains:
        chain.going = [(members, sent.pop(0)) for members, _ in chain.going]
        chain.exchange()
    return token


W_COLS = 6528
W_SPANS = ((0, 2944), (2944, 2944), (5888, 640))


def gather_kernel(
    count, inner, flag_ref, own_ref, norm_ref, conv_ref, bias_ref, inner_ref, tokens_ref,
    w_ref, wc_ref, g1_ref, g2_ref, u_ref,
    shard_ref, tile_ref, tiles_ref, kept, given,
    send_sem, recv_sem, tile_send, tile_recv, own_sem, give_send, give_recv,
):
    me = lax.axis_index("dp") * inner + lax.axis_index("fsdp")
    height = shard_ref.shape[0]
    x, core, y = flat_bit("fsdp", 0), flat_bit("dp", 0), flat_bit("dp", 1)
    far = [flat_bit("dp", bit) for bit in range(2, log2(lax.axis_size("dp")))]
    ways = (far + [y, x, core], far + [x, y, core], [x, y] + far[::-1] + [core])
    spans = [pl.ds(at, width) for at, width in W_SPANS]
    groups = range(len(spans))

    full = PROJ // 128 * 128
    shard_ref[:, 0:full] = own_ref[:, 0:full].astype(bf16)
    shard_ref[:, full:] = jnp.zeros((height, W_COLS - full), bf16)
    shard_ref[:, full:PROJ] = own_ref[:, full:].astype(bf16)
    tile_ref[...] = jnp.zeros_like(tile_ref)
    for row, ref in ((0, conv_ref), (4, bias_ref), (5, inner_ref), (6, norm_ref)):
        tile_ref[row : row + ref.shape[0], 0 : ref.shape[1]] = ref[...].astype(bf16).astype(f32)

    def place(away):
        return pl.ds(pl.multiple_of(jnp.bitwise_xor(me, away) * height, height), height)

    def link(bit):
        other = jnp.bitwise_xor(me, 2**bit)
        return (other // inner, other % inner)

    def last_step(half, away):
        return max((n for n, bit in enumerate(ways[half]) if (away >> bit) & 1), default=-1)

    def send(half, away, bit):
        src = shard_ref.at[:, spans[half]] if away == 0 else w_ref.at[place(away), spans[half]]
        return pltpu.make_async_remote_copy(
            src_ref=src,
            dst_ref=w_ref.at[place(away), spans[half]],
            send_sem=send_sem.at[half, away ^ 2**bit],
            recv_sem=recv_sem.at[half, away ^ 2**bit],
            device_id=link(bit),
            device_id_type=pl.DeviceIdType.MESH,
        )

    def receive(half, away):
        block = w_ref.at[place(away), spans[half]]
        return pltpu.make_async_remote_copy(
            src_ref=block,
            dst_ref=block,
            send_sem=send_sem.at[half, away],
            recv_sem=recv_sem.at[half, away],
            device_id=link(ways[half][last_step(half, away)]),
            device_id_type=pl.DeviceIdType.MESH,
        )

    def send_on(half, away):
        sends = [send(half, away, bit) for bit in ways[half][last_step(half, away) + 1 :]]
        for one in sends:
            one.start()
        return sends

    def tile_copy(n):
        other = jnp.bitwise_xor(me, n)
        return pltpu.make_async_remote_copy(
            src_ref=tile_ref,
            dst_ref=tiles_ref.at[me],
            send_sem=tile_send.at[n],
            recv_sem=tile_recv.at[n],
            device_id=(other // inner, other % inner),
            device_id_type=pl.DeviceIdType.MESH,
        )

    def start_tile(n, _):
        tile_copy(n).start()
        return 0

    def wait_tile(n, _):
        tile_copy(n).wait()
        return 0

    started = []
    for step in range(len(ways[0])):
        for half in groups:
            one = send(half, 0, ways[half][step])
            one.start()
            started.append(one)
    own = pltpu.make_async_copy(shard_ref, w_ref.at[place(0), :], own_sem.at[0])
    own.start()

    second = jnp.broadcast_to(flag_ref[0, 0], (1, D)) == 1
    rows = kept.shape[0]

    def choose(n, _):
        r = pl.ds(pl.multiple_of(n * 64, 64), 64)
        zero, one = tokens_ref[0, r, :].astype(f32), tokens_ref[1, r, :].astype(f32)
        kept[r, :] = jnp.where(second, one, zero).astype(bf16)
        given[r, :] = jnp.where(second, zero, one).astype(bf16)
        return 0

    lax.fori_loop(0, rows // 64, choose, 0)
    lax.fori_loop(1, count, start_tile, 0)
    tiles_ref[me] = tile_ref[...]

    blocks = [(half, away) for half in groups for away in range(1, count)]
    blocks.sort(key=lambda b: (b[1].bit_count(), last_step(*b), b[0]))
    tail = []
    for n, (half, away) in enumerate(blocks):
        receive(half, away).wait_recv()
        started += send_on(half, away)
        if n == 8:
            keep = pltpu.make_async_copy(kept, u_ref.at[pl.ds(0, rows), :], own_sem.at[1])
            give = pltpu.make_async_remote_copy(
                src_ref=given,
                dst_ref=u_ref.at[pl.ds(rows, rows), :],
                send_sem=give_send,
                recv_sem=give_recv,
                device_id=link(core),
                device_id_type=pl.DeviceIdType.MESH,
            )
            keep.start()
            give.start()
            tail = [keep, give]
        if n == 40:
            lax.fori_loop(1, count, wait_tile, 0)
            wc_ref[...] = jnp.zeros_like(wc_ref)
            for owner in range(count):
                for ref, row, tall in ((wc_ref, 0, 5), (g2_ref, 5, 1), (g1_ref, 6, 1)):
                    each = ref.shape[1] // count
                    ref[0:tall, owner * each : (owner + 1) * each] = tiles_ref[owner, row : row + tall, 0:each]
    for one in started:
        one.wait_send()
    for one in tail:
        one.wait()
    own.wait()


def gather(flag, own, norm, conv, bias, inner, tokens):
    count = lax.axis_size(AXES)
    slot = tokens.shape[1]
    whole = pl.BlockSpec(memory_space=pltpu.VMEM)
    anywhere = pl.BlockSpec(memory_space=pl.ANY)
    dma = pltpu.SemaphoreType.DMA
    return pl.pallas_call(
        functools.partial(gather_kernel, count, lax.axis_size("fsdp")),
        out_shape=(
            jax.ShapeDtypeStruct((D, W_COLS), bf16),
            jax.ShapeDtypeStruct((8, XBC), f32),
            jax.ShapeDtypeStruct((1, D), f32),
            jax.ShapeDtypeStruct((1, INNER), f32),
            jax.ShapeDtypeStruct((2 * slot, D), bf16),
        ),
        in_specs=[pl.BlockSpec(memory_space=pltpu.SMEM)] + [whole] * 6,
        out_specs=(anywhere, whole, whole, whole, anywhere),
        scratch_shapes=[
            pltpu.VMEM((own.shape[0], W_COLS), bf16),
            pltpu.VMEM((8, 128), f32),
            pltpu.VMEM((count, 8, 128), f32),
            pltpu.VMEM((slot, D), bf16),
            pltpu.VMEM((slot, D), bf16),
            dma((len(W_SPANS), count)),
            dma((len(W_SPANS), count)),
            dma((count,)),
            dma((count,)),
            dma((2,)),
            dma,
            dma,
        ],
        compiler_params=params(has_side_effects=True),
        cost_estimate=cost(1e6, 2 * D * W_COLS),
        name="gather",
    )(flag, own, norm, conv, bias, inner, tokens)


def sum_kernel(count, inner, sent_ref, out_ref, came, send_sem, recv_sem):
    me = lax.axis_index("dp") * inner + lax.axis_index("fsdp")

    def copy(n):
        other = jnp.bitwise_xor(me, n)
        return pltpu.make_async_remote_copy(
            src_ref=sent_ref.at[other],
            dst_ref=came.at[n],
            send_sem=send_sem.at[n],
            recv_sem=recv_sem.at[n],
            device_id=(other // inner, other % inner),
            device_id_type=pl.DeviceIdType.MESH,
        )

    def start(n, _):
        copy(n).start()
        return 0

    def add(n, total):
        copy(n).wait()
        return total + came[n]

    lax.fori_loop(1, count, start, 0)
    out_ref[...] = lax.fori_loop(1, count, add, sent_ref[me])


def sum_small(tiles):
    count = tiles.shape[0]
    whole = pl.BlockSpec(memory_space=pltpu.VMEM)
    return pl.pallas_call(
        functools.partial(sum_kernel, count, lax.axis_size("fsdp")),
        out_shape=jax.ShapeDtypeStruct(tiles.shape[1:], f32),
        in_specs=[whole],
        out_specs=whole,
        scratch_shapes=[
            pltpu.VMEM(tiles.shape, f32),
            pltpu.SemaphoreType.DMA((count,)),
            pltpu.SemaphoreType.DMA((count,)),
        ],
        compiler_params=pltpu.CompilerParams(has_side_effects=True),
        cost_estimate=cost(count * 1024, 8 * count * 1024),
        name="sum_small",
    )(tiles)


TILE_ROWS = 16
X_CUT = 1792
X_PIECES = tuple((which, 512 * n, width) for n in range(4) for which, width in ((0, 512 if n < 3 else 256), (1, 512 if n < 3 else 128)))


def finish_kernel(
    count, inner, m0, a0, b0, m1, a1, b1, gconv_ref, gpar_ref, par_ref, gskip_ref, gi_ref, gn_ref, given_ref,
    x_ref, tile_ref, back_ref, *scratch,
):
    sources = ((m0, a0, b0), (m1, a1, b1))
    terms, scratch = scratch[:2], scratch[2:]
    sent, scratch = [scratch[2 * n : 2 * n + 2] for n in range(3)], scratch[6:]
    came, scratch = [scratch[2 * n : 2 * n + 2] for n in range(3)], scratch[6:]
    tiles, tiles_in, load_sem, send_sem, recv_sem, tile_send, tile_recv, give_send, give_recv = scratch
    me = lax.axis_index("dp") * inner + lax.axis_index("fsdp")
    far = [flat_bit("dp", bit) for bit in (2, 3)]
    ways = ([flat_bit("dp", 1)] + far, [flat_bit("fsdp", 0)] + far)
    tall = terms[0].shape[1]

    def target(other):
        return {"device_id": (other // inner, other % inner), "device_id_type": pl.DeviceIdType.MESH}

    def load(n):
        which, at, width = X_PIECES[n]
        cols = pl.ds(at, width)
        return [
            pltpu.make_async_copy(ref.at[pl.ds(0, tall), cols], terms[which].at[i, :, cols], load_sem.at[n, i])
            for i, ref in enumerate(sources[which])
        ]

    def copy(n, phase):
        which, at, width = X_PIECES[n]
        cols = pl.ds(at, width)
        return pltpu.make_async_remote_copy(
            src_ref=sent[phase][which].at[:, cols],
            dst_ref=came[phase][which].at[:, cols],
            send_sem=send_sem.at[n, phase],
            recv_sem=recv_sem.at[n, phase],
            **target(jnp.bitwise_xor(me, 2 ** ways[which][phase])),
        )

    def total(n, phase, start, rows):
        which, at, width = X_PIECES[n]
        parts = [terms[which][i, start : start + rows, at : at + width] for i in range(3)]
        parts += [came[p][which][start : start + rows, at : at + width] for p in range(phase)]
        return sum(part.astype(f32) for part in parts)

    def go(n, phase):
        which, at, width = X_PIECES[n]
        rows = tall >> (phase + 1)
        sent[phase][which][:, at : at + width] = total(n, phase, rows, rows).astype(bf16)
        copy(n, phase).start()

    def tile_copy(n):
        other = jnp.bitwise_xor(me, n)
        return pltpu.make_async_remote_copy(
            src_ref=tiles.at[other],
            dst_ref=tiles_in.at[n],
            send_sem=tile_send.at[n],
            recv_sem=tile_recv.at[n],
            **target(other),
        )

    def start_tile(n, _):
        tile_copy(n).start()
        return 0

    def add_tile(n, value):
        tile_copy(n).wait()
        return value + tiles_in[n]

    give = pltpu.make_async_remote_copy(
        src_ref=given_ref,
        dst_ref=back_ref,
        send_sem=give_send,
        recv_sem=give_recv,
        **target(jnp.bitwise_xor(me, 2 ** flat_bit("dp", 0))),
    )
    pieces = len(X_PIECES)
    for n in range(pieces):
        for one in load(n):
            one.start()
    for n in range(pieces):
        for one in load(n):
            one.wait()
        go(n, 0)
    give.start()

    pick = lax.broadcasted_iota(jnp.int32, (INNER, 128), 0) // HEADDIM == lane_iota((INNER, 128))
    skips = dot_nn(
        jnp.broadcast_to(gskip_ref[...], (8, INNER)), pick.astype(f32), precision=lax.Precision.HIGHEST
    )
    tiles[...] = jnp.zeros_like(tiles)
    for owner in range(count):
        for row, ref in ((0, gconv_ref), (8, gi_ref), (9, gn_ref)):
            each = ref.shape[1] // count
            tiles[owner, row : row + ref.shape[0], 0:each] = ref[:, owner * each : (owner + 1) * each]
        tiles[owner, 10:11, :] = gpar_ref[0:1, :]
        tiles[owner, 11:12, :] = gpar_ref[1:2, :] * par_ref[1:2, :]
        tiles[owner, 12:13, :] = skips[0:1, :]

    lag = 2
    for n in range(pieces + 2 * lag):
        if n < pieces:
            copy(n, 0).wait_recv()
            go(n, 1)
        if n == 1:
            lax.fori_loop(1, count, start_tile, 0)
        if lag <= n < pieces + lag:
            copy(n - lag, 1).wait_recv()
            go(n - lag, 2)
        if n >= 2 * lag:
            which, at, width = X_PIECES[n - 2 * lag]
            copy(n - 2 * lag, 2).wait_recv()
            x_ref[:, which * X_CUT + at : which * X_CUT + at + width] = total(n - 2 * lag, 3, 0, tall >> 3)
    tile_ref[...] = lax.fori_loop(1, count, add_tile, tiles[me])
    for n in range(pieces):
        for phase in range(3):
            copy(n, phase).wait_send()
    give.wait()


def finish(chains, gconv, gpar, par, gskip, gi, gn, given):
    count = lax.axis_size(AXES)
    operands = [term.value for chain in chains for term, _ in chain.columns[0].terms]
    widths = [chain.columns[0].width for chain in chains]
    tall = chains[0].columns[0].rows
    dma = pltpu.SemaphoreType.DMA
    anywhere = pl.BlockSpec(memory_space=pl.ANY)
    whole = pl.BlockSpec(memory_space=pltpu.VMEM)
    halves = [pltpu.VMEM((tall >> (phase + 1), width), bf16) for phase in range(3) for width in widths]
    pieces = len(X_PIECES)
    return pl.pallas_call(
        functools.partial(finish_kernel, count, lax.axis_size("fsdp")),
        out_shape=(
            jax.ShapeDtypeStruct((tall >> 3, XE), f32),
            jax.ShapeDtypeStruct((TILE_ROWS, 128), f32),
            jax.ShapeDtypeStruct(given.shape, bf16),
        ),
        in_specs=[anywhere] * 6 + [whole] * 6 + [anywhere],
        out_specs=(whole, whole, anywhere),
        scratch_shapes=[
            *(pltpu.VMEM((3, tall, width), bf16) for width in widths),
            *halves,
            *halves,
            pltpu.VMEM((count, TILE_ROWS, 128), f32),
            pltpu.VMEM((count, TILE_ROWS, 128), f32),
            dma((pieces, 3)),
            dma((pieces, 3)),
            dma((pieces, 3)),
            dma((count,)),
            dma((count,)),
            dma,
            dma,
        ],
        compiler_params=params(has_side_effects=True),
        cost_estimate=cost(1e7, 2e7),
        name="finish",
    )(*operands, gconv, gpar, par, gskip, gi, gn, given)


def on_device(
    tokens, cotangent, lengths, balance, norm_gain, in_weight, conv_weight, conv_bias,
    step_bias, decay_log, skip_weight, inner_gain, out_weight,
):
    device = lax.axis_index(AXES)
    count = lax.axis_size(AXES)
    slot = tokens.shape[1]
    rows = 2 * slot
    first_source = balance[2 * device]
    second_source = balance[2 * device + 1]
    keep_second = first_source - 2 * device == 1
    cot = cotangent.reshape(rows, D)
    lens = [lengths[first_source], lengths[second_source]]
    chunks = [(n + Q - 1) // Q for n in lens]
    grouped = is_grouped()
    meta = jnp.stack([chunks[0] + chunks[1], chunks[0], lens[0], lens[1]]).astype(jnp.int32)

    sizes = [v.shape[0] for v in (norm_gain, inner_gain)]
    if grouped:
        flag = keep_second.astype(jnp.int32).reshape(1, 1)
        w1, wc, g1, g2, u = gather(
            flag, in_weight, norm_gain[None], conv_weight.T, conv_bias[None], inner_gain[None], tokens
        )
    else:
        outgoing = jnp.where(keep_second, tokens[0], tokens[1])
        incoming = partner(outgoing, "dp", 0)
        u = jnp.concatenate([jnp.where(keep_second, tokens[1], tokens[0]), incoming], axis=0)
        w1 = lax.all_gather(in_weight.astype(bf16), AXES, axis=0, tiled=True)
        small = [norm_gain, inner_gain, conv_bias, conv_weight.reshape(-1)]
        packed = jnp.concatenate(small).astype(bf16)
        packed = lax.all_gather(packed[None, :], AXES, axis=0, tiled=True).astype(f32)
        cuts = [sum(v.shape[0] for v in small[:n]) for n in range(5)]
        g1, g2, bias, taps = (packed[:, cuts[n] : cuts[n + 1]].reshape(1, -1) for n in range(4))
        wc = jnp.concatenate([taps.reshape(XBC, CONV).T, bias, jnp.zeros((3, XBC), f32)])
    w2_own, w1 = lax.optimization_barrier([out_weight.astype(bf16), w1])
    w2 = lax.all_gather(w2_own, AXES, axis=0, tiled=True)

    rate = -jnp.exp(decay_log)
    par = jnp.zeros((8, 128), f32).at[0, :HEADS].set(step_bias).at[1, :HEADS].set(rate)
    skip = jnp.repeat(skip_weight, HEADDIM)[None]

    proj, e, ht = project(meta, u, g1, w1)
    o, ot, y, sin, err = mixer(meta, proj, e, cot, wc, par, skip, g2)
    never = 1 << 20

    def both(width):
        return [Columns(width // 2, False), Columns(width // 2, True)]

    halves = weight_grad(meta, ot, err, 0, D, D // 2, 1 if grouped else never)
    c_out = Chain(halves, both(D), grouped)
    meta = tick(meta, [c_out], err)
    out, dy, dz, gi = gate(meta, u, err, w2, o, y, proj, g2)
    meta = tick(meta, [c_out], gi)
    halves = weight_grad(meta, ht, dz, 0, INNER, INNER // 4, 2 if grouped else never)
    c_z = Chain(halves, both(INNER), grouped)
    parts = 3
    carried = ()
    for part in range(parts):
        meta = tick(meta, [c_out, c_z] if part > 0 else [c_z], carried[2] if part > 0 else gi)
        carried = back(meta, part, parts, carried, proj, e, dy, sin, wc, par, skip)
    dx, gconv, gpar, gskip = carried
    meta = tick(meta, [c_out, c_z], gpar)
    cut = X_CUT
    halves = weight_grad(meta, ht, dx, 0, cut, cut // 2, never)
    c_x = Chain(halves, [Columns(cut, False)], grouped)
    meta = tick(meta, [c_z, c_x], halves[1])
    halves = weight_grad(meta, ht, dx, cut, XE - cut, cut // 2, 0 if grouped else never)
    c_x1 = Chain(halves, [Columns(XE - cut, True)], grouped)
    meta = tick(meta, [c_x, c_x1], halves[1])
    meta = tick(meta, [c_x1], c_x1.columns[0].terms[-1][0].value)
    kept_half, given_half, gn = input_grad_of(meta, u, err, g1, dz, dx, w1)
    conv_each = XBC // count
    if grouped:
        late = [chain.columns[0].terms[-1][0] for chain in (c_out, c_z)]
        *came, gn = lax.optimization_barrier([term.value for term in late] + [gn])
        for term, value in zip(late, came):
            term.value = value
        grad_x, tile, back_half = finish([c_x, c_x1], gconv, gpar, par, gskip, gi, gn, given_half)
        grad_x = [grad_x]
        grad_conv, grad_bias = tile[:CONV, :conv_each].T, tile[CONV, :conv_each]
        grad_inner, grad_norm = tile[8, : sizes[1]], tile[9, : sizes[0]]
        heads = [tile[10 + n, :HEADS] for n in range(3)]
    else:
        back_half = partner(given_half, "dp", 0)
        heads = jnp.concatenate(
            [gpar[0, :HEADS], gpar[1, :HEADS] * rate, gskip.reshape(HEADS, HEADDIM).sum(axis=1)]
        )
        owned = [gconv[:CONV].T.reshape(count, -1), gconv[CONV].reshape(count, -1), gi.reshape(count, -1)]
        tiles = jnp.concatenate(owned + [jnp.broadcast_to(heads, (count, 3 * HEADS)), gn.reshape(count, -1)], axis=1)
        tiles = jnp.pad(tiles, ((0, 0), (0, 1024 - tiles.shape[1]))).reshape(count, 8, 128)
        sums = sum_small(tiles).reshape(-1)
        grad_x = c_x.finish() + c_x1.finish()
        ends = [sum(v.shape[1] for v in owned[:n]) for n in range(4)]
        grad_conv = sums[: ends[1]].reshape(-1, CONV)
        grad_bias = sums[ends[1] : ends[2]]
        grad_inner = sums[ends[2] : ends[3]]
        heads = sums[ends[3] : ends[3] + 3 * HEADS].reshape(3, HEADS)
        grad_norm = sums[ends[3] + 3 * HEADS :][: sizes[0]]
    grad_out = jnp.concatenate(c_out.finish(), axis=1)
    grad_in = jnp.concatenate(c_z.finish() + grad_x, axis=1)[:, :PROJ]
    swapped = [jnp.stack([back_half, kept_half]), jnp.stack([kept_half, back_half])]
    input_grad = jnp.where(keep_second, *swapped)
    return (
        out.reshape(2, slot, D),
        input_grad,
        grad_norm,
        grad_in,
        grad_conv,
        grad_bias,
        heads[0],
        heads[1],
        heads[2],
        grad_inner,
        grad_out,
    )


def solution(mesh):
    flat = P(AXES)
    rowed = P(AXES, None)
    slots = P(AXES, None, None)
    return jax.shard_map(
        on_device,
        mesh=mesh,
        in_specs=(slots, slots, P(), P(), flat, rowed, rowed, flat, P(), P(), P(), flat, rowed),
        out_specs=(slots, slots, flat, rowed, rowed, flat, P(), P(), P(), flat, rowed),
        check_vma=False,
    )
```
